32 devices in a mesh: tower: 2 (over y), dp: 16 (over z, x, core).
Axes of the slice: x: 2, y: 2, z: 4, core: 2. Of those that a mesh axis runs over, the one named last changes fastest.
Arguments:
- tokens: bfloat16 [2, 4096, 768], P('tower', 'dp'), may hold values from -6 to 6
- query_lengths: int32 [64], P('dp'), may hold values from 8 to 64, as said below
- doc_lengths: int32 [16], P('dp'), may hold values from 32 to 256, as said below
- positives: int32 [64], replicated, may hold values from 0 to 15
- w_qkv: bfloat16 [768, 2304], P('dp'), may hold values from -0.21875 to 0.21875
- w_out: bfloat16 [768, 768], P('dp'), may hold values from -0.21875 to 0.21875
- w_gate: bfloat16 [768, 3072], P('dp'), may hold values from -0.21875 to 0.21875
- w_up: bfloat16 [768, 3072], P('dp'), may hold values from -0.21875 to 0.21875
- w_down: bfloat16 [3072, 768], P('dp'), may hold values from -0.109375 to 0.109375
- ln1_gain: bfloat16 [768], P('dp'), may hold values from 0.5 to 1.5
- first_layernorm_shift: bfloat16 [768], P('dp'), may hold values from -0.59765625 to 0.59765625
- ln2_gain: bfloat16 [768], P('dp'), may hold values from 0.5 to 1.5
- ln2_bias: bfloat16 [768], P('dp'), may hold values from -0.6 to 0.6
Outputs:
- loss: float32 [], replicated
- query_embeddings: float32 [64, 768], P('dp')
- doc_embeddings: float32 [16, 768], P('dp')
- token_grad: float32 [2, 4096, 768], P('tower', 'dp')
- w_qkv_grad: float32 [768, 2304], P('dp')
- w_out_grad: float32 [768, 768], P('dp')
- w_gate_grad: float32 [768, 3072], P('dp')
- w_up_grad: float32 [768, 3072], P('dp')
- w_down_grad: float32 [3072, 768], P('dp')
- ln1_gain_grad: float32 [768], P('dp')
- ln1_bias_grad: float32 [768], P('dp')
- ln2_gain_grad: float32 [768], P('dp')
- ln2_bias_grad: float32 [768], P('dp')
The draws below stay inside these ranges and needn't reach their ends.
Inputs may be any that keep to these rules, and one draw needn't show every extreme that they name: `query_lengths`: each query has 8 to 64 real tokens in the first slots of its block; some query has 64. `doc_lengths`: each document has 32 to 256 real tokens in the first slots; some document has 256.
All inputs are finite; a program needn't handle non-finite values.
Results may differ from the reference program's by a relative error of at most 0.0085.
Values may be sent and summed in bfloat16 or wider, within the bound.
A program may use at most 128 MiB of HBM per device.

```python
import jax
import jax.numpy as jnp
from jax import lax

D = 768
HEADS = 12
HEAD = 64
FF = 3072
QLEN = 64
TOK_DEV = 256
QPD = 4
ROWS = 4096
QUERIES = 64
DOCS = 16
N_DP = 16


def draw_tokens(key, part):
    first_key, second_key, third_key = jax.random.split(jax.random.fold_in(key, 11), 3)
    common_query = jax.random.normal(first_key, (QUERIES, D), jnp.float32)
    common_doc = jax.random.normal(second_key, (DOCS, D), jnp.float32)
    common = jnp.stack([jnp.repeat(common_query, QLEN, axis=0), jnp.repeat(common_doc, TOK_DEV, axis=0)], 0)
    noise = jax.random.normal(third_key, (2, ROWS, D), jnp.float32)
    return jnp.clip(0.8 * common + 0.6 * noise, -6.0, 6.0).astype(jnp.bfloat16)


def draw_query_lengths(key, part):
    first_key, second_key = jax.random.split(jax.random.fold_in(key, 23))
    token_counts_each = jax.random.randint(first_key, (QUERIES,), QLEN // 8, QLEN + 1)
    chosen = jax.random.randint(second_key, (), 0, QUERIES)
    return jnp.where(jnp.arange(QUERIES) == chosen, QLEN, token_counts_each).astype(jnp.int32)


def draw_doc_lengths(key, part):
    first_key, second_key = jax.random.split(jax.random.fold_in(key, 37))
    token_counts_each = jax.random.randint(first_key, (DOCS,), TOK_DEV // 8, TOK_DEV + 1)
    chosen = jax.random.randint(second_key, (), 0, DOCS)
    return jnp.where(jnp.arange(DOCS) == chosen, TOK_DEV, token_counts_each).astype(jnp.int32)


def draw_ln2_bias(key, part):
    first_key, second_key = jax.random.split(jax.random.fold_in(key, 53))
    signs = jnp.where(jax.random.bernoulli(first_key, 0.5, (D,)), 1.0, -1.0).astype(jnp.float32)
    magnitude = jax.random.uniform(second_key, (D,), jnp.float32, 0.4, 0.59765625)
    return (signs * magnitude).astype(jnp.bfloat16)


def place_ends(array, own_key, smallest, largest):
    longest = array.shape.index(max(array.shape))
    spots = []
    for shift in (0, 1):
        where = [jax.random.randint(jax.random.fold_in(own_key, axis), (), 0, length) for axis, length in enumerate(array.shape)]
        where[longest] = (where[longest] + shift) % array.shape[longest]
        spots.append(tuple(where))
    return array.at[spots[0]].set(smallest).at[spots[1]].set(largest)


def shard_levels(own_key, dims, shards, low, largest):
    factor_of, own = 1.0, jax.random.fold_in(own_key, 6)
    for axis_at, blocks in shards:
        draws = jnp.exp(jax.random.uniform(jax.random.fold_in(own, axis_at), (blocks,), jnp.float32, low / len(shards), largest / len(shards)))
        factor_of = factor_of * jnp.repeat(draws, dims[axis_at] // blocks).reshape([-1 if axis == axis_at else 1 for axis in range(len(dims))])
    return factor_of


def bell_draw(key, dims, scale, most, pieces=(), kind=jnp.bfloat16):
    array = scale * jax.random.normal(key, dims, jnp.float32)
    if pieces:
        array = array * shard_levels(key, dims, pieces, -0.22, 0.18)
    return jnp.clip(array, -most, most).astype(kind)


def setup_inputs(seed: int = 0) -> dict:
    key_of = jax.random.split(jax.random.key(seed), 14)
    return {
        "tokens": draw_tokens(jax.random.fold_in(key_of[13], 71), 0),
        "query_lengths": draw_query_lengths(jax.random.fold_in(key_of[13], 71), 0),
        "doc_lengths": draw_doc_lengths(jax.random.fold_in(key_of[13], 71), 0),
        "positives": place_ends(jax.random.randint(key_of[3], (QUERIES,), 0, DOCS), jax.random.fold_in(key_of[3], 1), 0, DOCS - 1).astype(jnp.int32),
        "w_qkv": bell_draw(key_of[4], (D, 3 * D), D ** -0.5, 0.21875, ((0, 16),)),
        "w_out": bell_draw(key_of[5], (D, D), D ** -0.5, 0.21875, ((0, 16),)),
        "w_gate": bell_draw(key_of[6], (D, FF), D ** -0.5, 0.21875, ((0, 16),)),
        "w_up": bell_draw(key_of[7], (D, FF), D ** -0.5, 0.21875, ((0, 16),)),
        "w_down": bell_draw(key_of[8], (FF, D), FF ** -0.5, 0.109375, ((0, 16),)),
        "ln1_gain": jnp.clip(1.0 + 0.1 * jax.random.normal(key_of[9], (D,), jnp.float32), 0.5, 1.5).astype(jnp.bfloat16),
        "first_layernorm_shift": bell_draw(key_of[10], (D,), 0.1, 0.59765625, ((0, 16),)),
        "ln2_gain": jnp.clip(1.0 + 0.1 * jax.random.normal(key_of[11], (D,), jnp.float32), 0.5, 1.5).astype(jnp.bfloat16),
        "ln2_bias": draw_ln2_bias(jax.random.fold_in(key_of[13], 71), 0),
    }


exact_product_accuracy = lax.Precision.HIGHEST
rope_base = 1000.0
contrast_sharpness_factor = 0.02

@jax.custom_vjp
def low(v):
    return lax.optimization_barrier(v.astype(jnp.bfloat16)).astype(jnp.float32)

@jax.custom_vjp
def low_back(v):
    return v

def low_keep(v):
    return (low(v), None)

def low_pass(kept, grad):
    return (grad,)

def back_keep(v):
    return (v, None)

def back_low(kept, grad):
    return (low(grad),)
low.defvjp(low_keep, low_pass)
low_back.defvjp(back_keep, back_low)

def rotary_tables(places):
    freqs = jnp.power(rope_base, -2.0 * jnp.arange(HEAD // 2).astype(jnp.float32) / HEAD)
    angles = places[:, None] * freqs[None, :]
    return (jnp.cos(angles)[:, None, :], jnp.sin(angles)[:, None, :])

def rotate(values, cosines, sines):
    half_dim = values.shape[-1] // 2
    first = values[..., :half_dim]
    second = values[..., half_dim:]
    return jnp.concatenate([first * cosines - second * sines, second * cosines + first * sines], axis=-1)

def layer_norm(hidden, gain, offset):
    average = lax.optimization_barrier(jnp.mean(hidden, -1, keepdims=True))
    centred = hidden - average
    variance = lax.optimization_barrier(jnp.mean(centred * centred, -1, keepdims=True))
    return centred * lax.rsqrt(variance + 1e-05) * gain + offset

def normalize(pooled):
    return pooled * lax.rsqrt(lax.optimization_barrier(jnp.sum(pooled * pooled, -1, keepdims=True)) + 1e-06)

def layout(tower_id, query_len, doc_len, count):
    places = jnp.arange(count).astype(jnp.int32)
    span = jnp.where(tower_id == 0, QLEN, count)
    segment = places // span
    offset_in = places - segment * span
    slots = jnp.arange(QPD).astype(jnp.int32)
    seg_limit = jnp.where(tower_id == 0, query_len, doc_len[0] * jnp.ones_like(query_len))
    limit = lax.optimization_barrier(jnp.sum(jnp.where(segment[:, None] == slots[None, :], seg_limit[None, :], 0), axis=1))
    valid = offset_in < limit
    allowed = (segment[:, None] == segment[None, :]) & valid[None, :]
    member = (segment[None, :] == slots[:, None]) & valid[None, :]
    pool_matrix = jnp.where(member, 1.0 / seg_limit[:, None].astype(jnp.float32), 0.0)
    return (offset_in.astype(jnp.float32), allowed, pool_matrix)

def block_forward(inputs, tower_id, query_len, doc_len, params):
    w_qkv, w_out, w_gate, w_up, w_down, gain_one, bias_one, gain_two, bias_two = params
    count = inputs.shape[0]
    places, allowed, pool_matrix = layout(tower_id, query_len, doc_len, count)
    cosines, sines = rotary_tables(places)
    packed = low_back(jnp.dot(inputs, w_qkv, precision=exact_product_accuracy))
    queries = low(rotate(packed[:, :D].reshape(count, HEADS, HEAD), cosines, sines))
    keys = low(rotate(packed[:, D:2 * D].reshape(count, HEADS, HEAD), cosines, sines))
    values = low(packed[:, 2 * D:].reshape(count, HEADS, HEAD))
    scores = low_back(jnp.einsum('ihd,jhd->hij', queries, keys, precision=exact_product_accuracy) * HEAD ** (-0.5))
    scores = jnp.where(allowed[None], scores, -1e+30)
    peak = lax.optimization_barrier(jnp.max(scores, -1, keepdims=True))
    total_exp = lax.optimization_barrier(jnp.sum(jnp.exp(scores - peak), -1, keepdims=True))
    probs = low(jnp.exp(scores - (peak + jnp.log(total_exp))))
    mixed = jnp.einsum('hij,jhd->ihd', probs, values, precision=exact_product_accuracy).reshape(count, D)
    mixed = low(low_back(mixed))
    attended = low_back(jnp.dot(mixed, w_out, precision=exact_product_accuracy))
    normed_one = layer_norm(inputs + attended, gain_one, bias_one)
    feed = low(normed_one)
    gate = low_back(jnp.dot(feed, w_gate, precision=exact_product_accuracy))
    up_part = low_back(jnp.dot(feed, w_up, precision=exact_product_accuracy))
    hidden = low(jax.nn.silu(gate) * up_part)
    branch = low_back(jnp.dot(hidden, w_down, precision=exact_product_accuracy))
    normed_two = layer_norm(normed_one + branch, gain_two, bias_two)
    return jnp.dot(pool_matrix, normed_two, precision=exact_product_accuracy)

def reference(tokens, query_lengths, doc_lengths, positives, w_qkv, w_out, w_gate, w_up, w_down, ln1_gain, first_layernorm_shift, ln2_gain, ln2_bias):
    towers = jnp.repeat(jnp.arange(2), N_DP).astype(jnp.int32)
    query_table = jnp.tile(query_lengths.reshape(N_DP, QPD), (2, 1))
    doc_table = jnp.tile(doc_lengths.reshape(N_DP, 1), (2, 1))
    blocks = tokens.astype(jnp.float32).reshape(2 * N_DP, TOK_DEV, D)
    params = tuple((item.astype(jnp.float32) for item in (w_qkv, w_out, w_gate, w_up, w_down, ln1_gain, first_layernorm_shift, ln2_gain, ln2_bias)))

    def objective(block_inputs, weights):

        def one_block(item):
            inputs, tower_id, query_len, doc_len = item
            return block_forward(inputs, tower_id, query_len, doc_len, weights)
        pooled = lax.map(jax.checkpoint(one_block), (block_inputs, towers, query_table, doc_table))
        question_embedding_matrix = normalize(pooled[:N_DP].reshape(QUERIES, D))
        passage_embedding_matrix = normalize(pooled[N_DP:, 0])
        pairwise_affinity_matrix = jnp.dot(question_embedding_matrix, passage_embedding_matrix.T, precision=exact_product_accuracy) / contrast_sharpness_factor
        peak = lax.optimization_barrier(jnp.max(pairwise_affinity_matrix, -1, keepdims=True))
        log_partition_norm = peak[:, 0] + jnp.log(lax.optimization_barrier(jnp.sum(jnp.exp(pairwise_affinity_matrix - peak), -1)))
        columns = jnp.arange(DOCS).astype(jnp.int32)
        picked = lax.optimization_barrier(jnp.sum(jnp.where(columns[None, :] == positives[:, None], pairwise_affinity_matrix, 0.0), -1))
        total = jnp.sum(log_partition_norm - picked)
        return (total, (question_embedding_matrix, passage_embedding_matrix))
    total, backward, extras = jax.vjp(objective, blocks, params, has_aux=True)
    block_grad, param_grad = backward(jnp.ones_like(total))
    question_embedding_matrix, passage_embedding_matrix = extras
    loss = total / QUERIES
    return (loss, question_embedding_matrix, passage_embedding_matrix, block_grad.reshape(2, ROWS, D), param_grad[0], param_grad[1], param_grad[2], param_grad[3], param_grad[4], param_grad[5], param_grad[6], param_grad[7], param_grad[8])
```

```python
import functools
from types import SimpleNamespace
from typing import Any, NamedTuple

import jax
import jax.numpy as jnp
import numpy as np
from jax import lax
from jax.experimental import pallas as pl
from jax.experimental.pallas import tpu as pltpu
from jax.sharding import PartitionSpec as P

TOWER = "tower"
DP = "dp"
D = 768
HEADS = 12
HEAD = 64
QLEN = 64
QPD = 4


exact_product_accuracy = lax.Precision.HIGHEST
rope_base = 1000.0
contrast_sharpness_factor = 0.02


def product(left, right):
    return jnp.dot(left, right, preferred_element_type=jnp.float32)


def rotary_tables(places):
    freqs = jnp.power(rope_base, -2.0 * jnp.arange(HEAD // 2).astype(jnp.float32) / HEAD)
    angles = places[:, None] * freqs[None, :]
    return (jnp.cos(angles)[:, None, :], jnp.sin(angles)[:, None, :])


def rotate(values, cosines, sines):
    half_dim = values.shape[-1] // 2
    first = values[..., :half_dim]
    second = values[..., half_dim:]
    return jnp.concatenate(
        [first * cosines - second * sines, second * cosines + first * sines], axis=-1
    )


def layer_norm(hidden, gain, offset):
    average = jnp.mean(hidden, -1, keepdims=True)
    centred = hidden - average
    variance = jnp.mean(centred * centred, -1, keepdims=True)
    return centred * lax.rsqrt(variance + 1e-05) * gain + offset


def normalize(pooled):
    return pooled * lax.rsqrt(jnp.sum(pooled * pooled, -1, keepdims=True) + 1e-06)


def layout(tower_id, query_len, doc_len, count):
    places = jnp.arange(count)
    span = jnp.where(tower_id == 0, QLEN, count)
    segment = places // span
    offset_in = places - segment * span
    slots = jnp.arange(QPD)
    seg_limit = jnp.where(tower_id == 0, query_len, doc_len[0] * jnp.ones_like(query_len))
    limit = jnp.sum(jnp.where(segment[:, None] == slots[None, :], seg_limit[None, :], 0), axis=1)
    valid = offset_in < limit
    allowed = (segment[:, None] == segment[None, :]) & valid[None, :]
    member = (segment[None, :] == slots[:, None]) & valid[None, :]
    pool_matrix = jnp.where(member, 1.0 / seg_limit[:, None].astype(jnp.float32), 0.0)
    return (offset_in.astype(jnp.float32), allowed, pool_matrix)


def swish_product(left, right):
    return jax.nn.silu(left) * right


def on_device(
    tokens,
    query_lengths,
    doc_lengths,
    positives,
    w_qkv,
    w_out,
    w_gate,
    w_up,
    w_down,
    ln1_gain,
    first_layernorm_shift,
    ln2_gain,
    ln2_bias,
):
    tower_id = lax.axis_index(TOWER)
    device_id = lax.axis_index(DP)
    groups = lax.axis_size(DP)
    full = (
        lax.all_gather(w_qkv, DP, axis=0, tiled=True),
        lax.all_gather(w_out, DP, axis=0, tiled=True),
        lax.all_gather(w_gate, DP, axis=0, tiled=True),
        lax.all_gather(w_up, DP, axis=0, tiled=True),
        lax.all_gather(w_down, DP, axis=0, tiled=True),
        lax.all_gather(ln1_gain, DP, axis=0, tiled=True),
        lax.all_gather(first_layernorm_shift, DP, axis=0, tiled=True),
        lax.all_gather(ln2_gain, DP, axis=0, tiled=True),
        lax.all_gather(ln2_bias, DP, axis=0, tiled=True),
    )
    qkv_full, out_full, gate_full, up_full, down_full = (
        full[0],
        full[1],
        full[2],
        full[3],
        full[4],
    )
    gain_one = full[5].astype(jnp.float32)
    bias_one = full[6].astype(jnp.float32)
    gain_two = full[7].astype(jnp.float32)
    bias_two = full[8].astype(jnp.float32)
    inputs = tokens[0]
    count = inputs.shape[0]
    places, allowed, pool_matrix = layout(tower_id, query_lengths, doc_lengths, count)
    cosines, sines = rotary_tables(places)
    packed = product(inputs, qkv_full)
    raw_query = packed[:, :D].reshape(count, HEADS, HEAD)
    raw_key = packed[:, D : 2 * D].reshape(count, HEADS, HEAD)

    def rotate_both(first, second):
        return (rotate(first, cosines, sines), rotate(second, cosines, sines))

    rotated, rotary_back = jax.vjp(rotate_both, raw_query, raw_key)
    query_low = rotated[0].astype(jnp.bfloat16)
    key_low = rotated[1].astype(jnp.bfloat16)
    value_low = packed[:, 2 * D :].reshape(count, HEADS, HEAD).astype(jnp.bfloat16)
    scale = HEAD ** (-0.5)

    def masked_scores():
        scores = (
            jnp.einsum("ihd,jhd->hij", query_low, key_low, preferred_element_type=jnp.float32)
            * scale
        )
        return jnp.where(allowed[None], scores, -1e30)

    scores = masked_scores()
    peak = jnp.max(scores, -1, keepdims=True)
    log_total = peak + jnp.log(jnp.sum(jnp.exp(scores - peak), -1, keepdims=True))
    probs_low = jnp.exp(scores - log_total).astype(jnp.bfloat16)
    mixed = jnp.einsum("hij,jhd->ihd", probs_low, value_low, preferred_element_type=jnp.float32)
    mixed_low = mixed.reshape(count, D).astype(jnp.bfloat16)
    attended = product(mixed_low, out_full)
    inputs_wide = inputs.astype(jnp.float32)
    normed_one, norm_one_back = jax.vjp(layer_norm, inputs_wide + attended, gain_one, bias_one)
    feed = normed_one.astype(jnp.bfloat16)
    gate = product(feed, gate_full)
    up_part = product(feed, up_full)
    hidden_wide, swish_back = jax.vjp(swish_product, gate, up_part)
    hidden = hidden_wide.astype(jnp.bfloat16)
    branch = product(hidden, down_full)
    normed_two, norm_two_back = jax.vjp(layer_norm, normed_one + branch, gain_two, bias_two)
    pooled = jnp.dot(pool_matrix, normed_two, precision=exact_product_accuracy)
    embedded, normal_back = jax.vjp(normalize, pooled)
    gathered = lax.all_gather(embedded, (TOWER, DP), axis=0, tiled=True)
    queries_total = groups * QPD
    gathered_query_rows = gathered[:queries_total]
    gathered_document_rows = gathered[queries_total:].reshape(groups, QPD, D)[:, 0]
    pairwise_affinity_matrix = (
        jnp.dot(gathered_query_rows, gathered_document_rows.T, precision=exact_product_accuracy)
        / contrast_sharpness_factor
    )
    peak_logit = jnp.max(pairwise_affinity_matrix, -1, keepdims=True)
    log_partition_norm = peak_logit + jnp.log(
        jnp.sum(jnp.exp(pairwise_affinity_matrix - peak_logit), -1, keepdims=True)
    )
    columns = lax.broadcasted_iota(jnp.int32, pairwise_affinity_matrix.shape, 1)
    matching_labels = columns == positives[:, None]
    picked = jnp.sum(jnp.where(matching_labels, pairwise_affinity_matrix, 0.0), -1, keepdims=True)
    total = jnp.sum(log_partition_norm - picked)
    loss = total / queries_total
    similarity_gradient = (
        jnp.exp(pairwise_affinity_matrix - log_partition_norm) - matching_labels.astype(jnp.float32)
    ) / contrast_sharpness_factor
    own_rows = lax.dynamic_slice_in_dim(similarity_gradient, device_id * QPD, QPD, 0)
    query_side = jnp.dot(own_rows, gathered_document_rows, precision=exact_product_accuracy)
    own_column = lax.dynamic_slice_in_dim(similarity_gradient, device_id, 1, 1)
    doc_side = jnp.dot(own_column.T, gathered_query_rows, precision=exact_product_accuracy)
    doc_side = jnp.concatenate([doc_side, jnp.zeros((QPD - 1, D), jnp.float32)], 0)
    embed_grad = jnp.where(tower_id == 0, query_side, doc_side)
    pooled_grad = normal_back(embed_grad)[0]
    top_grad = jnp.dot(pool_matrix.T, pooled_grad, precision=exact_product_accuracy)
    sum_two, gain_two_grad, bias_two_grad = norm_two_back(top_grad)
    attention_input_cotangent, out_back, gate_back, up_back, down_back = (
        qkv_full,
        out_full,
        gate_full,
        up_full,
        down_full,
    )
    branch_low = sum_two.astype(jnp.bfloat16)
    down_grad = product(hidden.T, branch_low)
    hidden_grad = product(branch_low, down_back.T)
    gate_grad_wide, up_grad_wide = swish_back(hidden_grad)
    gate_low = gate_grad_wide.astype(jnp.bfloat16)
    up_low = up_grad_wide.astype(jnp.bfloat16)
    gate_weight_grad = product(feed.T, gate_low)
    up_weight_grad = product(feed.T, up_low)
    feed_grad = sum_two + product(gate_low, gate_back.T) + product(up_low, up_back.T)
    sum_one, gain_one_grad, bias_one_grad = norm_one_back(feed_grad)
    attend_low = sum_one.astype(jnp.bfloat16)
    out_grad = product(mixed_low.T, attend_low)
    mixed_grad = product(attend_low, out_back.T).astype(jnp.bfloat16).reshape(count, HEADS, HEAD)
    probs_again = jnp.exp(masked_scores() - log_total)
    prob_grad = jnp.einsum(
        "ihd,jhd->hij", mixed_grad, value_low, preferred_element_type=jnp.float32
    )
    score_grad = probs_again * (prob_grad - jnp.sum(probs_again * prob_grad, -1, keepdims=True))
    score_low = score_grad.astype(jnp.bfloat16)
    query_grad = (
        jnp.einsum("hij,jhd->ihd", score_low, key_low, preferred_element_type=jnp.float32) * scale
    )
    key_grad = (
        jnp.einsum("hij,ihd->jhd", score_low, query_low, preferred_element_type=jnp.float32) * scale
    )
    value_grad = jnp.einsum(
        "hij,ihd->jhd",
        probs_again.astype(jnp.bfloat16),
        mixed_grad,
        preferred_element_type=jnp.float32,
    )
    raw_query_grad, raw_key_grad = rotary_back((query_grad, key_grad))
    packed_grad = jnp.concatenate(
        [
            raw_query_grad.reshape(count, D),
            raw_key_grad.reshape(count, D),
            value_grad.reshape(count, D),
        ],
        1,
    ).astype(jnp.bfloat16)
    qkv_grad = product(inputs.T, packed_grad)
    input_grad = sum_one + product(packed_grad, attention_input_cotangent.T)
    gradients = (
        qkv_grad,
        out_grad,
        gate_weight_grad,
        up_weight_grad,
        down_grad,
        gain_one_grad,
        bias_one_grad,
        gain_two_grad,
        bias_two_grad,
    )
    partial_sums = (
        lax.psum_scatter(gradients[0], DP, scatter_dimension=0, tiled=True),
        lax.psum_scatter(gradients[1], DP, scatter_dimension=0, tiled=True),
        lax.psum_scatter(gradients[2], DP, scatter_dimension=0, tiled=True),
        lax.psum_scatter(gradients[3], DP, scatter_dimension=0, tiled=True),
        lax.psum_scatter(gradients[4], DP, scatter_dimension=0, tiled=True),
        lax.psum_scatter(gradients[5], DP, scatter_dimension=0, tiled=True),
        lax.psum_scatter(gradients[6], DP, scatter_dimension=0, tiled=True),
        lax.psum_scatter(gradients[7], DP, scatter_dimension=0, tiled=True),
        lax.psum_scatter(gradients[8], DP, scatter_dimension=0, tiled=True),
    )
    tower_halves = (
        lax.psum_scatter(
            partial_sums[0].astype(jnp.bfloat16), TOWER, scatter_dimension=0, tiled=True
        ).astype(jnp.float32),
        lax.psum_scatter(
            partial_sums[1].astype(jnp.bfloat16), TOWER, scatter_dimension=0, tiled=True
        ).astype(jnp.float32),
        lax.psum_scatter(
            partial_sums[2].astype(jnp.bfloat16), TOWER, scatter_dimension=0, tiled=True
        ).astype(jnp.float32),
        lax.psum_scatter(
            partial_sums[3].astype(jnp.bfloat16), TOWER, scatter_dimension=0, tiled=True
        ).astype(jnp.float32),
        lax.psum_scatter(
            partial_sums[4].astype(jnp.bfloat16), TOWER, scatter_dimension=0, tiled=True
        ).astype(jnp.float32),
        lax.psum_scatter(
            partial_sums[5].astype(jnp.bfloat16), TOWER, scatter_dimension=0, tiled=True
        ).astype(jnp.float32),
        lax.psum_scatter(
            partial_sums[6].astype(jnp.bfloat16), TOWER, scatter_dimension=0, tiled=True
        ).astype(jnp.float32),
        lax.psum_scatter(
            partial_sums[7].astype(jnp.bfloat16), TOWER, scatter_dimension=0, tiled=True
        ).astype(jnp.float32),
        lax.psum_scatter(
            partial_sums[8].astype(jnp.bfloat16), TOWER, scatter_dimension=0, tiled=True
        ).astype(jnp.float32),
    )
    shares = (
        lax.all_gather(tower_halves[0].astype(jnp.bfloat16), TOWER, axis=0, tiled=True).astype(
            jnp.float32
        ),
        lax.all_gather(tower_halves[1].astype(jnp.bfloat16), TOWER, axis=0, tiled=True).astype(
            jnp.float32
        ),
        lax.all_gather(tower_halves[2].astype(jnp.bfloat16), TOWER, axis=0, tiled=True).astype(
            jnp.float32
        ),
        lax.all_gather(tower_halves[3].astype(jnp.bfloat16), TOWER, axis=0, tiled=True).astype(
            jnp.float32
        ),
        lax.all_gather(tower_halves[4].astype(jnp.bfloat16), TOWER, axis=0, tiled=True).astype(
            jnp.float32
        ),
        lax.all_gather(tower_halves[5].astype(jnp.bfloat16), TOWER, axis=0, tiled=True).astype(
            jnp.float32
        ),
        lax.all_gather(tower_halves[6].astype(jnp.bfloat16), TOWER, axis=0, tiled=True).astype(
            jnp.float32
        ),
        lax.all_gather(tower_halves[7].astype(jnp.bfloat16), TOWER, axis=0, tiled=True).astype(
            jnp.float32
        ),
        lax.all_gather(tower_halves[8].astype(jnp.bfloat16), TOWER, axis=0, tiled=True).astype(
            jnp.float32
        ),
    )
    query_rows = lax.dynamic_slice_in_dim(gathered_query_rows, device_id * QPD, QPD, 0)
    doc_row = lax.dynamic_slice_in_dim(gathered_document_rows, device_id, 1, 0)
    return (loss, query_rows, doc_row, input_grad[None]) + tuple(shares)


MESH = pl.DeviceIdType.MESH
BF = jnp.bfloat16
F32 = jnp.float32
LANES = 128


def dot_tt(left, right, precision=None):
    return lax.dot_general(
        left, right, (((1,), (1,)), ((), ())), preferred_element_type=F32, precision=precision
    )


def dot_t0(left, right):
    return lax.dot_general(left, right, (((0,), (0,)), ((), ())), preferred_element_type=F32)


def rotary_constants(count):
    freqs = np.power(
        np.float32(rope_base), (-2.0 * np.arange(HEAD // 2) / HEAD).astype(np.float32)
    ).astype(np.float32)
    angles = (np.arange(count, dtype=np.float32)[:, None] * freqs[None, :]).astype(np.float64)
    cosines, sines = np.cos(angles), np.sin(angles)
    return (
        np.tile(np.concatenate([cosines, cosines], 1), (1, 2)).astype(np.float32),
        np.tile(np.concatenate([-sines, sines], 1), (1, 2)).astype(np.float32),
    )


def aligned(start, unit):
    return start if isinstance(start, int) else pl.multiple_of(start, unit)


def both(first, second):
    return jnp.logical_and(first, second)


def do(condition, action):
    if condition is None:
        action()
    else:
        pl.when(condition)(action)


class Plan:
    def __init__(self, groups, count, shard, shard_ff, vec):
        self.groups = groups
        self.line = groups // 4
        self.count = count
        self.shard = shard
        self.shard_ff = shard_ff
        self.vec = vec
        self.width_a = 4 * D
        self.half_a = 2 * D
        self.ff = shard_ff * groups
        self.half_ff = self.ff // 2
        self.stripe = 2 * shard_ff


def semaphores(plan):
    line, groups = plan.line, plan.groups
    dma = pltpu.SemaphoreType.DMA
    chunks_gu, chunks_a = 4, 4
    return dict(
        loc=dma((20,)),
        ra=dma((groups, 2)),
        sa_z=dma((2, line)),
        sa_x=dma((line,)),
        sa_y=dma((line, 2)),
        sa_c=dma((line, 2, 2)),
        rg=dma((groups,)),
        sg_z=dma((2, line)),
        sg_x=dma((line,)),
        sg_c=dma((line, 2)),
        rd=dma((line, 2)),
        sd_x=dma((1,)),
        sd_z=dma((2, line)),
        sd_c=dma((line,)),
        rv=dma((groups,)),
        sv=dma((groups,)),
        sx=dma((4,)),
        rx=dma((4,)),
        r_doc=dma((groups,)),
        s_doc=dma((2, groups)),
        r_query=dma((groups,)),
        s_query=dma((groups,)),
        s_loss=dma((1,)),
        r_loss=dma((1,)),
        s_ln=dma((line.bit_length() + 2,)),
        r_ln=dma((line.bit_length() + 2,)),
        gd_c=dma((2, line)),
        gd_z=dma((2, 2, line)),
        gd_x=dma((2,)),
        gd_y=dma((2,)),
        gg_c=dma((2, chunks_gu)),
        gg_x=dma((2, chunks_gu)),
        gg_z=dma((2, chunks_gu, 2, line)),
        gg_y=dma((2, chunks_gu)),
        ga_c=dma((2, 2, chunks_a)),
        ga_t=dma((2, chunks_a)),
        ga_x=dma((2, chunks_a)),
        ga_z=dma((2, chunks_a, 2, line)),
        ga_y=dma((2, chunks_a)),
        fin=dma((9,)),
    )


def buffers(plan):
    line, count, shard, groups = plan.line, plan.count, plan.shard, plan.groups
    pair = 2 * count
    v = pltpu.VMEM
    return dict(
        wa=v((line, 2, 2, shard, plan.width_a), BF),
        wg=v((line, 2, 2, shard, plan.ff), BF),
        wd=v((line, 2, plan.shard_ff, D), BF),
        vt=v((groups, 16, LANES), BF),
        vec=v((16, D), F32),
        cos=v((count, LANES), F32),
        sin=v((count, LANES), F32),
        hide=v((count, count), F32),
        pw=v((count, 1), F32),
        qkv=v((count, 3 * D), BF),
        probs=v((HEADS, count, count), F32),
        mixed=v((count, D), BF),
        mixt=v((D, count), BF),
        tokt=v((D, count), BF),
        h1=v((count, D), F32),
        rs1=v((count, 1), F32),
        n1=v((count, D), F32),
        feed=v((pair, D), BF),
        feedt=v((D, pair), BF),
        gate=v((pair, plan.half_ff), F32),
        up=v((pair, plan.half_ff), F32),
        hidt=v((plan.half_ff, pair), BF),
        dgu=v((pair, plan.ff), BF),
        bown=v((count, D), F32),
        bsend=v((count, D), BF),
        brecv=v((count, D), BF),
        xh2=v((count, D), F32),
        rs2=v((count, 1), F32),
        dbr=v((pair, D), BF),
        dsend=v((count, D), BF),
        drecv=v((count, D), BF),
        datt=v((count, D), BF),
        pool=v((8, D), F32),
        dpool=v((8, D), F32),
        emb=v((8, D), F32),
        embd=v((1, D), F32),
        embq=v((QPD, D), F32),
        dbuf=v((groups, 1, D), F32),
        qbuf=v((groups, QPD, D), F32),
        dflat=v((groups, D), F32),
        qflat=v((groups * QPD, D), F32),
        loss=v((8, LANES), F32),
        lossr=v((8, LANES), F32),
        ln=v((line.bit_length() + 3, 8, D), F32),
        lnr=v((line.bit_length() + 2, 8, D), F32),
        gd=v((line, 2, plan.shard_ff, D), BF),
        gd_rc=v((line, plan.shard_ff, D), BF),
        gd_rz=v((line + 1, plan.shard_ff, D), BF),
        gd_rx=v((plan.shard_ff, D), BF),
        gd_f=v((plan.shard_ff, D), BF),
        gg=v((line, 2, 2, shard, plan.ff), BF),
        gg_rc=v((line, 2, shard, plan.ff), BF),
        gg_rx=v((line, shard, plan.ff), BF),
        gg_rz=v((line + 1, shard, plan.ff), BF),
        gg_f=v((shard, plan.ff), BF),
        ga_rc=v((line, 2, shard, plan.width_a), BF),
        ga_rt=v((line, 2, shard, plan.half_a), BF),
        ga_rx=v((line, shard, plan.half_a), BF),
        ga_rz=v((line + 1, shard, plan.half_a), BF),
        ga_f=v((shard, plan.half_a), BF),
    )


class Operands(NamedTuple):
    qlen: Any
    dlen: Any
    pos: Any
    posv: Any
    tok: Any
    tcos: Any
    tsin: Any
    tile: Any
    i_qkv: Any
    i_out: Any
    i_gate: Any
    i_up: Any
    i_down: Any


class Results(NamedTuple):
    o_tok: Any
    o_a: Any
    o_gu: Any
    o_dn: Any
    o_vec: Any
    o_q: Any
    o_d: Any
    o_loss: Any


def whole_step(plan, *refs):
    names = (Operands._fields + Results._fields + tuple(buffers(plan)) + tuple(semaphores(plan)))
    r = SimpleNamespace(**dict(zip(names, refs, strict=True)))
    line, groups, count = plan.line, plan.groups, plan.count
    shard, shard_ff, stripe = plan.shard, plan.shard_ff, plan.stripe
    half_a, half_ff, ff = plan.half_a, plan.half_ff, plan.ff
    quarter = QLEN
    shift = QLEN.bit_length() - 1

    t = lax.axis_index(TOWER)
    me = lax.axis_index(DP)
    z = me // 4
    x = (me // 2) % 2
    c = me % 2

    def at(zz, xx, cc):
        return (zz * 2 + xx) * 2 + cc

    dev_x = {TOWER: t, DP: at(z, 1 - x, c)}
    dev_c = {TOWER: t, DP: at(z, x, 1 - c)}
    dev_y = {TOWER: 1 - t, DP: me}

    def dev_z(zz):
        return {TOWER: t, DP: at(zz, x, c)}

    pending, tail = [], []

    def copy(src, dst, ssem, rsem, dev):
        return pltpu.make_async_remote_copy(
            src_ref=src, dst_ref=dst, send_sem=ssem, recv_sem=rsem,
            device_id=dev, device_id_type=MESH,
        )

    def send(cond, what, keep=pending):
        do(cond, what.start)
        keep.append((cond, what))

    def settle(keep):
        for cond, what in keep:
            do(cond, what.wait_send)
        keep.clear()

    def got(cond, ref, rsem):
        do(cond, copy(ref, ref, r.s_loss.at[0], rsem, dev_x).wait_recv)

    wa, wg, wd = r.wa, r.wg, r.wd
    out_w = half_a - 3 * D // 2
    local = []

    def near(src, dst, cond=None):
        what = pltpu.make_async_copy(src, dst, r.loc.at[len(local)])
        do(cond, what.start)
        local.append((cond, what))

    third = 3 * D // 2
    for h in range(2):
        near(r.i_qkv.at[:, pl.ds(h * third, third)],
             wa.at[z, x, c, :, pl.ds(h * half_a, third)])
        near(r.i_out.at[:, pl.ds(h * out_w, out_w)],
             wa.at[z, x, c, :, pl.ds(h * half_a + third, out_w)])
    near(r.i_down, wd.at[z, c], x == t)
    near(r.tile, r.vt.at[me])
    for s in range(line):
        for k, ref in enumerate((r.i_gate, r.i_up)):
            near(ref.at[:, pl.ds(aligned((2 * s + t) * stripe, LANES), stripe)],
                 wg.at[z, x, c, :, pl.ds(k * half_ff + s * stripe, stripe)])

    barrier = pltpu.get_barrier_semaphore()

    def greet(j, carry):
        other = jnp.logical_or(j // groups != t, j % groups != me)

        @pl.when(other)
        def _():
            pl.semaphore_signal(
                barrier, inc=1, device_id={TOWER: j // groups, DP: j % groups},
                device_id_type=MESH,
            )

        return carry

    lax.fori_loop(0, 2 * groups, greet, 0)
    pl.semaphore_wait(barrier, 2 * groups - 1)
    for cond, what in local:
        do(cond, what.wait)

    def piece_a(zz, xx, cc, h):
        return wa.at[zz, xx, cc, :, pl.ds(aligned(h * half_a, LANES), half_a)]

    def send_a(cond, sem, zz, xx, h, dev):
        ref = piece_a(zz, xx, c, h)
        send(cond, copy(ref, ref, sem, r.ra.at[at(zz, xx, c), h], dev))

    def got_a(cond, zz, xx, cc, h):
        got(cond, piece_a(zz, xx, cc, h), r.ra.at[at(zz, xx, cc), h])

    def sides(step):
        yield z - step, z >= step, z < line - 1, z + 1, 0
        yield z + step, z < line - step, z > 0, z - 1, 1

    def a_round(step):
        for zz, there, on, nxt, way in sides(step):
            if step:
                got_a(there, zz, x, c, t)
            send_a(both(there, on), r.sa_z.at[way, zz], zz, x, t, dev_z(nxt))
            if step or way == 0:
                send_a(there, r.sa_x.at[zz], zz, x, t, dev_x)
                if step:
                    send_a(there, r.sa_y.at[zz, x], zz, x, t, dev_y)
                send_a(there, r.sa_c.at[zz, x, t], zz, x, t, dev_c)
        if step == 0:
            send_a(None, r.sa_c.at[z, x, 1 - t], z, x, 1 - t, dev_c)

    def around(step):
        return list(sides(step))[: 1 if step == 0 else 2]

    def a_cross(step):
        for zz, there, _, _, _ in around(step):
            got_a(there, zz, 1 - x, c, t)
            send_a(there, r.sa_y.at[zz, 1 - x], zz, 1 - x, t, dev_y)
            send_a(there, r.sa_c.at[zz, 1 - x, t], zz, 1 - x, t, dev_c)

    def a_tower(step):
        for zz, there, _, _, _ in around(step):
            for xx in (x, 1 - x)[1 if step == 0 else 0:]:
                got_a(there, zz, xx, c, 1 - t)
                send_a(there, r.sa_c.at[zz, xx, 1 - t], zz, xx, 1 - t, dev_c)

    def a_sibling():
        for zz in range(line):
            for xx in range(2):
                for h in range(2):
                    got_a(None, zz, xx, 1 - c, h)

    def send_g(cond, sem, zz, xx, dev):
        ref = wg.at[zz, xx, c]
        send(cond, copy(ref, ref, sem, r.rg.at[at(zz, xx, c)], dev))

    def got_g(cond, zz, xx, cc):
        got(cond, wg.at[zz, xx, cc], r.rg.at[at(zz, xx, cc)])

    def g_round(step):
        for zz, there, on, nxt, way in sides(step):
            if step:
                got_g(there, zz, x, c)
            send_g(both(there, on), r.sg_z.at[way, zz], zz, x, dev_z(nxt))
            if step or way == 0:
                send_g(there, r.sg_x.at[zz], zz, x, dev_x)
                send_g(there, r.sg_c.at[zz, x], zz, x, dev_c)

    def g_cross(step):
        for zz, there, _, _, _ in around(step):
            got_g(there, zz, 1 - x, c)
            send_g(there, r.sg_c.at[zz, 1 - x], zz, 1 - x, dev_c)

    def g_sibling():
        for zz in range(line):
            for xx in range(2):
                got_g(None, zz, xx, 1 - c)

    def send_d(cond, sem, zz, dev):
        ref = wd.at[zz, c]
        send(cond, copy(ref, ref, sem, r.rd.at[zz, c], dev))

    def got_d(cond, zz, cc):
        got(cond, wd.at[zz, cc], r.rd.at[zz, cc])

    def d_cross():
        send_d(x == t, r.sd_x.at[0], z, dev_x)

    def d_round(step):
        for zz, there, on, nxt, way in sides(step):
            if step:
                got_d(there, zz, c)
            elif way == 0:
                got_d(x != t, z, c)
            send_d(both(there, on), r.sd_z.at[way, zz], zz, dev_z(nxt))
            if step or way == 0:
                send_d(there, r.sd_c.at[zz], zz, dev_c)

    def d_sibling():
        for zz in range(line):
            got_d(None, zz, 1 - c)

    def v_send(j, carry):
        @pl.when(j != me)
        def _():
            copy(r.vt.at[me], r.vt.at[me], r.sv.at[j], r.rv.at[me],
                 {TOWER: t, DP: j}).start()

        return carry

    def v_wait(j, carry):
        @pl.when(j != me)
        def _():
            copy(r.vt.at[me], r.vt.at[j], r.sv.at[j], r.rv.at[j],
                 {TOWER: t, DP: j}).wait()

        return carry

    a_round(0)
    d_cross()
    lax.fori_loop(0, groups, v_send, 0)

    tok = r.tok
    rows = lax.broadcasted_iota(jnp.int32, (count, count), 0)
    cols = lax.broadcasted_iota(jnp.int32, (count, count), 1)
    seg = cols >> shift
    limit = jnp.zeros_like(cols)
    for s in range(QPD):
        limit = jnp.where(seg == s, r.qlen[s], limit)
    limit = limit * (1 - t) + r.dlen[0] * t
    place = cols - seg * (quarter * (1 - t))
    apart = ((rows >> shift) - seg) * (1 - t)
    seen = both(apart == 0, place < limit)
    r.hide[...] = jnp.where(seen, 0.0, 1.0)
    for s in range(QPD):
        part = pl.ds(s * quarter, quarter)
        length = jnp.full((quarter, 1), r.qlen[s] * (1 - t) + r.dlen[0] * t, jnp.int32)
        slot = lax.broadcasted_iota(jnp.int32, (quarter, 1), 0) + s * quarter * t
        r.pw[part, :] = jnp.where(slot < length, 1.0 / length.astype(F32), 0.0)
        begin = aligned(s * quarter * t, quarter)
        r.cos[part, :] = r.tcos[pl.ds(begin, quarter), :]
        r.sin[part, :] = r.tsin[pl.ds(begin, quarter), :]
    lanes = lax.broadcasted_iota(jnp.int32, (count, LANES), 1)
    first_head = lanes < HEAD
    low_half = (lanes & (HEAD - 1)) < HEAD // 2

    def swap(a):
        return jnp.where(low_half, pltpu.roll(a, LANES - HEAD // 2, 1), pltpu.roll(a, HEAD // 2, 1))

    def turn(a):
        return a * r.cos[...] + swap(a) * r.sin[...]

    def turn_back(a):
        return a * r.cos[...] - swap(a) * r.sin[...]

    def transpose_into(dst, src, width):
        def body(j, carry):
            o = aligned(j * LANES, LANES)
            dst[pl.ds(o, LANES), :] = src[:, pl.ds(o, LANES)].T
            return carry

        lax.fori_loop(0, width // LANES, body, 0)

    def wide(ref, lo, n):
        return ref[:, :, :, :, pl.ds(lo, n)].reshape(groups * shard, n)

    def qkv_lane(u):
        split = 3 * D // 2 // LANES
        return aligned(jnp.where(u < split, u, u + out_w // LANES) * LANES, LANES)

    a_round(1)
    g_round(0)
    transpose_into(r.tokt, tok, D)
    for step in range(2, line):
        a_round(step)
    for step in range(line):
        a_cross(step)
    d_round(0)
    g_round(1)
    for step in range(line):
        a_tower(step)
    g_round(2)
    a_sibling()
    pairs = D // LANES

    def project(p, carry):
        w = jnp.concatenate(
            [wide(wa, qkv_lane(p + k * pairs), LANES) for k in range(3)], axis=1
        )
        packed = jnp.dot(tok[...], w, preferred_element_type=F32)
        o = aligned(p * LANES, LANES)
        r.qkv[:, pl.ds(o, LANES)] = turn(packed[:, :LANES]).astype(BF)
        r.qkv[:, pl.ds(D + o, LANES)] = turn(packed[:, LANES : 2 * LANES]).astype(BF)
        r.qkv[:, pl.ds(2 * D + o, LANES)] = packed[:, 2 * LANES :].astype(BF)
        return carry

    scale = HEAD ** (-0.5)

    def triple(p):
        o = aligned(p * LANES, LANES)
        return tuple(r.qkv[:, pl.ds(k * D + o, LANES)] for k in range(3))

    def only(h, a):
        return jnp.where(first_head if h == 0 else jnp.logical_not(first_head), a, jnp.zeros_like(a))

    def attend(p, carry):
        q2, k2, v2 = triple(p)
        outs = []
        for h in range(2):
            scores = dot_tt(only(h, q2), k2) * scale
            scores = jnp.where(r.hide[...] > 0.5, -1e30, scores)
            grown = jnp.exp(scores - jnp.max(scores, -1, keepdims=True))
            probs = grown * (1.0 / jnp.sum(grown, -1, keepdims=True))
            r.probs[2 * p + h] = probs
            outs.append(jnp.dot(probs.astype(BF), v2, preferred_element_type=F32))
        o = aligned(p * LANES, LANES)
        r.mixed[:, pl.ds(o, LANES)] = jnp.where(first_head, outs[0], outs[1]).astype(BF)
        return carry

    lax.fori_loop(0, pairs, project, 0)
    d_round(1)
    for step in range(3, line):
        g_round(step)
    for step in range(line):
        g_cross(step)
    lax.fori_loop(0, pairs // 2, attend, 0)
    d_round(2)
    lax.fori_loop(pairs // 2, pairs, attend, 0)
    for step in range(3, line):
        d_round(step)

    lax.fori_loop(0, groups, v_wait, 0)

    def widen_vec(j, acc):
        row = lax.broadcasted_iota(jnp.int32, (LANES, D), 0)
        col = lax.broadcasted_iota(jnp.int32, (LANES, D), 1)
        pick = jnp.where(col == row + j * plan.vec, 1.0, 0.0).astype(BF)
        return acc + jnp.dot(r.vt[j], pick, preferred_element_type=F32)

    r.vec[...] = lax.fori_loop(0, groups, widen_vec, jnp.zeros((16, D), F32))

    for h in range(2):
        part = jnp.dot(r.mixed[...], wide(wa, h * half_a + 3 * D // 2, out_w),
                       preferred_element_type=F32)
        r.h1[:, pl.ds(h * out_w, out_w)] = tok[:, pl.ds(h * out_w, out_w)].astype(F32) + part

    def moments(h):
        centred = h - jnp.mean(h, -1, keepdims=True)
        return centred, lax.rsqrt(jnp.mean(centred * centred, -1, keepdims=True) + 1e-05)

    blocks = count // quarter

    def norm_one(b, carry):
        part = pl.ds(aligned(b * quarter, quarter), quarter)
        centred, inverse = moments(r.h1[part, :])
        hat = centred * inverse
        normed = hat * r.vec[0:1, :] + r.vec[1:2, :]
        r.h1[part, :] = hat
        r.rs1[part, :] = inverse
        r.n1[part, :] = normed
        r.feed[pl.ds(aligned(t * count + b * quarter, quarter), quarter), :] = (
            normed.astype(BF))
        return carry

    lax.fori_loop(0, blocks, norm_one, 0)
    mine = pl.ds(aligned(t * count, count), count)
    theirs = pl.ds(aligned((1 - t) * count, count), count)

    def swap_rows(k, src, dst):
        send(None, copy(src, dst, r.sx.at[k], r.rx.at[k], dev_y), tail)

    def got_rows(k, ref):
        got(None, ref, r.rx.at[k])

    swap_rows(0, r.feed.at[mine], r.feed.at[mine])
    transpose_into(r.mixt, r.mixed, D)
    got_rows(0, r.feed.at[theirs])
    transpose_into(r.feedt, r.feed, D)
    g_sibling()

    step_ff = 2 * LANES

    def gated(j, carry):
        o = aligned(j * step_ff, step_ff)
        gate = jnp.dot(r.feed[...], wide(wg, o, step_ff), preferred_element_type=F32)
        up = jnp.dot(r.feed[...], wide(wg, half_ff + o, step_ff), preferred_element_type=F32)
        r.gate[:, pl.ds(o, step_ff)] = gate
        r.up[:, pl.ds(o, step_ff)] = up
        hidden = (gate * jax.nn.sigmoid(gate) * up).astype(BF)
        r.dgu[:, pl.ds(o, step_ff)] = hidden
        r.hidt[pl.ds(o, step_ff), :] = hidden.T
        return carry

    lax.fori_loop(0, half_ff // step_ff, gated, 0)
    d_sibling()

    def down(rows_of, store):
        def body(j, carry):
            o = aligned(j * step_ff, step_ff)
            w = wd[:, :, :, pl.ds(o, step_ff)].reshape(half_ff, step_ff)
            store(o, jnp.dot(r.dgu[rows_of, pl.ds(0, half_ff)], w, preferred_element_type=F32))
            return carry

        lax.fori_loop(0, D // step_ff, body, 0)

    def keep_send(o, val):
        r.bsend[:, pl.ds(o, step_ff)] = val.astype(BF)

    def keep_own(o, val):
        r.bown[:, pl.ds(o, step_ff)] = val

    down(theirs, keep_send)
    swap_rows(1, r.bsend, r.brecv)
    down(mine, keep_own)
    got_rows(1, r.brecv)

    r.pool[...] = jnp.zeros((8, D), F32)

    def norm_two(b, carry):
        part = pl.ds(aligned(b * quarter, quarter), quarter)
        h = r.n1[part, :] + (r.bown[part, :] + r.brecv[part, :].astype(F32))
        centred, inverse = moments(h)
        hat = centred * inverse
        normed = hat * r.vec[2:3, :] + r.vec[3:4, :]
        r.xh2[part, :] = hat
        r.rs2[part, :] = inverse
        r.pool[pl.ds(b, 1), :] = jnp.sum(normed * r.pw[part, :], 0, keepdims=True)
        return carry

    lax.fori_loop(0, blocks, norm_two, 0)
    row8 = lax.broadcasted_iota(jnp.int32, (8, D), 0)

    @pl.when(t == 1)
    def _():
        all_rows = jnp.sum(r.pool[...], 0, keepdims=True)
        r.pool[...] = jnp.where(row8 == 0, all_rows, 0.0)

    pooled = r.pool[...]
    shrink = lax.rsqrt(jnp.sum(pooled * pooled, -1, keepdims=True) + 1e-06)
    r.emb[...] = pooled * shrink

    @pl.when(t == 0)
    def _():
        r.embq[...] = r.emb[0:QPD, :]

        def give(step, carry):
            j = (me + step) % groups
            copy(r.embq, r.qbuf.at[me], r.s_query.at[j], r.r_query.at[me],
                 {TOWER: 1, DP: j}).start()
            return carry

        def take(j, carry):
            copy(r.embd, r.dbuf.at[j], r.s_doc.at[0, 0], r.r_doc.at[j],
                 {TOWER: 1, DP: j}).wait_recv()
            return carry

        lax.fori_loop(0, groups, give, 0)
        lax.fori_loop(0, groups, take, 0)

    @pl.when(t == 1)
    def _():
        r.embd[...] = r.emb[0:1, :]
        r.dbuf[me] = r.emb[0:1, :]

        def give(step, carry):
            j = (me + step) % groups
            copy(r.embd, r.dbuf.at[me], r.s_doc.at[0, j], r.r_doc.at[me],
                 {TOWER: 0, DP: j}).start()

            @pl.when(j != me)
            def _():
                copy(r.embd, r.dbuf.at[me], r.s_doc.at[1, j], r.r_doc.at[me],
                     {TOWER: 1, DP: j}).start()

            return carry

        def take(j, carry):
            copy(r.embq, r.qbuf.at[j], r.s_query.at[0], r.r_query.at[j],
                 {TOWER: 0, DP: j}).wait_recv()

            @pl.when(j != me)
            def _():
                copy(r.embd, r.dbuf.at[j], r.s_doc.at[0, 0], r.r_doc.at[j],
                     {TOWER: 0, DP: j}).wait_recv()

            return carry

        lax.fori_loop(0, groups, give, 0)
        lax.fori_loop(0, groups, take, 0)

    for j in range(groups):
        r.dflat[pl.ds(j, 1), :] = r.dbuf[j]
    best = exact_product_accuracy
    r.dpool[...] = jnp.zeros((8, D), F32)

    @pl.when(t == 0)
    def _():
        docs = r.dflat[...]
        logits = dot_tt(r.embq[...], docs, best) / contrast_sharpness_factor
        peak = jnp.max(logits, -1, keepdims=True)
        lse = peak + jnp.log(jnp.sum(jnp.exp(logits - peak), -1, keepdims=True))
        col = lax.broadcasted_iota(jnp.int32, (QPD, groups), 1)
        row = lax.broadcasted_iota(jnp.int32, (QPD, groups), 0)
        label = jnp.zeros((QPD, groups), jnp.int32)
        for s in range(QPD):
            label = jnp.where(row == s, r.pos[me * QPD + s], label)
        hot = jnp.where(col == label, 1.0, 0.0)
        slope = (jnp.exp(logits - lse) - hot) / contrast_sharpness_factor
        r.dpool[0:QPD, :] = jnp.dot(slope, docs, preferred_element_type=F32, precision=best)

    @pl.when(t == 1)
    def _():
        for j in range(groups):
            r.qflat[pl.ds(j * QPD, QPD), :] = r.qbuf[j]
        docs, queries = r.dflat[...], r.qflat[...]
        logits = dot_tt(docs, queries, best) / contrast_sharpness_factor
        peak = jnp.max(logits, 0, keepdims=True)
        lse = peak + jnp.log(jnp.sum(jnp.exp(logits - peak), 0, keepdims=True))
        row = lax.broadcasted_iota(jnp.int32, (groups, groups * QPD), 0)
        hit = row == r.posv[...]
        picked = jnp.sum(jnp.where(hit, logits, 0.0), 0, keepdims=True)
        total = jnp.sum(lse - picked, -1, keepdims=True)
        r.loss[...] = jnp.broadcast_to(total / (groups * QPD), (8, LANES))
        slope = (jnp.exp(logits - lse) - jnp.where(hit, 1.0, 0.0)) / contrast_sharpness_factor
        line_of = jnp.sum(jnp.where(row == me, slope, 0.0), 0, keepdims=True)
        r.dpool[0:1, :] = jnp.dot(line_of, queries, preferred_element_type=F32, precision=best)

    slope = r.dpool[...]
    emb = r.emb[...]
    dpool = shrink * (slope - emb * jnp.sum(slope * emb, -1, keepdims=True))

    @pl.when(t == 0)
    def _():
        r.dpool[...] = dpool

    @pl.when(t == 1)
    def _():
        r.dpool[...] = jnp.broadcast_to(dpool[0:1, :], (8, D))

    def norm_two_back(b, sums):
        part = pl.ds(aligned(b * quarter, quarter), quarter)
        top = r.pw[part, :] * r.dpool[pl.ds(b, 1), :]
        hat = r.xh2[part, :]
        inner = top * r.vec[2:3, :]
        grad = r.rs2[part, :] * (
            inner - jnp.mean(inner, -1, keepdims=True)
            - hat * jnp.mean(inner * hat, -1, keepdims=True))
        r.n1[part, :] = grad
        r.dbr[pl.ds(aligned(t * count + b * quarter, quarter), quarter), :] = (
            grad.astype(BF))
        return (sums[0] + jnp.sum(top * hat, 0, keepdims=True),
                sums[1] + jnp.sum(top, 0, keepdims=True))

    zero_row = jnp.zeros((1, D), F32)
    gain_two, bias_two = lax.fori_loop(0, blocks, norm_two_back, (zero_row, zero_row))
    swap_rows(2, r.dbr.at[mine], r.dbr.at[mine])

    send(t == 1, copy(r.loss, r.lossr, r.s_loss.at[0], r.r_loss.at[0], dev_y), tail)
    r.ln[0] = jnp.where(row8 == 2, gain_two, 0.0) + jnp.where(row8 == 3, bias_two, 0.0)

    def hidden_back(rows_of):
        def body(j, carry):
            o = aligned(j * stripe, LANES)
            w = wd[j].reshape(stripe, D)
            slope = dot_tt(r.dbr[rows_of, :], w)
            gate = r.gate[rows_of, pl.ds(o, stripe)]
            up = r.up[rows_of, pl.ds(o, stripe)]
            sig = jax.nn.sigmoid(gate)
            r.dgu[rows_of, pl.ds(o, stripe)] = (
                slope * up * (sig * (1.0 + gate * (1.0 - sig)))).astype(BF)
            r.dgu[rows_of, pl.ds(half_ff + o, stripe)] = (slope * (gate * sig)).astype(BF)
            return carry

        lax.fori_loop(0, line, body, 0)

    hidden_back(mine)
    got_rows(2, r.dbr.at[theirs])

    def along(step):
        for s in range(1, line):
            yield line - s, both(z == step, z < line - s), z + 1, 0
        for s in range(line - 1):
            yield s, both(z == line - 1 - step, z > s), z - 1, 1

    def added(refs):
        total = refs[0][...].astype(F32)
        for ref in refs[1:]:
            total = total + ref[...].astype(F32)
        return total

    def line_step(step, parts, sem, slot):
        for dest, cond, nxt, way in along(step):
            into = slot(dest + 1 if way == 0 else dest)
            refs = parts(dest)

            def move(into=into, refs=refs, dest=dest, way=way):
                if step:
                    copy(into, into, r.s_loss.at[0], sem(1, way, dest), dev_x).wait_recv()
                    refs[0][...] = added(refs + (into,)).astype(BF)
                else:
                    refs[0][...] = added(refs).astype(BF)

            do(cond, move)
            send(cond, copy(refs[0], into, sem(0, way, dest), sem(1, way, dest),
                            dev_z(nxt)), tail)

    def line_end(parts, sem, slot, put):
        for cond, ways in ((z == 0, (1,)), (z == line - 1, (0,)),
                           (both(z > 0, z < line - 1), (0, 1))):
            def finish(ways=ways):
                refs = parts(z)
                for way in ways:
                    into = slot(z + 1 if way == 0 else z)
                    copy(into, into, r.s_loss.at[0], sem(1, way, z), dev_x).wait_recv()
                    refs = refs + (into,)
                put[...] = added(refs).astype(BF)

            do(cond, finish)

    gd = r.gd

    def down_grad(s):
        gd[s] = jnp.dot(r.hidt[pl.ds(s * stripe, stripe), :], r.dbr[...],
                        preferred_element_type=F32).astype(BF).reshape(2, shard_ff, D)
        send(None, copy(gd.at[s, 1 - c], r.gd_rc.at[s], r.gd_c.at[0, s],
                        r.gd_c.at[1, s], dev_c), tail)

    def down_parts(dest):
        return gd.at[dest, c], r.gd_rc.at[dest]

    def down_arrive():
        for s in range(line):
            got(None, r.gd_rc.at[s], r.gd_c.at[1, s])

    def down_line(step):
        line_step(step, down_parts, lambda *i: r.gd_z.at[i], lambda k: r.gd_rz.at[k])

    def down_end():
        line_end(down_parts, lambda *i: r.gd_z.at[i], lambda k: r.gd_rz.at[k], r.gd_f)
        send(x != t, copy(r.gd_f, r.gd_rx, r.gd_x.at[0], r.gd_x.at[1], dev_x), tail)

    out_copies = []

    def keep_out(k, src, dst, cond=None):
        what = pltpu.make_async_copy(src, dst, r.fin.at[k])
        do(cond, what.start)
        out_copies.append((cond, what))

    def down_out():
        def total():
            copy(r.gd_rx, r.gd_rx, r.s_loss.at[0], r.gd_x.at[1], dev_x).wait_recv()
            r.gd_f[...] = added((r.gd_f, r.gd_rx)).astype(BF)

        do(x == t, total)
        keep_out(0, r.gd_f, r.o_dn, x == t)
        send(x == t, copy(r.gd_f, r.o_dn, r.gd_y.at[0], r.gd_y.at[1], dev_y), tail)

    gg = r.gg
    part_gu = ff // 4

    def gate_grad(k):
        span = pl.ds(k * part_gu, part_gu)
        val = jnp.dot(r.feedt[...], r.dgu[:, span], preferred_element_type=F32)
        gg[:, :, :, :, span] = val.astype(BF).reshape(line, 2, 2, shard, part_gu)
        send(None, copy(gg.at[:, :, 1 - c, :, span], r.gg_rc.at[:, :, :, span],
                        r.gg_c.at[0, k], r.gg_c.at[1, k], dev_c), tail)

    def gate_cross(k):
        span = pl.ds(k * part_gu, part_gu)
        got(None, r.gg_rc.at[:, :, :, span], r.gg_c.at[1, k])
        for s in range(line):
            mine_k = gg.at[s, 1 - x, c, :, span]
            mine_k[...] = added((mine_k, r.gg_rc.at[s, 1 - x, :, span])).astype(BF)
        send(None, copy(gg.at[:, 1 - x, c, :, span], r.gg_rx.at[:, :, span],
                        r.gg_x.at[0, k], r.gg_x.at[1, k], dev_x), tail)

    def gate_parts(k):
        span = pl.ds(k * part_gu, part_gu)
        return lambda dest: (gg.at[dest, x, c, :, span], r.gg_rc.at[dest, x, :, span],
                             r.gg_rx.at[dest, :, span])

    def gate_line(k, step):
        span = pl.ds(k * part_gu, part_gu)
        if step == 0:
            got(None, r.gg_rx.at[:, :, span], r.gg_x.at[1, k])
        line_step(step, gate_parts(k), lambda a, *i: r.gg_z.at[(a, k) + i], lambda s: r.gg_rz.at[s, :, span])

    def gate_end(k):
        span = pl.ds(k * part_gu, part_gu)
        line_end(gate_parts(k), lambda a, *i: r.gg_z.at[(a, k) + i], lambda s: r.gg_rz.at[s, :, span],
                 r.gg_f.at[:, span])
        keep_out(1 + k, r.gg_f.at[:, span], r.o_gu.at[t, :, span])
        send(None, copy(r.gg_f.at[:, span], r.o_gu.at[t, :, span], r.gg_y.at[0, k],
                        r.gg_y.at[1, k], dev_y), tail)

    ga = wg
    part_a = half_a // 4

    def cols_a(k, h):
        return pl.ds(aligned(h * half_a + k * part_a, LANES), part_a)

    def store_a(k, left, right):
        for h in range(2):
            val = jnp.dot(left[...], right[h], preferred_element_type=F32)
            ga[:, :, :, :, cols_a(k, h)] = val.astype(BF).reshape(line, 2, 2, shard, part_a)
            send(None, copy(ga.at[:, :, 1 - c, :, cols_a(k, h)],
                            r.ga_rc.at[:, :, :, cols_a(k, h)],
                            r.ga_c.at[0, h, k], r.ga_c.at[1, h, k], dev_c), tail)

    def span_a(k):
        return pl.ds(k * part_a, part_a)

    def tower_a(k):
        for h in range(2):
            got(None, r.ga_rc.at[:, :, :, cols_a(k, h)], r.ga_c.at[1, h, k])
        gone = cols_a(k, 1 - t)
        for s in range(line):
            for xx in range(2):
                ref = ga.at[s, xx, c, :, gone]
                ref[...] = added((ref, r.ga_rc.at[s, xx, :, gone])).astype(BF)
        send(None, copy(ga.at[:, :, c, :, gone], r.ga_rt.at[:, :, :, span_a(k)],
                        r.ga_t.at[0, k], r.ga_t.at[1, k], dev_y), tail)

    def cross_a(k):
        got(None, r.ga_rt.at[:, :, :, span_a(k)], r.ga_t.at[1, k])
        here = cols_a(k, t)
        for s in range(line):
            ref = ga.at[s, 1 - x, c, :, here]
            ref[...] = added((ref, r.ga_rc.at[s, 1 - x, :, here],
                              r.ga_rt.at[s, 1 - x, :, span_a(k)])).astype(BF)
        send(None, copy(ga.at[:, 1 - x, c, :, here], r.ga_rx.at[:, :, span_a(k)],
                        r.ga_x.at[0, k], r.ga_x.at[1, k], dev_x), tail)

    def parts_a(k):
        here = cols_a(k, t)
        return lambda dest: (ga.at[dest, x, c, :, here], r.ga_rc.at[dest, x, :, here],
                             r.ga_rt.at[dest, x, :, span_a(k)],
                             r.ga_rx.at[dest, :, span_a(k)])

    def line_a(k, step):
        if step == 0:
            got(None, r.ga_rx.at[:, :, span_a(k)], r.ga_x.at[1, k])
        line_step(step, parts_a(k), lambda a, *i: r.ga_z.at[(a, k) + i], lambda s: r.ga_rz.at[s, :, span_a(k)])

    def end_a(k):
        line_end(parts_a(k), lambda a, *i: r.ga_z.at[(a, k) + i], lambda s: r.ga_rz.at[s, :, span_a(k)],
                 r.ga_f.at[:, span_a(k)])
        keep_out(5 + k, r.ga_f.at[:, span_a(k)], r.o_a.at[:, cols_a(k, t)])
        send(None, copy(r.ga_f.at[:, span_a(k)], r.o_a.at[:, cols_a(k, t)],
                        r.ga_y.at[0, k], r.ga_y.at[1, k], dev_y), tail)

    some = 2 * 4 * shard

    def rows_of_weight(ref, j, lo, n):
        return ref[pl.ds(2 * j, 2), :, :, :, pl.ds(lo, n)].reshape(some, n)

    def feed_back(rows_of, store):
        def body(j, carry):
            store(pl.ds(aligned(j * some, LANES), some),
                  dot_tt(r.dgu[rows_of, :], rows_of_weight(wg, j, 0, ff)))
            return carry

        lax.fori_loop(0, line // 2, body, 0)

    def back_send(span, val):
        r.dsend[:, span] = val.astype(BF)

    def back_own(span, val):
        r.bown[:, span] = val

    for s in range(line):
        down_grad(s)
    hidden_back(theirs)
    down_arrive()
    down_line(0)
    feed_back(theirs, back_send)
    swap_rows(3, r.dsend, r.drecv)
    gate_grad(0)
    gate_grad(1)
    gate_cross(0)
    down_line(1)
    gate_grad(2)
    gate_cross(1)
    gate_line(0, 0)
    gate_grad(3)
    gate_cross(2)
    for step in range(2, line - 1):
        down_line(step)
    gate_line(1, 0)
    gate_line(0, 1)
    feed_back(mine, back_own)
    gate_cross(3)
    down_end()
    settle(pending)
    gate_line(2, 0)
    gate_line(1, 1)
    gate_line(0, 2)
    got_rows(3, r.drecv)

    def norm_one_back(b, sums):
        part = pl.ds(aligned(b * quarter, quarter), quarter)
        top = r.n1[part, :] + r.bown[part, :] + r.drecv[part, :].astype(F32)
        hat = r.h1[part, :]
        inner = top * r.vec[0:1, :]
        grad = r.rs1[part, :] * (
            inner - jnp.mean(inner, -1, keepdims=True)
            - hat * jnp.mean(inner * hat, -1, keepdims=True))
        r.n1[part, :] = grad
        r.datt[part, :] = grad.astype(BF)
        return (sums[0] + jnp.sum(top * hat, 0, keepdims=True),
                sums[1] + jnp.sum(top, 0, keepdims=True))

    gain_one, bias_one = lax.fori_loop(0, blocks, norm_one_back, (zero_row, zero_row))
    r.ln[0] = (r.ln[0] + jnp.where(row8 == 0, gain_one, 0.0)
                  + jnp.where(row8 == 1, bias_one, 0.0))

    ln_peers = [dev_c, dev_x, dev_y]
    for bit in range(line.bit_length() - 1):
        apart = 1 << bit
        ln_peers.append(dev_z(z + apart * (1 - 2 * ((z // apart) % 2))))
    last = len(ln_peers)

    def ln_send(k):
        send(None, copy(r.ln.at[k], r.lnr.at[k], r.s_ln.at[k], r.r_ln.at[k],
                        ln_peers[k]), tail)

    def ln_add(k):
        got(None, r.lnr.at[k], r.r_ln.at[k])
        r.ln[k + 1] = r.ln[k] + r.lnr[k]

    dqkv = r.dgu.at[pl.ds(0, count), pl.ds(0, 3 * D)]
    dmix = r.dgu.at[pl.ds(count, count), pl.ds(0, D)]

    ln_send(0)
    store_a(3, r.mixt, [r.datt[:, pl.ds(h * out_w, out_w)] for h in range(2)])

    def mixed_back(j, carry):
        val = sum(dot_tt(r.datt[:, pl.ds(h * out_w, out_w)],
                         rows_of_weight(wa, j, h * half_a + third, out_w)) for h in range(2))
        dmix[:, pl.ds(aligned(j * some, LANES), some)] = val.astype(BF)
        return carry

    lax.fori_loop(0, line // 2, mixed_back, 0)
    ln_add(0)
    ln_send(1)
    tower_a(3)
    gate_line(3, 0)
    gate_line(2, 1)
    gate_line(1, 2)
    down_out()
    gate_end(0)

    def attend_back(p, carry):
        q2, k2, v2 = triple(p)
        o = aligned(p * LANES, LANES)
        dm2 = dmix[:, pl.ds(o, LANES)]
        parts = []
        for h in range(2):
            probs = r.probs[2 * p + h]
            dprobs = dot_tt(only(h, dm2), v2)
            mean = jnp.sum(probs * dprobs, -1, keepdims=True)
            dscores = (probs * (dprobs - mean)).astype(BF)
            parts.append((jnp.dot(dscores, k2, preferred_element_type=F32),
                          dot_t0(dscores, q2), dot_t0(probs.astype(BF), dm2)))
        dq, dk, dv = (jnp.where(first_head, a, b) for a, b in zip(*parts))
        dqkv[:, pl.ds(o, LANES)] = turn_back(dq * scale).astype(BF)
        dqkv[:, pl.ds(D + o, LANES)] = turn_back(dk * scale).astype(BF)
        dqkv[:, pl.ds(2 * D + o, LANES)] = dv.astype(BF)
        return carry

    lax.fori_loop(0, 2, attend_back, 0)
    ln_add(1)
    ln_send(2)
    gate_line(3, 1)
    gate_line(2, 2)
    gate_end(1)
    lax.fori_loop(2, 4, attend_back, 0)
    ln_add(2)
    ln_send(3)
    cross_a(3)
    gate_line(3, 2)
    gate_end(2)
    lax.fori_loop(4, pairs, attend_back, 0)
    ln_add(3)
    ln_send(4)
    line_a(3, 0)
    gate_end(3)
    for k in range(3):
        store_a(k, r.tokt, [dqkv[:, pl.ds(h * third + k * part_a, part_a)]
                               for h in range(2)])
    line_a(3, 1)
    for k in range(3):
        tower_a(k)
    for k in range(4, last):
        ln_add(k)
        if k + 1 < last:
            ln_send(k + 1)
    r.o_vec[...] = r.ln[last]

    def token_back(j, carry):
        val = sum(dot_tt(dqkv[:, pl.ds(h * third, third)],
                         rows_of_weight(wa, j, h * half_a, third)) for h in range(2))
        span = pl.ds(aligned(j * some, LANES), some)
        r.o_tok[:, span] = r.n1[:, span] + val
        return carry

    lax.fori_loop(0, line // 2, token_back, 0)
    line_a(3, 2)
    for k in range(3):
        cross_a(k)
    end_a(3)
    for step in range(line - 1):
        for k in range(3):
            line_a(k, step)
    for k in range(3):
        end_a(k)

    @pl.when(t == 0)
    def _():
        got(None, r.lossr, r.r_loss.at[0])
        r.o_loss[...] = r.lossr[...]
        r.o_q[...] = r.embq[...]

    @pl.when(t == 1)
    def _():
        r.o_loss[...] = r.loss[...]
        r.o_q[...] = r.qbuf[me]

    r.o_d[...] = r.dbuf[me]

    @pl.when(t == 0)
    def _():
        def sent(j, carry):
            copy(r.embq, r.qbuf.at[me], r.s_query.at[j], r.r_query.at[me],
                 {TOWER: 1, DP: j}).wait_send()
            return carry

        lax.fori_loop(0, groups, sent, 0)

    @pl.when(t == 1)
    def _():
        def sent(j, carry):
            copy(r.embd, r.dbuf.at[me], r.s_doc.at[0, j], r.r_doc.at[me],
                 {TOWER: 0, DP: j}).wait_send()

            @pl.when(j != me)
            def _():
                copy(r.embd, r.dbuf.at[me], r.s_doc.at[1, j], r.r_doc.at[me],
                     {TOWER: 1, DP: j}).wait_send()

            return carry

        lax.fori_loop(0, groups, sent, 0)

    got(x != t, r.o_dn, r.gd_y.at[1])
    for k in range(4):
        got(None, r.o_gu.at[1 - t, :, pl.ds(k * part_gu, part_gu)], r.gg_y.at[1, k])
        got(None, r.o_a.at[:, cols_a(k, 1 - t)], r.ga_y.at[1, k])
    for cond, what in out_copies:
        do(cond, what.wait)
    settle(tail)


def finish(plan, *refs):
    (a_ref, gu_ref, dn_ref, vec_ref, tok_ref, q_ref, d_ref, loss_ref,
     o_loss, o_q, o_d, o_tok, o_qkv, o_out, o_gate, o_up, o_down, *o_vecs) = refs
    third, half_a, half_ff, stripe = 3 * D // 2, plan.half_a, plan.half_ff, plan.stripe
    out_w = half_a - third
    for h in range(2):
        o_qkv[:, h * third : (h + 1) * third] = a_ref[:, h * half_a : h * half_a + third].astype(F32)
        o_out[:, h * out_w : (h + 1) * out_w] = (
            a_ref[:, h * half_a + third : (h + 1) * half_a].astype(F32))
        for s in range(plan.line):
            to = pl.ds((2 * s + h) * stripe, stripe)
            o_gate[:, to] = gu_ref[h, :, pl.ds(s * stripe, stripe)].astype(F32)
            o_up[:, to] = gu_ref[h, :, pl.ds(half_ff + s * stripe, stripe)].astype(F32)
    o_down[...] = dn_ref[...].astype(F32)
    o_tok[0] = tok_ref[...]
    o_q[...] = q_ref[...]
    o_d[...] = d_ref[...]
    o_loss[...] = loss_ref[0:1, 0:1]
    first = lax.axis_index(DP) * plan.vec
    row = lax.broadcasted_iota(jnp.int32, (D, LANES), 0)
    col = lax.broadcasted_iota(jnp.int32, (D, LANES), 1)
    pick = jnp.where(row == first + col, 1.0, 0.0)
    own = jnp.dot(vec_ref[...], pick, preferred_element_type=F32, precision=exact_product_accuracy)
    for k, out in enumerate(o_vecs):
        out[...] = own[k : k + 1, 0 : plan.vec]


def on_device_kernel(plan, tokens, query_lengths, doc_lengths, positives, w_qkv, w_out, w_gate,
                     w_up, w_down, ln1_gain, first_layernorm_shift, ln2_gain, ln2_bias):
    count, groups, shard, vec = plan.count, plan.groups, plan.shard, plan.vec
    cosines, sines = rotary_constants(count)
    tile = jnp.pad(jnp.stack([ln1_gain, first_layernorm_shift, ln2_gain, ln2_bias]),
                   ((0, 12), (0, LANES - vec)))
    vmem = pl.BlockSpec(memory_space=pltpu.VMEM)
    smem = pl.BlockSpec(memory_space=pltpu.SMEM)
    hbm = pl.BlockSpec(memory_space=pl.ANY)
    shape = jax.ShapeDtypeStruct
    made = pl.pallas_call(
        functools.partial(whole_step, plan),
        out_shape=(
            shape((count, D), F32), shape((shard, plan.width_a), BF), shape((2, shard, plan.ff), BF),
            shape((plan.shard_ff, D), BF), shape((8, D), F32), shape((QPD, D), F32),
            shape((1, D), F32), shape((8, LANES), F32),
        ),
        in_specs=[smem, smem, smem, vmem, vmem, vmem, vmem, vmem] + [hbm] * 5,
        out_specs=(vmem, hbm, hbm, hbm, vmem, vmem, vmem, vmem),
        scratch_shapes=list(buffers(plan).values()) + list(semaphores(plan).values()),
        compiler_params=pltpu.CompilerParams(
            collective_id=0, has_side_effects=True, vmem_limit_bytes=63 * 1000 * 1000),
        name="whole_step",
    )(query_lengths, doc_lengths, positives, positives[None], tokens[0], cosines, sines, tile,
      w_qkv, w_out, w_gate, w_up, w_down)
    o_tok, o_a, o_gu, o_dn, o_vec, o_q, o_d, o_loss = made
    outs = pl.pallas_call(
        functools.partial(finish, plan),
        out_shape=(
            shape((1, 1), F32), shape((QPD, D), F32), shape((1, D), F32),
            shape((1, count, D), F32), shape((shard, 3 * D), F32), shape((shard, D), F32),
            shape((shard, plan.ff), F32), shape((shard, plan.ff), F32),
            shape((plan.shard_ff, D), F32),
        ) + (shape((1, vec), F32),) * 4,
        in_specs=[vmem] * 8,
        out_specs=[vmem] * 13,
        name="finish",
    )(o_a, o_gu, o_dn, o_vec, o_tok, o_q, o_d, o_loss)
    return (outs[0].reshape(()),) + tuple(outs[1:9]) + tuple(v.reshape(vec) for v in outs[9:])


def fits(plan, towers):
    line = plan.line
    return (towers == 2 and plan.groups % 4 == 0 and line & (line - 1) == 0 and line > 1
            and plan.shard % 16 == 0 and plan.shard_ff % 16 == 0 and plan.stripe % LANES == 0
            and plan.count == QPD * QLEN)


def solution(mesh):
    groups = mesh.shape[DP]

    def local_step(*args):
        plan = Plan(groups, args[0].shape[1], args[4].shape[0], args[8].shape[0], args[9].shape[0])
        if fits(plan, mesh.shape[TOWER]):
            return on_device_kernel(plan, *args)
        return on_device(*args)

    return jax.shard_map(
        local_step,
        mesh=mesh,
        in_specs=(
            P(TOWER, DP, None),
            P(DP),
            P(DP),
            P(),
            P(DP, None),
            P(DP, None),
            P(DP, None),
            P(DP, None),
            P(DP, None),
            P(DP),
            P(DP),
            P(DP),
            P(DP),
        ),
        out_specs=(
            P(),
            P(DP, None),
            P(DP, None),
            P(TOWER, DP, None),
            P(DP, None),
            P(DP, None),
            P(DP, None),
            P(DP, None),
            P(DP, None),
            P(DP),
            P(DP),
            P(DP),
            P(DP),
        ),
        check_vma=False,
    )
```

```python
import functools
from types import SimpleNamespace
from typing import Any, NamedTuple

import jax
import jax.numpy as jnp
import numpy as np
from jax import lax
from jax.experimental import pallas as pl
from jax.experimental.pallas import tpu as pltpu
from jax.sharding import PartitionSpec as P

TOWER = "tower"
DP = "dp"
D = 768
HEADS = 12
HEAD = 64
QLEN = 64
QPD = 4


exact_product_accuracy = lax.Precision.HIGHEST
rope_base = 1000.0
contrast_sharpness_factor = 0.02


def product(left, right):
    return jnp.dot(left, right, preferred_element_type=jnp.float32)


def rotary_tables(places):
    freqs = jnp.power(rope_base, -2.0 * jnp.arange(HEAD // 2).astype(jnp.float32) / HEAD)
    angles = places[:, None] * freqs[None, :]
    return (jnp.cos(angles)[:, None, :], jnp.sin(angles)[:, None, :])


def rotate(values, cosines, sines):
    half_dim = values.shape[-1] // 2
    first = values[..., :half_dim]
    second = values[..., half_dim:]
    return jnp.concatenate(
        [first * cosines - second * sines, second * cosines + first * sines], axis=-1
    )


def layer_norm(hidden, gain, offset):
    average = jnp.mean(hidden, -1, keepdims=True)
    centred = hidden - average
    variance = jnp.mean(centred * centred, -1, keepdims=True)
    return centred * lax.rsqrt(variance + 1e-05) * gain + offset


def normalize(pooled):
    return pooled * lax.rsqrt(jnp.sum(pooled * pooled, -1, keepdims=True) + 1e-06)


def layout(tower_id, query_len, doc_len, count):
    places = jnp.arange(count)
    span = jnp.where(tower_id == 0, QLEN, count)
    segment = places // span
    offset_in = places - segment * span
    slots = jnp.arange(QPD)
    seg_limit = jnp.where(tower_id == 0, query_len, doc_len[0] * jnp.ones_like(query_len))
    limit = jnp.sum(jnp.where(segment[:, None] == slots[None, :], seg_limit[None, :], 0), axis=1)
    valid = offset_in < limit
    allowed = (segment[:, None] == segment[None, :]) & valid[None, :]
    member = (segment[None, :] == slots[:, None]) & valid[None, :]
    pool_matrix = jnp.where(member, 1.0 / seg_limit[:, None].astype(jnp.float32), 0.0)
    return (offset_in.astype(jnp.float32), allowed, pool_matrix)


def swish_product(left, right):
    return jax.nn.silu(left) * right


def on_device(
    tokens,
    query_lengths,
    doc_lengths,
    positives,
    w_qkv,
    w_out,
    w_gate,
    w_up,
    w_down,
    ln1_gain,
    first_layernorm_shift,
    ln2_gain,
    ln2_bias,
):
    tower_id = lax.axis_index(TOWER)
    device_id = lax.axis_index(DP)
    groups = lax.axis_size(DP)
    full = (
        lax.all_gather(w_qkv, DP, axis=0, tiled=True),
        lax.all_gather(w_out, DP, axis=0, tiled=True),
        lax.all_gather(w_gate, DP, axis=0, tiled=True),
        lax.all_gather(w_up, DP, axis=0, tiled=True),
        lax.all_gather(w_down, DP, axis=0, tiled=True),
        lax.all_gather(ln1_gain, DP, axis=0, tiled=True),
        lax.all_gather(first_layernorm_shift, DP, axis=0, tiled=True),
        lax.all_gather(ln2_gain, DP, axis=0, tiled=True),
        lax.all_gather(ln2_bias, DP, axis=0, tiled=True),
    )
    qkv_full, out_full, gate_full, up_full, down_full = (
        full[0],
        full[1],
        full[2],
        full[3],
        full[4],
    )
    gain_one = full[5].astype(jnp.float32)
    bias_one = full[6].astype(jnp.float32)
    gain_two = full[7].astype(jnp.float32)
    bias_two = full[8].astype(jnp.float32)
    inputs = tokens[0]
    count = inputs.shape[0]
    places, allowed, pool_matrix = layout(tower_id, query_lengths, doc_lengths, count)
    cosines, sines = rotary_tables(places)
    packed = product(inputs, qkv_full)
    raw_query = packed[:, :D].reshape(count, HEADS, HEAD)
    raw_key = packed[:, D : 2 * D].reshape(count, HEADS, HEAD)

    def rotate_both(first, second):
        return (rotate(first, cosines, sines), rotate(second, cosines, sines))

    rotated, rotary_back = jax.vjp(rotate_both, raw_query, raw_key)
    query_low = rotated[0].astype(jnp.bfloat16)
    key_low = rotated[1].astype(jnp.bfloat16)
    value_low = packed[:, 2 * D :].reshape(count, HEADS, HEAD).astype(jnp.bfloat16)
    scale = HEAD ** (-0.5)

    def masked_scores():
        scores = (
            jnp.einsum("ihd,jhd->hij", query_low, key_low, preferred_element_type=jnp.float32)
            * scale
        )
        return jnp.where(allowed[None], scores, -1e30)

    scores = masked_scores()
    peak = jnp.max(scores, -1, keepdims=True)
    log_total = peak + jnp.log(jnp.sum(jnp.exp(scores - peak), -1, keepdims=True))
    probs_low = jnp.exp(scores - log_total).astype(jnp.bfloat16)
    mixed = jnp.einsum("hij,jhd->ihd", probs_low, value_low, preferred_element_type=jnp.float32)
    mixed_low = mixed.reshape(count, D).astype(jnp.bfloat16)
    attended = product(mixed_low, out_full)
    inputs_wide = inputs.astype(jnp.float32)
    normed_one, norm_one_back = jax.vjp(layer_norm, inputs_wide + attended, gain_one, bias_one)
    feed = normed_one.astype(jnp.bfloat16)
    gate = product(feed, gate_full)
    up_part = product(feed, up_full)
    hidden_wide, swish_back = jax.vjp(swish_product, gate, up_part)
    hidden = hidden_wide.astype(jnp.bfloat16)
    branch = product(hidden, down_full)
    normed_two, norm_two_back = jax.vjp(layer_norm, normed_one + branch, gain_two, bias_two)
    pooled = jnp.dot(pool_matrix, normed_two, precision=exact_product_accuracy)
    embedded, normal_back = jax.vjp(normalize, pooled)
    gathered = lax.all_gather(embedded, (TOWER, DP), axis=0, tiled=True)
    queries_total = groups * QPD
    gathered_query_rows = gathered[:queries_total]
    gathered_document_rows = gathered[queries_total:].reshape(groups, QPD, D)[:, 0]
    pairwise_affinity_matrix = (
        jnp.dot(gathered_query_rows, gathered_document_rows.T, precision=exact_product_accuracy)
        / contrast_sharpness_factor
    )
    peak_logit = jnp.max(pairwise_affinity_matrix, -1, keepdims=True)
    log_partition_norm = peak_logit + jnp.log(
        jnp.sum(jnp.exp(pairwise_affinity_matrix - peak_logit), -1, keepdims=True)
    )
    columns = lax.broadcasted_iota(jnp.int32, pairwise_affinity_matrix.shape, 1)
    matching_labels = columns == positives[:, None]
    picked = jnp.sum(jnp.where(matching_labels, pairwise_affinity_matrix, 0.0), -1, keepdims=True)
    total = jnp.sum(log_partition_norm - picked)
    loss = total / queries_total
    similarity_gradient = (
        jnp.exp(pairwise_affinity_matrix - log_partition_norm) - matching_labels.astype(jnp.float32)
    ) / contrast_sharpness_factor
    own_rows = lax.dynamic_slice_in_dim(similarity_gradient, device_id * QPD, QPD, 0)
    query_side = jnp.dot(own_rows, gathered_document_rows, precision=exact_product_accuracy)
    own_column = lax.dynamic_slice_in_dim(similarity_gradient, device_id, 1, 1)
    doc_side = jnp.dot(own_column.T, gathered_query_rows, precision=exact_product_accuracy)
    doc_side = jnp.concatenate([doc_side, jnp.zeros((QPD - 1, D), jnp.float32)], 0)
    embed_grad = jnp.where(tower_id == 0, query_side, doc_side)
    pooled_grad = normal_back(embed_grad)[0]
    top_grad = jnp.dot(pool_matrix.T, pooled_grad, precision=exact_product_accuracy)
    sum_two, gain_two_grad, bias_two_grad = norm_two_back(top_grad)
    attention_input_cotangent, out_back, gate_back, up_back, down_back = (
        qkv_full,
        out_full,
        gate_full,
        up_full,
        down_full,
    )
    branch_low = sum_two.astype(jnp.bfloat16)
    down_grad = product(hidden.T, branch_low)
    hidden_grad = product(branch_low, down_back.T)
    gate_grad_wide, up_grad_wide = swish_back(hidden_grad)
    gate_low = gate_grad_wide.astype(jnp.bfloat16)
    up_low = up_grad_wide.astype(jnp.bfloat16)
    gate_weight_grad = product(feed.T, gate_low)
    up_weight_grad = product(feed.T, up_low)
    feed_grad = sum_two + product(gate_low, gate_back.T) + product(up_low, up_back.T)
    sum_one, gain_one_grad, bias_one_grad = norm_one_back(feed_grad)
    attend_low = sum_one.astype(jnp.bfloat16)
    out_grad = product(mixed_low.T, attend_low)
    mixed_grad = product(attend_low, out_back.T).astype(jnp.bfloat16).reshape(count, HEADS, HEAD)
    probs_again = jnp.exp(masked_scores() - log_total)
    prob_grad = jnp.einsum(
        "ihd,jhd->hij", mixed_grad, value_low, preferred_element_type=jnp.float32
    )
    score_grad = probs_again * (prob_grad - jnp.sum(probs_again * prob_grad, -1, keepdims=True))
    score_low = score_grad.astype(jnp.bfloat16)
    query_grad = (
        jnp.einsum("hij,jhd->ihd", score_low, key_low, preferred_element_type=jnp.float32) * scale
    )
    key_grad = (
        jnp.einsum("hij,ihd->jhd", score_low, query_low, preferred_element_type=jnp.float32) * scale
    )
    value_grad = jnp.einsum(
        "hij,ihd->jhd",
        probs_again.astype(jnp.bfloat16),
        mixed_grad,
        preferred_element_type=jnp.float32,
    )
    raw_query_grad, raw_key_grad = rotary_back((query_grad, key_grad))
    packed_grad = jnp.concatenate(
        [
            raw_query_grad.reshape(count, D),
            raw_key_grad.reshape(count, D),
            value_grad.reshape(count, D),
        ],
        1,
    ).astype(jnp.bfloat16)
    qkv_grad = product(inputs.T, packed_grad)
    input_grad = sum_one + product(packed_grad, attention_input_cotangent.T)
    gradients = (
        qkv_grad,
        out_grad,
        gate_weight_grad,
        up_weight_grad,
        down_grad,
        gain_one_grad,
        bias_one_grad,
        gain_two_grad,
        bias_two_grad,
    )
    partial_sums = (
        lax.psum_scatter(gradients[0], DP, scatter_dimension=0, tiled=True),
        lax.psum_scatter(gradients[1], DP, scatter_dimension=0, tiled=True),
        lax.psum_scatter(gradients[2], DP, scatter_dimension=0, tiled=True),
        lax.psum_scatter(gradients[3], DP, scatter_dimension=0, tiled=True),
        lax.psum_scatter(gradients[4], DP, scatter_dimension=0, tiled=True),
        lax.psum_scatter(gradients[5], DP, scatter_dimension=0, tiled=True),
        lax.psum_scatter(gradients[6], DP, scatter_dimension=0, tiled=True),
        lax.psum_scatter(gradients[7], DP, scatter_dimension=0, tiled=True),
        lax.psum_scatter(gradients[8], DP, scatter_dimension=0, tiled=True),
    )
    tower_halves = (
        lax.psum_scatter(
            partial_sums[0].astype(jnp.bfloat16), TOWER, scatter_dimension=0, tiled=True
        ).astype(jnp.float32),
        lax.psum_scatter(
            partial_sums[1].astype(jnp.bfloat16), TOWER, scatter_dimension=0, tiled=True
        ).astype(jnp.float32),
        lax.psum_scatter(
            partial_sums[2].astype(jnp.bfloat16), TOWER, scatter_dimension=0, tiled=True
        ).astype(jnp.float32),
        lax.psum_scatter(
            partial_sums[3].astype(jnp.bfloat16), TOWER, scatter_dimension=0, tiled=True
        ).astype(jnp.float32),
        lax.psum_scatter(
            partial_sums[4].astype(jnp.bfloat16), TOWER, scatter_dimension=0, tiled=True
        ).astype(jnp.float32),
        lax.psum_scatter(
            partial_sums[5].astype(jnp.bfloat16), TOWER, scatter_dimension=0, tiled=True
        ).astype(jnp.float32),
        lax.psum_scatter(
            partial_sums[6].astype(jnp.bfloat16), TOWER, scatter_dimension=0, tiled=True
        ).astype(jnp.float32),
        lax.psum_scatter(
            partial_sums[7].astype(jnp.bfloat16), TOWER, scatter_dimension=0, tiled=True
        ).astype(jnp.float32),
        lax.psum_scatter(
            partial_sums[8].astype(jnp.bfloat16), TOWER, scatter_dimension=0, tiled=True
        ).astype(jnp.float32),
    )
    shares = (
        lax.all_gather(tower_halves[0].astype(jnp.bfloat16), TOWER, axis=0, tiled=True).astype(
            jnp.float32
        ),
        lax.all_gather(tower_halves[1].astype(jnp.bfloat16), TOWER, axis=0, tiled=True).astype(
            jnp.float32
        ),
        lax.all_gather(tower_halves[2].astype(jnp.bfloat16), TOWER, axis=0, tiled=True).astype(
            jnp.float32
        ),
        lax.all_gather(tower_halves[3].astype(jnp.bfloat16), TOWER, axis=0, tiled=True).astype(
            jnp.float32
        ),
        lax.all_gather(tower_halves[4].astype(jnp.bfloat16), TOWER, axis=0, tiled=True).astype(
            jnp.float32
        ),
        lax.all_gather(tower_halves[5].astype(jnp.bfloat16), TOWER, axis=0, tiled=True).astype(
            jnp.float32
        ),
        lax.all_gather(tower_halves[6].astype(jnp.bfloat16), TOWER, axis=0, tiled=True).astype(
            jnp.float32
        ),
        lax.all_gather(tower_halves[7].astype(jnp.bfloat16), TOWER, axis=0, tiled=True).astype(
            jnp.float32
        ),
        lax.all_gather(tower_halves[8].astype(jnp.bfloat16), TOWER, axis=0, tiled=True).astype(
            jnp.float32
        ),
    )
    query_rows = lax.dynamic_slice_in_dim(gathered_query_rows, device_id * QPD, QPD, 0)
    doc_row = lax.dynamic_slice_in_dim(gathered_document_rows, device_id, 1, 0)
    return (loss, query_rows, doc_row, input_grad[None]) + tuple(shares)


MESH = pl.DeviceIdType.MESH
BF = jnp.bfloat16
F32 = jnp.float32
LANES = 128


def dot_tt(left, right, precision=None):
    return lax.dot_general(
        left, right, (((1,), (1,)), ((), ())), preferred_element_type=F32, precision=precision
    )


def dot_t0(left, right, precision=None):
    return lax.dot_general(
        left, right, (((0,), (0,)), ((), ())), preferred_element_type=F32, precision=precision
    )


def rotary_constants(count):
    freqs = np.power(
        np.float32(rope_base), (-2.0 * np.arange(HEAD // 2) / HEAD).astype(np.float32)
    ).astype(np.float32)
    angles = (np.arange(count, dtype=np.float32)[:, None] * freqs[None, :]).astype(np.float64)
    cosines, sines = np.cos(angles), np.sin(angles)
    return (
        np.tile(np.concatenate([cosines, cosines], 1), (1, 2)).astype(np.float32),
        np.tile(np.concatenate([-sines, sines], 1), (1, 2)).astype(np.float32),
    )


def aligned(start, unit):
    return start if isinstance(start, int) else pl.multiple_of(start, unit)


def both(first, second):
    return jnp.logical_and(first, second)


def do(condition, action):
    if condition is None:
        action()
    else:
        pl.when(condition)(action)


class Plan:
    def __init__(self, groups, count, shard, shard_ff, vec):
        self.groups = groups
        self.line = groups // 4
        self.count = count
        self.shard = shard
        self.shard_ff = shard_ff
        self.vec = vec
        self.width_a = 4 * D
        self.half_a = 2 * D
        self.ff = shard_ff * groups
        self.half_ff = self.ff // 2
        self.stripe = 2 * shard_ff


def semaphores(plan):
    line, groups = plan.line, plan.groups
    dma = pltpu.SemaphoreType.DMA
    chunks_gu, chunks_a = 4, 4
    return dict(
        loc=dma((20,)),
        ra=dma((groups, 2)),
        sa_z=dma((2, line)),
        sa_x=dma((line, 2)),
        sa_y=dma((line, 2)),
        sa_c=dma((line, 2, 2)),
        rg=dma((groups,)),
        sg_z=dma((2, line)),
        sg_x=dma((line,)),
        sg_c=dma((line, 2)),
        rd=dma((line, 2)),
        sd_x=dma((1,)),
        sd_z=dma((2, line)),
        sd_c=dma((line,)),
        rv=dma((groups,)),
        sv=dma((groups,)),
        sx=dma((4,)),
        rx=dma((4,)),
        r_doc=dma((groups,)),
        s_doc=dma((groups,)),
        r_slope=dma((groups,)),
        s_slope=dma((groups,)),
        r_query=dma((1,)),
        s_query=dma((1,)),
        s_ln=dma((line.bit_length() + 2,)),
        r_ln=dma((line.bit_length() + 2,)),
        gd_c=dma((2, line)),
        gd_z=dma((2, 2, line)),
        gd_x=dma((2,)),
        gd_y=dma((2,)),
        gg_c=dma((2, chunks_gu)),
        gg_x=dma((2, chunks_gu)),
        gg_z=dma((2, chunks_gu, 2, line)),
        gg_y=dma((2, chunks_gu)),
        ga_c=dma((2, 2, chunks_a)),
        ga_t=dma((2, chunks_a)),
        ga_x=dma((2, chunks_a)),
        ga_z=dma((2, chunks_a, 2, line)),
        ga_y=dma((2, chunks_a)),
        fin=dma((9,)),
    )


def buffers(plan):
    line, count, shard, groups = plan.line, plan.count, plan.shard, plan.groups
    pair = 2 * count
    v = pltpu.VMEM
    return dict(
        wa=v((line, 2, 2, shard, plan.width_a), BF),
        wg=v((line, 2, 2, shard, plan.ff), BF),
        wd=v((line, 2, plan.shard_ff, D), BF),
        vt=v((groups, 16, LANES), BF),
        vec=v((16, D), F32),
        cos=v((count, LANES), F32),
        sin=v((count, LANES), F32),
        hide=v((count, count), F32),
        pw=v((count, 1), F32),
        qkv=v((count, 3 * D), BF),
        probs=v((HEADS, count, count), F32),
        mixed=v((count, D), BF),
        mixt=v((D, count), BF),
        tokt=v((D, count), BF),
        h1=v((count, D), F32),
        rs1=v((count, 1), F32),
        n1=v((count, D), F32),
        feed=v((pair, D), BF),
        feedt=v((D, pair), BF),
        gate=v((pair, plan.half_ff), F32),
        up=v((pair, plan.half_ff), F32),
        hidt=v((plan.half_ff, pair), BF),
        dgu=v((pair, plan.ff), BF),
        bown=v((count, D), F32),
        bsend=v((count, D), BF),
        brecv=v((count, D), BF),
        xh2=v((count, D), F32),
        rs2=v((count, 1), F32),
        dbr=v((pair, D), BF),
        dsend=v((count, D), BF),
        drecv=v((count, D), BF),
        datt=v((count, D), BF),
        pool=v((8, D), F32),
        dpool=v((8, D), F32),
        emb=v((8, D), F32),
        embd=v((1, D), F32),
        embq=v((QPD, D), F32),
        dbuf=v((groups, 1, D), F32),
        cbuf=v((groups, 1, D), F32),
        csend=v((groups, 1, D), F32),
        qrecv=v((QPD, D), F32),
        dflat=v((groups, D), F32),
        ln=v((line.bit_length() + 3, 8, D), F32),
        lnr=v((line.bit_length() + 2, 8, D), F32),
        gd=v((line, 2, plan.shard_ff, D), BF),
        gd_rc=v((line, plan.shard_ff, D), BF),
        gd_rz=v((line + 1, plan.shard_ff, D), BF),
        gd_rx=v((plan.shard_ff, D), BF),
        gd_f=v((plan.shard_ff, D), BF),
        gg=v((line, 2, 2, shard, plan.ff), BF),
        gg_rc=v((line, 2, shard, plan.ff), BF),
        gg_rx=v((line, shard, plan.ff), BF),
        gg_rz=v((line + 1, shard, plan.ff), BF),
        gg_f=v((shard, plan.ff), BF),
        ga_rc=v((line, 2, shard, plan.width_a), BF),
        ga_rt=v((line, 2, shard, plan.half_a), BF),
        ga_rx=v((line, shard, plan.half_a), BF),
        ga_rz=v((line + 1, shard, plan.half_a), BF),
        ga_f=v((shard, plan.half_a), BF),
    )


class Operands(NamedTuple):
    qlen: Any
    dlen: Any
    pos: Any
    posv: Any
    tok: Any
    tcos: Any
    tsin: Any
    tile: Any
    i_qkv: Any
    i_out: Any
    i_gate: Any
    i_up: Any
    i_down: Any


class Results(NamedTuple):
    o_tok: Any
    o_a: Any
    o_gu: Any
    o_dn: Any
    o_vec: Any
    o_q: Any
    o_d: Any
    o_loss: Any


def whole_step(plan, *refs):
    names = (Operands._fields + Results._fields + tuple(buffers(plan)) + tuple(semaphores(plan)))
    r = SimpleNamespace(**dict(zip(names, refs, strict=True)))
    line, groups, count = plan.line, plan.groups, plan.count
    shard, shard_ff, stripe = plan.shard, plan.shard_ff, plan.stripe
    half_a, half_ff, ff = plan.half_a, plan.half_ff, plan.ff
    quarter = QLEN
    shift = QLEN.bit_length() - 1

    t = lax.axis_index(TOWER)
    me = lax.axis_index(DP)
    z = me // 4
    x = (me // 2) % 2
    c = me % 2

    def at(zz, xx, cc):
        return (zz * 2 + xx) * 2 + cc

    dev_x = {TOWER: t, DP: at(z, 1 - x, c)}
    dev_c = {TOWER: t, DP: at(z, x, 1 - c)}
    dev_y = {TOWER: 1 - t, DP: me}

    def dev_z(zz):
        return {TOWER: t, DP: at(zz, x, c)}

    pending, tail = [], []

    def copy(src, dst, ssem, rsem, dev):
        return pltpu.make_async_remote_copy(
            src_ref=src, dst_ref=dst, send_sem=ssem, recv_sem=rsem,
            device_id=dev, device_id_type=MESH,
        )

    def send(cond, what, keep=pending):
        do(cond, what.start)
        keep.append((cond, what))

    def settle(keep):
        for cond, what in keep:
            do(cond, what.wait_send)
        keep.clear()

    def got(cond, ref, rsem):
        do(cond, copy(ref, ref, r.s_query.at[0], rsem, dev_x).wait_recv)

    wa, wg, wd = r.wa, r.wg, r.wd
    out_w = half_a - 3 * D // 2
    local = []

    def near(src, dst, cond=None):
        what = pltpu.make_async_copy(src, dst, r.loc.at[len(local)])
        do(cond, what.start)
        local.append((cond, what))

    third = 3 * D // 2
    for h in range(2):
        near(r.i_qkv.at[:, pl.ds(h * third, third)],
             wa.at[z, x, c, :, pl.ds(h * half_a, third)])
        near(r.i_out.at[:, pl.ds(h * out_w, out_w)],
             wa.at[z, x, c, :, pl.ds(h * half_a + third, out_w)])
    near(r.i_down, wd.at[z, c], x == t)
    near(r.tile, r.vt.at[me])
    for s in range(line):
        for k, ref in enumerate((r.i_gate, r.i_up)):
            near(ref.at[:, pl.ds(aligned((2 * s + t) * stripe, LANES), stripe)],
                 wg.at[z, x, c, :, pl.ds(k * half_ff + s * stripe, stripe)])

    barrier = pltpu.get_barrier_semaphore()

    def greet(j, carry):
        other = jnp.logical_or(j // groups != t, j % groups != me)

        @pl.when(other)
        def _():
            pl.semaphore_signal(
                barrier, inc=1, device_id={TOWER: j // groups, DP: j % groups},
                device_id_type=MESH,
            )

        return carry

    lax.fori_loop(0, 2 * groups, greet, 0)
    pl.semaphore_wait(barrier, 2 * groups - 1)
    for cond, what in local:
        do(cond, what.wait)

    def piece_a(zz, xx, cc, h):
        return wa.at[zz, xx, cc, :, pl.ds(aligned(h * half_a, LANES), half_a)]

    def send_a(cond, sem, zz, xx, h, dev):
        ref = piece_a(zz, xx, c, h)
        send(cond, copy(ref, ref, sem, r.ra.at[at(zz, xx, c), h], dev))

    def got_a(cond, zz, xx, cc, h):
        got(cond, piece_a(zz, xx, cc, h), r.ra.at[at(zz, xx, cc), h])

    def sides(step):
        yield z - step, z >= step, z < line - 1, z + 1, 0
        yield z + step, z < line - step, z > 0, z - 1, 1

    def a_round(step):
        for zz, there, on, nxt, way in sides(step):
            if step:
                got_a(there, zz, x, c, t)
            send_a(both(there, on), r.sa_z.at[way, zz], zz, x, t, dev_z(nxt))
            if step or way == 0:
                send_a(there, r.sa_x.at[zz, t], zz, x, t, dev_x)
                if step:
                    send_a(there, r.sa_y.at[zz, x], zz, x, t, dev_y)
                else:
                    send_a(None, r.sa_x.at[zz, 1 - t], zz, x, 1 - t, dev_x)
                send_a(there, r.sa_c.at[zz, x, t], zz, x, t, dev_c)
        if step == 0:
            send_a(None, r.sa_c.at[z, x, 1 - t], z, x, 1 - t, dev_c)

    def around(step):
        return list(sides(step))[: 1 if step == 0 else 2]

    def a_cross(step):
        for zz, there, _, _, _ in around(step):
            got_a(there, zz, 1 - x, c, t)
            if step:
                send_a(there, r.sa_y.at[zz, 1 - x], zz, 1 - x, t, dev_y)
            else:
                got_a(None, zz, 1 - x, c, 1 - t)
                send_a(None, r.sa_c.at[zz, 1 - x, 1 - t], zz, 1 - x, 1 - t, dev_c)
            send_a(there, r.sa_c.at[zz, 1 - x, t], zz, 1 - x, t, dev_c)

    def a_tower(step):
        for zz, there, _, _, _ in sides(step):
            for xx in (x, 1 - x):
                got_a(there, zz, xx, c, 1 - t)
                send_a(there, r.sa_c.at[zz, xx, 1 - t], zz, xx, 1 - t, dev_c)

    def a_sibling():
        for zz in range(line):
            for xx in range(2):
                for h in range(2):
                    got_a(None, zz, xx, 1 - c, h)

    def send_g(cond, sem, zz, xx, dev):
        ref = wg.at[zz, xx, c]
        send(cond, copy(ref, ref, sem, r.rg.at[at(zz, xx, c)], dev))

    def got_g(cond, zz, xx, cc):
        got(cond, wg.at[zz, xx, cc], r.rg.at[at(zz, xx, cc)])

    def g_line(step):
        for zz, there, on, nxt, way in sides(step):
            if step:
                got_g(there, zz, x, c)
            send_g(both(there, on), r.sg_z.at[way, zz], zz, x, dev_z(nxt))

    def g_spread(step):
        for zz, there, _, _, _ in around(step):
            send_g(there, r.sg_x.at[zz], zz, x, dev_x)
            send_g(there, r.sg_c.at[zz, x], zz, x, dev_c)

    def g_cross(step):
        for zz, there, _, _, _ in around(step):
            got_g(there, zz, 1 - x, c)
            send_g(there, r.sg_c.at[zz, 1 - x], zz, 1 - x, dev_c)

    def g_sibling():
        for zz in range(line):
            for xx in range(2):
                got_g(None, zz, xx, 1 - c)

    def send_d(cond, sem, zz, dev):
        ref = wd.at[zz, c]
        send(cond, copy(ref, ref, sem, r.rd.at[zz, c], dev))

    def got_d(cond, zz, cc):
        got(cond, wd.at[zz, cc], r.rd.at[zz, cc])

    def d_cross():
        send_d(x == t, r.sd_x.at[0], z, dev_x)

    def d_round(step):
        for zz, there, on, nxt, way in sides(step):
            if step:
                got_d(there, zz, c)
            elif way == 0:
                got_d(x != t, z, c)
            send_d(both(there, on), r.sd_z.at[way, zz], zz, dev_z(nxt))
            if step or way == 0:
                send_d(there, r.sd_c.at[zz], zz, dev_c)

    def d_sibling():
        for zz in range(line):
            got_d(None, zz, 1 - c)

    def v_send(j, carry):
        @pl.when(j != me)
        def _():
            copy(r.vt.at[me], r.vt.at[me], r.sv.at[j], r.rv.at[me],
                 {TOWER: t, DP: j}).start()

        return carry

    def v_wait(j, carry):
        @pl.when(j != me)
        def _():
            copy(r.vt.at[me], r.vt.at[j], r.sv.at[j], r.rv.at[j],
                 {TOWER: t, DP: j}).wait()

        return carry

    a_round(0)
    lax.fori_loop(0, groups, v_send, 0)

    tok = r.tok
    rows = lax.broadcasted_iota(jnp.int32, (count, count), 0)
    cols = lax.broadcasted_iota(jnp.int32, (count, count), 1)
    seg = cols >> shift
    limit = jnp.zeros_like(cols)
    for s in range(QPD):
        limit = jnp.where(seg == s, r.qlen[s], limit)
    limit = limit * (1 - t) + r.dlen[0] * t
    place = cols - seg * (quarter * (1 - t))
    apart = ((rows >> shift) - seg) * (1 - t)
    seen = both(apart == 0, place < limit)
    r.hide[...] = jnp.where(seen, 0.0, -1e30)
    for s in range(QPD):
        part = pl.ds(s * quarter, quarter)
        length = jnp.full((quarter, 1), r.qlen[s] * (1 - t) + r.dlen[0] * t, jnp.int32)
        slot = lax.broadcasted_iota(jnp.int32, (quarter, 1), 0) + s * quarter * t
        r.pw[part, :] = jnp.where(slot < length, 1.0 / length.astype(F32), 0.0)
        begin = aligned(s * quarter * t, quarter)
        r.cos[part, :] = r.tcos[pl.ds(begin, quarter), :]
        r.sin[part, :] = r.tsin[pl.ds(begin, quarter), :]
    lanes = lax.broadcasted_iota(jnp.int32, (count, LANES), 1)
    first_head = lanes < HEAD
    low_half = (lanes & (HEAD - 1)) < HEAD // 2

    def swap(a):
        return jnp.where(low_half, pltpu.roll(a, LANES - HEAD // 2, 1), pltpu.roll(a, HEAD // 2, 1))

    def turn(a):
        return a * r.cos[...] + swap(a) * r.sin[...]

    def turn_back(a):
        return a * r.cos[...] - swap(a) * r.sin[...]

    def transpose_into(dst, src, width):
        def body(j, carry):
            o = aligned(j * LANES, LANES)
            dst[pl.ds(o, LANES), :] = src[:, pl.ds(o, LANES)].T
            return carry

        lax.fori_loop(0, width // LANES, body, 0)

    def wide(ref, lo, n):
        return ref[:, :, :, :, pl.ds(lo, n)].reshape(groups * shard, n)

    def qkv_lane(u):
        split = 3 * D // 2 // LANES
        return aligned(jnp.where(u < split, u, u + out_w // LANES) * LANES, LANES)

    def widen_vec(j, acc):
        row = lax.broadcasted_iota(jnp.int32, (LANES, D), 0)
        col = lax.broadcasted_iota(jnp.int32, (LANES, D), 1)
        pick = jnp.where(col == row + j * plan.vec, 1.0, 0.0).astype(BF)
        return acc + jnp.dot(r.vt[j], pick, preferred_element_type=F32)

    transpose_into(r.tokt, tok, D)
    a_round(1)
    a_cross(0)
    for step in range(2, line):
        a_round(step)
        if step == 2:
            g_line(0)
        a_cross(step - 1)
    g_spread(0)
    d_cross()
    lax.fori_loop(0, groups, v_wait, 0)
    r.vec[...] = lax.fori_loop(0, groups, widen_vec, jnp.zeros((16, D), F32))
    a_tower(1)
    a_cross(line - 1)
    g_line(1)
    g_spread(1)
    d_round(0)
    for step in range(2, line):
        a_tower(step)
    a_sibling()
    pairs = D // LANES

    scale = HEAD ** (-0.5)

    def project(p, carry):
        w = jnp.concatenate(
            [wide(wa, qkv_lane(p + k * pairs), LANES) for k in range(3)], axis=1
        )
        packed = jnp.dot(tok[...], w, preferred_element_type=F32)
        o = aligned(p * LANES, LANES)
        r.qkv[:, pl.ds(o, LANES)] = (turn(packed[:, :LANES]) * scale).astype(BF)
        r.qkv[:, pl.ds(D + o, LANES)] = turn(packed[:, LANES : 2 * LANES]).astype(BF)
        r.qkv[:, pl.ds(2 * D + o, LANES)] = packed[:, 2 * LANES :].astype(BF)
        return carry

    def triple(p):
        o = aligned(p * LANES, LANES)
        return tuple(r.qkv[:, pl.ds(k * D + o, LANES)] for k in range(3))

    def only(h, a):
        return jnp.where(first_head if h == 0 else jnp.logical_not(first_head), a, jnp.zeros_like(a))

    def attend(p, carry):
        q2, k2, v2 = triple(p)
        outs = []
        for h in range(2):
            scores = dot_tt(only(h, q2), k2) + r.hide[...]
            grown = jnp.exp(scores - jnp.max(scores, -1, keepdims=True))
            probs = grown * (1.0 / jnp.sum(grown, -1, keepdims=True))
            r.probs[2 * p + h] = probs
            outs.append(jnp.dot(probs.astype(BF), v2, preferred_element_type=F32))
        o = aligned(p * LANES, LANES)
        r.mixed[:, pl.ds(o, LANES)] = jnp.where(first_head, outs[0], outs[1]).astype(BF)
        return carry

    lax.fori_loop(0, pairs, project, 0)
    g_line(2)
    g_cross(0)
    g_spread(2)
    lax.fori_loop(0, pairs // 2, attend, 0)
    for step in range(3, line):
        g_line(step)
    d_round(1)
    g_cross(1)
    for step in range(3, line):
        g_spread(step)
    lax.fori_loop(pairs // 2, pairs, attend, 0)

    for h in range(2):
        part = jnp.dot(r.mixed[...], wide(wa, h * half_a + 3 * D // 2, out_w),
                       preferred_element_type=F32)
        r.h1[:, pl.ds(h * out_w, out_w)] = tok[:, pl.ds(h * out_w, out_w)].astype(F32) + part

    def moments(h):
        centred = h - jnp.mean(h, -1, keepdims=True)
        return centred, lax.rsqrt(jnp.mean(centred * centred, -1, keepdims=True) + 1e-05)

    blocks = count // quarter

    def norm_one(b, carry):
        part = pl.ds(aligned(b * quarter, quarter), quarter)
        centred, inverse = moments(r.h1[part, :])
        hat = centred * inverse
        normed = hat * r.vec[0:1, :] + r.vec[1:2, :]
        r.h1[part, :] = hat
        r.rs1[part, :] = inverse
        r.n1[part, :] = normed
        r.feed[pl.ds(aligned(t * count + b * quarter, quarter), quarter), :] = (
            normed.astype(BF))
        return carry

    lax.fori_loop(0, blocks, norm_one, 0)
    mine = pl.ds(aligned(t * count, count), count)
    theirs = pl.ds(aligned((1 - t) * count, count), count)

    def swap_rows(k, src, dst):
        send(None, copy(src, dst, r.sx.at[k], r.rx.at[k], dev_y), tail)

    def got_rows(k, ref):
        got(None, ref, r.rx.at[k])

    swap_rows(0, r.feed.at[mine], r.feed.at[mine])
    transpose_into(r.mixt, r.mixed, D)
    for step in range(2, line):
        g_cross(step)
        d_round(step)
    g_sibling()

    step_ff = 2 * LANES

    def gated(j, carry):
        o = aligned(j * step_ff, step_ff)
        gate = jnp.dot(r.feed[...], wide(wg, o, step_ff), preferred_element_type=F32)
        up = jnp.dot(r.feed[...], wide(wg, half_ff + o, step_ff), preferred_element_type=F32)
        r.gate[:, pl.ds(o, step_ff)] = gate
        r.up[:, pl.ds(o, step_ff)] = up
        hidden = (gate * jax.nn.sigmoid(gate) * up).astype(BF)
        r.dgu[:, pl.ds(o, step_ff)] = hidden
        r.hidt[pl.ds(o, step_ff), :] = hidden.T
        return carry

    got_rows(0, r.feed.at[theirs])
    lax.fori_loop(0, half_ff // step_ff, gated, 0)
    d_sibling()

    def down(rows_of, store):
        def body(j, carry):
            o = aligned(j * step_ff, step_ff)
            w = wd[:, :, :, pl.ds(o, step_ff)].reshape(half_ff, step_ff)
            store(o, jnp.dot(r.dgu[rows_of, pl.ds(0, half_ff)], w, preferred_element_type=F32))
            return carry

        lax.fori_loop(0, D // step_ff, body, 0)

    def keep_send(o, val):
        r.bsend[:, pl.ds(o, step_ff)] = val.astype(BF)

    def keep_own(o, val):
        r.bown[:, pl.ds(o, step_ff)] = val

    down(theirs, keep_send)
    swap_rows(1, r.bsend, r.brecv)
    down(mine, keep_own)
    transpose_into(r.feedt, r.feed, D)
    got_rows(1, r.brecv)

    r.pool[...] = jnp.zeros((8, D), F32)

    def norm_two(b, carry):
        part = pl.ds(aligned(b * quarter, quarter), quarter)
        h = r.n1[part, :] + (r.bown[part, :] + r.brecv[part, :].astype(F32))
        centred, inverse = moments(h)
        hat = centred * inverse
        normed = hat * r.vec[2:3, :] + r.vec[3:4, :]
        r.xh2[part, :] = hat
        r.rs2[part, :] = inverse
        r.pool[pl.ds(b, 1), :] = jnp.sum(normed * r.pw[part, :], 0, keepdims=True)
        return carry

    lax.fori_loop(0, blocks, norm_two, 0)
    row8 = lax.broadcasted_iota(jnp.int32, (8, D), 0)

    @pl.when(t == 1)
    def _():
        all_rows = jnp.sum(r.pool[...], 0, keepdims=True)
        r.pool[...] = jnp.where(row8 == 0, all_rows, 0.0)

    pooled = r.pool[...]
    shrink = lax.rsqrt(jnp.sum(pooled * pooled, -1, keepdims=True) + 1e-06)
    r.emb[...] = pooled * shrink

    best = exact_product_accuracy
    r.dpool[...] = jnp.zeros((8, D), F32)
    r.ln[0] = jnp.zeros((8, D), F32)

    def to_all(tower, src, dst, ssem, rsem):
        def give(step, carry):
            j = (me + step) % groups
            copy(src(j), dst.at[me], ssem.at[j], rsem.at[me], {TOWER: tower, DP: j}).start()
            return carry

        lax.fori_loop(0, groups, give, 0)

    def from_all(dst, ssem, rsem):
        def take(j, carry):
            copy(dst.at[j], dst.at[j], ssem.at[j], rsem.at[j], dev_x).wait_recv()
            return carry

        lax.fori_loop(0, groups, take, 0)

    @pl.when(t == 1)
    def _():
        r.embd[...] = r.emb[0:1, :]
        r.dbuf[me] = r.emb[0:1, :]
        to_all(0, lambda j: r.embd, r.dbuf, r.s_doc, r.r_doc)
        from_all(r.cbuf, r.s_slope, r.r_slope)
        total = r.cbuf[0]
        for j in range(1, groups):
            total = total + r.cbuf[j]
        r.dpool[0:1, :] = total

    @pl.when(t == 0)
    def _():
        r.embq[...] = r.emb[0:QPD, :]
        from_all(r.dbuf, r.s_doc, r.r_doc)
        for j in range(groups):
            r.dflat[pl.ds(j, 1), :] = r.dbuf[j]
        docs, queries = r.dflat[...], r.embq[...]
        logits = dot_tt(queries, docs, best) / contrast_sharpness_factor
        peak = jnp.max(logits, -1, keepdims=True)
        lse = peak + jnp.log(jnp.sum(jnp.exp(logits - peak), -1, keepdims=True))
        col = lax.broadcasted_iota(jnp.int32, (QPD, groups), 1)
        row = lax.broadcasted_iota(jnp.int32, (QPD, groups), 0)
        label = jnp.zeros((QPD, groups), jnp.int32)
        for s in range(QPD):
            label = jnp.where(row == s, r.pos[me * QPD + s], label)
        hot = jnp.where(col == label, 1.0, 0.0)
        slope = (jnp.exp(logits - lse) - hot) / contrast_sharpness_factor
        back = dot_t0(slope, queries, best)
        for j in range(groups):
            r.csend[j] = back[j : j + 1, :]
        to_all(1, lambda j: r.csend.at[j], r.cbuf, r.s_slope, r.r_slope)
        r.dpool[0:QPD, :] = jnp.dot(slope, docs, preferred_element_type=F32, precision=best)
        picked = jnp.sum(jnp.where(hot > 0.5, logits, 0.0), -1, keepdims=True)
        total = jnp.sum(lse - picked, 0, keepdims=True)
        r.ln[0] = jnp.where(row8 == 4, total, 0.0)

    slope = r.dpool[...]
    emb = r.emb[...]
    dpool = shrink * (slope - emb * jnp.sum(slope * emb, -1, keepdims=True))

    @pl.when(t == 0)
    def _():
        r.dpool[...] = dpool

    @pl.when(t == 1)
    def _():
        r.dpool[...] = jnp.broadcast_to(dpool[0:1, :], (8, D))

    def norm_two_back(b, sums):
        part = pl.ds(aligned(b * quarter, quarter), quarter)
        top = r.pw[part, :] * r.dpool[pl.ds(b, 1), :]
        hat = r.xh2[part, :]
        inner = top * r.vec[2:3, :]
        grad = r.rs2[part, :] * (
            inner - jnp.mean(inner, -1, keepdims=True)
            - hat * jnp.mean(inner * hat, -1, keepdims=True))
        r.n1[part, :] = grad
        r.dbr[pl.ds(aligned(t * count + b * quarter, quarter), quarter), :] = (
            grad.astype(BF))
        return (sums[0] + jnp.sum(top * hat, 0, keepdims=True),
                sums[1] + jnp.sum(top, 0, keepdims=True))

    zero_row = jnp.zeros((1, D), F32)
    gain_two, bias_two = lax.fori_loop(0, blocks, norm_two_back, (zero_row, zero_row))
    swap_rows(2, r.dbr.at[mine], r.dbr.at[mine])

    send(t == 0, copy(r.embq, r.qrecv, r.s_query.at[0], r.r_query.at[0], dev_y), tail)
    r.ln[0] = (r.ln[0] + jnp.where(row8 == 2, gain_two, 0.0)
               + jnp.where(row8 == 3, bias_two, 0.0))

    def hidden_back(rows_of):
        def body(j, carry):
            o = aligned(j * stripe, LANES)
            w = wd[j].reshape(stripe, D)
            slope = dot_tt(r.dbr[rows_of, :], w)
            gate = r.gate[rows_of, pl.ds(o, stripe)]
            up = r.up[rows_of, pl.ds(o, stripe)]
            sig = jax.nn.sigmoid(gate)
            r.dgu[rows_of, pl.ds(o, stripe)] = (
                slope * up * (sig * (1.0 + gate * (1.0 - sig)))).astype(BF)
            r.dgu[rows_of, pl.ds(half_ff + o, stripe)] = (slope * (gate * sig)).astype(BF)
            return carry

        lax.fori_loop(0, line, body, 0)

    def along(step):
        for s in range(1, line):
            yield line - s, both(z == step, z < line - s), z + 1, 0
        for s in range(line - 1):
            yield s, both(z == line - 1 - step, z > s), z - 1, 1

    def added(refs):
        total = refs[0][...].astype(F32)
        for ref in refs[1:]:
            total = total + ref[...].astype(F32)
        return total

    def line_step(step, parts, sem, slot, only_at=None):
        for k, (dest, cond, nxt, way) in enumerate(along(step)):
            if only_at is not None and k % (line - 1) != only_at:
                continue
            into = slot(dest + 1 if way == 0 else dest)
            refs = parts(dest)

            def move(into=into, refs=refs, dest=dest, way=way):
                if step:
                    copy(into, into, r.s_query.at[0], sem(1, way, dest), dev_x).wait_recv()
                    refs[0][...] = added(refs + (into,)).astype(BF)
                else:
                    refs[0][...] = added(refs).astype(BF)

            do(cond, move)
            send(cond, copy(refs[0], into, sem(0, way, dest), sem(1, way, dest),
                            dev_z(nxt)), tail)

    def line_end(parts, sem, slot, put):
        for cond, ways in ((z == 0, (1,)), (z == line - 1, (0,)),
                           (both(z > 0, z < line - 1), (0, 1))):
            def finish(ways=ways):
                refs = parts(z)
                for way in ways:
                    into = slot(z + 1 if way == 0 else z)
                    copy(into, into, r.s_query.at[0], sem(1, way, z), dev_x).wait_recv()
                    refs = refs + (into,)
                put[...] = added(refs).astype(BF)

            do(cond, finish)

    gd = r.gd

    def down_half(s, rows_of):
        return jnp.dot(r.hidt[pl.ds(s * stripe, stripe), rows_of], r.dbr[rows_of, :],
                       preferred_element_type=F32)

    def down_own(s):
        gd[s] = down_half(s, mine).astype(BF).reshape(2, shard_ff, D)

    def down_grad(s):
        val = down_half(s, theirs) + gd[s].reshape(stripe, D).astype(F32)
        gd[s] = val.astype(BF).reshape(2, shard_ff, D)
        send(None, copy(gd.at[s, 1 - c], r.gd_rc.at[s], r.gd_c.at[0, s],
                        r.gd_c.at[1, s], dev_c), tail)

    def down_parts(dest):
        return gd.at[dest, c], r.gd_rc.at[dest]

    def down_arrive():
        for s in range(line):
            got(None, r.gd_rc.at[s], r.gd_c.at[1, s])

    def down_line(step, only_at=None):
        line_step(step, down_parts, lambda *i: r.gd_z.at[i], lambda k: r.gd_rz.at[k], only_at)

    def down_end():
        line_end(down_parts, lambda *i: r.gd_z.at[i], lambda k: r.gd_rz.at[k], r.gd_f)
        send(x != t, copy(r.gd_f, r.gd_rx, r.gd_x.at[0], r.gd_x.at[1], dev_x), tail)

    out_copies = []

    def keep_out(k, src, dst, cond=None):
        what = pltpu.make_async_copy(src, dst, r.fin.at[k])
        do(cond, what.start)
        out_copies.append((cond, what))

    def down_out():
        def total():
            copy(r.gd_rx, r.gd_rx, r.s_query.at[0], r.gd_x.at[1], dev_x).wait_recv()
            r.gd_f[...] = added((r.gd_f, r.gd_rx)).astype(BF)

        do(x == t, total)
        keep_out(0, r.gd_f, r.o_dn, x == t)
        send(x == t, copy(r.gd_f, r.o_dn, r.gd_y.at[0], r.gd_y.at[1], dev_y), tail)

    gg = r.gg
    part_gu = ff // 4

    def gate_half(k, rows_of):
        return jnp.dot(r.feedt[:, rows_of], r.dgu[rows_of, pl.ds(k * part_gu, part_gu)],
                       preferred_element_type=F32)

    def gate_own(k):
        gg[:, :, :, :, pl.ds(k * part_gu, part_gu)] = gate_half(k, mine).astype(BF).reshape(
            line, 2, 2, shard, part_gu)

    def gate_grad(k):
        span = pl.ds(k * part_gu, part_gu)
        val = gate_half(k, theirs) + gg[:, :, :, :, span].reshape(groups * shard, part_gu).astype(F32)
        gg[:, :, :, :, span] = val.astype(BF).reshape(line, 2, 2, shard, part_gu)
        send(None, copy(gg.at[:, :, 1 - c, :, span], r.gg_rc.at[:, :, :, span],
                        r.gg_c.at[0, k], r.gg_c.at[1, k], dev_c), tail)

    def gate_cross(k):
        span = pl.ds(k * part_gu, part_gu)
        got(None, r.gg_rc.at[:, :, :, span], r.gg_c.at[1, k])
        for s in range(line):
            mine_k = gg.at[s, 1 - x, c, :, span]
            mine_k[...] = added((mine_k, r.gg_rc.at[s, 1 - x, :, span])).astype(BF)
        send(None, copy(gg.at[:, 1 - x, c, :, span], r.gg_rx.at[:, :, span],
                        r.gg_x.at[0, k], r.gg_x.at[1, k], dev_x), tail)

    def gate_parts(k):
        span = pl.ds(k * part_gu, part_gu)
        return lambda dest: (gg.at[dest, x, c, :, span], r.gg_rc.at[dest, x, :, span],
                             r.gg_rx.at[dest, :, span])

    def gate_line(k, step):
        span = pl.ds(k * part_gu, part_gu)
        if step == 0:
            got(None, r.gg_rx.at[:, :, span], r.gg_x.at[1, k])
        line_step(step, gate_parts(k), lambda a, *i: r.gg_z.at[(a, k) + i], lambda s: r.gg_rz.at[s, :, span])

    def gate_end(k):
        span = pl.ds(k * part_gu, part_gu)
        line_end(gate_parts(k), lambda a, *i: r.gg_z.at[(a, k) + i], lambda s: r.gg_rz.at[s, :, span],
                 r.gg_f.at[:, span])
        keep_out(1 + k, r.gg_f.at[:, span], r.o_gu.at[t, :, span])
        send(None, copy(r.gg_f.at[:, span], r.o_gu.at[t, :, span], r.gg_y.at[0, k],
                        r.gg_y.at[1, k], dev_y), tail)

    ga = wg
    part_a = half_a // 4

    def cols_a(k, h):
        return pl.ds(aligned(h * half_a + k * part_a, LANES), part_a)

    def store_a(k, left, right):
        for h in range(2):
            val = jnp.dot(left[...], right[h], preferred_element_type=F32)
            ga[:, :, :, :, cols_a(k, h)] = val.astype(BF).reshape(line, 2, 2, shard, part_a)
            send(None, copy(ga.at[:, :, 1 - c, :, cols_a(k, h)],
                            r.ga_rc.at[:, :, :, cols_a(k, h)],
                            r.ga_c.at[0, h, k], r.ga_c.at[1, h, k], dev_c), tail)

    def span_a(k):
        return pl.ds(k * part_a, part_a)

    def tower_a(k):
        for h in range(2):
            got(None, r.ga_rc.at[:, :, :, cols_a(k, h)], r.ga_c.at[1, h, k])
        gone = cols_a(k, 1 - t)
        for s in range(line):
            for xx in range(2):
                ref = ga.at[s, xx, c, :, gone]
                ref[...] = added((ref, r.ga_rc.at[s, xx, :, gone])).astype(BF)
        send(None, copy(ga.at[:, :, c, :, gone], r.ga_rt.at[:, :, :, span_a(k)],
                        r.ga_t.at[0, k], r.ga_t.at[1, k], dev_y), tail)

    def cross_a(k):
        got(None, r.ga_rt.at[:, :, :, span_a(k)], r.ga_t.at[1, k])
        here = cols_a(k, t)
        for s in range(line):
            ref = ga.at[s, 1 - x, c, :, here]
            ref[...] = added((ref, r.ga_rc.at[s, 1 - x, :, here],
                              r.ga_rt.at[s, 1 - x, :, span_a(k)])).astype(BF)
        send(None, copy(ga.at[:, 1 - x, c, :, here], r.ga_rx.at[:, :, span_a(k)],
                        r.ga_x.at[0, k], r.ga_x.at[1, k], dev_x), tail)

    def parts_a(k):
        here = cols_a(k, t)
        return lambda dest: (ga.at[dest, x, c, :, here], r.ga_rc.at[dest, x, :, here],
                             r.ga_rt.at[dest, x, :, span_a(k)],
                             r.ga_rx.at[dest, :, span_a(k)])

    def line_a(k, step):
        if step == 0:
            got(None, r.ga_rx.at[:, :, span_a(k)], r.ga_x.at[1, k])
        line_step(step, parts_a(k), lambda a, *i: r.ga_z.at[(a, k) + i], lambda s: r.ga_rz.at[s, :, span_a(k)])

    def end_a(k):
        line_end(parts_a(k), lambda a, *i: r.ga_z.at[(a, k) + i], lambda s: r.ga_rz.at[s, :, span_a(k)],
                 r.ga_f.at[:, span_a(k)])
        keep_out(5 + k, r.ga_f.at[:, span_a(k)], r.o_a.at[:, cols_a(k, t)])
        send(None, copy(r.ga_f.at[:, span_a(k)], r.o_a.at[:, cols_a(k, t)],
                        r.ga_y.at[0, k], r.ga_y.at[1, k], dev_y), tail)

    some = 2 * 4 * shard

    def rows_of_weight(ref, j, lo, n):
        return ref[pl.ds(2 * j, 2), :, :, :, pl.ds(lo, n)].reshape(some, n)

    def feed_back(rows_of, store):
        def body(j, carry):
            store(pl.ds(aligned(j * some, LANES), some),
                  dot_tt(r.dgu[rows_of, :], rows_of_weight(wg, j, 0, ff)))
            return carry

        lax.fori_loop(0, line // 2, body, 0)

    def back_send(span, val):
        r.dsend[:, span] = val.astype(BF)

    def back_own(span, val):
        r.bown[:, span] = val

    hidden_back(mine)
    feed_back(mine, back_own)
    for s in range(line):
        down_own(s)
    for k in range(4):
        gate_own(k)
    got_rows(2, r.dbr.at[theirs])
    for s in range(line):
        down_grad(s)
    hidden_back(theirs)
    down_arrive()
    down_line(0)
    feed_back(theirs, back_send)
    swap_rows(3, r.dsend, r.drecv)
    gate_grad(0)
    gate_grad(1)
    gate_cross(0)
    gate_grad(2)
    gate_cross(1)
    gate_grad(3)
    settle(pending)
    gate_cross(2)
    gate_cross(3)
    down_line(1, 0)
    got_rows(3, r.drecv)

    def norm_one_back(b, sums):
        part = pl.ds(aligned(b * quarter, quarter), quarter)
        top = r.n1[part, :] + r.bown[part, :] + r.drecv[part, :].astype(F32)
        hat = r.h1[part, :]
        inner = top * r.vec[0:1, :]
        grad = r.rs1[part, :] * (
            inner - jnp.mean(inner, -1, keepdims=True)
            - hat * jnp.mean(inner * hat, -1, keepdims=True))
        r.n1[part, :] = grad
        r.datt[part, :] = grad.astype(BF)
        return (sums[0] + jnp.sum(top * hat, 0, keepdims=True),
                sums[1] + jnp.sum(top, 0, keepdims=True))

    gain_one, bias_one = lax.fori_loop(0, blocks, norm_one_back, (zero_row, zero_row))
    r.ln[0] = (r.ln[0] + jnp.where(row8 == 0, gain_one, 0.0)
                  + jnp.where(row8 == 1, bias_one, 0.0))

    ln_peers = [dev_y, dev_c, dev_x]
    for bit in range(line.bit_length() - 1):
        apart = 1 << bit
        ln_peers.append(dev_z(z + apart * (1 - 2 * ((z // apart) % 2))))
    last = len(ln_peers)

    def ln_send(k):
        send(None, copy(r.ln.at[k], r.lnr.at[k], r.s_ln.at[k], r.r_ln.at[k],
                        ln_peers[k]), tail)

    def ln_add(k):
        got(None, r.lnr.at[k], r.r_ln.at[k])
        r.ln[k + 1] = r.ln[k] + r.lnr[k]

    dqkv = r.dgu.at[pl.ds(0, count), pl.ds(0, 3 * D)]
    dmix = r.dgu.at[pl.ds(count, count), pl.ds(0, D)]

    def mixed_back(j, carry):
        val = sum(dot_tt(r.datt[:, pl.ds(h * out_w, out_w)],
                         rows_of_weight(wa, j, h * half_a + third, out_w)) for h in range(2))
        dmix[:, pl.ds(aligned(j * some, LANES), some)] = val.astype(BF)
        return carry

    def attend_back(p, carry):
        q2, k2, v2 = triple(p)
        o = aligned(p * LANES, LANES)
        dm2 = dmix[:, pl.ds(o, LANES)]
        parts = []
        for h in range(2):
            probs = r.probs[2 * p + h]
            dprobs = dot_tt(only(h, dm2), v2)
            mean = jnp.sum(probs * dprobs, -1, keepdims=True)
            dscores = (probs * (dprobs - mean)).astype(BF)
            parts.append((jnp.dot(dscores, k2, preferred_element_type=F32),
                          dot_t0(dscores, q2), dot_t0(probs.astype(BF), dm2)))
        dq, dk, dv = (jnp.where(first_head, a, b) for a, b in zip(*parts))
        dqkv[:, pl.ds(o, LANES)] = turn_back(dq * scale).astype(BF)
        dqkv[:, pl.ds(D + o, LANES)] = turn_back(dk).astype(BF)
        dqkv[:, pl.ds(2 * D + o, LANES)] = dv.astype(BF)
        return carry

    def token_back(j, carry):
        val = sum(dot_tt(dqkv[:, pl.ds(h * third, third)],
                         rows_of_weight(wa, j, h * half_a, third)) for h in range(2))
        span = pl.ds(aligned(j * some, LANES), some)
        r.o_tok[:, span] = r.n1[:, span] + val
        return carry

    ln_send(0)
    store_a(3, r.mixt, [r.datt[:, pl.ds(h * out_w, out_w)] for h in range(2)])
    lax.fori_loop(0, line // 2, mixed_back, 0)
    ln_add(0)
    ln_send(1)
    tower_a(3)
    gate_line(0, 0)
    lax.fori_loop(0, 2, attend_back, 0)
    down_line(1, 1)
    lax.fori_loop(2, 4, attend_back, 0)
    gate_line(0, 1)
    gate_line(1, 0)
    down_line(2, 0)
    lax.fori_loop(4, pairs, attend_back, 0)
    for k in range(3):
        store_a(k, r.tokt, [dqkv[:, pl.ds(h * third + k * part_a, part_a)] for h in range(2)])
    for k in range(3):
        tower_a(k)
    ln_add(1)
    gate_line(0, 2)
    gate_line(1, 1)
    lax.fori_loop(0, line // 2, token_back, 0)
    gate_line(2, 0)
    cross_a(3)
    down_end()
    gate_end(0)
    gate_line(1, 2)
    gate_line(2, 1)
    gate_line(3, 0)
    line_a(3, 0)
    cross_a(0)
    gate_line(2, 2)
    gate_end(1)
    down_out()
    gate_line(3, 1)
    line_a(3, 1)
    line_a(0, 0)
    cross_a(1)
    gate_end(2)
    gate_line(3, 2)
    line_a(3, 2)
    line_a(0, 1)
    line_a(1, 0)
    gate_end(3)
    line_a(0, 2)
    end_a(3)
    cross_a(2)
    ln_send(2)
    line_a(1, 1)
    end_a(0)
    ln_add(2)
    line_a(2, 0)
    ln_send(3)
    line_a(1, 2)
    line_a(2, 1)
    end_a(1)
    for k in range(3, last):
        ln_add(k)
        if k + 1 < last:
            ln_send(k + 1)
    line_a(2, 2)
    end_a(2)

    r.o_vec[...] = r.ln[last]
    r.o_loss[...] = r.ln[last][:, 0:LANES] * (1.0 / (groups * QPD))

    r.o_d[...] = r.dbuf[me]

    def sent(ssem):
        def body(j, carry):
            copy(r.embd, r.embd, ssem.at[j], r.r_query.at[0], dev_x).wait_send()
            return carry

        lax.fori_loop(0, groups, body, 0)

    @pl.when(t == 0)
    def _():
        r.o_q[...] = r.embq[...]
        sent(r.s_slope)

    @pl.when(t == 1)
    def _():
        got(None, r.qrecv, r.r_query.at[0])
        r.o_q[...] = r.qrecv[...]
        sent(r.s_doc)

    got(x != t, r.o_dn, r.gd_y.at[1])
    for k in range(4):
        got(None, r.o_gu.at[1 - t, :, pl.ds(k * part_gu, part_gu)], r.gg_y.at[1, k])
        got(None, r.o_a.at[:, cols_a(k, 1 - t)], r.ga_y.at[1, k])
    for cond, what in out_copies:
        do(cond, what.wait)
    settle(tail)


def finish(plan, *refs):
    (a_ref, gu_ref, dn_ref, vec_ref, tok_ref, q_ref, d_ref, loss_ref,
     o_loss, o_q, o_d, o_tok, o_qkv, o_out, o_gate, o_up, o_down, *o_vecs) = refs
    third, half_a, half_ff, stripe = 3 * D // 2, plan.half_a, plan.half_ff, plan.stripe
    out_w = half_a - third
    for h in range(2):
        o_qkv[:, h * third : (h + 1) * third] = a_ref[:, h * half_a : h * half_a + third].astype(F32)
        o_out[:, h * out_w : (h + 1) * out_w] = (
            a_ref[:, h * half_a + third : (h + 1) * half_a].astype(F32))
        for s in range(plan.line):
            to = pl.ds((2 * s + h) * stripe, stripe)
            o_gate[:, to] = gu_ref[h, :, pl.ds(s * stripe, stripe)].astype(F32)
            o_up[:, to] = gu_ref[h, :, pl.ds(half_ff + s * stripe, stripe)].astype(F32)
    o_down[...] = dn_ref[...].astype(F32)
    o_tok[0] = tok_ref[...]
    o_q[...] = q_ref[...]
    o_d[...] = d_ref[...]
    o_loss[...] = loss_ref[4:5, 0:1]
    first = lax.axis_index(DP) * plan.vec
    row = lax.broadcasted_iota(jnp.int32, (D, LANES), 0)
    col = lax.broadcasted_iota(jnp.int32, (D, LANES), 1)
    pick = jnp.where(row == first + col, 1.0, 0.0)
    own = jnp.dot(vec_ref[...], pick, preferred_element_type=F32, precision=exact_product_accuracy)
    for k, out in enumerate(o_vecs):
        out[...] = own[k : k + 1, 0 : plan.vec]


def on_device_kernel(plan, tokens, query_lengths, doc_lengths, positives, w_qkv, w_out, w_gate,
                     w_up, w_down, ln1_gain, first_layernorm_shift, ln2_gain, ln2_bias):
    count, groups, shard, vec = plan.count, plan.groups, plan.shard, plan.vec
    cosines, sines = rotary_constants(count)
    tile = jnp.pad(jnp.stack([ln1_gain, first_layernorm_shift, ln2_gain, ln2_bias]),
                   ((0, 12), (0, LANES - vec)))
    vmem = pl.BlockSpec(memory_space=pltpu.VMEM)
    smem = pl.BlockSpec(memory_space=pltpu.SMEM)
    hbm = pl.BlockSpec(memory_space=pl.ANY)
    shape = jax.ShapeDtypeStruct
    made = pl.pallas_call(
        functools.partial(whole_step, plan),
        out_shape=(
            shape((count, D), F32), shape((shard, plan.width_a), BF), shape((2, shard, plan.ff), BF),
            shape((plan.shard_ff, D), BF), shape((8, D), F32), shape((QPD, D), F32),
            shape((1, D), F32), shape((8, LANES), F32),
        ),
        in_specs=[smem, smem, smem, vmem, vmem, vmem, vmem, vmem] + [hbm] * 5,
        out_specs=(vmem, hbm, hbm, hbm, vmem, vmem, vmem, vmem),
        scratch_shapes=list(buffers(plan).values()) + list(semaphores(plan).values()),
        compiler_params=pltpu.CompilerParams(
            collective_id=0, has_side_effects=True, vmem_limit_bytes=63 * 1000 * 1000),
        name="whole_step",
    )(query_lengths, doc_lengths, positives, positives[None], tokens[0], cosines, sines, tile,
      w_qkv, w_out, w_gate, w_up, w_down)
    o_tok, o_a, o_gu, o_dn, o_vec, o_q, o_d, o_loss = made
    outs = pl.pallas_call(
        functools.partial(finish, plan),
        out_shape=(
            shape((1, 1), F32), shape((QPD, D), F32), shape((1, D), F32),
            shape((1, count, D), F32), shape((shard, 3 * D), F32), shape((shard, D), F32),
            shape((shard, plan.ff), F32), shape((shard, plan.ff), F32),
            shape((plan.shard_ff, D), F32),
        ) + (shape((1, vec), F32),) * 4,
        in_specs=[vmem] * 8,
        out_specs=[vmem] * 13,
        name="finish",
    )(o_a, o_gu, o_dn, o_vec, o_tok, o_q, o_d, o_loss)
    return (outs[0].reshape(()),) + tuple(outs[1:9]) + tuple(v.reshape(vec) for v in outs[9:])


def fits(plan, towers):
    line = plan.line
    return (towers == 2 and plan.groups % 4 == 0 and line & (line - 1) == 0 and line > 1
            and plan.shard % 16 == 0 and plan.shard_ff % 16 == 0 and plan.stripe % LANES == 0
            and plan.count == QPD * QLEN)


def solution(mesh):
    groups = mesh.shape[DP]

    def local_step(*args):
        plan = Plan(groups, args[0].shape[1], args[4].shape[0], args[8].shape[0], args[9].shape[0])
        if fits(plan, mesh.shape[TOWER]):
            return on_device_kernel(plan, *args)
        return on_device(*args)

    return jax.shard_map(
        local_step,
        mesh=mesh,
        in_specs=(
            P(TOWER, DP, None),
            P(DP),
            P(DP),
            P(),
            P(DP, None),
            P(DP, None),
            P(DP, None),
            P(DP, None),
            P(DP, None),
            P(DP),
            P(DP),
            P(DP),
            P(DP),
        ),
        out_specs=(
            P(),
            P(DP, None),
            P(DP, None),
            P(TOWER, DP, None),
            P(DP, None),
            P(DP, None),
            P(DP, None),
            P(DP, None),
            P(DP, None),
            P(DP),
            P(DP),
            P(DP),
            P(DP),
        ),
        check_vma=False,
    )
```

```python
import functools
from types import SimpleNamespace
from typing import Any, NamedTuple

import jax
import jax.numpy as jnp
import numpy as np
from jax import lax
from jax.experimental import pallas as pl
from jax.experimental.pallas import tpu as pltpu
from jax.sharding import PartitionSpec as P

TOWER = "tower"
DP = "dp"
D = 768
HEADS = 12
HEAD = 64
QLEN = 64
QPD = 4


exact_product_accuracy = lax.Precision.HIGHEST
rope_base = 1000.0
contrast_sharpness_factor = 0.02


def product(left, right):
    return jnp.dot(left, right, preferred_element_type=jnp.float32)


def rotary_tables(places):
    freqs = jnp.power(rope_base, -2.0 * jnp.arange(HEAD // 2).astype(jnp.float32) / HEAD)
    angles = places[:, None] * freqs[None, :]
    return (jnp.cos(angles)[:, None, :], jnp.sin(angles)[:, None, :])


def rotate(values, cosines, sines):
    half_dim = values.shape[-1] // 2
    first = values[..., :half_dim]
    second = values[..., half_dim:]
    return jnp.concatenate(
        [first * cosines - second * sines, second * cosines + first * sines], axis=-1
    )


def layer_norm(hidden, gain, offset):
    average = jnp.mean(hidden, -1, keepdims=True)
    centred = hidden - average
    variance = jnp.mean(centred * centred, -1, keepdims=True)
    return centred * lax.rsqrt(variance + 1e-05) * gain + offset


def normalize(pooled):
    return pooled * lax.rsqrt(jnp.sum(pooled * pooled, -1, keepdims=True) + 1e-06)


def layout(tower_id, query_len, doc_len, count):
    places = jnp.arange(count)
    span = jnp.where(tower_id == 0, QLEN, count)
    segment = places // span
    offset_in = places - segment * span
    slots = jnp.arange(QPD)
    seg_limit = jnp.where(tower_id == 0, query_len, doc_len[0] * jnp.ones_like(query_len))
    limit = jnp.sum(jnp.where(segment[:, None] == slots[None, :], seg_limit[None, :], 0), axis=1)
    valid = offset_in < limit
    allowed = (segment[:, None] == segment[None, :]) & valid[None, :]
    member = (segment[None, :] == slots[:, None]) & valid[None, :]
    pool_matrix = jnp.where(member, 1.0 / seg_limit[:, None].astype(jnp.float32), 0.0)
    return (offset_in.astype(jnp.float32), allowed, pool_matrix)


def swish_product(left, right):
    return jax.nn.silu(left) * right


def on_device(
    tokens,
    query_lengths,
    doc_lengths,
    positives,
    w_qkv,
    w_out,
    w_gate,
    w_up,
    w_down,
    ln1_gain,
    first_layernorm_shift,
    ln2_gain,
    ln2_bias,
):
    tower_id = lax.axis_index(TOWER)
    device_id = lax.axis_index(DP)
    groups = lax.axis_size(DP)
    full = (
        lax.all_gather(w_qkv, DP, axis=0, tiled=True),
        lax.all_gather(w_out, DP, axis=0, tiled=True),
        lax.all_gather(w_gate, DP, axis=0, tiled=True),
        lax.all_gather(w_up, DP, axis=0, tiled=True),
        lax.all_gather(w_down, DP, axis=0, tiled=True),
        lax.all_gather(ln1_gain, DP, axis=0, tiled=True),
        lax.all_gather(first_layernorm_shift, DP, axis=0, tiled=True),
        lax.all_gather(ln2_gain, DP, axis=0, tiled=True),
        lax.all_gather(ln2_bias, DP, axis=0, tiled=True),
    )
    qkv_full, out_full, gate_full, up_full, down_full = (
        full[0],
        full[1],
        full[2],
        full[3],
        full[4],
    )
    gain_one = full[5].astype(jnp.float32)
    bias_one = full[6].astype(jnp.float32)
    gain_two = full[7].astype(jnp.float32)
    bias_two = full[8].astype(jnp.float32)
    inputs = tokens[0]
    count = inputs.shape[0]
    places, allowed, pool_matrix = layout(tower_id, query_lengths, doc_lengths, count)
    cosines, sines = rotary_tables(places)
    packed = product(inputs, qkv_full)
    raw_query = packed[:, :D].reshape(count, HEADS, HEAD)
    raw_key = packed[:, D : 2 * D].reshape(count, HEADS, HEAD)

    def rotate_both(first, second):
        return (rotate(first, cosines, sines), rotate(second, cosines, sines))

    rotated, rotary_back = jax.vjp(rotate_both, raw_query, raw_key)
    query_low = rotated[0].astype(jnp.bfloat16)
    key_low = rotated[1].astype(jnp.bfloat16)
    value_low = packed[:, 2 * D :].reshape(count, HEADS, HEAD).astype(jnp.bfloat16)
    scale = HEAD ** (-0.5)

    def masked_scores():
        scores = (
            jnp.einsum("ihd,jhd->hij", query_low, key_low, preferred_element_type=jnp.float32)
            * scale
        )
        return jnp.where(allowed[None], scores, -1e30)

    scores = masked_scores()
    peak = jnp.max(scores, -1, keepdims=True)
    log_total = peak + jnp.log(jnp.sum(jnp.exp(scores - peak), -1, keepdims=True))
    probs_low = jnp.exp(scores - log_total).astype(jnp.bfloat16)
    mixed = jnp.einsum("hij,jhd->ihd", probs_low, value_low, preferred_element_type=jnp.float32)
    mixed_low = mixed.reshape(count, D).astype(jnp.bfloat16)
    attended = product(mixed_low, out_full)
    inputs_wide = inputs.astype(jnp.float32)
    normed_one, norm_one_back = jax.vjp(layer_norm, inputs_wide + attended, gain_one, bias_one)
    feed = normed_one.astype(jnp.bfloat16)
    gate = product(feed, gate_full)
    up_part = product(feed, up_full)
    hidden_wide, swish_back = jax.vjp(swish_product, gate, up_part)
    hidden = hidden_wide.astype(jnp.bfloat16)
    branch = product(hidden, down_full)
    normed_two, norm_two_back = jax.vjp(layer_norm, normed_one + branch, gain_two, bias_two)
    pooled = jnp.dot(pool_matrix, normed_two, precision=exact_product_accuracy)
    embedded, normal_back = jax.vjp(normalize, pooled)
    gathered = lax.all_gather(embedded, (TOWER, DP), axis=0, tiled=True)
    queries_total = groups * QPD
    gathered_query_rows = gathered[:queries_total]
    gathered_document_rows = gathered[queries_total:].reshape(groups, QPD, D)[:, 0]
    pairwise_affinity_matrix = (
        jnp.dot(gathered_query_rows, gathered_document_rows.T, precision=exact_product_accuracy)
        / contrast_sharpness_factor
    )
    peak_logit = jnp.max(pairwise_affinity_matrix, -1, keepdims=True)
    log_partition_norm = peak_logit + jnp.log(
        jnp.sum(jnp.exp(pairwise_affinity_matrix - peak_logit), -1, keepdims=True)
    )
    columns = lax.broadcasted_iota(jnp.int32, pairwise_affinity_matrix.shape, 1)
    matching_labels = columns == positives[:, None]
    picked = jnp.sum(jnp.where(matching_labels, pairwise_affinity_matrix, 0.0), -1, keepdims=True)
    total = jnp.sum(log_partition_norm - picked)
    loss = total / queries_total
    similarity_gradient = (
        jnp.exp(pairwise_affinity_matrix - log_partition_norm) - matching_labels.astype(jnp.float32)
    ) / contrast_sharpness_factor
    own_rows = lax.dynamic_slice_in_dim(similarity_gradient, device_id * QPD, QPD, 0)
    query_side = jnp.dot(own_rows, gathered_document_rows, precision=exact_product_accuracy)
    own_column = lax.dynamic_slice_in_dim(similarity_gradient, device_id, 1, 1)
    doc_side = jnp.dot(own_column.T, gathered_query_rows, precision=exact_product_accuracy)
    doc_side = jnp.concatenate([doc_side, jnp.zeros((QPD - 1, D), jnp.float32)], 0)
    embed_grad = jnp.where(tower_id == 0, query_side, doc_side)
    pooled_grad = normal_back(embed_grad)[0]
    top_grad = jnp.dot(pool_matrix.T, pooled_grad, precision=exact_product_accuracy)
    sum_two, gain_two_grad, bias_two_grad = norm_two_back(top_grad)
    attention_input_cotangent, out_back, gate_back, up_back, down_back = (
        qkv_full,
        out_full,
        gate_full,
        up_full,
        down_full,
    )
    branch_low = sum_two.astype(jnp.bfloat16)
    down_grad = product(hidden.T, branch_low)
    hidden_grad = product(branch_low, down_back.T)
    gate_grad_wide, up_grad_wide = swish_back(hidden_grad)
    gate_low = gate_grad_wide.astype(jnp.bfloat16)
    up_low = up_grad_wide.astype(jnp.bfloat16)
    gate_weight_grad = product(feed.T, gate_low)
    up_weight_grad = product(feed.T, up_low)
    feed_grad = sum_two + product(gate_low, gate_back.T) + product(up_low, up_back.T)
    sum_one, gain_one_grad, bias_one_grad = norm_one_back(feed_grad)
    attend_low = sum_one.astype(jnp.bfloat16)
    out_grad = product(mixed_low.T, attend_low)
    mixed_grad = product(attend_low, out_back.T).astype(jnp.bfloat16).reshape(count, HEADS, HEAD)
    probs_again = jnp.exp(masked_scores() - log_total)
    prob_grad = jnp.einsum(
        "ihd,jhd->hij", mixed_grad, value_low, preferred_element_type=jnp.float32
    )
    score_grad = probs_again * (prob_grad - jnp.sum(probs_again * prob_grad, -1, keepdims=True))
    score_low = score_grad.astype(jnp.bfloat16)
    query_grad = (
        jnp.einsum("hij,jhd->ihd", score_low, key_low, preferred_element_type=jnp.float32) * scale
    )
    key_grad = (
        jnp.einsum("hij,ihd->jhd", score_low, query_low, preferred_element_type=jnp.float32) * scale
    )
    value_grad = jnp.einsum(
        "hij,ihd->jhd",
        probs_again.astype(jnp.bfloat16),
        mixed_grad,
        preferred_element_type=jnp.float32,
    )
    raw_query_grad, raw_key_grad = rotary_back((query_grad, key_grad))
    packed_grad = jnp.concatenate(
        [
            raw_query_grad.reshape(count, D),
            raw_key_grad.reshape(count, D),
            value_grad.reshape(count, D),
        ],
        1,
    ).astype(jnp.bfloat16)
    qkv_grad = product(inputs.T, packed_grad)
    input_grad = sum_one + product(packed_grad, attention_input_cotangent.T)
    gradients = (
        qkv_grad,
        out_grad,
        gate_weight_grad,
        up_weight_grad,
        down_grad,
        gain_one_grad,
        bias_one_grad,
        gain_two_grad,
        bias_two_grad,
    )
    partial_sums = (
        lax.psum_scatter(gradients[0], DP, scatter_dimension=0, tiled=True),
        lax.psum_scatter(gradients[1], DP, scatter_dimension=0, tiled=True),
        lax.psum_scatter(gradients[2], DP, scatter_dimension=0, tiled=True),
        lax.psum_scatter(gradients[3], DP, scatter_dimension=0, tiled=True),
        lax.psum_scatter(gradients[4], DP, scatter_dimension=0, tiled=True),
        lax.psum_scatter(gradients[5], DP, scatter_dimension=0, tiled=True),
        lax.psum_scatter(gradients[6], DP, scatter_dimension=0, tiled=True),
        lax.psum_scatter(gradients[7], DP, scatter_dimension=0, tiled=True),
        lax.psum_scatter(gradients[8], DP, scatter_dimension=0, tiled=True),
    )
    tower_halves = (
        lax.psum_scatter(
            partial_sums[0].astype(jnp.bfloat16), TOWER, scatter_dimension=0, tiled=True
        ).astype(jnp.float32),
        lax.psum_scatter(
            partial_sums[1].astype(jnp.bfloat16), TOWER, scatter_dimension=0, tiled=True
        ).astype(jnp.float32),
        lax.psum_scatter(
            partial_sums[2].astype(jnp.bfloat16), TOWER, scatter_dimension=0, tiled=True
        ).astype(jnp.float32),
        lax.psum_scatter(
            partial_sums[3].astype(jnp.bfloat16), TOWER, scatter_dimension=0, tiled=True
        ).astype(jnp.float32),
        lax.psum_scatter(
            partial_sums[4].astype(jnp.bfloat16), TOWER, scatter_dimension=0, tiled=True
        ).astype(jnp.float32),
        lax.psum_scatter(
            partial_sums[5].astype(jnp.bfloat16), TOWER, scatter_dimension=0, tiled=True
        ).astype(jnp.float32),
        lax.psum_scatter(
            partial_sums[6].astype(jnp.bfloat16), TOWER, scatter_dimension=0, tiled=True
        ).astype(jnp.float32),
        lax.psum_scatter(
            partial_sums[7].astype(jnp.bfloat16), TOWER, scatter_dimension=0, tiled=True
        ).astype(jnp.float32),
        lax.psum_scatter(
            partial_sums[8].astype(jnp.bfloat16), TOWER, scatter_dimension=0, tiled=True
        ).astype(jnp.float32),
    )
    shares = (
        lax.all_gather(tower_halves[0].astype(jnp.bfloat16), TOWER, axis=0, tiled=True).astype(
            jnp.float32
        ),
        lax.all_gather(tower_halves[1].astype(jnp.bfloat16), TOWER, axis=0, tiled=True).astype(
            jnp.float32
        ),
        lax.all_gather(tower_halves[2].astype(jnp.bfloat16), TOWER, axis=0, tiled=True).astype(
            jnp.float32
        ),
        lax.all_gather(tower_halves[3].astype(jnp.bfloat16), TOWER, axis=0, tiled=True).astype(
            jnp.float32
        ),
        lax.all_gather(tower_halves[4].astype(jnp.bfloat16), TOWER, axis=0, tiled=True).astype(
            jnp.float32
        ),
        lax.all_gather(tower_halves[5].astype(jnp.bfloat16), TOWER, axis=0, tiled=True).astype(
            jnp.float32
        ),
        lax.all_gather(tower_halves[6].astype(jnp.bfloat16), TOWER, axis=0, tiled=True).astype(
            jnp.float32
        ),
        lax.all_gather(tower_halves[7].astype(jnp.bfloat16), TOWER, axis=0, tiled=True).astype(
            jnp.float32
        ),
        lax.all_gather(tower_halves[8].astype(jnp.bfloat16), TOWER, axis=0, tiled=True).astype(
            jnp.float32
        ),
    )
    query_rows = lax.dynamic_slice_in_dim(gathered_query_rows, device_id * QPD, QPD, 0)
    doc_row = lax.dynamic_slice_in_dim(gathered_document_rows, device_id, 1, 0)
    return (loss, query_rows, doc_row, input_grad[None]) + tuple(shares)


MESH = pl.DeviceIdType.MESH
BF = jnp.bfloat16
F32 = jnp.float32
LANES = 128


def dot_tt(left, right, precision=None):
    return lax.dot_general(
        left, right, (((1,), (1,)), ((), ())), preferred_element_type=F32, precision=precision
    )


def dot_t0(left, right, precision=None):
    return lax.dot_general(
        left, right, (((0,), (0,)), ((), ())), preferred_element_type=F32, precision=precision
    )


def rotary_constants(count):
    freqs = np.power(
        np.float32(rope_base), (-2.0 * np.arange(HEAD // 2) / HEAD).astype(np.float32)
    ).astype(np.float32)
    angles = (np.arange(count, dtype=np.float32)[:, None] * freqs[None, :]).astype(np.float64)
    cosines, sines = np.cos(angles), np.sin(angles)
    return (
        np.tile(np.concatenate([cosines, cosines], 1), (1, 2)).astype(np.float32),
        np.tile(np.concatenate([-sines, sines], 1), (1, 2)).astype(np.float32),
    )


def aligned(start, unit):
    return start if isinstance(start, int) else pl.multiple_of(start, unit)


def both(first, second):
    return jnp.logical_and(first, second)


def do(condition, action):
    if condition is None:
        action()
    else:
        pl.when(condition)(action)


class Plan:
    def __init__(self, groups, count, shard, shard_ff, vec):
        self.groups = groups
        self.line = groups // 4
        self.count = count
        self.shard = shard
        self.shard_ff = shard_ff
        self.vec = vec
        self.width_a = 4 * D
        self.half_a = 2 * D
        self.ff = shard_ff * groups
        self.half_ff = self.ff // 2
        self.stripe = 2 * shard_ff


def semaphores(plan):
    line, groups = plan.line, plan.groups
    dma = pltpu.SemaphoreType.DMA
    chunks_gu, chunks_a = 4, 4
    return dict(
        loc=dma((24,)),
        ra=dma((groups, 2)),
        sa_z=dma((2, line)),
        sa_x=dma((line, 2)),
        sa_y=dma((line, 2)),
        sa_c=dma((line, 2, 2)),
        rg=dma((groups,)),
        sg_z=dma((2, line)),
        sg_x=dma((line,)),
        sg_c=dma((line, 2)),
        rd=dma((line, 2)),
        sd_x=dma((1,)),
        sd_z=dma((2, line)),
        sd_c=dma((line,)),
        rv=dma((groups,)),
        sv=dma((groups,)),
        s_back=dma((line,)),
        r_back=dma((line,)),
        sx=dma((4,)),
        rx=dma((4,)),
        r_doc=dma((groups,)),
        s_doc=dma((groups,)),
        r_slope=dma((groups,)),
        s_slope=dma((groups,)),
        r_query=dma((1,)),
        s_query=dma((1,)),
        s_ln=dma((line.bit_length() + 2,)),
        r_ln=dma((line.bit_length() + 2,)),
        gd_c=dma((2, line)),
        gd_z=dma((2, 2, line)),
        gd_x=dma((2,)),
        gd_y=dma((2,)),
        gg_c=dma((2, chunks_gu)),
        gg_x=dma((2, chunks_gu)),
        gg_z=dma((2, chunks_gu, 2, line)),
        gg_y=dma((2, chunks_gu)),
        ga_c=dma((2, 2, chunks_a)),
        ga_t=dma((2, chunks_a)),
        ga_x=dma((2, chunks_a)),
        ga_z=dma((2, chunks_a, 2, line)),
        ga_y=dma((2, chunks_a)),
        fin=dma((9,)),
    )


def buffers(plan):
    line, count, shard, groups = plan.line, plan.count, plan.shard, plan.groups
    pair = 2 * count
    v = pltpu.VMEM
    return dict(
        wa=v((line, 2, 2, shard, plan.width_a), BF),
        wg=v((line, 2, 2, shard, plan.ff), BF),
        wd=v((line, 2, plan.shard_ff, D), BF),
        vt=v((groups, 16, LANES), BF),
        vec=v((16, D), F32),
        cos=v((count, LANES), F32),
        sin=v((count, LANES), F32),
        hide=v((count, count), F32),
        pw=v((count, 1), F32),
        qkv=v((count, 3 * D), BF),
        probs=v((HEADS, count, count), F32),
        mixed=v((count, D), BF),
        mixt=v((D, count), BF),
        tokt=v((D, count), BF),
        h1=v((count, D), F32),
        rs1=v((count, 1), F32),
        n1=v((count, D), F32),
        feed=v((pair, D), BF),
        feedt=v((D, pair), BF),
        gate=v((pair, plan.half_ff), F32),
        up=v((pair, plan.half_ff), F32),
        hidt=v((plan.half_ff, pair), BF),
        dgu=v((pair, plan.ff), BF),
        bown=v((count, D), F32),
        bsend=v((count, D), BF),
        brecv=v((count, D), BF),
        xh2=v((count, D), F32),
        rs2=v((count, 1), F32),
        dbr=v((pair, D), BF),
        dsend=v((count, D), BF),
        drecv=v((count, D), BF),
        datt=v((count, D), BF),
        pool=v((8, D), F32),
        dpool=v((8, D), F32),
        emb=v((8, D), F32),
        embd=v((1, D), F32),
        embq=v((QPD, D), F32),
        dbuf=v((groups, 1, D), F32),
        cbuf=v((groups, 1, D), F32),
        csend=v((groups, 1, D), F32),
        qrecv=v((QPD, D), F32),
        dflat=v((groups, D), F32),
        ln=v((line.bit_length() + 3, 8, D), F32),
        lnr=v((line.bit_length() + 2, 8, D), F32),
        gd=v((line, 2, plan.shard_ff, D), BF),
        gd_rc=v((line, plan.shard_ff, D), BF),
        gd_rz=v((line + 1, plan.shard_ff, D), BF),
        gd_rx=v((plan.shard_ff, D), BF),
        gd_f=v((plan.shard_ff, D), BF),
        gg=v((line, 2, 2, shard, plan.ff), BF),
        gg_rc=v((line, 2, shard, plan.ff), BF),
        gg_rx=v((line, shard, plan.ff), BF),
        gg_rz=v((line + 1, shard, plan.ff), BF),
        gg_f=v((shard, plan.ff), BF),
        ga_rc=v((line, 2, shard, plan.width_a), BF),
        ga_rt=v((line, 2, shard, plan.half_a), BF),
        ga_rx=v((line, shard, plan.half_a), BF),
        ga_rz=v((line + 1, shard, plan.half_a), BF),
        ga_f=v((shard, plan.half_a), BF),
    )


class Operands(NamedTuple):
    qlen: Any
    dlen: Any
    pos: Any
    posv: Any
    tok: Any
    tcos: Any
    tsin: Any
    tile: Any
    i_qkv: Any
    i_out: Any
    i_gate: Any
    i_up: Any
    i_down: Any


class Results(NamedTuple):
    o_tok: Any
    o_a: Any
    o_gu: Any
    o_dn: Any
    o_vec: Any
    o_q: Any
    o_d: Any
    o_loss: Any


def whole_step(plan, *refs):
    names = (Operands._fields + Results._fields + tuple(buffers(plan)) + tuple(semaphores(plan)))
    r = SimpleNamespace(**dict(zip(names, refs, strict=True)))
    line, groups, count = plan.line, plan.groups, plan.count
    shard, shard_ff, stripe = plan.shard, plan.shard_ff, plan.stripe
    half_a, half_ff, ff = plan.half_a, plan.half_ff, plan.ff
    quarter = QLEN
    shift = QLEN.bit_length() - 1

    t = lax.axis_index(TOWER)
    me = lax.axis_index(DP)
    z = me // 4
    x = (me // 2) % 2
    c = me % 2

    def at(zz, xx, cc):
        return (zz * 2 + xx) * 2 + cc

    dev_x = {TOWER: t, DP: at(z, 1 - x, c)}
    dev_c = {TOWER: t, DP: at(z, x, 1 - c)}
    dev_y = {TOWER: 1 - t, DP: me}

    def dev_z(zz):
        return {TOWER: t, DP: at(zz, x, c)}

    pending, tail = [], []

    def copy(src, dst, ssem, rsem, dev):
        return pltpu.make_async_remote_copy(
            src_ref=src, dst_ref=dst, send_sem=ssem, recv_sem=rsem,
            device_id=dev, device_id_type=MESH,
        )

    def send(cond, what, keep=pending):
        do(cond, what.start)
        keep.append((cond, what))

    def settle(keep):
        for cond, what in keep:
            do(cond, what.wait_send)
        keep.clear()

    def got(cond, ref, rsem):
        do(cond, copy(ref, ref, r.s_query.at[0], rsem, dev_x).wait_recv)

    wa, wg, wd = r.wa, r.wg, r.wd
    out_w = half_a - 3 * D // 2
    local = []

    def near(src, dst, cond=None):
        what = pltpu.make_async_copy(src, dst, r.loc.at[len(local)])
        do(cond, what.start)
        local.append((cond, what))

    third = 3 * D // 2
    half_d = D // 2
    for h in range(2):
        for k in range(3):
            near(r.i_qkv.at[:, pl.ds(k * D + h * half_d, half_d)],
                 wa.at[z, x, c, :, pl.ds(h * half_a + k * half_d, half_d)])
        near(r.i_out.at[:, pl.ds(h * out_w, out_w)],
             wa.at[z, x, c, :, pl.ds(h * half_a + third, out_w)])
    near(r.i_down, wd.at[z, c], x == t)
    near(r.tile, r.vt.at[me])
    for s in range(line):
        for k, ref in enumerate((r.i_gate, r.i_up)):
            near(ref.at[:, pl.ds(aligned((2 * s + t) * stripe, LANES), stripe)],
                 wg.at[z, x, c, :, pl.ds(k * half_ff + s * stripe, stripe)])

    barrier = pltpu.get_barrier_semaphore()

    def greet(j, carry):
        other = jnp.logical_or(j // groups != t, j % groups != me)

        @pl.when(other)
        def _():
            pl.semaphore_signal(
                barrier, inc=1, device_id={TOWER: j // groups, DP: j % groups},
                device_id_type=MESH,
            )

        return carry

    lax.fori_loop(0, 2 * groups, greet, 0)
    pl.semaphore_wait(barrier, 2 * groups - 1)
    for cond, what in local:
        do(cond, what.wait)

    def piece_a(zz, xx, cc, h):
        return wa.at[zz, xx, cc, :, pl.ds(aligned(h * half_a, LANES), half_a)]

    def send_a(cond, sem, zz, xx, h, dev):
        ref = piece_a(zz, xx, c, h)
        send(cond, copy(ref, ref, sem, r.ra.at[at(zz, xx, c), h], dev))

    def got_a(cond, zz, xx, cc, h):
        got(cond, piece_a(zz, xx, cc, h), r.ra.at[at(zz, xx, cc), h])

    def sides(step):
        yield z - step, z >= step, z < line - 1, z + 1, 0
        yield z + step, z < line - step, z > 0, z - 1, 1

    def a_round(step):
        for zz, there, on, nxt, way in sides(step):
            if step:
                got_a(there, zz, x, c, t)
            send_a(both(there, on), r.sa_z.at[way, zz], zz, x, t, dev_z(nxt))
            if step or way == 0:
                send_a(there, r.sa_x.at[zz, t], zz, x, t, dev_x)
                if step:
                    send_a(there, r.sa_y.at[zz, x], zz, x, t, dev_y)
                else:
                    send_a(x != t, r.sa_x.at[zz, 1 - t], zz, x, 1 - t, dev_x)
                send_a(there, r.sa_c.at[zz, x, t], zz, x, t, dev_c)
        if step == 0:
            send_a(None, r.sa_c.at[z, x, 1 - t], z, x, 1 - t, dev_c)

    def around(step):
        return list(sides(step))[: 1 if step == 0 else 2]

    def a_cross(step):
        for zz, there, _, _, _ in around(step):
            got_a(there, zz, 1 - x, c, t)
            send_a(there if step else x == t, r.sa_y.at[zz, 1 - x], zz, 1 - x, t, dev_y)
            send_a(there, r.sa_c.at[zz, 1 - x, t], zz, 1 - x, t, dev_c)

    def a_tower(step):
        if step == 0:
            got_a(None, z, 1 - x, c, 1 - t)
            send_a(None, r.sa_c.at[z, 1 - x, 1 - t], z, 1 - x, 1 - t, dev_c)
            return
        for zz, there, _, _, _ in sides(step):
            for xx in (x, 1 - x):
                got_a(there, zz, xx, c, 1 - t)
                send_a(there, r.sa_c.at[zz, xx, 1 - t], zz, xx, 1 - t, dev_c)

    def a_sibling(h):
        for zz in range(line):
            for xx in range(2):
                got_a(None, zz, xx, 1 - c, h)

    def send_g(cond, sem, zz, xx, dev):
        ref = wg.at[zz, xx, c]
        send(cond, copy(ref, ref, sem, r.rg.at[at(zz, xx, c)], dev))

    def got_g(cond, zz, xx, cc):
        got(cond, wg.at[zz, xx, cc], r.rg.at[at(zz, xx, cc)])

    def g_line(step):
        for zz, there, on, nxt, way in sides(step):
            if step:
                got_g(there, zz, x, c)
            send_g(both(there, on), r.sg_z.at[way, zz], zz, x, dev_z(nxt))

    def g_spread(step):
        for zz, there, _, _, _ in around(step):
            send_g(there, r.sg_x.at[zz], zz, x, dev_x)
            send_g(there, r.sg_c.at[zz, x], zz, x, dev_c)

    def g_cross(step):
        for zz, there, _, _, _ in around(step):
            got_g(there, zz, 1 - x, c)
            send_g(there, r.sg_c.at[zz, 1 - x], zz, 1 - x, dev_c)

    def g_sibling():
        for zz in range(line):
            for xx in range(2):
                got_g(None, zz, xx, 1 - c)

    def send_d(cond, sem, zz, dev):
        ref = wd.at[zz, c]
        send(cond, copy(ref, ref, sem, r.rd.at[zz, c], dev))

    def got_d(cond, zz, cc):
        got(cond, wd.at[zz, cc], r.rd.at[zz, cc])

    def d_cross():
        send_d(x == t, r.sd_x.at[0], z, dev_x)

    def d_start():
        got_d(x != t, z, c)
        for zz, _, on, nxt, way in sides(0):
            send_d(on, r.sd_z.at[way, zz], zz, dev_z(nxt))
        send_d(None, r.sd_c.at[z], z, dev_c)

    def d_round(step, ends):
        for zz, there, on, nxt, way in sides(step):
            cond = both(there, jnp.logical_not(on) if ends else on)
            got_d(cond, zz, c)
            if not ends:
                send_d(cond, r.sd_z.at[way, zz], zz, dev_z(nxt))
            send_d(cond, r.sd_c.at[zz], zz, dev_c)

    def d_sibling():
        for zz in range(line):
            got_d(None, zz, 1 - c)

    def v_send(j, carry):
        @pl.when(j != me)
        def _():
            copy(r.vt.at[me], r.vt.at[me], r.sv.at[j], r.rv.at[me],
                 {TOWER: t, DP: j}).start()

        return carry

    def v_wait(j, carry):
        @pl.when(j != me)
        def _():
            copy(r.vt.at[me], r.vt.at[j], r.sv.at[j], r.rv.at[j],
                 {TOWER: t, DP: j}).wait()

        return carry

    a_round(0)
    lax.fori_loop(0, groups, v_send, 0)

    tok = r.tok
    rows = lax.broadcasted_iota(jnp.int32, (count, count), 0)
    cols = lax.broadcasted_iota(jnp.int32, (count, count), 1)
    seg = cols >> shift
    limit = jnp.zeros_like(cols)
    for s in range(QPD):
        limit = jnp.where(seg == s, r.qlen[s], limit)
    limit = limit * (1 - t) + r.dlen[0] * t
    place = cols - seg * (quarter * (1 - t))
    apart = ((rows >> shift) - seg) * (1 - t)
    seen = both(apart == 0, place < limit)
    r.hide[...] = jnp.where(seen, 0.0, -1e30)
    for s in range(QPD):
        part = pl.ds(s * quarter, quarter)
        length = jnp.full((quarter, 1), r.qlen[s] * (1 - t) + r.dlen[0] * t, jnp.int32)
        slot = lax.broadcasted_iota(jnp.int32, (quarter, 1), 0) + s * quarter * t
        r.pw[part, :] = jnp.where(slot < length, 1.0 / length.astype(F32), 0.0)
        begin = aligned(s * quarter * t, quarter)
        r.cos[part, :] = r.tcos[pl.ds(begin, quarter), :]
        r.sin[part, :] = r.tsin[pl.ds(begin, quarter), :]
    lanes = lax.broadcasted_iota(jnp.int32, (count, LANES), 1)
    first_head = lanes < HEAD
    low_half = (lanes & (HEAD - 1)) < HEAD // 2

    def swap(a):
        return jnp.where(low_half, pltpu.roll(a, LANES - HEAD // 2, 1), pltpu.roll(a, HEAD // 2, 1))

    def turn(a):
        return a * r.cos[...] + swap(a) * r.sin[...]

    def turn_back(a):
        return a * r.cos[...] - swap(a) * r.sin[...]

    def transpose_into(dst, src, width):
        def body(j, carry):
            o = aligned(j * LANES, LANES)
            dst[pl.ds(o, LANES), :] = src[:, pl.ds(o, LANES)].T
            return carry

        lax.fori_loop(0, width // LANES, body, 0)

    def wide(ref, lo, n):
        return ref[:, :, :, :, pl.ds(lo, n)].reshape(groups * shard, n)

    def widen_vec():
        lane = lax.broadcasted_iota(jnp.int32, (16, LANES), 1)
        parts = [jnp.zeros((16, LANES), F32) for _ in range(D // LANES)]
        for j in range(groups):
            block, first = divmod(j * plan.vec, LANES)
            piece = r.vt[j].astype(F32)
            if first:
                piece = pltpu.roll(piece, first, 1)
            parts[block] = parts[block] + jnp.where(lane >= first, piece, 0.0)
            if first + plan.vec > LANES:
                parts[block + 1] = parts[block + 1] + jnp.where(lane < first, piece, 0.0)
        r.vec[...] = jnp.concatenate(parts, axis=1)

    pairs = D // LANES
    half_pairs = pairs // 2

    scale = HEAD ** (-0.5)

    def project(h):
        for k in range(3):
            packed = jnp.dot(tok[...], wide(wa, aligned(h * half_a + k * half_d, LANES), half_d),
                             preferred_element_type=F32)
            for i in range(half_pairs):
                part = packed[:, i * LANES : (i + 1) * LANES]
                if k < 2:
                    part = turn(part)
                if k == 0:
                    part = part * scale
                r.qkv[:, pl.ds(aligned(k * D + h * half_d + i * LANES, LANES), LANES)] = (
                    part.astype(BF))

    def triple(p):
        o = aligned(p * LANES, LANES)
        return tuple(r.qkv[:, pl.ds(k * D + o, LANES)] for k in range(3))

    def only(h, a):
        return jnp.where(first_head if h == 0 else jnp.logical_not(first_head), a, jnp.zeros_like(a))

    def attend(p):
        q2, k2, v2 = triple(p)
        outs = []
        for h in range(2):
            scores = dot_tt(only(h, q2), k2) + r.hide[...]
            grown = jnp.exp(scores - jnp.max(scores, -1, keepdims=True))
            probs = grown * (1.0 / jnp.sum(grown, -1, keepdims=True))
            r.probs[2 * p + h] = probs
            outs.append(jnp.dot(probs.astype(BF), v2, preferred_element_type=F32))
        o = aligned(p * LANES, LANES)
        r.mixed[:, pl.ds(o, LANES)] = jnp.where(first_head, outs[0], outs[1]).astype(BF)

    def over_pairs(h, body, lo=0, hi=half_pairs):
        def step(i, carry):
            body(h * half_pairs + i)
            return carry

        lax.fori_loop(lo, hi, step, 0)

    g_line(0)
    transpose_into(r.tokt, tok, D)
    a_round(1)
    g_spread(0)
    a_cross(0)
    for step in range(2, line):
        a_round(step)
        a_cross(step - 1)
    d_cross()
    g_line(1)
    g_spread(1)
    a_cross(line - 1)
    lax.fori_loop(0, groups, v_wait, 0)
    widen_vec()
    a_sibling(t)
    project(t)
    for step in range(2):
        a_tower(step)
    g_line(2)
    over_pairs(t, attend)
    for step in range(2, line):
        a_tower(step)
    g_spread(2)
    d_start()
    a_sibling(1 - t)
    project(1 - t)
    g_cross(0)
    over_pairs(1 - t, attend, 0, 1)
    d_round(1, False)
    over_pairs(1 - t, attend, 1)

    for h in range(2):
        part = jnp.dot(r.mixed[...], wide(wa, h * half_a + 3 * D // 2, out_w),
                       preferred_element_type=F32)
        r.h1[:, pl.ds(h * out_w, out_w)] = tok[:, pl.ds(h * out_w, out_w)].astype(F32) + part

    def moments(h):
        centred = h - jnp.mean(h, -1, keepdims=True)
        return centred, lax.rsqrt(jnp.mean(centred * centred, -1, keepdims=True) + 1e-05)

    blocks = count // quarter

    def norm_one(b, carry):
        part = pl.ds(aligned(b * quarter, quarter), quarter)
        centred, inverse = moments(r.h1[part, :])
        hat = centred * inverse
        normed = hat * r.vec[0:1, :] + r.vec[1:2, :]
        r.h1[part, :] = hat
        r.rs1[part, :] = inverse
        r.n1[part, :] = normed
        r.feed[pl.ds(aligned(t * count + b * quarter, quarter), quarter), :] = (
            normed.astype(BF))
        return carry

    lax.fori_loop(0, blocks, norm_one, 0)
    mine = pl.ds(aligned(t * count, count), count)
    theirs = pl.ds(aligned((1 - t) * count, count), count)

    def swap_rows(k, src, dst):
        send(None, copy(src, dst, r.sx.at[k], r.rx.at[k], dev_y), tail)

    def got_rows(k, ref):
        got(None, ref, r.rx.at[k])

    swap_rows(0, r.feed.at[mine], r.feed.at[mine])
    transpose_into(r.mixt, r.mixed, D)
    for step in range(3, line):
        g_line(step)
        g_spread(step)
    g_cross(1)
    for step in range(2, line):
        g_cross(step)
        if step < line - 1:
            d_round(step, False)
    g_sibling()

    step_ff = 2 * LANES

    def gated(j, carry):
        o = aligned(j * step_ff, step_ff)
        gate = jnp.dot(r.feed[...], wide(wg, o, step_ff), preferred_element_type=F32)
        up = jnp.dot(r.feed[...], wide(wg, half_ff + o, step_ff), preferred_element_type=F32)
        r.gate[:, pl.ds(o, step_ff)] = gate
        r.up[:, pl.ds(o, step_ff)] = up
        hidden = (gate * jax.nn.sigmoid(gate) * up).astype(BF)
        r.dgu[:, pl.ds(o, step_ff)] = hidden
        r.hidt[pl.ds(o, step_ff), :] = hidden.T
        return carry

    got_rows(0, r.feed.at[theirs])
    lax.fori_loop(0, half_ff // step_ff, gated, 0)
    for step in range(1, line):
        d_round(step, True)
    d_sibling()

    def down(rows_of, store):
        def body(j, carry):
            o = aligned(j * step_ff, step_ff)
            w = wd[:, :, :, pl.ds(o, step_ff)].reshape(half_ff, step_ff)
            store(o, jnp.dot(r.dgu[rows_of, pl.ds(0, half_ff)], w, preferred_element_type=F32))
            return carry

        lax.fori_loop(0, D // step_ff, body, 0)

    def keep_send(o, val):
        r.bsend[:, pl.ds(o, step_ff)] = val.astype(BF)

    def keep_own(o, val):
        r.bown[:, pl.ds(o, step_ff)] = val

    down(theirs, keep_send)
    swap_rows(1, r.bsend, r.brecv)
    down(mine, keep_own)
    transpose_into(r.feedt, r.feed, D)
    got_rows(1, r.brecv)

    r.pool[...] = jnp.zeros((8, D), F32)

    def norm_two(b, carry):
        part = pl.ds(aligned(b * quarter, quarter), quarter)
        h = r.n1[part, :] + (r.bown[part, :] + r.brecv[part, :].astype(F32))
        centred, inverse = moments(h)
        hat = centred * inverse
        normed = hat * r.vec[2:3, :] + r.vec[3:4, :]
        r.xh2[part, :] = hat
        r.rs2[part, :] = inverse
        r.pool[pl.ds(b, 1), :] = jnp.sum(normed * r.pw[part, :], 0, keepdims=True)
        return carry

    lax.fori_loop(0, blocks, norm_two, 0)
    row8 = lax.broadcasted_iota(jnp.int32, (8, D), 0)

    @pl.when(t == 1)
    def _():
        all_rows = jnp.sum(r.pool[...], 0, keepdims=True)
        r.pool[...] = jnp.where(row8 == 0, all_rows, 0.0)

    pooled = r.pool[...]
    shrink = lax.rsqrt(jnp.sum(pooled * pooled, -1, keepdims=True) + 1e-06)
    r.emb[...] = pooled * shrink

    best = exact_product_accuracy
    r.dpool[...] = jnp.zeros((8, D), F32)
    r.ln[0] = jnp.zeros((8, D), F32)

    def to_all(tower, src, dst, ssem, rsem):
        def give(step, carry):
            j = (me + step) % groups
            copy(src(j), dst.at[me], ssem.at[j], rsem.at[me], {TOWER: tower, DP: j}).start()
            return carry

        lax.fori_loop(0, groups, give, 0)

    def from_all(dst, ssem, rsem):
        def take(j, carry):
            copy(dst.at[j], dst.at[j], ssem.at[j], rsem.at[j], dev_x).wait_recv()
            return carry

        lax.fori_loop(0, groups, take, 0)

    @pl.when(t == 1)
    def _():
        r.embd[...] = r.emb[0:1, :]
        r.dbuf[me] = r.emb[0:1, :]
        to_all(0, lambda j: r.embd, r.dbuf, r.s_doc, r.r_doc)
        from_all(r.cbuf, r.s_slope, r.r_slope)
        total = r.cbuf[0]
        for j in range(1, groups):
            total = total + r.cbuf[j]
        r.dpool[0:1, :] = total

    @pl.when(t == 0)
    def _():
        r.embq[...] = r.emb[0:QPD, :]
        from_all(r.dbuf, r.s_doc, r.r_doc)
        for j in range(groups):
            r.dflat[pl.ds(j, 1), :] = r.dbuf[j]
        docs, queries = r.dflat[...], r.embq[...]
        logits = dot_tt(queries, docs, best) / contrast_sharpness_factor
        peak = jnp.max(logits, -1, keepdims=True)
        lse = peak + jnp.log(jnp.sum(jnp.exp(logits - peak), -1, keepdims=True))
        col = lax.broadcasted_iota(jnp.int32, (QPD, groups), 1)
        row = lax.broadcasted_iota(jnp.int32, (QPD, groups), 0)
        label = jnp.zeros((QPD, groups), jnp.int32)
        for s in range(QPD):
            label = jnp.where(row == s, r.pos[me * QPD + s], label)
        hot = jnp.where(col == label, 1.0, 0.0)
        slope = (jnp.exp(logits - lse) - hot) / contrast_sharpness_factor
        back = dot_t0(slope, queries, best)
        for j in range(groups):
            r.csend[j] = back[j : j + 1, :]
        to_all(1, lambda j: r.csend.at[j], r.cbuf, r.s_slope, r.r_slope)
        r.dpool[0:QPD, :] = jnp.dot(slope, docs, preferred_element_type=F32, precision=best)
        picked = jnp.sum(jnp.where(hot > 0.5, logits, 0.0), -1, keepdims=True)
        total = jnp.sum(lse - picked, 0, keepdims=True)
        r.ln[0] = jnp.where(row8 == 4, total, 0.0)

    slope = r.dpool[...]
    emb = r.emb[...]
    dpool = shrink * (slope - emb * jnp.sum(slope * emb, -1, keepdims=True))

    @pl.when(t == 0)
    def _():
        r.dpool[...] = dpool

    @pl.when(t == 1)
    def _():
        r.dpool[...] = jnp.broadcast_to(dpool[0:1, :], (8, D))

    def norm_two_back(b, sums):
        part = pl.ds(aligned(b * quarter, quarter), quarter)
        top = r.pw[part, :] * r.dpool[pl.ds(b, 1), :]
        hat = r.xh2[part, :]
        inner = top * r.vec[2:3, :]
        grad = r.rs2[part, :] * (
            inner - jnp.mean(inner, -1, keepdims=True)
            - hat * jnp.mean(inner * hat, -1, keepdims=True))
        r.n1[part, :] = grad
        r.dbr[pl.ds(aligned(t * count + b * quarter, quarter), quarter), :] = (
            grad.astype(BF))
        return (sums[0] + jnp.sum(top * hat, 0, keepdims=True),
                sums[1] + jnp.sum(top, 0, keepdims=True))

    zero_row = jnp.zeros((1, D), F32)
    gain_two, bias_two = lax.fori_loop(0, blocks, norm_two_back, (zero_row, zero_row))
    swap_rows(2, r.dbr.at[mine], r.dbr.at[mine])

    send(t == 0, copy(r.embq, r.qrecv, r.s_query.at[0], r.r_query.at[0], dev_y), tail)
    r.ln[0] = (r.ln[0] + jnp.where(row8 == 2, gain_two, 0.0)
               + jnp.where(row8 == 3, bias_two, 0.0))

    def hidden_back(rows_of):
        def body(j, carry):
            o = aligned(j * stripe, LANES)
            w = wd[j].reshape(stripe, D)
            slope = dot_tt(r.dbr[rows_of, :], w)
            gate = r.gate[rows_of, pl.ds(o, stripe)]
            up = r.up[rows_of, pl.ds(o, stripe)]
            sig = jax.nn.sigmoid(gate)
            r.dgu[rows_of, pl.ds(o, stripe)] = (
                slope * up * (sig * (1.0 + gate * (1.0 - sig)))).astype(BF)
            r.dgu[rows_of, pl.ds(half_ff + o, stripe)] = (slope * (gate * sig)).astype(BF)
            return carry

        lax.fori_loop(0, line, body, 0)

    def along(step):
        for s in range(1, line):
            yield line - s, both(z == step, z < line - s), z + 1, 0
        for s in range(line - 1):
            yield s, both(z == line - 1 - step, z > s), z - 1, 1

    def added(refs):
        total = refs[0][...].astype(F32)
        for ref in refs[1:]:
            total = total + ref[...].astype(F32)
        return total

    def line_step(step, parts, sem, slot, nth):
        for k, (dest, cond, nxt, way) in enumerate(along(step)):
            if k % (line - 1) != nth:
                continue
            into = slot(dest + 1 if way == 0 else dest)
            refs = parts(dest)

            def move(into=into, refs=refs, dest=dest, way=way):
                if step:
                    copy(into, into, r.s_query.at[0], sem(1, way, dest), dev_x).wait_recv()
                    refs[0][...] = added(refs + (into,)).astype(BF)
                else:
                    refs[0][...] = added(refs).astype(BF)

            do(cond, move)
            send(cond, copy(refs[0], into, sem(0, way, dest), sem(1, way, dest),
                            dev_z(nxt)), tail)

    def line_end(parts, sem, slot, put):
        for cond, ways in ((z == 0, (1,)), (z == line - 1, (0,)),
                           (both(z > 0, z < line - 1), (0, 1))):
            def finish(ways=ways):
                refs = parts(z)
                for way in ways:
                    into = slot(z + 1 if way == 0 else z)
                    copy(into, into, r.s_query.at[0], sem(1, way, z), dev_x).wait_recv()
                    refs = refs + (into,)
                put[...] = added(refs).astype(BF)

            do(cond, finish)

    gd = r.gd

    def down_half(s, rows_of):
        return jnp.dot(r.hidt[pl.ds(s * stripe, stripe), rows_of], r.dbr[rows_of, :],
                       preferred_element_type=F32)

    def down_own(s):
        gd[s] = down_half(s, mine).astype(BF).reshape(2, shard_ff, D)

    def down_grad(s):
        val = down_half(s, theirs) + gd[s].reshape(stripe, D).astype(F32)
        gd[s] = val.astype(BF).reshape(2, shard_ff, D)
        send(None, copy(gd.at[s, 1 - c], r.gd_rc.at[s], r.gd_c.at[0, s],
                        r.gd_c.at[1, s], dev_c), tail)

    def down_parts(dest):
        return gd.at[dest, c], r.gd_rc.at[dest]

    def down_arrive():
        for s in range(line):
            got(None, r.gd_rc.at[s], r.gd_c.at[1, s])

    def down_line(step, nth):
        line_step(step, down_parts, lambda *i: r.gd_z.at[i], lambda k: r.gd_rz.at[k], nth)

    def down_end():
        line_end(down_parts, lambda *i: r.gd_z.at[i], lambda k: r.gd_rz.at[k], r.gd_f)
        send(x != t, copy(r.gd_f, r.gd_rx, r.gd_x.at[0], r.gd_x.at[1], dev_x), tail)

    out_copies = []

    def keep_out(k, src, dst, cond=None):
        what = pltpu.make_async_copy(src, dst, r.fin.at[k])
        do(cond, what.start)
        out_copies.append((cond, what))

    def down_out():
        def total():
            copy(r.gd_rx, r.gd_rx, r.s_query.at[0], r.gd_x.at[1], dev_x).wait_recv()
            r.gd_f[...] = added((r.gd_f, r.gd_rx)).astype(BF)

        do(x == t, total)
        keep_out(0, r.gd_f, r.o_dn, x == t)
        send(x == t, copy(r.gd_f, r.o_dn, r.gd_y.at[0], r.gd_y.at[1], dev_y), tail)

    gg = r.gg
    part_gu = ff // 4

    def gate_half(k, rows_of):
        return jnp.dot(r.feedt[:, rows_of], r.dgu[rows_of, pl.ds(k * part_gu, part_gu)],
                       preferred_element_type=F32)

    def gate_own(k):
        gg[:, :, :, :, pl.ds(k * part_gu, part_gu)] = gate_half(k, mine).astype(BF).reshape(
            line, 2, 2, shard, part_gu)

    def gate_grad(k):
        span = pl.ds(k * part_gu, part_gu)
        val = gate_half(k, theirs) + gg[:, :, :, :, span].reshape(groups * shard, part_gu).astype(F32)
        gg[:, :, :, :, span] = val.astype(BF).reshape(line, 2, 2, shard, part_gu)
        send(None, copy(gg.at[:, :, 1 - c, :, span], r.gg_rc.at[:, :, :, span],
                        r.gg_c.at[0, k], r.gg_c.at[1, k], dev_c), tail)

    def gate_cross(k):
        span = pl.ds(k * part_gu, part_gu)
        got(None, r.gg_rc.at[:, :, :, span], r.gg_c.at[1, k])
        for s in range(line):
            mine_k = gg.at[s, 1 - x, c, :, span]
            mine_k[...] = added((mine_k, r.gg_rc.at[s, 1 - x, :, span])).astype(BF)
        send(None, copy(gg.at[:, 1 - x, c, :, span], r.gg_rx.at[:, :, span],
                        r.gg_x.at[0, k], r.gg_x.at[1, k], dev_x), tail)

    def gate_parts(k):
        span = pl.ds(k * part_gu, part_gu)
        return lambda dest: (gg.at[dest, x, c, :, span], r.gg_rc.at[dest, x, :, span],
                             r.gg_rx.at[dest, :, span])

    def gate_ready(k):
        span = pl.ds(k * part_gu, part_gu)
        got(None, r.gg_rx.at[:, :, span], r.gg_x.at[1, k])

    def gate_line(k, step, nth):
        span = pl.ds(k * part_gu, part_gu)
        line_step(step, gate_parts(k), lambda a, *i: r.gg_z.at[(a, k) + i],
                  lambda s: r.gg_rz.at[s, :, span], nth)

    def gate_end(k):
        span = pl.ds(k * part_gu, part_gu)
        line_end(gate_parts(k), lambda a, *i: r.gg_z.at[(a, k) + i], lambda s: r.gg_rz.at[s, :, span],
                 r.gg_f.at[:, span])
        keep_out(1 + k, r.gg_f.at[:, span], r.o_gu.at[t, :, span])
        send(None, copy(r.gg_f.at[:, span], r.o_gu.at[t, :, span], r.gg_y.at[0, k],
                        r.gg_y.at[1, k], dev_y), tail)

    ga = wg
    sizes = (3 * LANES, 3 * LANES, 3 * LANES, out_w)
    starts = (0, 3 * LANES, 6 * LANES, third)

    def cols_a(k, h):
        return pl.ds(aligned(h * half_a + starts[k], LANES), sizes[k])

    def store_a(k, h, left, right):
        val = jnp.dot(left[...], right, preferred_element_type=F32)
        ga[:, :, :, :, cols_a(k, h)] = val.astype(BF).reshape(line, 2, 2, shard, sizes[k])
        send(None, copy(ga.at[:, :, 1 - c, :, cols_a(k, h)],
                        r.ga_rc.at[:, :, :, cols_a(k, h)],
                        r.ga_c.at[0, h, k], r.ga_c.at[1, h, k], dev_c), tail)

    def store_qkv(k, h):
        store_a(k, h, r.tokt, dqkv[:, pl.ds(aligned(h * third + starts[k], LANES), sizes[k])])

    def span_a(k):
        return pl.ds(starts[k], sizes[k])

    def tower_a(k):
        gone = cols_a(k, 1 - t)
        got(None, r.ga_rc.at[:, :, :, gone], r.ga_c.at[1, 1 - t, k])
        for s in range(line):
            for xx in range(2):
                ref = ga.at[s, xx, c, :, gone]
                ref[...] = added((ref, r.ga_rc.at[s, xx, :, gone])).astype(BF)
        send(None, copy(ga.at[:, :, c, :, gone], r.ga_rt.at[:, :, :, span_a(k)],
                        r.ga_t.at[0, k], r.ga_t.at[1, k], dev_y), tail)

    def cross_a(k):
        got(None, r.ga_rt.at[:, :, :, span_a(k)], r.ga_t.at[1, k])
        here = cols_a(k, t)
        got(None, r.ga_rc.at[:, :, :, here], r.ga_c.at[1, t, k])
        for s in range(line):
            ref = ga.at[s, 1 - x, c, :, here]
            ref[...] = added((ref, r.ga_rc.at[s, 1 - x, :, here],
                              r.ga_rt.at[s, 1 - x, :, span_a(k)])).astype(BF)
        send(None, copy(ga.at[:, 1 - x, c, :, here], r.ga_rx.at[:, :, span_a(k)],
                        r.ga_x.at[0, k], r.ga_x.at[1, k], dev_x), tail)

    def parts_a(k):
        here = cols_a(k, t)
        return lambda dest: (ga.at[dest, x, c, :, here], r.ga_rc.at[dest, x, :, here],
                             r.ga_rt.at[dest, x, :, span_a(k)],
                             r.ga_rx.at[dest, :, span_a(k)])

    def ready_a(k):
        got(None, r.ga_rx.at[:, :, span_a(k)], r.ga_x.at[1, k])

    def line_a(k, step, nth):
        line_step(step, parts_a(k), lambda a, *i: r.ga_z.at[(a, k) + i],
                  lambda s: r.ga_rz.at[s, :, span_a(k)], nth)

    def end_a(k):
        line_end(parts_a(k), lambda a, *i: r.ga_z.at[(a, k) + i], lambda s: r.ga_rz.at[s, :, span_a(k)],
                 r.ga_f.at[:, span_a(k)])
        keep_out(5 + k, r.ga_f.at[:, span_a(k)], r.o_a.at[:, cols_a(k, t)])
        send(None, copy(r.ga_f.at[:, span_a(k)], r.o_a.at[:, cols_a(k, t)],
                        r.ga_y.at[0, k], r.ga_y.at[1, k], dev_y), tail)

    some = 2 * 4 * shard

    def rows_of_weight(ref, j, lo, n):
        return ref[pl.ds(2 * j, 2), :, :, :, pl.ds(lo, n)].reshape(some, n)

    def feed_part(rows_of, j, store):
        store(j, pl.ds(j * some, some), dot_tt(r.dgu[rows_of, :], rows_of_weight(wg, j, 0, ff)))

    def back_send(j, span, val):
        r.dsend[:, span] = val.astype(BF)
        send(None, copy(r.dsend.at[:, span], r.drecv.at[:, span], r.s_back.at[j], r.r_back.at[j],
                        dev_y), tail)

    def back_own(j, span, val):
        r.bown[:, span] = val

    hidden_back(mine)
    for j in range(line // 2):
        feed_part(mine, j, back_own)
    for s in range(line):
        down_own(s)
    for k in range(4):
        gate_own(k)
    got_rows(2, r.dbr.at[theirs])
    def norm_one_back(b, sums):
        part = pl.ds(aligned(b * quarter, quarter), quarter)
        top = r.n1[part, :] + r.bown[part, :] + r.drecv[part, :].astype(F32)
        hat = r.h1[part, :]
        inner = top * r.vec[0:1, :]
        grad = r.rs1[part, :] * (
            inner - jnp.mean(inner, -1, keepdims=True)
            - hat * jnp.mean(inner * hat, -1, keepdims=True))
        r.n1[part, :] = grad
        r.datt[part, :] = grad.astype(BF)
        return (sums[0] + jnp.sum(top * hat, 0, keepdims=True),
                sums[1] + jnp.sum(top, 0, keepdims=True))

    def norm_back():
        for j in range(line // 2):
            got(None, r.drecv.at[:, pl.ds(j * some, some)], r.r_back.at[j])
        gain_one, bias_one = lax.fori_loop(0, blocks, norm_one_back, (zero_row, zero_row))
        r.ln[0] = (r.ln[0] + jnp.where(row8 == 0, gain_one, 0.0)
                   + jnp.where(row8 == 1, bias_one, 0.0))

    ln_peers = [dev_y, dev_c, dev_x]
    for bit in range(line.bit_length() - 1):
        apart = 1 << bit
        ln_peers.append(dev_z(z + apart * (1 - 2 * ((z // apart) % 2))))
    last = len(ln_peers)

    def small_sums(k):
        if k:
            got(None, r.lnr.at[k - 1], r.r_ln.at[k - 1])
            r.ln[k] = r.ln[k - 1] + r.lnr[k - 1]
        if k < last:
            send(None, copy(r.ln.at[k], r.lnr.at[k], r.s_ln.at[k], r.r_ln.at[k],
                            ln_peers[k]), tail)

    def out_grad():
        for h in range(2):
            store_a(3, h, r.mixt, r.datt[:, pl.ds(h * out_w, out_w)])

    def mix_back():
        lax.fori_loop(0, line // 2, mixed_back, 0)

    dqkv = r.dgu.at[pl.ds(0, count), pl.ds(0, 3 * D)]
    dmix = r.dgu.at[pl.ds(count, count), pl.ds(0, D)]

    def mixed_back(j, carry):
        val = sum(dot_tt(r.datt[:, pl.ds(h * out_w, out_w)],
                         rows_of_weight(wa, j, h * half_a + third, out_w)) for h in range(2))
        dmix[:, pl.ds(aligned(j * some, LANES), some)] = val.astype(BF)
        return carry

    def attend_back(p):
        q2, k2, v2 = triple(p)
        o = aligned(p * LANES, LANES)
        dm2 = dmix[:, pl.ds(o, LANES)]
        parts = []
        for h in range(2):
            probs = r.probs[2 * p + h]
            dprobs = dot_tt(only(h, dm2), v2)
            mean = jnp.sum(probs * dprobs, -1, keepdims=True)
            dscores = (probs * (dprobs - mean)).astype(BF)
            parts.append((jnp.dot(dscores, k2, preferred_element_type=F32),
                          dot_t0(dscores, q2), dot_t0(probs.astype(BF), dm2)))
        dq, dk, dv = (jnp.where(first_head, a, b) for a, b in zip(*parts))
        half = p // half_pairs
        o = half * third + (p - half * half_pairs) * LANES
        for k, part in enumerate((turn_back(dq * scale), turn_back(dk), dv)):
            dqkv[:, pl.ds(aligned(o + k * half_d, LANES), LANES)] = part.astype(BF)

    def token_back(j, carry):
        val = sum(dot_tt(dqkv[:, pl.ds(h * third, third)],
                         rows_of_weight(wa, j, h * half_a, third)) for h in range(2))
        span = pl.ds(aligned(j * some, LANES), some)
        r.o_tok[:, span] = r.n1[:, span] + val
        return carry

    hidden_back(theirs)
    gate_grad(0)
    feed_part(theirs, 0, back_send)
    down_grad(3)
    down_grad(0)
    down_grad(1)
    gate_cross(0)
    down_grad(2)
    feed_part(theirs, 1, back_send)
    down_arrive()
    down_line(0, 0)
    gate_grad(1)
    gate_cross(1)
    gate_grad(3)
    gate_grad(2)
    down_line(0, 1)
    norm_back()
    settle(pending)
    out_grad()
    small_sums(0)
    gate_cross(2)
    mix_back()
    over_pairs(1 - t, attend_back, 0, 2)
    gate_ready(0)
    tower_a(3)
    over_pairs(1 - t, attend_back, 2, 3)
    gate_ready(1)
    gate_line(0, 0, 1)
    down_line(1, 0)
    gate_cross(3)
    store_qkv(0, 1 - t)
    gate_line(0, 0, 0)
    gate_line(0, 0, 2)
    store_qkv(2, 1 - t)
    gate_line(1, 0, 0)
    store_qkv(1, 1 - t)
    over_pairs(t, attend_back, 0, 1)
    down_line(1, 1)
    down_line(0, 2)
    over_pairs(t, attend_back, 1, 2)
    tower_a(0)
    down_line(2, 0)
    over_pairs(t, attend_back, 2, 3)
    tower_a(2)
    store_qkv(0, t)
    gate_ready(2)
    store_qkv(2, t)
    cross_a(3)
    store_qkv(1, t)
    gate_line(2, 0, 1)
    gate_line(1, 0, 2)
    gate_ready(3)
    gate_line(0, 1, 0)
    tower_a(1)
    cross_a(0)
    down_end()
    ready_a(3)
    gate_line(2, 0, 0)
    gate_line(1, 1, 0)
    gate_line(3, 0, 0)
    gate_line(0, 1, 1)
    line_a(3, 0, 1)
    line_a(3, 0, 0)
    gate_line(3, 0, 1)
    gate_line(2, 1, 1)
    gate_line(0, 2, 0)
    gate_line(1, 0, 1)
    lax.fori_loop(0, line // 2, token_back, 0)
    gate_line(3, 1, 0)
    gate_end(0)
    ready_a(0)
    small_sums(1)
    gate_line(2, 1, 0)
    line_a(0, 0, 0)
    cross_a(2)
    gate_line(3, 0, 2)
    down_out()
    cross_a(1)
    gate_line(3, 2, 0)
    gate_line(2, 2, 0)
    gate_line(1, 1, 1)
    gate_line(1, 2, 0)
    gate_line(2, 0, 2)
    line_a(0, 1, 0)
    ready_a(2)
    line_a(3, 1, 0)
    line_a(2, 0, 0)
    line_a(2, 0, 1)
    line_a(0, 0, 1)
    small_sums(2)
    line_a(3, 1, 1)
    line_a(2, 1, 0)
    ready_a(1)
    gate_line(3, 1, 1)
    line_a(1, 0, 0)
    line_a(1, 0, 1)
    line_a(3, 0, 2)
    gate_end(2)
    line_a(3, 2, 0)
    line_a(0, 1, 1)
    gate_end(1)
    line_a(1, 1, 0)
    line_a(0, 0, 2)
    line_a(2, 0, 2)
    line_a(0, 2, 0)
    line_a(2, 1, 1)
    gate_end(3)
    line_a(1, 0, 2)
    line_a(1, 1, 1)
    line_a(2, 2, 0)
    small_sums(3)
    end_a(3)
    line_a(1, 2, 0)
    end_a(0)
    end_a(2)
    small_sums(4)
    end_a(1)
    small_sums(5)

    r.o_vec[...] = r.ln[last]
    r.o_loss[...] = r.ln[last][:, 0:LANES] * (1.0 / (groups * QPD))

    r.o_d[...] = r.dbuf[me]

    def sent(ssem):
        def body(j, carry):
            copy(r.embd, r.embd, ssem.at[j], r.r_query.at[0], dev_x).wait_send()
            return carry

        lax.fori_loop(0, groups, body, 0)

    @pl.when(t == 0)
    def _():
        r.o_q[...] = r.embq[...]
        sent(r.s_slope)

    @pl.when(t == 1)
    def _():
        got(None, r.qrecv, r.r_query.at[0])
        r.o_q[...] = r.qrecv[...]
        sent(r.s_doc)

    got(x != t, r.o_dn, r.gd_y.at[1])
    for k in range(4):
        got(None, r.o_gu.at[1 - t, :, pl.ds(k * part_gu, part_gu)], r.gg_y.at[1, k])
        got(None, r.o_a.at[:, cols_a(k, 1 - t)], r.ga_y.at[1, k])
    for cond, what in out_copies:
        do(cond, what.wait)
    settle(tail)


def finish(plan, *refs):
    (a_ref, gu_ref, dn_ref, vec_ref, tok_ref, q_ref, d_ref, loss_ref,
     o_loss, o_q, o_d, o_tok, o_qkv, o_out, o_gate, o_up, o_down, *o_vecs) = refs
    third, half_a, half_ff, stripe = 3 * D // 2, plan.half_a, plan.half_ff, plan.stripe
    out_w = half_a - third
    for h in range(2):
        for k in range(3):
            o_qkv[:, pl.ds(k * D + h * (D // 2), D // 2)] = (
                a_ref[:, pl.ds(h * half_a + k * (D // 2), D // 2)].astype(F32))
        o_out[:, h * out_w : (h + 1) * out_w] = (
            a_ref[:, h * half_a + third : (h + 1) * half_a].astype(F32))
        for s in range(plan.line):
            to = pl.ds((2 * s + h) * stripe, stripe)
            o_gate[:, to] = gu_ref[h, :, pl.ds(s * stripe, stripe)].astype(F32)
            o_up[:, to] = gu_ref[h, :, pl.ds(half_ff + s * stripe, stripe)].astype(F32)
    o_down[...] = dn_ref[...].astype(F32)
    o_tok[0] = tok_ref[...]
    o_q[...] = q_ref[...]
    o_d[...] = d_ref[...]
    o_loss[...] = loss_ref[4:5, 0:1]
    first = lax.axis_index(DP) * plan.vec
    row = lax.broadcasted_iota(jnp.int32, (D, LANES), 0)
    col = lax.broadcasted_iota(jnp.int32, (D, LANES), 1)
    pick = jnp.where(row == first + col, 1.0, 0.0)
    own = jnp.dot(vec_ref[...], pick, preferred_element_type=F32, precision=exact_product_accuracy)
    for k, out in enumerate(o_vecs):
        out[...] = own[k : k + 1, 0 : plan.vec]


def on_device_kernel(plan, tokens, query_lengths, doc_lengths, positives, w_qkv, w_out, w_gate,
                     w_up, w_down, ln1_gain, first_layernorm_shift, ln2_gain, ln2_bias):
    count, groups, shard, vec = plan.count, plan.groups, plan.shard, plan.vec
    cosines, sines = rotary_constants(count)
    tile = jnp.pad(jnp.stack([ln1_gain, first_layernorm_shift, ln2_gain, ln2_bias]),
                   ((0, 12), (0, LANES - vec)))
    vmem = pl.BlockSpec(memory_space=pltpu.VMEM)
    smem = pl.BlockSpec(memory_space=pltpu.SMEM)
    hbm = pl.BlockSpec(memory_space=pl.ANY)
    shape = jax.ShapeDtypeStruct
    made = pl.pallas_call(
        functools.partial(whole_step, plan),
        out_shape=(
            shape((count, D), F32), shape((shard, plan.width_a), BF), shape((2, shard, plan.ff), BF),
            shape((plan.shard_ff, D), BF), shape((8, D), F32), shape((QPD, D), F32),
            shape((1, D), F32), shape((8, LANES), F32),
        ),
        in_specs=[smem, smem, smem, vmem, vmem, vmem, vmem, vmem] + [hbm] * 5,
        out_specs=(vmem, hbm, hbm, hbm, vmem, vmem, vmem, vmem),
        scratch_shapes=list(buffers(plan).values()) + list(semaphores(plan).values()),
        compiler_params=pltpu.CompilerParams(
            collective_id=0, has_side_effects=True, vmem_limit_bytes=63 * 1000 * 1000),
        name="whole_step",
    )(query_lengths, doc_lengths, positives, positives[None], tokens[0], cosines, sines, tile,
      w_qkv, w_out, w_gate, w_up, w_down)
    o_tok, o_a, o_gu, o_dn, o_vec, o_q, o_d, o_loss = made
    outs = pl.pallas_call(
        functools.partial(finish, plan),
        out_shape=(
            shape((1, 1), F32), shape((QPD, D), F32), shape((1, D), F32),
            shape((1, count, D), F32), shape((shard, 3 * D), F32), shape((shard, D), F32),
            shape((shard, plan.ff), F32), shape((shard, plan.ff), F32),
            shape((plan.shard_ff, D), F32),
        ) + (shape((1, vec), F32),) * 4,
        in_specs=[vmem] * 8,
        out_specs=[vmem] * 13,
        name="finish",
    )(o_a, o_gu, o_dn, o_vec, o_tok, o_q, o_d, o_loss)
    return (outs[0].reshape(()),) + tuple(outs[1:9]) + tuple(v.reshape(vec) for v in outs[9:])


def fits(plan, towers):
    line = plan.line
    return (towers == 2 and plan.groups % 4 == 0 and line == 4
            and plan.shard % 16 == 0 and plan.shard_ff % 16 == 0 and plan.stripe % LANES == 0
            and plan.count == QPD * QLEN)


def solution(mesh):
    groups = mesh.shape[DP]

    def local_step(*args):
        plan = Plan(groups, args[0].shape[1], args[4].shape[0], args[8].shape[0], args[9].shape[0])
        if fits(plan, mesh.shape[TOWER]):
            return on_device_kernel(plan, *args)
        return on_device(*args)

    return jax.shard_map(
        local_step,
        mesh=mesh,
        in_specs=(
            P(TOWER, DP, None),
            P(DP),
            P(DP),
            P(),
            P(DP, None),
            P(DP, None),
            P(DP, None),
            P(DP, None),
            P(DP, None),
            P(DP),
            P(DP),
            P(DP),
            P(DP),
        ),
        out_specs=(
            P(),
            P(DP, None),
            P(DP, None),
            P(TOWER, DP, None),
            P(DP, None),
            P(DP, None),
            P(DP, None),
            P(DP, None),
            P(DP, None),
            P(DP),
            P(DP),
            P(DP),
            P(DP),
        ),
        check_vma=False,
    )
```

```python
import functools
from types import SimpleNamespace
from typing import Any, NamedTuple

import jax
import jax.numpy as jnp
import numpy as np
from jax import lax
from jax.experimental import pallas as pl
from jax.experimental.pallas import tpu as pltpu
from jax.sharding import PartitionSpec as P

TOWER = "tower"
DP = "dp"
D = 768
HEADS = 12
HEAD = 64
QLEN = 64
QPD = 4


exact_product_accuracy = lax.Precision.HIGHEST
rope_base = 1000.0
contrast_sharpness_factor = 0.02


def product(left, right):
    return jnp.dot(left, right, preferred_element_type=jnp.float32)


def rotary_tables(places):
    freqs = jnp.power(rope_base, -2.0 * jnp.arange(HEAD // 2).astype(jnp.float32) / HEAD)
    angles = places[:, None] * freqs[None, :]
    return (jnp.cos(angles)[:, None, :], jnp.sin(angles)[:, None, :])


def rotate(values, cosines, sines):
    half_dim = values.shape[-1] // 2
    first = values[..., :half_dim]
    second = values[..., half_dim:]
    return jnp.concatenate(
        [first * cosines - second * sines, second * cosines + first * sines], axis=-1
    )


def layer_norm(hidden, gain, offset):
    average = jnp.mean(hidden, -1, keepdims=True)
    centred = hidden - average
    variance = jnp.mean(centred * centred, -1, keepdims=True)
    return centred * lax.rsqrt(variance + 1e-05) * gain + offset


def normalize(pooled):
    return pooled * lax.rsqrt(jnp.sum(pooled * pooled, -1, keepdims=True) + 1e-06)


def layout(tower_id, query_len, doc_len, count):
    places = jnp.arange(count)
    span = jnp.where(tower_id == 0, QLEN, count)
    segment = places // span
    offset_in = places - segment * span
    slots = jnp.arange(QPD)
    seg_limit = jnp.where(tower_id == 0, query_len, doc_len[0] * jnp.ones_like(query_len))
    limit = jnp.sum(jnp.where(segment[:, None] == slots[None, :], seg_limit[None, :], 0), axis=1)
    valid = offset_in < limit
    allowed = (segment[:, None] == segment[None, :]) & valid[None, :]
    member = (segment[None, :] == slots[:, None]) & valid[None, :]
    pool_matrix = jnp.where(member, 1.0 / seg_limit[:, None].astype(jnp.float32), 0.0)
    return (offset_in.astype(jnp.float32), allowed, pool_matrix)


def swish_product(left, right):
    return jax.nn.silu(left) * right


def on_device(
    tokens,
    query_lengths,
    doc_lengths,
    positives,
    w_qkv,
    w_out,
    w_gate,
    w_up,
    w_down,
    ln1_gain,
    first_layernorm_shift,
    ln2_gain,
    ln2_bias,
):
    tower_id = lax.axis_index(TOWER)
    device_id = lax.axis_index(DP)
    groups = lax.axis_size(DP)
    full = (
        lax.all_gather(w_qkv, DP, axis=0, tiled=True),
        lax.all_gather(w_out, DP, axis=0, tiled=True),
        lax.all_gather(w_gate, DP, axis=0, tiled=True),
        lax.all_gather(w_up, DP, axis=0, tiled=True),
        lax.all_gather(w_down, DP, axis=0, tiled=True),
        lax.all_gather(ln1_gain, DP, axis=0, tiled=True),
        lax.all_gather(first_layernorm_shift, DP, axis=0, tiled=True),
        lax.all_gather(ln2_gain, DP, axis=0, tiled=True),
        lax.all_gather(ln2_bias, DP, axis=0, tiled=True),
    )
    qkv_full, out_full, gate_full, up_full, down_full = (
        full[0],
        full[1],
        full[2],
        full[3],
        full[4],
    )
    gain_one = full[5].astype(jnp.float32)
    bias_one = full[6].astype(jnp.float32)
    gain_two = full[7].astype(jnp.float32)
    bias_two = full[8].astype(jnp.float32)
    inputs = tokens[0]
    count = inputs.shape[0]
    places, allowed, pool_matrix = layout(tower_id, query_lengths, doc_lengths, count)
    cosines, sines = rotary_tables(places)
    packed = product(inputs, qkv_full)
    raw_query = packed[:, :D].reshape(count, HEADS, HEAD)
    raw_key = packed[:, D : 2 * D].reshape(count, HEADS, HEAD)

    def rotate_both(first, second):
        return (rotate(first, cosines, sines), rotate(second, cosines, sines))

    rotated, rotary_back = jax.vjp(rotate_both, raw_query, raw_key)
    query_low = rotated[0].astype(jnp.bfloat16)
    key_low = rotated[1].astype(jnp.bfloat16)
    value_low = packed[:, 2 * D :].reshape(count, HEADS, HEAD).astype(jnp.bfloat16)
    scale = HEAD ** (-0.5)

    def masked_scores():
        scores = (
            jnp.einsum("ihd,jhd->hij", query_low, key_low, preferred_element_type=jnp.float32)
            * scale
        )
        return jnp.where(allowed[None], scores, -1e30)

    scores = masked_scores()
    peak = jnp.max(scores, -1, keepdims=True)
    log_total = peak + jnp.log(jnp.sum(jnp.exp(scores - peak), -1, keepdims=True))
    probs_low = jnp.exp(scores - log_total).astype(jnp.bfloat16)
    mixed = jnp.einsum("hij,jhd->ihd", probs_low, value_low, preferred_element_type=jnp.float32)
    mixed_low = mixed.reshape(count, D).astype(jnp.bfloat16)
    attended = product(mixed_low, out_full)
    inputs_wide = inputs.astype(jnp.float32)
    normed_one, norm_one_back = jax.vjp(layer_norm, inputs_wide + attended, gain_one, bias_one)
    feed = normed_one.astype(jnp.bfloat16)
    gate = product(feed, gate_full)
    up_part = product(feed, up_full)
    hidden_wide, swish_back = jax.vjp(swish_product, gate, up_part)
    hidden = hidden_wide.astype(jnp.bfloat16)
    branch = product(hidden, down_full)
    normed_two, norm_two_back = jax.vjp(layer_norm, normed_one + branch, gain_two, bias_two)
    pooled = jnp.dot(pool_matrix, normed_two, precision=exact_product_accuracy)
    embedded, normal_back = jax.vjp(normalize, pooled)
    gathered = lax.all_gather(embedded, (TOWER, DP), axis=0, tiled=True)
    queries_total = groups * QPD
    gathered_query_rows = gathered[:queries_total]
    gathered_document_rows = gathered[queries_total:].reshape(groups, QPD, D)[:, 0]
    pairwise_affinity_matrix = (
        jnp.dot(gathered_query_rows, gathered_document_rows.T, precision=exact_product_accuracy)
        / contrast_sharpness_factor
    )
    peak_logit = jnp.max(pairwise_affinity_matrix, -1, keepdims=True)
    log_partition_norm = peak_logit + jnp.log(
        jnp.sum(jnp.exp(pairwise_affinity_matrix - peak_logit), -1, keepdims=True)
    )
    columns = lax.broadcasted_iota(jnp.int32, pairwise_affinity_matrix.shape, 1)
    matching_labels = columns == positives[:, None]
    picked = jnp.sum(jnp.where(matching_labels, pairwise_affinity_matrix, 0.0), -1, keepdims=True)
    total = jnp.sum(log_partition_norm - picked)
    loss = total / queries_total
    similarity_gradient = (
        jnp.exp(pairwise_affinity_matrix - log_partition_norm) - matching_labels.astype(jnp.float32)
    ) / contrast_sharpness_factor
    own_rows = lax.dynamic_slice_in_dim(similarity_gradient, device_id * QPD, QPD, 0)
    query_side = jnp.dot(own_rows, gathered_document_rows, precision=exact_product_accuracy)
    own_column = lax.dynamic_slice_in_dim(similarity_gradient, device_id, 1, 1)
    doc_side = jnp.dot(own_column.T, gathered_query_rows, precision=exact_product_accuracy)
    doc_side = jnp.concatenate([doc_side, jnp.zeros((QPD - 1, D), jnp.float32)], 0)
    embed_grad = jnp.where(tower_id == 0, query_side, doc_side)
    pooled_grad = normal_back(embed_grad)[0]
    top_grad = jnp.dot(pool_matrix.T, pooled_grad, precision=exact_product_accuracy)
    sum_two, gain_two_grad, bias_two_grad = norm_two_back(top_grad)
    attention_input_cotangent, out_back, gate_back, up_back, down_back = (
        qkv_full,
        out_full,
        gate_full,
        up_full,
        down_full,
    )
    branch_low = sum_two.astype(jnp.bfloat16)
    down_grad = product(hidden.T, branch_low)
    hidden_grad = product(branch_low, down_back.T)
    gate_grad_wide, up_grad_wide = swish_back(hidden_grad)
    gate_low = gate_grad_wide.astype(jnp.bfloat16)
    up_low = up_grad_wide.astype(jnp.bfloat16)
    gate_weight_grad = product(feed.T, gate_low)
    up_weight_grad = product(feed.T, up_low)
    feed_grad = sum_two + product(gate_low, gate_back.T) + product(up_low, up_back.T)
    sum_one, gain_one_grad, bias_one_grad = norm_one_back(feed_grad)
    attend_low = sum_one.astype(jnp.bfloat16)
    out_grad = product(mixed_low.T, attend_low)
    mixed_grad = product(attend_low, out_back.T).astype(jnp.bfloat16).reshape(count, HEADS, HEAD)
    probs_again = jnp.exp(masked_scores() - log_total)
    prob_grad = jnp.einsum(
        "ihd,jhd->hij", mixed_grad, value_low, preferred_element_type=jnp.float32
    )
    score_grad = probs_again * (prob_grad - jnp.sum(probs_again * prob_grad, -1, keepdims=True))
    score_low = score_grad.astype(jnp.bfloat16)
    query_grad = (
        jnp.einsum("hij,jhd->ihd", score_low, key_low, preferred_element_type=jnp.float32) * scale
    )
    key_grad = (
        jnp.einsum("hij,ihd->jhd", score_low, query_low, preferred_element_type=jnp.float32) * scale
    )
    value_grad = jnp.einsum(
        "hij,ihd->jhd",
        probs_again.astype(jnp.bfloat16),
        mixed_grad,
        preferred_element_type=jnp.float32,
    )
    raw_query_grad, raw_key_grad = rotary_back((query_grad, key_grad))
    packed_grad = jnp.concatenate(
        [
            raw_query_grad.reshape(count, D),
            raw_key_grad.reshape(count, D),
            value_grad.reshape(count, D),
        ],
        1,
    ).astype(jnp.bfloat16)
    qkv_grad = product(inputs.T, packed_grad)
    input_grad = sum_one + product(packed_grad, attention_input_cotangent.T)
    gradients = (
        qkv_grad,
        out_grad,
        gate_weight_grad,
        up_weight_grad,
        down_grad,
        gain_one_grad,
        bias_one_grad,
        gain_two_grad,
        bias_two_grad,
    )
    partial_sums = (
        lax.psum_scatter(gradients[0], DP, scatter_dimension=0, tiled=True),
        lax.psum_scatter(gradients[1], DP, scatter_dimension=0, tiled=True),
        lax.psum_scatter(gradients[2], DP, scatter_dimension=0, tiled=True),
        lax.psum_scatter(gradients[3], DP, scatter_dimension=0, tiled=True),
        lax.psum_scatter(gradients[4], DP, scatter_dimension=0, tiled=True),
        lax.psum_scatter(gradients[5], DP, scatter_dimension=0, tiled=True),
        lax.psum_scatter(gradients[6], DP, scatter_dimension=0, tiled=True),
        lax.psum_scatter(gradients[7], DP, scatter_dimension=0, tiled=True),
        lax.psum_scatter(gradients[8], DP, scatter_dimension=0, tiled=True),
    )
    tower_halves = (
        lax.psum_scatter(
            partial_sums[0].astype(jnp.bfloat16), TOWER, scatter_dimension=0, tiled=True
        ).astype(jnp.float32),
        lax.psum_scatter(
            partial_sums[1].astype(jnp.bfloat16), TOWER, scatter_dimension=0, tiled=True
        ).astype(jnp.float32),
        lax.psum_scatter(
            partial_sums[2].astype(jnp.bfloat16), TOWER, scatter_dimension=0, tiled=True
        ).astype(jnp.float32),
        lax.psum_scatter(
            partial_sums[3].astype(jnp.bfloat16), TOWER, scatter_dimension=0, tiled=True
        ).astype(jnp.float32),
        lax.psum_scatter(
            partial_sums[4].astype(jnp.bfloat16), TOWER, scatter_dimension=0, tiled=True
        ).astype(jnp.float32),
        lax.psum_scatter(
            partial_sums[5].astype(jnp.bfloat16), TOWER, scatter_dimension=0, tiled=True
        ).astype(jnp.float32),
        lax.psum_scatter(
            partial_sums[6].astype(jnp.bfloat16), TOWER, scatter_dimension=0, tiled=True
        ).astype(jnp.float32),
        lax.psum_scatter(
            partial_sums[7].astype(jnp.bfloat16), TOWER, scatter_dimension=0, tiled=True
        ).astype(jnp.float32),
        lax.psum_scatter(
            partial_sums[8].astype(jnp.bfloat16), TOWER, scatter_dimension=0, tiled=True
        ).astype(jnp.float32),
    )
    shares = (
        lax.all_gather(tower_halves[0].astype(jnp.bfloat16), TOWER, axis=0, tiled=True).astype(
            jnp.float32
        ),
        lax.all_gather(tower_halves[1].astype(jnp.bfloat16), TOWER, axis=0, tiled=True).astype(
            jnp.float32
        ),
        lax.all_gather(tower_halves[2].astype(jnp.bfloat16), TOWER, axis=0, tiled=True).astype(
            jnp.float32
        ),
        lax.all_gather(tower_halves[3].astype(jnp.bfloat16), TOWER, axis=0, tiled=True).astype(
            jnp.float32
        ),
        lax.all_gather(tower_halves[4].astype(jnp.bfloat16), TOWER, axis=0, tiled=True).astype(
            jnp.float32
        ),
        lax.all_gather(tower_halves[5].astype(jnp.bfloat16), TOWER, axis=0, tiled=True).astype(
            jnp.float32
        ),
        lax.all_gather(tower_halves[6].astype(jnp.bfloat16), TOWER, axis=0, tiled=True).astype(
            jnp.float32
        ),
        lax.all_gather(tower_halves[7].astype(jnp.bfloat16), TOWER, axis=0, tiled=True).astype(
            jnp.float32
        ),
        lax.all_gather(tower_halves[8].astype(jnp.bfloat16), TOWER, axis=0, tiled=True).astype(
            jnp.float32
        ),
    )
    query_rows = lax.dynamic_slice_in_dim(gathered_query_rows, device_id * QPD, QPD, 0)
    doc_row = lax.dynamic_slice_in_dim(gathered_document_rows, device_id, 1, 0)
    return (loss, query_rows, doc_row, input_grad[None]) + tuple(shares)


MESH = pl.DeviceIdType.MESH
BF = jnp.bfloat16
F32 = jnp.float32
LANES = 128


def dot_tt(left, right, precision=None):
    return lax.dot_general(
        left, right, (((1,), (1,)), ((), ())), preferred_element_type=F32, precision=precision
    )


def dot_t0(left, right, precision=None):
    return lax.dot_general(
        left, right, (((0,), (0,)), ((), ())), preferred_element_type=F32, precision=precision
    )


def rotary_constants(count):
    freqs = np.power(
        np.float32(rope_base), (-2.0 * np.arange(HEAD // 2) / HEAD).astype(np.float32)
    ).astype(np.float32)
    angles = (np.arange(count, dtype=np.float32)[:, None] * freqs[None, :]).astype(np.float64)
    cosines, sines = np.cos(angles), np.sin(angles)
    return (
        np.tile(np.concatenate([cosines, cosines], 1), (1, 2)).astype(np.float32),
        np.tile(np.concatenate([-sines, sines], 1), (1, 2)).astype(np.float32),
    )


def aligned(start, unit):
    return start if isinstance(start, int) else pl.multiple_of(start, unit)


def both(first, second):
    return jnp.logical_and(first, second)


def do(condition, action):
    if condition is None:
        action()
    else:
        pl.when(condition)(action)


class Plan:
    def __init__(self, groups, count, shard, shard_ff, vec):
        self.groups = groups
        self.line = groups // 4
        self.count = count
        self.shard = shard
        self.shard_ff = shard_ff
        self.vec = vec
        self.width_a = 4 * D
        self.half_a = 2 * D
        self.ff = shard_ff * groups
        self.half_ff = self.ff // 2
        self.stripe = 2 * shard_ff


def semaphores(plan):
    line, groups = plan.line, plan.groups
    dma = pltpu.SemaphoreType.DMA
    chunks_gu, chunks_a = 4, 4
    return dict(
        loc=dma((40,)),
        ra=dma((groups, 2)),
        sa_z=dma((2, line)),
        sa_x=dma((line, 2)),
        sa_y=dma((line, 2)),
        sa_c=dma((line, 2, 2)),
        rg=dma((groups, 2)),
        sg_z=dma((2, line, 2)),
        sg_x=dma((line, 2)),
        sg_c=dma((line, 2, 2)),
        rd=dma((line, 2)),
        sd_x=dma((1,)),
        sd_z=dma((2, line)),
        sd_c=dma((line,)),
        rv=dma((groups,)),
        sv=dma((groups,)),
        s_part=dma((D // (2 * LANES),)),
        r_part=dma((D // (2 * LANES),)),
        s_back=dma((line,)),
        r_back=dma((line,)),
        sx=dma((4,)),
        rx=dma((4,)),
        r_doc=dma((groups,)),
        s_doc=dma((groups,)),
        r_slope=dma((groups,)),
        s_slope=dma((groups,)),
        r_query=dma((1,)),
        s_query=dma((1,)),
        s_ln=dma((line.bit_length() + 2,)),
        r_ln=dma((line.bit_length() + 2,)),
        gd_c=dma((2, line)),
        gd_z=dma((2, 2, line)),
        gd_x=dma((2,)),
        gd_y=dma((2,)),
        gg_c=dma((2, chunks_gu)),
        gg_x=dma((2, chunks_gu)),
        gg_z=dma((2, chunks_gu, 2, line)),
        gg_y=dma((2, chunks_gu)),
        ga_c=dma((2, 2, chunks_a)),
        ga_t=dma((2, chunks_a)),
        ga_x=dma((2, chunks_a)),
        ga_z=dma((2, chunks_a, 2, line)),
        ga_y=dma((2, chunks_a)),
        fin=dma((10,)),
    )


def buffers(plan):
    line, count, shard, groups = plan.line, plan.count, plan.shard, plan.groups
    pair = 2 * count
    v = pltpu.VMEM
    return dict(
        wa=v((line, 2, 2, shard, plan.width_a), BF),
        wg=v((line, 2, 2, shard, plan.ff), BF),
        wd=v((line, 2, plan.shard_ff, D), BF),
        tok=v((count, D), BF),
        vt=v((groups, 8, LANES), F32),
        vec=v((8, D), F32),
        cos=v((count, LANES), F32),
        sin=v((count, LANES), F32),
        hide=v((count, count), F32),
        pw=v((count, 1), F32),
        qkv=v((count, 3 * D), BF),
        probs=v((HEADS, count, count), F32),
        mixed=v((count, D), BF),
        mixt=v((D, count), BF),
        tokt=v((D, count), BF),
        h1=v((count, D), F32),
        rs1=v((count, 1), F32),
        n1=v((count, D), F32),
        feed=v((pair, D), BF),
        feedt=v((D, pair), BF),
        gate=v((pair, plan.half_ff), F32),
        up=v((pair, plan.half_ff), F32),
        hidt=v((plan.half_ff, pair), BF),
        dgu=v((pair, plan.ff), BF),
        bown=v((count, D), F32),
        bsend=v((count, D), BF),
        brecv=v((count, D), BF),
        xh2=v((count, D), F32),
        rs2=v((count, 1), F32),
        dbr=v((pair, D), BF),
        dsend=v((count, D), BF),
        drecv=v((count, D), BF),
        datt=v((count, D), BF),
        pool=v((8, D), F32),
        dpool=v((8, D), F32),
        emb=v((8, D), F32),
        embd=v((1, D), F32),
        embq=v((QPD, D), F32),
        dbuf=v((groups, 1, D), F32),
        cbuf=v((groups, 1, D), F32),
        csend=v((groups, 1, D), F32),
        qrecv=v((QPD, D), F32),
        dflat=v((groups, D), F32),
        ln=v((line.bit_length() + 3, 8, D), F32),
        lnr=v((line.bit_length() + 2, 8, D), F32),
        gd=v((line, 2, plan.shard_ff, D), BF),
        gd_rc=v((line, plan.shard_ff, D), BF),
        gd_rz=v((line + 1, plan.shard_ff, D), BF),
        gd_rx=v((plan.shard_ff, D), BF),
        gd_f=v((plan.shard_ff, D), BF),
        gg=v((line, 2, 2, shard, plan.ff), BF),
        gg_rc=v((line, 2, shard, plan.ff), BF),
        gg_rx=v((line, shard, plan.ff), BF),
        gg_rz=v((line + 1, shard, plan.ff), BF),
        gg_f=v((shard, plan.ff), BF),
        ga_rc=v((line, 2, shard, plan.width_a), BF),
        ga_rt=v((line, 2, shard, plan.half_a), BF),
        ga_rx=v((line, shard, plan.half_a), BF),
        ga_rz=v((line + 1, shard, plan.half_a), BF),
        ga_f=v((shard, plan.half_a), BF),
    )


class Operands(NamedTuple):
    qlen: Any
    dlen: Any
    pos: Any
    i_tok: Any
    tcos: Any
    tsin: Any
    g_one: Any
    b_one: Any
    g_two: Any
    b_two: Any
    i_qkv: Any
    i_out: Any
    i_gate: Any
    i_up: Any
    i_down: Any


class Results(NamedTuple):
    o_tok: Any
    o_a: Any
    o_gu: Any
    o_dn: Any
    o_vec: Any
    o_q: Any
    o_d: Any
    o_loss: Any


def whole_step(plan, *refs):
    names = (Operands._fields + Results._fields + tuple(buffers(plan)) + tuple(semaphores(plan)))
    r = SimpleNamespace(**dict(zip(names, refs, strict=True)))
    line, groups, count = plan.line, plan.groups, plan.count
    shard, shard_ff, stripe = plan.shard, plan.shard_ff, plan.stripe
    half_a, half_ff, ff = plan.half_a, plan.half_ff, plan.ff
    quarter = QLEN
    shift = QLEN.bit_length() - 1

    t = lax.axis_index(TOWER)
    me = lax.axis_index(DP)
    z = me // 4
    x = (me // 2) % 2
    c = me % 2

    def at(zz, xx, cc):
        return (zz * 2 + xx) * 2 + cc

    dev_x = {TOWER: t, DP: at(z, 1 - x, c)}
    dev_c = {TOWER: t, DP: at(z, x, 1 - c)}
    dev_y = {TOWER: 1 - t, DP: me}

    def dev_z(zz):
        return {TOWER: t, DP: at(zz, x, c)}

    pending, tail = [], []

    def copy(src, dst, ssem, rsem, dev):
        return pltpu.make_async_remote_copy(
            src_ref=src, dst_ref=dst, send_sem=ssem, recv_sem=rsem,
            device_id=dev, device_id_type=MESH,
        )

    def send(cond, what, keep=pending):
        do(cond, what.start)
        keep.append((cond, what))

    def settle(keep):
        for cond, what in keep:
            do(cond, what.wait_send)
        keep.clear()

    def got(cond, ref, rsem):
        do(cond, copy(ref, ref, r.s_query.at[0], rsem, dev_x).wait_recv)

    wa, wg, wd = r.wa, r.wg, r.wd
    out_w = half_a - 3 * D // 2
    local = []

    def near(src, dst, cond=None):
        what = pltpu.make_async_copy(src, dst, r.loc.at[len(local)])
        do(cond, what.start)
        local.append((cond, what))

    third = 3 * D // 2
    half_d = D // 2
    for h in range(2):
        for k in range(3):
            near(r.i_qkv.at[:, pl.ds(k * D + h * half_d, half_d)],
                 wa.at[z, x, c, :, pl.ds(h * half_a + k * half_d, half_d)])
        near(r.i_out.at[:, pl.ds(h * out_w, out_w)],
             wa.at[z, x, c, :, pl.ds(h * half_a + third, out_w)])
    near(r.i_down, wd.at[z, c], x == t)
    near(r.i_tok, r.tok)
    for s in range(QPD):
        begin = aligned(s * QLEN * t, QLEN)
        near(r.tcos.at[pl.ds(begin, QLEN)], r.cos.at[pl.ds(s * QLEN, QLEN)])
        near(r.tsin.at[pl.ds(begin, QLEN)], r.sin.at[pl.ds(s * QLEN, QLEN)])
    part_ff = half_ff // 2
    per_part = line // 2

    def stripe_at(k, s):
        return (2 * (s // per_part) + k) * part_ff + (s % per_part) * stripe

    for s in range(line):
        for k, ref in enumerate((r.i_gate, r.i_up)):
            near(ref.at[:, pl.ds(aligned((2 * s + t) * stripe, LANES), stripe)],
                 wg.at[z, x, c, :, pl.ds(stripe_at(k, s), stripe)])

    r.vt[me] = jnp.zeros((8, LANES), F32)
    for k, ref in enumerate((r.g_one, r.b_one, r.g_two, r.b_two)):
        r.vt[me, pl.ds(k, 1), pl.ds(0, plan.vec)] = ref[...].astype(F32)

    barrier = pltpu.get_barrier_semaphore()

    def greet(j, carry):
        other = jnp.logical_or(j // groups != t, j % groups != me)

        @pl.when(other)
        def _():
            pl.semaphore_signal(
                barrier, inc=1, device_id={TOWER: j // groups, DP: j % groups},
                device_id_type=MESH,
            )

        return carry

    lax.fori_loop(0, 2 * groups, greet, 0)
    pl.semaphore_wait(barrier, 2 * groups - 1)
    for cond, what in local:
        do(cond, what.wait)

    def piece_a(zz, xx, cc, h):
        return wa.at[zz, xx, cc, :, pl.ds(aligned(h * half_a, LANES), half_a)]

    def send_a(cond, sem, zz, xx, h, dev):
        ref = piece_a(zz, xx, c, h)
        send(cond, copy(ref, ref, sem, r.ra.at[at(zz, xx, c), h], dev))

    def got_a(cond, zz, xx, cc, h):
        got(cond, piece_a(zz, xx, cc, h), r.ra.at[at(zz, xx, cc), h])

    def sides(step):
        return ((z - step, z >= step, z < line - 1, z + 1), (z + step, z < line - step, z > 0, z - 1))

    def a_start():
        for way, (_, _, on, nxt) in enumerate(sides(0)):
            send_a(on, r.sa_z.at[way, z], z, x, t, dev_z(nxt))
        send_a(None, r.sa_x.at[z, t], z, x, t, dev_x)
        send_a(x != t, r.sa_x.at[z, 1 - t], z, x, 1 - t, dev_x)
        send_a(None, r.sa_c.at[z, x, t], z, x, t, dev_c)
        send_a(None, r.sa_c.at[z, x, 1 - t], z, x, 1 - t, dev_c)

    def a_round(step, way):
        zz, there, on, nxt = sides(step)[way]
        got_a(there, zz, x, c, t)
        send_a(both(there, on), r.sa_z.at[way, zz], zz, x, t, dev_z(nxt))
        send_a(there, r.sa_x.at[zz, t], zz, x, t, dev_x)
        send_a(there, r.sa_y.at[zz, x], zz, x, t, dev_y)
        send_a(there, r.sa_c.at[zz, x, t], zz, x, t, dev_c)

    def a_cross(step, way):
        zz, there, _, _ = sides(step)[way]
        got_a(there, zz, 1 - x, c, t)
        send_a(there if step else x == t, r.sa_y.at[zz, 1 - x], zz, 1 - x, t, dev_y)
        send_a(there, r.sa_c.at[zz, 1 - x, t], zz, 1 - x, t, dev_c)

    def a_tower(step, way):
        zz, there, _, _ = sides(step)[way]
        for xx in (x, 1 - x) if step else (1 - x,):
            got_a(there, zz, xx, c, 1 - t)
            send_a(there, r.sa_c.at[zz, xx, 1 - t], zz, xx, 1 - t, dev_c)

    def a_sibling(h):
        for zz in range(line):
            for xx in range(2):
                got_a(None, zz, xx, 1 - c, h)

    def piece_g(zz, xx, cc, h):
        return wg.at[zz, xx, cc, :, pl.ds(h * half_ff, half_ff)]

    def send_g(cond, sem, zz, xx, h, dev):
        ref = piece_g(zz, xx, c, h)
        send(cond, copy(ref, ref, sem, r.rg.at[at(zz, xx, c), h], dev))

    def got_g(cond, zz, xx, cc, h):
        got(cond, piece_g(zz, xx, cc, h), r.rg.at[at(zz, xx, cc), h])

    def g_start(h):
        for way, (_, _, on, nxt) in enumerate(sides(0)):
            send_g(on, r.sg_z.at[way, z, h], z, x, h, dev_z(nxt))

    def g_line(step, way, h):
        zz, there, on, nxt = sides(step)[way]
        got_g(there, zz, x, c, h)
        send_g(both(there, on), r.sg_z.at[way, zz, h], zz, x, h, dev_z(nxt))

    def g_spread(step, way, h):
        zz, there, _, _ = sides(step)[way]
        send_g(there, r.sg_x.at[zz, h], zz, x, h, dev_x)
        send_g(there, r.sg_c.at[zz, x, h], zz, x, h, dev_c)

    def g_cross(step, way, h):
        zz, there, _, _ = sides(step)[way]
        got_g(there, zz, 1 - x, c, h)
        send_g(there, r.sg_c.at[zz, 1 - x, h], zz, 1 - x, h, dev_c)

    def g_sibling(h):
        for zz in range(line):
            for xx in range(2):
                got_g(None, zz, xx, 1 - c, h)

    def send_d(cond, sem, zz, dev):
        ref = wd.at[zz, c]
        send(cond, copy(ref, ref, sem, r.rd.at[zz, c], dev))

    def got_d(cond, zz, cc):
        got(cond, wd.at[zz, cc], r.rd.at[zz, cc])

    def d_cross():
        send_d(x == t, r.sd_x.at[0], z, dev_x)

    def d_start():
        got_d(x != t, z, c)
        for way, (_, _, on, nxt) in enumerate(sides(0)):
            send_d(on, r.sd_z.at[way, z], z, dev_z(nxt))
        send_d(None, r.sd_c.at[z], z, dev_c)

    def d_round(step, way, ends):
        zz, there, on, nxt = sides(step)[way]
        cond = both(there, jnp.logical_not(on) if ends else on)
        got_d(cond, zz, c)
        if not ends:
            send_d(cond, r.sd_z.at[way, zz], zz, dev_z(nxt))
        send_d(cond, r.sd_c.at[zz], zz, dev_c)

    def d_sibling():
        for zz in range(line):
            got_d(None, zz, 1 - c)

    def v_send(j, carry):
        @pl.when(j != me)
        def _():
            copy(r.vt.at[me], r.vt.at[me], r.sv.at[j], r.rv.at[me],
                 {TOWER: t, DP: j}).start()

        return carry

    def v_wait(j, carry):
        @pl.when(j != me)
        def _():
            copy(r.vt.at[me], r.vt.at[j], r.sv.at[j], r.rv.at[j],
                 {TOWER: t, DP: j}).wait()

        return carry

    a_start()
    lax.fori_loop(0, groups, v_send, 0)

    tok = r.tok
    rows = lax.broadcasted_iota(jnp.int32, (count, count), 0)
    cols = lax.broadcasted_iota(jnp.int32, (count, count), 1)
    seg = cols >> shift
    limit = jnp.zeros_like(cols)
    for s in range(QPD):
        limit = jnp.where(seg == s, r.qlen[s], limit)
    limit = limit * (1 - t) + r.dlen[0] * t
    place = cols - seg * (quarter * (1 - t))
    apart = ((rows >> shift) - seg) * (1 - t)
    seen = both(apart == 0, place < limit)
    r.hide[...] = jnp.where(seen, 0.0, -1e30)
    for s in range(QPD):
        part = pl.ds(s * quarter, quarter)
        length = jnp.full((quarter, 1), r.qlen[s] * (1 - t) + r.dlen[0] * t, jnp.int32)
        slot = lax.broadcasted_iota(jnp.int32, (quarter, 1), 0) + s * quarter * t
        r.pw[part, :] = jnp.where(slot < length, 1.0 / length.astype(F32), 0.0)
    lanes = lax.broadcasted_iota(jnp.int32, (count, LANES), 1)
    first_head = lanes < HEAD
    low_half = (lanes & (HEAD - 1)) < HEAD // 2

    def swap(a):
        return jnp.where(low_half, pltpu.roll(a, LANES - HEAD // 2, 1), pltpu.roll(a, HEAD // 2, 1))

    def turn(a):
        return a * r.cos[...] + swap(a) * r.sin[...]

    def turn_back(a):
        return a * r.cos[...] - swap(a) * r.sin[...]

    def transpose_into(dst, src, width):
        def body(j, carry):
            o = aligned(j * LANES, LANES)
            dst[pl.ds(o, LANES), :] = src[:, pl.ds(o, LANES)].T
            return carry

        lax.fori_loop(0, width // LANES, body, 0)

    def wide(ref, lo, n):
        return ref[:, :, :, :, pl.ds(lo, n)].reshape(groups * shard, n)

    def widen_vec():
        lane = lax.broadcasted_iota(jnp.int32, (8, LANES), 1)
        parts = [jnp.zeros((8, LANES), F32) for _ in range(D // LANES)]
        for j in range(groups):
            block, first = divmod(j * plan.vec, LANES)
            piece = r.vt[j]
            if first:
                piece = pltpu.roll(piece, first, 1)
            parts[block] = parts[block] + jnp.where(lane >= first, piece, 0.0)
            if first + plan.vec > LANES:
                parts[block + 1] = parts[block + 1] + jnp.where(lane < first, piece, 0.0)
        r.vec[...] = jnp.concatenate(parts, axis=1)

    pairs = D // LANES
    half_pairs = pairs // 2

    scale = HEAD ** (-0.5)

    def project(h):
        for k in range(3):
            packed = jnp.dot(tok[...], wide(wa, aligned(h * half_a + k * half_d, LANES), half_d),
                             preferred_element_type=F32)
            for i in range(half_pairs):
                part = packed[:, i * LANES : (i + 1) * LANES]
                if k < 2:
                    part = turn(part)
                if k == 0:
                    part = part * scale
                r.qkv[:, pl.ds(aligned(k * D + h * half_d + i * LANES, LANES), LANES)] = (
                    part.astype(BF))

    def triple(p):
        o = aligned(p * LANES, LANES)
        return tuple(r.qkv[:, pl.ds(k * D + o, LANES)] for k in range(3))

    def only(h, a):
        return jnp.where(first_head if h == 0 else jnp.logical_not(first_head), a, jnp.zeros_like(a))

    def attend(p):
        q2, k2, v2 = triple(p)
        outs = []
        for h in range(2):
            scores = dot_tt(only(h, q2), k2) + r.hide[...]
            grown = jnp.exp(scores - jnp.max(scores, -1, keepdims=True))
            probs = grown * (1.0 / jnp.sum(grown, -1, keepdims=True))
            r.probs[2 * p + h] = probs
            outs.append(jnp.dot(probs.astype(BF), v2, preferred_element_type=F32))
        o = aligned(p * LANES, LANES)
        r.mixed[:, pl.ds(o, LANES)] = jnp.where(first_head, outs[0], outs[1]).astype(BF)

    def over_pairs(h, body, lo=0, hi=half_pairs):
        def step(i, carry):
            body(h * half_pairs + i)
            return carry

        lax.fori_loop(lo, hi, step, 0)

    def vectors():
        lax.fori_loop(0, groups, v_wait, 0)
        widen_vec()

    def out_project():
        for h in range(2):
            part = jnp.dot(r.mixed[...], wide(wa, h * half_a + third, out_w),
                           preferred_element_type=F32)
            r.h1[:, pl.ds(h * out_w, out_w)] = tok[:, pl.ds(h * out_w, out_w)].astype(F32) + part

    def moments(h):
        centred = h - jnp.mean(h, -1, keepdims=True)
        return centred, lax.rsqrt(jnp.mean(centred * centred, -1, keepdims=True) + 1e-05)

    blocks = count // quarter

    def norm_one(b, carry):
        part = pl.ds(aligned(b * quarter, quarter), quarter)
        centred, inverse = moments(r.h1[part, :])
        hat = centred * inverse
        normed = hat * r.vec[0:1, :] + r.vec[1:2, :]
        r.h1[part, :] = hat
        r.rs1[part, :] = inverse
        r.n1[part, :] = normed
        r.feed[pl.ds(aligned(t * count + b * quarter, quarter), quarter), :] = (
            normed.astype(BF))
        return carry

    mine = pl.ds(aligned(t * count, count), count)
    theirs = pl.ds(aligned((1 - t) * count, count), count)

    def swap_rows(k, src, dst):
        send(None, copy(src, dst, r.sx.at[k], r.rx.at[k], dev_y), tail)

    def got_rows(k, ref):
        got(None, ref, r.rx.at[k])

    def norm_rows():
        lax.fori_loop(0, blocks, norm_one, 0)
        swap_rows(0, r.feed.at[mine], r.feed.at[mine])

    step_ff = 2 * LANES

    steps_part = part_ff // step_ff

    def gated(part):
        def body(j, carry):
            o = aligned(part * part_ff + j * step_ff, step_ff)
            w = 2 * part * part_ff + j * step_ff
            gate = jnp.dot(r.feed[...], wide(wg, aligned(w, step_ff), step_ff),
                           preferred_element_type=F32)
            up = jnp.dot(r.feed[...], wide(wg, aligned(w + part_ff, step_ff), step_ff),
                         preferred_element_type=F32)
            r.gate[:, pl.ds(o, step_ff)] = gate
            r.up[:, pl.ds(o, step_ff)] = up
            hidden = (gate * jax.nn.sigmoid(gate) * up).astype(BF)
            r.dgu[:, pl.ds(o, step_ff)] = hidden
            r.hidt[pl.ds(o, step_ff), :] = hidden.T
            return carry

        lax.fori_loop(0, steps_part, body, 0)

    def down(rows_of, store):
        def body(j):
            o = j * step_ff
            w = wd[:, :, :, pl.ds(o, step_ff)].reshape(half_ff, step_ff)
            store(o, jnp.dot(r.dgu[rows_of, pl.ds(0, half_ff)], w, preferred_element_type=F32))

        for j in range(D // step_ff):
            body(j)

    def keep_send(o, val):
        span = pl.ds(o, step_ff)
        r.bsend[:, span] = val.astype(BF)
        send(None, copy(r.bsend.at[:, span], r.brecv.at[:, span], r.s_part.at[o // step_ff],
                        r.r_part.at[o // step_ff], dev_y), tail)

    def keep_own(o, val):
        r.bown[:, pl.ds(o, step_ff)] = val

    g_start(0)
    d_cross()
    a_round(1, 0)
    a_round(1, 1)
    g_line(1, 0, 0)
    g_line(1, 1, 0)
    a_cross(0, 0)
    a_round(2, 1)
    a_round(2, 0)
    a_cross(1, 0)
    g_start(1)
    g_spread(0, 0, 1)
    a_cross(1, 1)
    g_line(2, 1, 0)
    g_line(2, 0, 0)
    a_round(3, 0)
    a_round(3, 1)
    g_line(1, 0, 1)
    a_cross(2, 0)
    a_cross(2, 1)
    g_spread(1, 1, 0)
    g_line(1, 1, 1)
    g_spread(2, 0, 0)
    g_spread(2, 1, 0)
    d_start()
    a_tower(1, 0)
    g_spread(1, 0, 0)
    g_line(3, 0, 0)
    g_spread(1, 0, 1)
    g_spread(0, 0, 0)
    a_cross(3, 0)
    a_tower(0, 0)
    a_cross(3, 1)
    vectors()
    g_line(2, 0, 1)
    a_sibling(t)
    g_spread(3, 0, 0)
    project(t)
    over_pairs(t, attend, 0, 1)
    g_cross(0, 0, 1)
    over_pairs(t, attend, 1, 2)
    g_spread(1, 1, 1)
    g_line(2, 1, 1)
    g_line(3, 1, 0)
    g_spread(3, 1, 0)
    a_tower(3, 0)
    over_pairs(t, attend, 2, 3)
    a_tower(1, 1)
    a_tower(3, 1)
    a_tower(2, 0)
    a_tower(2, 1)
    d_round(1, 0, False)
    a_sibling(1 - t)
    project(1 - t)
    over_pairs(1 - t, attend, 0, 1)
    d_round(1, 1, False)
    over_pairs(1 - t, attend, 1, 3)
    out_project()
    norm_rows()
    g_spread(2, 0, 1)
    g_cross(2, 1, 0)
    d_round(2, 0, False)
    g_line(3, 0, 1)
    d_round(1, 1, True)
    g_spread(3, 0, 1)
    d_round(1, 0, True)
    d_round(2, 0, True)
    g_line(3, 1, 1)
    g_cross(2, 0, 0)
    g_cross(1, 0, 0)
    g_cross(0, 0, 0)
    g_cross(3, 0, 0)
    g_spread(3, 1, 1)
    g_cross(3, 1, 0)
    g_spread(2, 1, 1)
    g_cross(1, 1, 0)
    d_round(2, 1, False)
    g_sibling(0)
    g_cross(3, 1, 1)
    transpose_into(r.tokt, tok, D)
    g_cross(1, 1, 1)
    g_cross(1, 0, 1)
    g_cross(2, 0, 1)
    d_round(2, 1, True)
    g_cross(3, 0, 1)
    g_cross(2, 1, 1)
    got_rows(0, r.feed.at[theirs])
    gated(0)
    g_sibling(1)
    d_round(3, 1, True)
    d_round(3, 0, True)
    gated(1)
    d_sibling()
    transpose_into(r.mixt, r.mixed, D)
    down(theirs, keep_send)
    down(mine, keep_own)
    transpose_into(r.feedt, r.feed, D)
    for j in range(D // step_ff):
        got(None, r.brecv.at[:, pl.ds(j * step_ff, step_ff)], r.r_part.at[j])

    r.pool[...] = jnp.zeros((8, D), F32)

    def norm_two(b, carry):
        part = pl.ds(aligned(b * quarter, quarter), quarter)
        h = r.n1[part, :] + (r.bown[part, :] + r.brecv[part, :].astype(F32))
        centred, inverse = moments(h)
        hat = centred * inverse
        normed = hat * r.vec[2:3, :] + r.vec[3:4, :]
        r.xh2[part, :] = hat
        r.rs2[part, :] = inverse
        r.pool[pl.ds(b, 1), :] = jnp.sum(normed * r.pw[part, :], 0, keepdims=True)
        return carry

    lax.fori_loop(0, blocks, norm_two, 0)
    row8 = lax.broadcasted_iota(jnp.int32, (8, D), 0)

    @pl.when(t == 1)
    def _():
        all_rows = jnp.sum(r.pool[...], 0, keepdims=True)
        r.pool[...] = jnp.where(row8 == 0, all_rows, 0.0)

    pooled = r.pool[...]
    shrink = lax.rsqrt(jnp.sum(pooled * pooled, -1, keepdims=True) + 1e-06)
    r.emb[...] = pooled * shrink

    best = exact_product_accuracy
    r.dpool[...] = jnp.zeros((8, D), F32)
    r.ln[0] = jnp.zeros((8, D), F32)

    def to_all(tower, src, dst, ssem, rsem):
        def give(step, carry):
            j = (me + step) % groups
            copy(src(j), dst.at[me], ssem.at[j], rsem.at[me], {TOWER: tower, DP: j}).start()
            return carry

        lax.fori_loop(0, groups, give, 0)

    def from_all(dst, ssem, rsem):
        def take(j, carry):
            copy(dst.at[j], dst.at[j], ssem.at[j], rsem.at[j], dev_x).wait_recv()
            return carry

        lax.fori_loop(0, groups, take, 0)

    @pl.when(t == 1)
    def _():
        r.embd[...] = r.emb[0:1, :]
        r.dbuf[me] = r.emb[0:1, :]
        to_all(0, lambda j: r.embd, r.dbuf, r.s_doc, r.r_doc)
        from_all(r.cbuf, r.s_slope, r.r_slope)
        total = r.cbuf[0]
        for j in range(1, groups):
            total = total + r.cbuf[j]
        r.dpool[0:1, :] = total

    @pl.when(t == 0)
    def _():
        r.embq[...] = r.emb[0:QPD, :]
        from_all(r.dbuf, r.s_doc, r.r_doc)
        for j in range(groups):
            r.dflat[pl.ds(j, 1), :] = r.dbuf[j]
        docs, queries = r.dflat[...], r.embq[...]
        logits = dot_tt(queries, docs, best) / contrast_sharpness_factor
        peak = jnp.max(logits, -1, keepdims=True)
        lse = peak + jnp.log(jnp.sum(jnp.exp(logits - peak), -1, keepdims=True))
        col = lax.broadcasted_iota(jnp.int32, (QPD, groups), 1)
        row = lax.broadcasted_iota(jnp.int32, (QPD, groups), 0)
        label = jnp.zeros((QPD, groups), jnp.int32)
        for s in range(QPD):
            label = jnp.where(row == s, r.pos[me * QPD + s], label)
        hot = jnp.where(col == label, 1.0, 0.0)
        slope = (jnp.exp(logits - lse) - hot) / contrast_sharpness_factor
        back = dot_t0(slope, queries, best)
        for j in range(groups):
            r.csend[j] = back[j : j + 1, :]
        to_all(1, lambda j: r.csend.at[j], r.cbuf, r.s_slope, r.r_slope)
        r.dpool[0:QPD, :] = jnp.dot(slope, docs, preferred_element_type=F32, precision=best)
        picked = jnp.sum(jnp.where(hot > 0.5, logits, 0.0), -1, keepdims=True)
        total = jnp.sum(lse - picked, 0, keepdims=True)
        r.ln[0] = jnp.where(row8 == 4, total, 0.0)

    slope = r.dpool[...]
    emb = r.emb[...]
    dpool = shrink * (slope - emb * jnp.sum(slope * emb, -1, keepdims=True))

    @pl.when(t == 0)
    def _():
        r.dpool[...] = dpool

    @pl.when(t == 1)
    def _():
        r.dpool[...] = jnp.broadcast_to(dpool[0:1, :], (8, D))

    def norm_two_back(b, sums):
        part = pl.ds(aligned(b * quarter, quarter), quarter)
        top = r.pw[part, :] * r.dpool[pl.ds(b, 1), :]
        hat = r.xh2[part, :]
        inner = top * r.vec[2:3, :]
        grad = r.rs2[part, :] * (
            inner - jnp.mean(inner, -1, keepdims=True)
            - hat * jnp.mean(inner * hat, -1, keepdims=True))
        r.n1[part, :] = grad
        r.dbr[pl.ds(aligned(t * count + b * quarter, quarter), quarter), :] = (
            grad.astype(BF))
        return (sums[0] + jnp.sum(top * hat, 0, keepdims=True),
                sums[1] + jnp.sum(top, 0, keepdims=True))

    zero_row = jnp.zeros((1, D), F32)
    gain_two, bias_two = lax.fori_loop(0, blocks, norm_two_back, (zero_row, zero_row))
    swap_rows(2, r.dbr.at[mine], r.dbr.at[mine])

    send(t == 0, copy(r.embq, r.qrecv, r.s_query.at[0], r.r_query.at[0], dev_y), tail)
    r.ln[0] = (r.ln[0] + jnp.where(row8 == 2, gain_two, 0.0)
               + jnp.where(row8 == 3, bias_two, 0.0))

    def hidden_back(rows_of):
        def body(j, carry):
            o = aligned(j * stripe, LANES)
            w = wd[j].reshape(stripe, D)
            slope = dot_tt(r.dbr[rows_of, :], w)
            gate = r.gate[rows_of, pl.ds(o, stripe)]
            up = r.up[rows_of, pl.ds(o, stripe)]
            sig = jax.nn.sigmoid(gate)
            w_at = aligned((2 * (j // per_part)) * part_ff + (j % per_part) * stripe, LANES)
            r.dgu[rows_of, pl.ds(w_at, stripe)] = (
                slope * up * (sig * (1.0 + gate * (1.0 - sig)))).astype(BF)
            r.dgu[rows_of, pl.ds(aligned(w_at + part_ff, LANES), stripe)] = (slope * (gate * sig)).astype(BF)
            return carry

        lax.fori_loop(0, line, body, 0)

    def along(step):
        for s in range(1, line):
            yield line - s, both(z == step, z < line - s), z + 1, 0
        for s in range(line - 1):
            yield s, both(z == line - 1 - step, z > s), z - 1, 1

    def added(refs):
        total = refs[0][...].astype(F32)
        for ref in refs[1:]:
            total = total + ref[...].astype(F32)
        return total

    def line_step(step, parts, sem, slot, nth):
        for k, (dest, cond, nxt, way) in enumerate(along(step)):
            if k % (line - 1) != nth:
                continue
            into = slot(dest + 1 if way == 0 else dest)
            refs = parts(dest)

            def move(into=into, refs=refs, dest=dest, way=way):
                if step:
                    copy(into, into, r.s_query.at[0], sem(1, way, dest), dev_x).wait_recv()
                    refs[0][...] = added(refs + (into,)).astype(BF)
                else:
                    refs[0][...] = added(refs).astype(BF)

            do(cond, move)
            send(cond, copy(refs[0], into, sem(0, way, dest), sem(1, way, dest),
                            dev_z(nxt)), tail)

    def line_end(parts, sem, slot, put):
        for cond, ways in ((z == 0, (1,)), (z == line - 1, (0,)),
                           (both(z > 0, z < line - 1), (0, 1))):
            def finish(ways=ways):
                refs = parts(z)
                for way in ways:
                    into = slot(z + 1 if way == 0 else z)
                    copy(into, into, r.s_query.at[0], sem(1, way, z), dev_x).wait_recv()
                    refs = refs + (into,)
                put[...] = added(refs).astype(BF)

            do(cond, finish)

    gd = r.gd

    def down_half(s, rows_of):
        return jnp.dot(r.hidt[pl.ds(s * stripe, stripe), rows_of], r.dbr[rows_of, :],
                       preferred_element_type=F32)

    def down_own(s):
        gd[s] = down_half(s, mine).astype(BF).reshape(2, shard_ff, D)

    def down_grad(s):
        val = down_half(s, theirs) + gd[s].reshape(stripe, D).astype(F32)
        gd[s] = val.astype(BF).reshape(2, shard_ff, D)
        send(None, copy(gd.at[s, 1 - c], r.gd_rc.at[s], r.gd_c.at[0, s],
                        r.gd_c.at[1, s], dev_c), tail)

    def down_parts(dest):
        return gd.at[dest, c], r.gd_rc.at[dest]

    def down_arrive():
        for s in range(line):
            got(None, r.gd_rc.at[s], r.gd_c.at[1, s])

    def down_line(step, nth):
        line_step(step, down_parts, lambda *i: r.gd_z.at[i], lambda k: r.gd_rz.at[k], nth)

    def down_end():
        line_end(down_parts, lambda *i: r.gd_z.at[i], lambda k: r.gd_rz.at[k], r.gd_f)
        send(x != t, copy(r.gd_f, r.gd_rx, r.gd_x.at[0], r.gd_x.at[1], dev_x), tail)

    out_copies = []

    def keep_out(k, src, dst, cond=None):
        what = pltpu.make_async_copy(src, dst, r.fin.at[k])
        do(cond, what.start)
        out_copies.append((cond, what))

    def down_out():
        def total():
            copy(r.gd_rx, r.gd_rx, r.s_query.at[0], r.gd_x.at[1], dev_x).wait_recv()
            r.gd_f[...] = added((r.gd_f, r.gd_rx)).astype(BF)

        do(x == t, total)
        keep_out(0, r.gd_f, r.o_dn, x == t)
        send(x == t, copy(r.gd_f, r.o_dn, r.gd_y.at[0], r.gd_y.at[1], dev_y), tail)

    gg = r.gg
    part_gu = ff // 4

    def gate_half(k, rows_of):
        return jnp.dot(r.feedt[:, rows_of], r.dgu[rows_of, pl.ds(k * part_gu, part_gu)],
                       preferred_element_type=F32)

    def gate_own(k):
        gg[:, :, :, :, pl.ds(k * part_gu, part_gu)] = gate_half(k, mine).astype(BF).reshape(
            line, 2, 2, shard, part_gu)

    def gate_grad(k):
        span = pl.ds(k * part_gu, part_gu)
        val = gate_half(k, theirs) + gg[:, :, :, :, span].reshape(groups * shard, part_gu).astype(F32)
        gg[:, :, :, :, span] = val.astype(BF).reshape(line, 2, 2, shard, part_gu)
        send(None, copy(gg.at[:, :, 1 - c, :, span], r.gg_rc.at[:, :, :, span],
                        r.gg_c.at[0, k], r.gg_c.at[1, k], dev_c), tail)

    def gate_cross(k):
        span = pl.ds(k * part_gu, part_gu)
        got(None, r.gg_rc.at[:, :, :, span], r.gg_c.at[1, k])
        for s in range(line):
            mine_k = gg.at[s, 1 - x, c, :, span]
            mine_k[...] = added((mine_k, r.gg_rc.at[s, 1 - x, :, span])).astype(BF)
        send(None, copy(gg.at[:, 1 - x, c, :, span], r.gg_rx.at[:, :, span],
                        r.gg_x.at[0, k], r.gg_x.at[1, k], dev_x), tail)

    def gate_parts(k):
        span = pl.ds(k * part_gu, part_gu)
        return lambda dest: (gg.at[dest, x, c, :, span], r.gg_rc.at[dest, x, :, span],
                             r.gg_rx.at[dest, :, span])

    def gate_ready(k):
        span = pl.ds(k * part_gu, part_gu)
        got(None, r.gg_rx.at[:, :, span], r.gg_x.at[1, k])

    def gate_line(k, step, nth):
        span = pl.ds(k * part_gu, part_gu)
        line_step(step, gate_parts(k), lambda a, *i: r.gg_z.at[(a, k) + i],
                  lambda s: r.gg_rz.at[s, :, span], nth)

    def gate_end(k):
        span = pl.ds(k * part_gu, part_gu)
        line_end(gate_parts(k), lambda a, *i: r.gg_z.at[(a, k) + i], lambda s: r.gg_rz.at[s, :, span],
                 r.gg_f.at[:, span])
        keep_out(1 + k, r.gg_f.at[:, span], r.o_gu.at[t, :, span])
        send(None, copy(r.gg_f.at[:, span], r.o_gu.at[t, :, span], r.gg_y.at[0, k],
                        r.gg_y.at[1, k], dev_y), tail)

    ga = wg
    sizes = (3 * LANES, 3 * LANES, 3 * LANES, out_w)
    starts = (0, 3 * LANES, 6 * LANES, third)

    def cols_a(k, h):
        return pl.ds(aligned(h * half_a + starts[k], LANES), sizes[k])

    def store_a(k, h, left, right):
        val = jnp.dot(left[...], right, preferred_element_type=F32)
        ga[:, :, :, :, cols_a(k, h)] = val.astype(BF).reshape(line, 2, 2, shard, sizes[k])
        send(None, copy(ga.at[:, :, 1 - c, :, cols_a(k, h)],
                        r.ga_rc.at[:, :, :, cols_a(k, h)],
                        r.ga_c.at[0, h, k], r.ga_c.at[1, h, k], dev_c), tail)

    def store_qkv(k, h):
        store_a(k, h, r.tokt, dqkv[:, pl.ds(aligned(h * third + starts[k], LANES), sizes[k])])

    def span_a(k):
        return pl.ds(starts[k], sizes[k])

    def tower_a(k):
        gone = cols_a(k, 1 - t)
        got(None, r.ga_rc.at[:, :, :, gone], r.ga_c.at[1, 1 - t, k])
        for s in range(line):
            for xx in range(2):
                ref = ga.at[s, xx, c, :, gone]
                ref[...] = added((ref, r.ga_rc.at[s, xx, :, gone])).astype(BF)
        send(None, copy(ga.at[:, :, c, :, gone], r.ga_rt.at[:, :, :, span_a(k)],
                        r.ga_t.at[0, k], r.ga_t.at[1, k], dev_y), tail)

    def cross_a(k):
        got(None, r.ga_rt.at[:, :, :, span_a(k)], r.ga_t.at[1, k])
        here = cols_a(k, t)
        got(None, r.ga_rc.at[:, :, :, here], r.ga_c.at[1, t, k])
        for s in range(line):
            ref = ga.at[s, 1 - x, c, :, here]
            ref[...] = added((ref, r.ga_rc.at[s, 1 - x, :, here],
                              r.ga_rt.at[s, 1 - x, :, span_a(k)])).astype(BF)
        send(None, copy(ga.at[:, 1 - x, c, :, here], r.ga_rx.at[:, :, span_a(k)],
                        r.ga_x.at[0, k], r.ga_x.at[1, k], dev_x), tail)

    def parts_a(k):
        here = cols_a(k, t)
        return lambda dest: (ga.at[dest, x, c, :, here], r.ga_rc.at[dest, x, :, here],
                             r.ga_rt.at[dest, x, :, span_a(k)],
                             r.ga_rx.at[dest, :, span_a(k)])

    def ready_a(k):
        got(None, r.ga_rx.at[:, :, span_a(k)], r.ga_x.at[1, k])

    def line_a(k, step, nth):
        line_step(step, parts_a(k), lambda a, *i: r.ga_z.at[(a, k) + i],
                  lambda s: r.ga_rz.at[s, :, span_a(k)], nth)

    def end_a(k):
        line_end(parts_a(k), lambda a, *i: r.ga_z.at[(a, k) + i], lambda s: r.ga_rz.at[s, :, span_a(k)],
                 r.ga_f.at[:, span_a(k)])
        keep_out(5 + k, r.ga_f.at[:, span_a(k)], r.o_a.at[:, cols_a(k, t)])
        send(None, copy(r.ga_f.at[:, span_a(k)], r.o_a.at[:, cols_a(k, t)],
                        r.ga_y.at[0, k], r.ga_y.at[1, k], dev_y), tail)

    some = 2 * 4 * shard

    def rows_of_weight(ref, j, lo, n):
        return ref[pl.ds(2 * j, 2), :, :, :, pl.ds(lo, n)].reshape(some, n)

    def feed_part(rows_of, j, store):
        store(j, pl.ds(j * some, some), dot_tt(r.dgu[rows_of, :], rows_of_weight(wg, j, 0, ff)))

    def back_send(j, span, val):
        r.dsend[:, span] = val.astype(BF)
        send(None, copy(r.dsend.at[:, span], r.drecv.at[:, span], r.s_back.at[j], r.r_back.at[j],
                        dev_y), tail)

    def back_own(j, span, val):
        r.bown[:, span] = val

    hidden_back(mine)
    for j in range(line // 2):
        feed_part(mine, j, back_own)
    for s in range(line):
        down_own(s)
    for k in range(4):
        gate_own(k)
    got_rows(2, r.dbr.at[theirs])
    def norm_one_back(b, sums):
        part = pl.ds(aligned(b * quarter, quarter), quarter)
        top = r.n1[part, :] + r.bown[part, :] + r.drecv[part, :].astype(F32)
        hat = r.h1[part, :]
        inner = top * r.vec[0:1, :]
        grad = r.rs1[part, :] * (
            inner - jnp.mean(inner, -1, keepdims=True)
            - hat * jnp.mean(inner * hat, -1, keepdims=True))
        r.n1[part, :] = grad
        r.datt[part, :] = grad.astype(BF)
        return (sums[0] + jnp.sum(top * hat, 0, keepdims=True),
                sums[1] + jnp.sum(top, 0, keepdims=True))

    def norm_back():
        for j in range(line // 2):
            got(None, r.drecv.at[:, pl.ds(j * some, some)], r.r_back.at[j])
        gain_one, bias_one = lax.fori_loop(0, blocks, norm_one_back, (zero_row, zero_row))
        r.ln[0] = (r.ln[0] + jnp.where(row8 == 0, gain_one, 0.0)
                   + jnp.where(row8 == 1, bias_one, 0.0))

    ln_peers = [dev_y, dev_c, dev_x]
    for bit in range(line.bit_length() - 1):
        apart = 1 << bit
        ln_peers.append(dev_z(z + apart * (1 - 2 * ((z // apart) % 2))))
    last = len(ln_peers)

    def small_sums(k):
        if k:
            got(None, r.lnr.at[k - 1], r.r_ln.at[k - 1])
            r.ln[k] = r.ln[k - 1] + r.lnr[k - 1]
        if k < last:
            send(None, copy(r.ln.at[k], r.lnr.at[k], r.s_ln.at[k], r.r_ln.at[k],
                            ln_peers[k]), tail)

    def out_grad():
        for h in range(2):
            store_a(3, h, r.mixt, r.datt[:, pl.ds(h * out_w, out_w)])

    def mix_back():
        lax.fori_loop(0, line // 2, mixed_back, 0)

    dqkv = r.dgu.at[pl.ds(0, count), pl.ds(0, 3 * D)]
    dmix = r.dgu.at[pl.ds(count, count), pl.ds(0, D)]

    def mixed_back(j, carry):
        val = sum(dot_tt(r.datt[:, pl.ds(h * out_w, out_w)],
                         rows_of_weight(wa, j, h * half_a + third, out_w)) for h in range(2))
        dmix[:, pl.ds(aligned(j * some, LANES), some)] = val.astype(BF)
        return carry

    def attend_back(p):
        q2, k2, v2 = triple(p)
        o = aligned(p * LANES, LANES)
        dm2 = dmix[:, pl.ds(o, LANES)]
        parts = []
        for h in range(2):
            probs = r.probs[2 * p + h]
            dprobs = dot_tt(only(h, dm2), v2)
            mean = jnp.sum(probs * dprobs, -1, keepdims=True)
            dscores = (probs * (dprobs - mean)).astype(BF)
            parts.append((jnp.dot(dscores, k2, preferred_element_type=F32),
                          dot_t0(dscores, q2), dot_t0(probs.astype(BF), dm2)))
        dq, dk, dv = (jnp.where(first_head, a, b) for a, b in zip(*parts))
        half = p // half_pairs
        o = half * third + (p - half * half_pairs) * LANES
        for k, part in enumerate((turn_back(dq * scale), turn_back(dk), dv)):
            dqkv[:, pl.ds(aligned(o + k * half_d, LANES), LANES)] = part.astype(BF)

    def token_back(j, carry):
        val = sum(dot_tt(dqkv[:, pl.ds(h * third, third)],
                         rows_of_weight(wa, j, h * half_a, third)) for h in range(2))
        span = pl.ds(aligned(j * some, LANES), some)
        r.xh2[:, span] = r.n1[:, span] + val
        return carry

    hidden_back(theirs)
    gate_grad(0)
    feed_part(theirs, 0, back_send)
    down_grad(3)
    down_grad(0)
    down_grad(1)
    gate_cross(0)
    down_grad(2)
    feed_part(theirs, 1, back_send)
    down_arrive()
    down_line(0, 0)
    gate_grad(1)
    gate_cross(1)
    gate_grad(3)
    gate_grad(2)
    down_line(0, 1)
    norm_back()
    settle(pending)
    out_grad()
    small_sums(0)
    gate_cross(2)
    mix_back()
    over_pairs(1 - t, attend_back, 0, 2)
    gate_ready(0)
    tower_a(3)
    over_pairs(1 - t, attend_back, 2, 3)
    gate_ready(1)
    gate_line(0, 0, 1)
    down_line(1, 0)
    gate_cross(3)
    store_qkv(0, 1 - t)
    gate_line(0, 0, 0)
    gate_line(0, 0, 2)
    store_qkv(2, 1 - t)
    gate_line(1, 0, 0)
    store_qkv(1, 1 - t)
    over_pairs(t, attend_back, 0, 1)
    down_line(1, 1)
    down_line(0, 2)
    over_pairs(t, attend_back, 1, 2)
    tower_a(0)
    down_line(2, 0)
    over_pairs(t, attend_back, 2, 3)
    tower_a(2)
    store_qkv(0, t)
    gate_ready(2)
    store_qkv(2, t)
    cross_a(3)
    store_qkv(1, t)
    gate_line(2, 0, 1)
    gate_line(1, 0, 2)
    gate_ready(3)
    gate_line(0, 1, 0)
    tower_a(1)
    cross_a(0)
    down_end()
    ready_a(3)
    gate_line(2, 0, 0)
    gate_line(1, 1, 0)
    gate_line(3, 0, 0)
    gate_line(0, 1, 1)
    line_a(3, 0, 1)
    line_a(3, 0, 0)
    gate_line(3, 0, 1)
    gate_line(2, 1, 1)
    gate_line(0, 2, 0)
    gate_line(1, 0, 1)
    lax.fori_loop(0, line // 2, token_back, 0)
    keep_out(9, r.xh2, r.o_tok)
    gate_line(3, 1, 0)
    gate_end(0)
    ready_a(0)
    small_sums(1)
    gate_line(2, 1, 0)
    line_a(0, 0, 0)
    cross_a(2)
    gate_line(3, 0, 2)
    down_out()
    cross_a(1)
    gate_line(3, 2, 0)
    gate_line(2, 2, 0)
    gate_line(1, 1, 1)
    gate_line(1, 2, 0)
    gate_line(2, 0, 2)
    line_a(0, 1, 0)
    ready_a(2)
    line_a(3, 1, 0)
    line_a(2, 0, 0)
    line_a(2, 0, 1)
    line_a(0, 0, 1)
    small_sums(2)
    line_a(3, 1, 1)
    line_a(2, 1, 0)
    ready_a(1)
    gate_line(3, 1, 1)
    line_a(1, 0, 0)
    line_a(1, 0, 1)
    line_a(3, 0, 2)
    gate_end(2)
    line_a(3, 2, 0)
    line_a(0, 1, 1)
    gate_end(1)
    line_a(1, 1, 0)
    line_a(0, 0, 2)
    line_a(2, 0, 2)
    line_a(0, 2, 0)
    line_a(2, 1, 1)
    gate_end(3)
    line_a(1, 0, 2)
    line_a(1, 1, 1)
    line_a(2, 2, 0)
    small_sums(3)
    end_a(3)
    line_a(1, 2, 0)
    end_a(0)
    end_a(2)
    small_sums(4)
    end_a(1)
    small_sums(5)

    r.o_vec[...] = r.ln[last]
    r.o_loss[...] = r.ln[last][:, 0:LANES] * (1.0 / (groups * QPD))

    r.o_d[...] = r.dbuf[me]

    def sent(ssem):
        def body(j, carry):
            copy(r.embd, r.embd, ssem.at[j], r.r_query.at[0], dev_x).wait_send()
            return carry

        lax.fori_loop(0, groups, body, 0)

    @pl.when(t == 0)
    def _():
        r.o_q[...] = r.embq[...]
        sent(r.s_slope)

    @pl.when(t == 1)
    def _():
        got(None, r.qrecv, r.r_query.at[0])
        r.o_q[...] = r.qrecv[...]
        sent(r.s_doc)

    got(x != t, r.o_dn, r.gd_y.at[1])
    for k in range(4):
        got(None, r.o_gu.at[1 - t, :, pl.ds(k * part_gu, part_gu)], r.gg_y.at[1, k])
        got(None, r.o_a.at[:, cols_a(k, 1 - t)], r.ga_y.at[1, k])
    for cond, what in out_copies:
        do(cond, what.wait)
    settle(tail)


def finish(plan, *refs):
    (a_ref, gu_ref, dn_ref, vec_ref, tok_ref, q_ref, d_ref, loss_ref,
     o_loss, o_q, o_d, o_tok, o_qkv, o_out, o_gate, o_up, o_down, *o_vecs) = refs
    third, half_a, half_ff, stripe = 3 * D // 2, plan.half_a, plan.half_ff, plan.stripe
    out_w = half_a - third
    for h in range(2):
        for k in range(3):
            o_qkv[:, pl.ds(k * D + h * (D // 2), D // 2)] = (
                a_ref[:, pl.ds(h * half_a + k * (D // 2), D // 2)].astype(F32))
        o_out[:, h * out_w : (h + 1) * out_w] = (
            a_ref[:, h * half_a + third : (h + 1) * half_a].astype(F32))
        for s in range(plan.line):
            to = pl.ds((2 * s + h) * stripe, stripe)
            per_part, part_ff = plan.line // 2, half_ff // 2
            lo = 2 * (s // per_part) * part_ff + (s % per_part) * stripe
            o_gate[:, to] = gu_ref[h, :, pl.ds(lo, stripe)].astype(F32)
            o_up[:, to] = gu_ref[h, :, pl.ds(lo + part_ff, stripe)].astype(F32)
    o_down[...] = dn_ref[...].astype(F32)
    o_tok[0] = tok_ref[...]
    o_q[...] = q_ref[...]
    o_d[...] = d_ref[...]
    o_loss[...] = loss_ref[4:5, 0:1]
    first = lax.axis_index(DP) * plan.vec
    row = lax.broadcasted_iota(jnp.int32, (D, LANES), 0)
    col = lax.broadcasted_iota(jnp.int32, (D, LANES), 1)
    pick = jnp.where(row == first + col, 1.0, 0.0)
    own = jnp.dot(vec_ref[...], pick, preferred_element_type=F32, precision=exact_product_accuracy)
    for k, out in enumerate(o_vecs):
        out[...] = own[k : k + 1, 0 : plan.vec]


def on_device_kernel(plan, tokens, query_lengths, doc_lengths, positives, w_qkv, w_out, w_gate,
                     w_up, w_down, ln1_gain, first_layernorm_shift, ln2_gain, ln2_bias):
    count, groups, shard, vec = plan.count, plan.groups, plan.shard, plan.vec
    cosines, sines = rotary_constants(count)
    vmem = pl.BlockSpec(memory_space=pltpu.VMEM)
    smem = pl.BlockSpec(memory_space=pltpu.SMEM)
    hbm = pl.BlockSpec(memory_space=pl.ANY)
    shape = jax.ShapeDtypeStruct
    made = pl.pallas_call(
        functools.partial(whole_step, plan),
        out_shape=(
            shape((count, D), F32), shape((shard, plan.width_a), BF), shape((2, shard, plan.ff), BF),
            shape((plan.shard_ff, D), BF), shape((8, D), F32), shape((QPD, D), F32),
            shape((1, D), F32), shape((8, LANES), F32),
        ),
        in_specs=[smem] * 3 + [hbm] * 3 + [vmem] * 4 + [hbm] * 5,
        out_specs=(hbm, hbm, hbm, hbm, vmem, vmem, vmem, vmem),
        scratch_shapes=list(buffers(plan).values()) + list(semaphores(plan).values()),
        compiler_params=pltpu.CompilerParams(
            collective_id=0, has_side_effects=True, vmem_limit_bytes=63 * 1000 * 1000),
        name="whole_step",
    )(query_lengths, doc_lengths, positives, tokens[0], cosines, sines, ln1_gain[None],
      first_layernorm_shift[None], ln2_gain[None], ln2_bias[None],
      w_qkv, w_out, w_gate, w_up, w_down)
    o_tok, o_a, o_gu, o_dn, o_vec, o_q, o_d, o_loss = made
    outs = pl.pallas_call(
        functools.partial(finish, plan),
        out_shape=(
            shape((1, 1), F32), shape((QPD, D), F32), shape((1, D), F32),
            shape((1, count, D), F32), shape((shard, 3 * D), F32), shape((shard, D), F32),
            shape((shard, plan.ff), F32), shape((shard, plan.ff), F32),
            shape((plan.shard_ff, D), F32),
        ) + (shape((1, vec), F32),) * 4,
        in_specs=[vmem] * 8,
        out_specs=[vmem] * 13,
        name="finish",
    )(o_a, o_gu, o_dn, o_vec, o_tok, o_q, o_d, o_loss)
    return (outs[0].reshape(()),) + tuple(outs[1:9]) + tuple(v.reshape(vec) for v in outs[9:])


def fits(plan, towers):
    line = plan.line
    return (towers == 2 and plan.groups % 4 == 0 and line == 4
            and plan.shard % 16 == 0 and plan.shard_ff % 16 == 0 and plan.stripe % LANES == 0
            and plan.count == QPD * QLEN)


def solution(mesh):
    groups = mesh.shape[DP]

    def local_step(*args):
        plan = Plan(groups, args[0].shape[1], args[4].shape[0], args[8].shape[0], args[9].shape[0])
        if fits(plan, mesh.shape[TOWER]):
            return on_device_kernel(plan, *args)
        return on_device(*args)

    return jax.shard_map(
        local_step,
        mesh=mesh,
        in_specs=(
            P(TOWER, DP, None),
            P(DP),
            P(DP),
            P(),
            P(DP, None),
            P(DP, None),
            P(DP, None),
            P(DP, None),
            P(DP, None),
            P(DP),
            P(DP),
            P(DP),
            P(DP),
        ),
        out_specs=(
            P(),
            P(DP, None),
            P(DP, None),
            P(TOWER, DP, None),
            P(DP, None),
            P(DP, None),
            P(DP, None),
            P(DP, None),
            P(DP, None),
            P(DP),
            P(DP),
            P(DP),
            P(DP),
        ),
        check_vma=False,
    )
```

```python
import functools
from types import SimpleNamespace
from typing import Any, NamedTuple

import jax
import jax.numpy as jnp
import numpy as np
from jax import lax
from jax.experimental import pallas as pl
from jax.experimental.pallas import tpu as pltpu
from jax.sharding import PartitionSpec as P

TOWER = "tower"
DP = "dp"
D = 768
HEADS = 12
HEAD = 64
QLEN = 64
QPD = 4


exact_product_accuracy = lax.Precision.HIGHEST
rope_base = 1000.0
contrast_sharpness_factor = 0.02


def product(left, right):
    return jnp.dot(left, right, preferred_element_type=jnp.float32)


def rotary_tables(places):
    freqs = jnp.power(rope_base, -2.0 * jnp.arange(HEAD // 2).astype(jnp.float32) / HEAD)
    angles = places[:, None] * freqs[None, :]
    return (jnp.cos(angles)[:, None, :], jnp.sin(angles)[:, None, :])


def rotate(values, cosines, sines):
    half_dim = values.shape[-1] // 2
    first = values[..., :half_dim]
    second = values[..., half_dim:]
    return jnp.concatenate(
        [first * cosines - second * sines, second * cosines + first * sines], axis=-1
    )


def layer_norm(hidden, gain, offset):
    average = jnp.mean(hidden, -1, keepdims=True)
    centred = hidden - average
    variance = jnp.mean(centred * centred, -1, keepdims=True)
    return centred * lax.rsqrt(variance + 1e-05) * gain + offset


def normalize(pooled):
    return pooled * lax.rsqrt(jnp.sum(pooled * pooled, -1, keepdims=True) + 1e-06)


def layout(tower_id, query_len, doc_len, count):
    places = jnp.arange(count)
    span = jnp.where(tower_id == 0, QLEN, count)
    segment = places // span
    offset_in = places - segment * span
    slots = jnp.arange(QPD)
    seg_limit = jnp.where(tower_id == 0, query_len, doc_len[0] * jnp.ones_like(query_len))
    limit = jnp.sum(jnp.where(segment[:, None] == slots[None, :], seg_limit[None, :], 0), axis=1)
    valid = offset_in < limit
    allowed = (segment[:, None] == segment[None, :]) & valid[None, :]
    member = (segment[None, :] == slots[:, None]) & valid[None, :]
    pool_matrix = jnp.where(member, 1.0 / seg_limit[:, None].astype(jnp.float32), 0.0)
    return (offset_in.astype(jnp.float32), allowed, pool_matrix)


def swish_product(left, right):
    return jax.nn.silu(left) * right


def on_device(
    tokens,
    query_lengths,
    doc_lengths,
    positives,
    w_qkv,
    w_out,
    w_gate,
    w_up,
    w_down,
    ln1_gain,
    first_layernorm_shift,
    ln2_gain,
    ln2_bias,
):
    tower_id = lax.axis_index(TOWER)
    device_id = lax.axis_index(DP)
    groups = lax.axis_size(DP)
    full = (
        lax.all_gather(w_qkv, DP, axis=0, tiled=True),
        lax.all_gather(w_out, DP, axis=0, tiled=True),
        lax.all_gather(w_gate, DP, axis=0, tiled=True),
        lax.all_gather(w_up, DP, axis=0, tiled=True),
        lax.all_gather(w_down, DP, axis=0, tiled=True),
        lax.all_gather(ln1_gain, DP, axis=0, tiled=True),
        lax.all_gather(first_layernorm_shift, DP, axis=0, tiled=True),
        lax.all_gather(ln2_gain, DP, axis=0, tiled=True),
        lax.all_gather(ln2_bias, DP, axis=0, tiled=True),
    )
    qkv_full, out_full, gate_full, up_full, down_full = (
        full[0],
        full[1],
        full[2],
        full[3],
        full[4],
    )
    gain_one = full[5].astype(jnp.float32)
    bias_one = full[6].astype(jnp.float32)
    gain_two = full[7].astype(jnp.float32)
    bias_two = full[8].astype(jnp.float32)
    inputs = tokens[0]
    count = inputs.shape[0]
    places, allowed, pool_matrix = layout(tower_id, query_lengths, doc_lengths, count)
    cosines, sines = rotary_tables(places)
    packed = product(inputs, qkv_full)
    raw_query = packed[:, :D].reshape(count, HEADS, HEAD)
    raw_key = packed[:, D : 2 * D].reshape(count, HEADS, HEAD)

    def rotate_both(first, second):
        return (rotate(first, cosines, sines), rotate(second, cosines, sines))

    rotated, rotary_back = jax.vjp(rotate_both, raw_query, raw_key)
    query_low = rotated[0].astype(jnp.bfloat16)
    key_low = rotated[1].astype(jnp.bfloat16)
    value_low = packed[:, 2 * D :].reshape(count, HEADS, HEAD).astype(jnp.bfloat16)
    scale = HEAD ** (-0.5)

    def masked_scores():
        scores = (
            jnp.einsum("ihd,jhd->hij", query_low, key_low, preferred_element_type=jnp.float32)
            * scale
        )
        return jnp.where(allowed[None], scores, -1e30)

    scores = masked_scores()
    peak = jnp.max(scores, -1, keepdims=True)
    log_total = peak + jnp.log(jnp.sum(jnp.exp(scores - peak), -1, keepdims=True))
    probs_low = jnp.exp(scores - log_total).astype(jnp.bfloat16)
    mixed = jnp.einsum("hij,jhd->ihd", probs_low, value_low, preferred_element_type=jnp.float32)
    mixed_low = mixed.reshape(count, D).astype(jnp.bfloat16)
    attended = product(mixed_low, out_full)
    inputs_wide = inputs.astype(jnp.float32)
    normed_one, norm_one_back = jax.vjp(layer_norm, inputs_wide + attended, gain_one, bias_one)
    feed = normed_one.astype(jnp.bfloat16)
    gate = product(feed, gate_full)
    up_part = product(feed, up_full)
    hidden_wide, swish_back = jax.vjp(swish_product, gate, up_part)
    hidden = hidden_wide.astype(jnp.bfloat16)
    branch = product(hidden, down_full)
    normed_two, norm_two_back = jax.vjp(layer_norm, normed_one + branch, gain_two, bias_two)
    pooled = jnp.dot(pool_matrix, normed_two, precision=exact_product_accuracy)
    embedded, normal_back = jax.vjp(normalize, pooled)
    gathered = lax.all_gather(embedded, (TOWER, DP), axis=0, tiled=True)
    queries_total = groups * QPD
    gathered_query_rows = gathered[:queries_total]
    gathered_document_rows = gathered[queries_total:].reshape(groups, QPD, D)[:, 0]
    pairwise_affinity_matrix = (
        jnp.dot(gathered_query_rows, gathered_document_rows.T, precision=exact_product_accuracy)
        / contrast_sharpness_factor
    )
    peak_logit = jnp.max(pairwise_affinity_matrix, -1, keepdims=True)
    log_partition_norm = peak_logit + jnp.log(
        jnp.sum(jnp.exp(pairwise_affinity_matrix - peak_logit), -1, keepdims=True)
    )
    columns = lax.broadcasted_iota(jnp.int32, pairwise_affinity_matrix.shape, 1)
    matching_labels = columns == positives[:, None]
    picked = jnp.sum(jnp.where(matching_labels, pairwise_affinity_matrix, 0.0), -1, keepdims=True)
    total = jnp.sum(log_partition_norm - picked)
    loss = total / queries_total
    similarity_gradient = (
        jnp.exp(pairwise_affinity_matrix - log_partition_norm) - matching_labels.astype(jnp.float32)
    ) / contrast_sharpness_factor
    own_rows = lax.dynamic_slice_in_dim(similarity_gradient, device_id * QPD, QPD, 0)
    query_side = jnp.dot(own_rows, gathered_document_rows, precision=exact_product_accuracy)
    own_column = lax.dynamic_slice_in_dim(similarity_gradient, device_id, 1, 1)
    doc_side = jnp.dot(own_column.T, gathered_query_rows, precision=exact_product_accuracy)
    doc_side = jnp.concatenate([doc_side, jnp.zeros((QPD - 1, D), jnp.float32)], 0)
    embed_grad = jnp.where(tower_id == 0, query_side, doc_side)
    pooled_grad = normal_back(embed_grad)[0]
    top_grad = jnp.dot(pool_matrix.T, pooled_grad, precision=exact_product_accuracy)
    sum_two, gain_two_grad, bias_two_grad = norm_two_back(top_grad)
    attention_input_cotangent, out_back, gate_back, up_back, down_back = (
        qkv_full,
        out_full,
        gate_full,
        up_full,
        down_full,
    )
    branch_low = sum_two.astype(jnp.bfloat16)
    down_grad = product(hidden.T, branch_low)
    hidden_grad = product(branch_low, down_back.T)
    gate_grad_wide, up_grad_wide = swish_back(hidden_grad)
    gate_low = gate_grad_wide.astype(jnp.bfloat16)
    up_low = up_grad_wide.astype(jnp.bfloat16)
    gate_weight_grad = product(feed.T, gate_low)
    up_weight_grad = product(feed.T, up_low)
    feed_grad = sum_two + product(gate_low, gate_back.T) + product(up_low, up_back.T)
    sum_one, gain_one_grad, bias_one_grad = norm_one_back(feed_grad)
    attend_low = sum_one.astype(jnp.bfloat16)
    out_grad = product(mixed_low.T, attend_low)
    mixed_grad = product(attend_low, out_back.T).astype(jnp.bfloat16).reshape(count, HEADS, HEAD)
    probs_again = jnp.exp(masked_scores() - log_total)
    prob_grad = jnp.einsum(
        "ihd,jhd->hij", mixed_grad, value_low, preferred_element_type=jnp.float32
    )
    score_grad = probs_again * (prob_grad - jnp.sum(probs_again * prob_grad, -1, keepdims=True))
    score_low = score_grad.astype(jnp.bfloat16)
    query_grad = (
        jnp.einsum("hij,jhd->ihd", score_low, key_low, preferred_element_type=jnp.float32) * scale
    )
    key_grad = (
        jnp.einsum("hij,ihd->jhd", score_low, query_low, preferred_element_type=jnp.float32) * scale
    )
    value_grad = jnp.einsum(
        "hij,ihd->jhd",
        probs_again.astype(jnp.bfloat16),
        mixed_grad,
        preferred_element_type=jnp.float32,
    )
    raw_query_grad, raw_key_grad = rotary_back((query_grad, key_grad))
    packed_grad = jnp.concatenate(
        [
            raw_query_grad.reshape(count, D),
            raw_key_grad.reshape(count, D),
            value_grad.reshape(count, D),
        ],
        1,
    ).astype(jnp.bfloat16)
    qkv_grad = product(inputs.T, packed_grad)
    input_grad = sum_one + product(packed_grad, attention_input_cotangent.T)
    gradients = (
        qkv_grad,
        out_grad,
        gate_weight_grad,
        up_weight_grad,
        down_grad,
        gain_one_grad,
        bias_one_grad,
        gain_two_grad,
        bias_two_grad,
    )
    partial_sums = (
        lax.psum_scatter(gradients[0], DP, scatter_dimension=0, tiled=True),
        lax.psum_scatter(gradients[1], DP, scatter_dimension=0, tiled=True),
        lax.psum_scatter(gradients[2], DP, scatter_dimension=0, tiled=True),
        lax.psum_scatter(gradients[3], DP, scatter_dimension=0, tiled=True),
        lax.psum_scatter(gradients[4], DP, scatter_dimension=0, tiled=True),
        lax.psum_scatter(gradients[5], DP, scatter_dimension=0, tiled=True),
        lax.psum_scatter(gradients[6], DP, scatter_dimension=0, tiled=True),
        lax.psum_scatter(gradients[7], DP, scatter_dimension=0, tiled=True),
        lax.psum_scatter(gradients[8], DP, scatter_dimension=0, tiled=True),
    )
    tower_halves = (
        lax.psum_scatter(
            partial_sums[0].astype(jnp.bfloat16), TOWER, scatter_dimension=0, tiled=True
        ).astype(jnp.float32),
        lax.psum_scatter(
            partial_sums[1].astype(jnp.bfloat16), TOWER, scatter_dimension=0, tiled=True
        ).astype(jnp.float32),
        lax.psum_scatter(
            partial_sums[2].astype(jnp.bfloat16), TOWER, scatter_dimension=0, tiled=True
        ).astype(jnp.float32),
        lax.psum_scatter(
            partial_sums[3].astype(jnp.bfloat16), TOWER, scatter_dimension=0, tiled=True
        ).astype(jnp.float32),
        lax.psum_scatter(
            partial_sums[4].astype(jnp.bfloat16), TOWER, scatter_dimension=0, tiled=True
        ).astype(jnp.float32),
        lax.psum_scatter(
            partial_sums[5].astype(jnp.bfloat16), TOWER, scatter_dimension=0, tiled=True
        ).astype(jnp.float32),
        lax.psum_scatter(
            partial_sums[6].astype(jnp.bfloat16), TOWER, scatter_dimension=0, tiled=True
        ).astype(jnp.float32),
        lax.psum_scatter(
            partial_sums[7].astype(jnp.bfloat16), TOWER, scatter_dimension=0, tiled=True
        ).astype(jnp.float32),
        lax.psum_scatter(
            partial_sums[8].astype(jnp.bfloat16), TOWER, scatter_dimension=0, tiled=True
        ).astype(jnp.float32),
    )
    shares = (
        lax.all_gather(tower_halves[0].astype(jnp.bfloat16), TOWER, axis=0, tiled=True).astype(
            jnp.float32
        ),
        lax.all_gather(tower_halves[1].astype(jnp.bfloat16), TOWER, axis=0, tiled=True).astype(
            jnp.float32
        ),
        lax.all_gather(tower_halves[2].astype(jnp.bfloat16), TOWER, axis=0, tiled=True).astype(
            jnp.float32
        ),
        lax.all_gather(tower_halves[3].astype(jnp.bfloat16), TOWER, axis=0, tiled=True).astype(
            jnp.float32
        ),
        lax.all_gather(tower_halves[4].astype(jnp.bfloat16), TOWER, axis=0, tiled=True).astype(
            jnp.float32
        ),
        lax.all_gather(tower_halves[5].astype(jnp.bfloat16), TOWER, axis=0, tiled=True).astype(
            jnp.float32
        ),
        lax.all_gather(tower_halves[6].astype(jnp.bfloat16), TOWER, axis=0, tiled=True).astype(
            jnp.float32
        ),
        lax.all_gather(tower_halves[7].astype(jnp.bfloat16), TOWER, axis=0, tiled=True).astype(
            jnp.float32
        ),
        lax.all_gather(tower_halves[8].astype(jnp.bfloat16), TOWER, axis=0, tiled=True).astype(
            jnp.float32
        ),
    )
    query_rows = lax.dynamic_slice_in_dim(gathered_query_rows, device_id * QPD, QPD, 0)
    doc_row = lax.dynamic_slice_in_dim(gathered_document_rows, device_id, 1, 0)
    return (loss, query_rows, doc_row, input_grad[None]) + tuple(shares)


MESH = pl.DeviceIdType.MESH
BF = jnp.bfloat16
F32 = jnp.float32
LANES = 128


def dot_tt(left, right, precision=None):
    return lax.dot_general(
        left, right, (((1,), (1,)), ((), ())), preferred_element_type=F32, precision=precision
    )


def dot_t0(left, right, precision=None):
    return lax.dot_general(
        left, right, (((0,), (0,)), ((), ())), preferred_element_type=F32, precision=precision
    )


def rotary_constants(count):
    freqs = np.power(
        np.float32(rope_base), (-2.0 * np.arange(HEAD // 2) / HEAD).astype(np.float32)
    ).astype(np.float32)
    angles = (np.arange(count, dtype=np.float32)[:, None] * freqs[None, :]).astype(np.float64)
    cosines, sines = np.cos(angles), np.sin(angles)
    return (
        np.tile(np.concatenate([cosines, cosines], 1), (1, 2)).astype(np.float32),
        np.tile(np.concatenate([-sines, sines], 1), (1, 2)).astype(np.float32),
    )


def aligned(start, unit):
    return start if isinstance(start, int) else pl.multiple_of(start, unit)


def both(first, second):
    return jnp.logical_and(first, second)


def do(condition, action):
    if condition is None:
        action()
    else:
        pl.when(condition)(action)


class Plan:
    def __init__(self, groups, count, shard, shard_ff, vec):
        self.groups = groups
        self.line = groups // 4
        self.count = count
        self.shard = shard
        self.shard_ff = shard_ff
        self.vec = vec
        self.width_a = 4 * D
        self.half_a = 2 * D
        self.ff = shard_ff * groups
        self.half_ff = self.ff // 2
        self.stripe = 2 * shard_ff


def semaphores(plan):
    line, groups = plan.line, plan.groups
    dma = pltpu.SemaphoreType.DMA
    chunks_gu, chunks_a = 4, 4
    return dict(
        loc=dma((40,)),
        ra=dma((groups, 2)),
        sa_z=dma((2, line)),
        sa_x=dma((line, 2)),
        sa_y=dma((line, 2)),
        sa_c=dma((line, 2, 2)),
        rg=dma((groups, 2)),
        sg_z=dma((2, line, 2)),
        sg_x=dma((line, 2)),
        sg_c=dma((line, 2, 2)),
        rd=dma((line, 2)),
        sd_x=dma((1,)),
        sd_z=dma((2, line)),
        sd_c=dma((line,)),
        rv=dma((groups,)),
        sv=dma((groups,)),
        s_part=dma((D // (2 * LANES),)),
        r_part=dma((D // (2 * LANES),)),
        s_back=dma((line,)),
        r_back=dma((line,)),
        sx=dma((4,)),
        rx=dma((4,)),
        r_doc=dma((groups,)),
        s_doc=dma((groups,)),
        r_slope=dma((groups,)),
        s_slope=dma((groups,)),
        s_slope_q=dma((groups,)),
        r_query=dma((1,)),
        s_query=dma((1,)),
        s_ln=dma((line.bit_length() + 2,)),
        r_ln=dma((line.bit_length() + 2,)),
        gd_c=dma((2, line)),
        gd_z=dma((2, 2, line)),
        gd_x=dma((2,)),
        gd_y=dma((2,)),
        gg_c=dma((2, chunks_gu)),
        gg_x=dma((2, chunks_gu)),
        gg_z=dma((2, chunks_gu, 2, line)),
        gg_y=dma((2, chunks_gu)),
        ga_c=dma((2, 2, chunks_a)),
        ga_t=dma((2, chunks_a)),
        ga_x=dma((2, chunks_a)),
        ga_z=dma((2, chunks_a, 2, line)),
        ga_y=dma((2, chunks_a)),
        fin=dma((10,)),
    )


def buffers(plan):
    line, count, shard, groups = plan.line, plan.count, plan.shard, plan.groups
    pair = 2 * count
    v = pltpu.VMEM
    return dict(
        wa=v((line, 2, 2, shard, plan.width_a), BF),
        wg=v((line, 2, 2, shard, plan.ff), BF),
        wd=v((line, 2, plan.shard_ff, D), BF),
        tok=v((count, D), BF),
        vt=v((groups, 8, LANES), F32),
        vec=v((8, D), F32),
        cos=v((count, LANES), F32),
        sin=v((count, LANES), F32),
        hide=v((count, count), F32),
        pw=v((count, 1), F32),
        qkv=v((count, 3 * D), BF),
        probs=v((HEADS, count, count), F32),
        mixed=v((count, D), BF),
        mixt=v((D, count), BF),
        tokt=v((D, count), BF),
        h1=v((count, D), F32),
        rs1=v((count, 1), F32),
        n1=v((count, D), F32),
        feed=v((pair, D), BF),
        feedt=v((D, pair), BF),
        gate=v((pair, plan.half_ff), F32),
        up=v((pair, plan.half_ff), F32),
        hidt=v((plan.half_ff, pair), BF),
        dgu=v((pair, plan.ff), BF),
        bown=v((count, D), F32),
        bsend=v((count, D), BF),
        brecv=v((count, D), BF),
        xh2=v((count, D), F32),
        rs2=v((count, 1), F32),
        xh2b=v((count, D), F32),
        rs2b=v((count, 1), F32),
        pwb=v((count, 1), F32),
        brest=v((count, D), BF),
        dpoolb=v((8, D), F32),
        dpoolr=v((8, D), F32),
        dbr=v((pair, D), BF),
        dsend=v((count, D), BF),
        drecv=v((count, D), BF),
        datt=v((count, D), BF),
        pool=v((8, D), F32),
        dpool=v((8, D), F32),
        emb=v((8, D), F32),
        embd=v((1, D + LANES), F32),
        embq=v((QPD, D), F32),
        dbuf=v((groups, 1, D + LANES), F32),
        cbuf=v((groups, 1, D), F32),
        csend=v((groups, 1, D), F32),
        qrecv=v((QPD, D), F32),
        dflat=v((groups, D), F32),
        ln=v((line.bit_length() + 3, 8, D), F32),
        lnr=v((line.bit_length() + 2, 8, D), F32),
        gd=v((line, 2, plan.shard_ff, D), BF),
        gd_rc=v((line, plan.shard_ff, D), BF),
        gd_rz=v((line + 1, plan.shard_ff, D), BF),
        gd_rx=v((plan.shard_ff, D), BF),
        gd_f=v((plan.shard_ff, D), BF),
        gg=v((line, 2, 2, shard, plan.ff), BF),
        gg_rc=v((line, 2, shard, plan.ff), BF),
        gg_rx=v((line, shard, plan.ff), BF),
        gg_rz=v((line + 1, shard, plan.ff), BF),
        gg_f=v((shard, plan.ff), BF),
        ga_rc=v((line, 2, shard, plan.width_a), BF),
        ga_rt=v((line, 2, shard, plan.half_a), BF),
        ga_rx=v((line, shard, plan.half_a), BF),
        ga_rz=v((line + 1, shard, plan.half_a), BF),
        ga_f=v((shard, plan.half_a), BF),
    )


class Operands(NamedTuple):
    qlen: Any
    dlen: Any
    pos: Any
    i_tok: Any
    tcos: Any
    tsin: Any
    g_one: Any
    b_one: Any
    g_two: Any
    b_two: Any
    i_qkv: Any
    i_out: Any
    i_gate: Any
    i_up: Any
    i_down: Any


class Results(NamedTuple):
    o_tok: Any
    o_a: Any
    o_gu: Any
    o_dn: Any
    o_vec: Any
    o_q: Any
    o_d: Any
    o_loss: Any


def whole_step(plan, *refs):
    names = (Operands._fields + Results._fields + tuple(buffers(plan)) + tuple(semaphores(plan)))
    r = SimpleNamespace(**dict(zip(names, refs, strict=True)))
    line, groups, count = plan.line, plan.groups, plan.count
    shard, shard_ff, stripe = plan.shard, plan.shard_ff, plan.stripe
    half_a, half_ff, ff = plan.half_a, plan.half_ff, plan.ff
    quarter = QLEN
    shift = QLEN.bit_length() - 1

    t = lax.axis_index(TOWER)
    me = lax.axis_index(DP)
    z = me // 4
    x = (me // 2) % 2
    c = me % 2

    def at(zz, xx, cc):
        return (zz * 2 + xx) * 2 + cc

    dev_x = {TOWER: t, DP: at(z, 1 - x, c)}
    dev_c = {TOWER: t, DP: at(z, x, 1 - c)}
    dev_y = {TOWER: 1 - t, DP: me}

    def dev_z(zz):
        return {TOWER: t, DP: at(zz, x, c)}

    pending, tail = [], []

    def copy(src, dst, ssem, rsem, dev):
        return pltpu.make_async_remote_copy(
            src_ref=src, dst_ref=dst, send_sem=ssem, recv_sem=rsem,
            device_id=dev, device_id_type=MESH,
        )

    def send(cond, what, keep=pending):
        do(cond, what.start)
        keep.append((cond, what))

    def settle(keep):
        for cond, what in keep:
            do(cond, what.wait_send)
        keep.clear()

    def got(cond, ref, rsem):
        do(cond, copy(ref, ref, r.s_query.at[0], rsem, dev_x).wait_recv)

    wa, wg, wd = r.wa, r.wg, r.wd
    out_w = half_a - 3 * D // 2
    local = []

    def near(src, dst, cond=None):
        what = pltpu.make_async_copy(src, dst, r.loc.at[len(local)])
        do(cond, what.start)
        local.append((cond, what))

    third = 3 * D // 2
    half_d = D // 2
    for h in range(2):
        for k in range(3):
            near(r.i_qkv.at[:, pl.ds(k * D + h * half_d, half_d)],
                 wa.at[z, x, c, :, pl.ds(h * half_a + k * half_d, half_d)])
        near(r.i_out.at[:, pl.ds(h * out_w, out_w)],
             wa.at[z, x, c, :, pl.ds(h * half_a + third, out_w)])
    near(r.i_down, wd.at[z, c], x == t)
    near(r.i_tok, r.tok)
    for s in range(QPD):
        begin = aligned(s * QLEN * t, QLEN)
        near(r.tcos.at[pl.ds(begin, QLEN)], r.cos.at[pl.ds(s * QLEN, QLEN)])
        near(r.tsin.at[pl.ds(begin, QLEN)], r.sin.at[pl.ds(s * QLEN, QLEN)])
    part_ff = half_ff // 2
    per_part = line // 2

    def stripe_at(k, s):
        return (2 * (s // per_part) + k) * part_ff + (s % per_part) * stripe

    for s in range(line):
        for k, ref in enumerate((r.i_gate, r.i_up)):
            near(ref.at[:, pl.ds(aligned((2 * s + t) * stripe, LANES), stripe)],
                 wg.at[z, x, c, :, pl.ds(stripe_at(k, s), stripe)])

    r.vt[me] = jnp.zeros((8, LANES), F32)
    for k, ref in enumerate((r.g_one, r.b_one, r.g_two, r.b_two)):
        r.vt[me, pl.ds(k, 1), pl.ds(0, plan.vec)] = ref[...].astype(F32)

    barrier = pltpu.get_barrier_semaphore()

    def greet(j, carry):
        other = jnp.logical_or(j // groups != t, j % groups != me)

        @pl.when(other)
        def _():
            pl.semaphore_signal(
                barrier, inc=1, device_id={TOWER: j // groups, DP: j % groups},
                device_id_type=MESH,
            )

        return carry

    lax.fori_loop(0, 2 * groups, greet, 0)
    pl.semaphore_wait(barrier, 2 * groups - 1)
    for cond, what in local:
        do(cond, what.wait)

    def piece_a(zz, xx, cc, h):
        return wa.at[zz, xx, cc, :, pl.ds(aligned(h * half_a, LANES), half_a)]

    def send_a(cond, sem, zz, xx, h, dev):
        ref = piece_a(zz, xx, c, h)
        send(cond, copy(ref, ref, sem, r.ra.at[at(zz, xx, c), h], dev))

    def got_a(cond, zz, xx, cc, h):
        got(cond, piece_a(zz, xx, cc, h), r.ra.at[at(zz, xx, cc), h])

    def sides(step):
        return ((z - step, z >= step, z < line - 1, z + 1), (z + step, z < line - step, z > 0, z - 1))

    def a_start():
        for way, (_, _, on, nxt) in enumerate(sides(0)):
            send_a(on, r.sa_z.at[way, z], z, x, t, dev_z(nxt))
        send_a(None, r.sa_x.at[z, t], z, x, t, dev_x)
        send_a(x != t, r.sa_x.at[z, 1 - t], z, x, 1 - t, dev_x)
        send_a(None, r.sa_c.at[z, x, t], z, x, t, dev_c)
        send_a(None, r.sa_c.at[z, x, 1 - t], z, x, 1 - t, dev_c)

    def a_round(step, way):
        zz, there, on, nxt = sides(step)[way]
        got_a(there, zz, x, c, t)
        send_a(both(there, on), r.sa_z.at[way, zz], zz, x, t, dev_z(nxt))
        send_a(there, r.sa_x.at[zz, t], zz, x, t, dev_x)
        send_a(there, r.sa_y.at[zz, x], zz, x, t, dev_y)
        send_a(there, r.sa_c.at[zz, x, t], zz, x, t, dev_c)

    def a_cross(step, way):
        zz, there, _, _ = sides(step)[way]
        got_a(there, zz, 1 - x, c, t)
        send_a(there if step else x == t, r.sa_y.at[zz, 1 - x], zz, 1 - x, t, dev_y)
        send_a(there, r.sa_c.at[zz, 1 - x, t], zz, 1 - x, t, dev_c)

    def a_tower(step, way):
        zz, there, _, _ = sides(step)[way]
        for xx in (x, 1 - x) if step else (1 - x,):
            got_a(there, zz, xx, c, 1 - t)
            send_a(there, r.sa_c.at[zz, xx, 1 - t], zz, xx, 1 - t, dev_c)

    def a_sibling(h):
        for zz in range(line):
            for xx in range(2):
                got_a(None, zz, xx, 1 - c, h)

    def piece_g(zz, xx, cc, h):
        return wg.at[zz, xx, cc, :, pl.ds(h * half_ff, half_ff)]

    def send_g(cond, sem, zz, xx, h, dev):
        ref = piece_g(zz, xx, c, h)
        send(cond, copy(ref, ref, sem, r.rg.at[at(zz, xx, c), h], dev))

    def got_g(cond, zz, xx, cc, h):
        got(cond, piece_g(zz, xx, cc, h), r.rg.at[at(zz, xx, cc), h])

    def g_start(h):
        for way, (_, _, on, nxt) in enumerate(sides(0)):
            send_g(on, r.sg_z.at[way, z, h], z, x, h, dev_z(nxt))

    def g_line(step, way, h):
        zz, there, on, nxt = sides(step)[way]
        got_g(there, zz, x, c, h)
        send_g(both(there, on), r.sg_z.at[way, zz, h], zz, x, h, dev_z(nxt))

    def g_spread(step, way, h):
        zz, there, _, _ = sides(step)[way]
        send_g(there, r.sg_x.at[zz, h], zz, x, h, dev_x)
        send_g(there, r.sg_c.at[zz, x, h], zz, x, h, dev_c)

    def g_cross(step, way, h):
        zz, there, _, _ = sides(step)[way]
        got_g(there, zz, 1 - x, c, h)
        send_g(there, r.sg_c.at[zz, 1 - x, h], zz, 1 - x, h, dev_c)

    def g_sibling(h):
        for zz in range(line):
            for xx in range(2):
                got_g(None, zz, xx, 1 - c, h)

    def send_d(cond, sem, zz, dev):
        ref = wd.at[zz, c]
        send(cond, copy(ref, ref, sem, r.rd.at[zz, c], dev))

    def got_d(cond, zz, cc):
        got(cond, wd.at[zz, cc], r.rd.at[zz, cc])

    def d_cross():
        send_d(x == t, r.sd_x.at[0], z, dev_x)

    def d_start():
        got_d(x != t, z, c)
        for way, (_, _, on, nxt) in enumerate(sides(0)):
            send_d(on, r.sd_z.at[way, z], z, dev_z(nxt))
        send_d(None, r.sd_c.at[z], z, dev_c)

    def d_round(step, way, ends):
        zz, there, on, nxt = sides(step)[way]
        cond = both(there, jnp.logical_not(on) if ends else on)
        got_d(cond, zz, c)
        if not ends:
            send_d(cond, r.sd_z.at[way, zz], zz, dev_z(nxt))
        send_d(cond, r.sd_c.at[zz], zz, dev_c)

    def d_sibling():
        for zz in range(line):
            got_d(None, zz, 1 - c)

    def v_send(j, carry):
        @pl.when(j != me)
        def _():
            copy(r.vt.at[me], r.vt.at[me], r.sv.at[j], r.rv.at[me],
                 {TOWER: t, DP: j}).start()

        return carry

    def v_wait(j, carry):
        @pl.when(j != me)
        def _():
            copy(r.vt.at[me], r.vt.at[j], r.sv.at[j], r.rv.at[j],
                 {TOWER: t, DP: j}).wait()

        return carry

    a_start()
    lax.fori_loop(0, groups, v_send, 0)

    tok = r.tok
    rows = lax.broadcasted_iota(jnp.int32, (count, count), 0)
    cols = lax.broadcasted_iota(jnp.int32, (count, count), 1)
    seg = cols >> shift
    limit = jnp.zeros_like(cols)
    for s in range(QPD):
        limit = jnp.where(seg == s, r.qlen[s], limit)
    limit = limit * (1 - t) + r.dlen[0] * t
    place = cols - seg * (quarter * (1 - t))
    apart = ((rows >> shift) - seg) * (1 - t)
    seen = both(apart == 0, place < limit)
    r.hide[...] = jnp.where(seen, 0.0, -1e30)
    for s in range(QPD):
        part = pl.ds(s * quarter, quarter)
        for tower, weights in ((t, r.pw), (1 - t, r.pwb)):
            length = jnp.full((quarter, 1), r.qlen[s] * (1 - tower) + r.dlen[0] * tower, jnp.int32)
            slot = lax.broadcasted_iota(jnp.int32, (quarter, 1), 0) + s * quarter * tower
            weights[part, :] = jnp.where(slot < length, 1.0 / length.astype(F32), 0.0)
    lanes = lax.broadcasted_iota(jnp.int32, (count, LANES), 1)
    first_head = lanes < HEAD
    low_half = (lanes & (HEAD - 1)) < HEAD // 2

    def swap(a):
        return jnp.where(low_half, pltpu.roll(a, LANES - HEAD // 2, 1), pltpu.roll(a, HEAD // 2, 1))

    def turn(a):
        return a * r.cos[...] + swap(a) * r.sin[...]

    def turn_back(a):
        return a * r.cos[...] - swap(a) * r.sin[...]

    def transpose_into(dst, src, width):
        def body(j, carry):
            o = aligned(j * LANES, LANES)
            dst[pl.ds(o, LANES), :] = src[:, pl.ds(o, LANES)].T
            return carry

        lax.fori_loop(0, width // LANES, body, 0)

    def wide(ref, lo, n):
        return ref[:, :, :, :, pl.ds(lo, n)].reshape(groups * shard, n)

    def widen_vec():
        lane = lax.broadcasted_iota(jnp.int32, (8, LANES), 1)
        parts = [jnp.zeros((8, LANES), F32) for _ in range(D // LANES)]
        for j in range(groups):
            block, first = divmod(j * plan.vec, LANES)
            piece = r.vt[j]
            if first:
                piece = pltpu.roll(piece, first, 1)
            parts[block] = parts[block] + jnp.where(lane >= first, piece, 0.0)
            if first + plan.vec > LANES:
                parts[block + 1] = parts[block + 1] + jnp.where(lane < first, piece, 0.0)
        r.vec[...] = jnp.concatenate(parts, axis=1)

    pairs = D // LANES
    half_pairs = pairs // 2

    scale = HEAD ** (-0.5)

    def project(h):
        for k in range(3):
            packed = jnp.dot(tok[...], wide(wa, aligned(h * half_a + k * half_d, LANES), half_d),
                             preferred_element_type=F32)
            for i in range(half_pairs):
                part = packed[:, i * LANES : (i + 1) * LANES]
                if k < 2:
                    part = turn(part)
                if k == 0:
                    part = part * scale
                r.qkv[:, pl.ds(aligned(k * D + h * half_d + i * LANES, LANES), LANES)] = (
                    part.astype(BF))

    def triple(p):
        o = aligned(p * LANES, LANES)
        return tuple(r.qkv[:, pl.ds(k * D + o, LANES)] for k in range(3))

    def only(h, a):
        return jnp.where(first_head if h == 0 else jnp.logical_not(first_head), a, jnp.zeros_like(a))

    def attend(p):
        q2, k2, v2 = triple(p)
        outs = []
        for h in range(2):
            scores = dot_tt(only(h, q2), k2) + r.hide[...]
            grown = jnp.exp(scores - jnp.max(scores, -1, keepdims=True))
            probs = grown * (1.0 / jnp.sum(grown, -1, keepdims=True))
            r.probs[2 * p + h] = probs
            outs.append(jnp.dot(probs.astype(BF), v2, preferred_element_type=F32))
        o = aligned(p * LANES, LANES)
        r.mixed[:, pl.ds(o, LANES)] = jnp.where(first_head, outs[0], outs[1]).astype(BF)

    def over_pairs(h, body, lo=0, hi=half_pairs):
        def step(i, carry):
            body(h * half_pairs + i)
            return carry

        lax.fori_loop(lo, hi, step, 0)

    def vectors():
        lax.fori_loop(0, groups, v_wait, 0)
        widen_vec()

    def out_project():
        for h in range(2):
            part = jnp.dot(r.mixed[...], wide(wa, h * half_a + third, out_w),
                           preferred_element_type=F32)
            r.h1[:, pl.ds(h * out_w, out_w)] = tok[:, pl.ds(h * out_w, out_w)].astype(F32) + part

    def moments(h):
        centred = h - jnp.mean(h, -1, keepdims=True)
        return centred, lax.rsqrt(jnp.mean(centred * centred, -1, keepdims=True) + 1e-05)

    blocks = count // quarter

    def norm_one(b, carry):
        part = pl.ds(aligned(b * quarter, quarter), quarter)
        centred, inverse = moments(r.h1[part, :])
        hat = centred * inverse
        normed = hat * r.vec[0:1, :] + r.vec[1:2, :]
        r.h1[part, :] = hat
        r.rs1[part, :] = inverse
        r.n1[part, :] = normed
        r.feed[pl.ds(aligned(t * count + b * quarter, quarter), quarter), :] = (
            normed.astype(BF))
        return carry

    mine = pl.ds(aligned(t * count, count), count)
    theirs = pl.ds(aligned((1 - t) * count, count), count)

    def swap_rows(k, src, dst):
        send(None, copy(src, dst, r.sx.at[k], r.rx.at[k], dev_y), tail)

    def got_rows(k, ref):
        got(None, ref, r.rx.at[k])

    def norm_rows():
        lax.fori_loop(0, blocks, norm_one, 0)
        swap_rows(0, r.feed.at[mine], r.feed.at[mine])

    step_ff = 2 * LANES

    steps_part = part_ff // step_ff

    def gated(part):
        def body(j, carry):
            o = aligned(part * part_ff + j * step_ff, step_ff)
            w = 2 * part * part_ff + j * step_ff
            gate = jnp.dot(r.feed[...], wide(wg, aligned(w, step_ff), step_ff),
                           preferred_element_type=F32)
            up = jnp.dot(r.feed[...], wide(wg, aligned(w + part_ff, step_ff), step_ff),
                         preferred_element_type=F32)
            r.gate[:, pl.ds(o, step_ff)] = gate
            r.up[:, pl.ds(o, step_ff)] = up
            hidden = (gate * jax.nn.sigmoid(gate) * up).astype(BF)
            r.dgu[:, pl.ds(o, step_ff)] = hidden
            r.hidt[pl.ds(o, step_ff), :] = hidden.T
            return carry

        lax.fori_loop(0, steps_part, body, 0)

    def down(rows_of, store):
        def body(j):
            o = j * step_ff
            w = wd[:, :, :, pl.ds(o, step_ff)].reshape(half_ff, step_ff)
            store(o, jnp.dot(r.dgu[rows_of, pl.ds(0, half_ff)], w, preferred_element_type=F32))

        for j in range(D // step_ff):
            body(j)

    def keep_send(o, val):
        span = pl.ds(o, step_ff)
        r.bsend[:, span] = val.astype(BF)
        send(None, copy(r.bsend.at[:, span], r.brecv.at[:, span], r.s_part.at[o // step_ff],
                        r.r_part.at[o // step_ff], dev_y), tail)

    def keep_own(o, val):
        r.bown[:, pl.ds(o, step_ff)] = val
        r.dsend[:, pl.ds(o, step_ff)] = val.astype(BF)

    rest = copy(r.dsend, r.brest, r.sx.at[1], r.rx.at[1], dev_y)

    def norm_two_partner():
        got_rows(1, r.brest)

        def body(b, carry):
            part = pl.ds(aligned(b * quarter, quarter), quarter)
            feed = r.feed[pl.ds(aligned((1 - t) * count + b * quarter, quarter), quarter), :]
            h = feed.astype(F32) + (r.bsend[part, :].astype(F32) + r.brest[part, :].astype(F32))
            centred, inverse = moments(h)
            r.xh2b[part, :] = centred * inverse
            r.rs2b[part, :] = inverse
            return carry

        lax.fori_loop(0, blocks, body, 0)

    g_start(0)
    d_cross()
    a_round(1, 0)
    a_round(1, 1)
    g_line(1, 0, 0)
    g_line(1, 1, 0)
    a_cross(0, 0)
    a_round(2, 1)
    a_round(2, 0)
    a_cross(1, 0)
    g_start(1)
    g_spread(0, 0, 1)
    a_cross(1, 1)
    g_line(2, 1, 0)
    g_line(2, 0, 0)
    a_round(3, 0)
    a_round(3, 1)
    g_line(1, 0, 1)
    a_cross(2, 0)
    a_cross(2, 1)
    g_spread(1, 1, 0)
    g_line(1, 1, 1)
    g_spread(2, 0, 0)
    g_spread(2, 1, 0)
    d_start()
    a_tower(1, 0)
    g_spread(1, 0, 0)
    g_line(3, 0, 0)
    g_spread(1, 0, 1)
    g_spread(0, 0, 0)
    a_cross(3, 0)
    a_tower(0, 0)
    a_cross(3, 1)
    vectors()
    g_line(2, 0, 1)
    a_sibling(t)
    g_spread(3, 0, 0)
    project(t)
    over_pairs(t, attend, 0, 1)
    g_cross(0, 0, 1)
    over_pairs(t, attend, 1, 2)
    g_spread(1, 1, 1)
    g_line(2, 1, 1)
    g_line(3, 1, 0)
    g_spread(3, 1, 0)
    a_tower(3, 0)
    over_pairs(t, attend, 2, 3)
    a_tower(1, 1)
    a_tower(3, 1)
    a_tower(2, 0)
    a_tower(2, 1)
    d_round(1, 0, False)
    a_sibling(1 - t)
    project(1 - t)
    over_pairs(1 - t, attend, 0, 1)
    d_round(1, 1, False)
    over_pairs(1 - t, attend, 1, 3)
    out_project()
    norm_rows()
    g_spread(2, 0, 1)
    g_cross(2, 1, 0)
    d_round(2, 0, False)
    g_line(3, 0, 1)
    d_round(1, 1, True)
    g_spread(3, 0, 1)
    d_round(1, 0, True)
    d_round(2, 0, True)
    g_line(3, 1, 1)
    g_cross(2, 0, 0)
    g_cross(1, 0, 0)
    g_cross(0, 0, 0)
    g_cross(3, 0, 0)
    g_spread(3, 1, 1)
    g_cross(3, 1, 0)
    g_spread(2, 1, 1)
    g_cross(1, 1, 0)
    d_round(2, 1, False)
    g_sibling(0)
    g_cross(3, 1, 1)
    transpose_into(r.tokt, tok, D)
    g_cross(1, 1, 1)
    g_cross(1, 0, 1)
    g_cross(2, 0, 1)
    d_round(2, 1, True)
    g_cross(3, 0, 1)
    g_cross(2, 1, 1)
    got_rows(0, r.feed.at[theirs])
    gated(0)
    g_sibling(1)
    d_round(3, 1, True)
    d_round(3, 0, True)
    gated(1)
    d_sibling()
    transpose_into(r.mixt, r.mixed, D)
    down(theirs, keep_send)
    down(mine, keep_own)
    do(t == 0, rest.start)
    transpose_into(r.feedt, r.feed, D)
    for j in range(D // step_ff):
        got(None, r.brecv.at[:, pl.ds(j * step_ff, step_ff)], r.r_part.at[j])

    r.pool[...] = jnp.zeros((8, D), F32)

    def norm_two(b, carry):
        part = pl.ds(aligned(b * quarter, quarter), quarter)
        h = r.n1[part, :] + (r.bown[part, :] + r.brecv[part, :].astype(F32))
        centred, inverse = moments(h)
        hat = centred * inverse
        normed = hat * r.vec[2:3, :] + r.vec[3:4, :]
        r.xh2[part, :] = hat
        r.rs2[part, :] = inverse
        r.pool[pl.ds(b, 1), :] = jnp.sum(normed * r.pw[part, :], 0, keepdims=True)
        return carry

    lax.fori_loop(0, blocks, norm_two, 0)
    row8 = lax.broadcasted_iota(jnp.int32, (8, D), 0)

    @pl.when(t == 1)
    def _():
        all_rows = jnp.sum(r.pool[...], 0, keepdims=True)
        r.pool[...] = jnp.where(row8 == 0, all_rows, 0.0)

    pooled = r.pool[...]
    shrink = lax.rsqrt(jnp.sum(pooled * pooled, -1, keepdims=True) + 1e-06)
    r.emb[...] = pooled * shrink

    best = exact_product_accuracy
    r.dpool[...] = jnp.zeros((8, D), F32)
    r.ln[0] = jnp.zeros((8, D), F32)

    def to_all(tower, src, dst, ssem, rsem, others=False):
        def give(step, carry):
            j = (me + step) % groups
            copy(src(j), dst.at[me], ssem.at[j], rsem.at[me], {TOWER: tower, DP: j}).start()
            return carry

        lax.fori_loop(1 if others else 0, groups, give, 0)

    def from_all(dst, ssem, rsem, others=False):
        def take(step, carry):
            j = (me + step) % groups
            copy(dst.at[j], dst.at[j], ssem.at[j], rsem.at[j], dev_x).wait_recv()
            return carry

        lax.fori_loop(1 if others else 0, groups, take, 0)

    zero_row = jnp.zeros((1, D), F32)

    def norm_two_back(weights, slopes, hats, inverses, tower, own):
        def body(b, sums):
            part = pl.ds(aligned(b * quarter, quarter), quarter)
            top = weights[part, :] * slopes[pl.ds(b, 1), :]
            hat = hats[part, :]
            inner = top * r.vec[2:3, :]
            grad = inverses[part, :] * (
                inner - jnp.mean(inner, -1, keepdims=True)
                - hat * jnp.mean(inner * hat, -1, keepdims=True))
            r.dbr[pl.ds(aligned(tower * count + b * quarter, quarter), quarter), :] = (
                grad.astype(BF))
            if not own:
                return sums
            r.n1[part, :] = grad
            return (sums[0] + jnp.sum(top * hat, 0, keepdims=True),
                    sums[1] + jnp.sum(top, 0, keepdims=True))

        sums = lax.fori_loop(0, blocks, body, (zero_row, zero_row))
        if own:
            r.ln[0] = (r.ln[0] + jnp.where(row8 == 2, sums[0], 0.0)
                       + jnp.where(row8 == 3, sums[1], 0.0))

    def back_own():
        norm_two_back(r.pw, r.dpool, r.xh2, r.rs2, t, True)

    def back_partner():
        norm_two_back(r.pwb, r.dpoolb, r.xh2b, r.rs2b, 1 - t, False)

    def hidden_back(rows_of):
        def body(j, carry):
            o = aligned(j * stripe, LANES)
            w = wd[j].reshape(stripe, D)
            slope = dot_tt(r.dbr[rows_of, :], w)
            gate = r.gate[rows_of, pl.ds(o, stripe)]
            up = r.up[rows_of, pl.ds(o, stripe)]
            sig = jax.nn.sigmoid(gate)
            w_at = aligned((2 * (j // per_part)) * part_ff + (j % per_part) * stripe, LANES)
            r.dgu[rows_of, pl.ds(w_at, stripe)] = (
                slope * up * (sig * (1.0 + gate * (1.0 - sig)))).astype(BF)
            r.dgu[rows_of, pl.ds(aligned(w_at + part_ff, LANES), stripe)] = (slope * (gate * sig)).astype(BF)
            return carry

        lax.fori_loop(0, line, body, 0)

    def slope_back(slope, emb, scale_of):
        return scale_of * (slope - emb * jnp.sum(slope * emb, -1, keepdims=True))

    def doc_slope():
        total = r.cbuf[0]
        for j in range(1, groups):
            total = total + r.cbuf[j]
        return total

    pool_slope = copy(r.dpool, r.dpoolr, r.sx.at[2], r.rx.at[2], dev_y)
    tail.append((t == 0, pool_slope))

    @pl.when(t == 0)
    def _():
        r.embq[...] = r.emb[0:QPD, :]
        from_all(r.dbuf, r.s_doc, r.r_doc)
        for j in range(groups):
            r.dflat[pl.ds(j, 1), :] = r.dbuf[j, :, pl.ds(0, D)]
        docs, queries = r.dflat[...], r.embq[...]
        logits = dot_tt(queries, docs, best) / contrast_sharpness_factor
        peak = jnp.max(logits, -1, keepdims=True)
        lse = peak + jnp.log(jnp.sum(jnp.exp(logits - peak), -1, keepdims=True))
        col = lax.broadcasted_iota(jnp.int32, (QPD, groups), 1)
        row = lax.broadcasted_iota(jnp.int32, (QPD, groups), 0)
        label = jnp.zeros((QPD, groups), jnp.int32)
        for s in range(QPD):
            label = jnp.where(row == s, r.pos[me * QPD + s], label)
        hot = jnp.where(col == label, 1.0, 0.0)
        slope = (jnp.exp(logits - lse) - hot) / contrast_sharpness_factor
        back = dot_t0(slope, queries, best)
        for j in range(groups):
            r.csend[j] = back[j : j + 1, :]
        to_all(1, lambda j: r.csend.at[j], r.cbuf, r.s_slope, r.r_slope)
        to_all(0, lambda j: r.csend.at[j], r.cbuf, r.s_slope_q, r.r_slope, True)
        r.cbuf[me] = r.csend[me]
        r.dpool[0:QPD, :] = jnp.dot(slope, docs, preferred_element_type=F32, precision=best)
        r.dpool[...] = slope_back(r.dpool[...], r.emb[...], shrink)
        pool_slope.start()
        picked = jnp.sum(jnp.where(hot > 0.5, logits, 0.0), -1, keepdims=True)
        total = jnp.sum(lse - picked, 0, keepdims=True)
        r.ln[0] = jnp.where(row8 == 4, total, 0.0)
        back_own()

    @pl.when(t == 1)
    def _():
        r.embd[:, 0:D] = r.emb[0:1, :]
        r.embd[:, D:] = jnp.broadcast_to(shrink[0:1, :], (1, LANES))
        r.dbuf[me] = r.embd[...]
        to_all(0, lambda j: r.embd, r.dbuf, r.s_doc, r.r_doc)
        rest.start()
        norm_two_partner()
        got_rows(2, r.dpoolr)
        r.dpoolb[...] = r.dpoolr[...]
        back_partner()

    hidden_back(pl.ds(0, count))

    @pl.when(t == 1)
    def _():
        from_all(r.cbuf, r.s_slope, r.r_slope)
        row = slope_back(doc_slope(), r.emb[0:1, :], shrink[0:1, :])
        r.dpool[...] = jnp.broadcast_to(row, (8, D))
        back_own()

    @pl.when(t == 0)
    def _():
        norm_two_partner()
        from_all(r.cbuf, r.s_slope_q, r.r_slope, True)
        doc = r.dbuf[me]
        row = slope_back(doc_slope(), doc[:, 0:D], doc[:, D : D + 1])
        r.dpoolb[...] = jnp.broadcast_to(row, (8, D))
        back_partner()

    hidden_back(pl.ds(count, count))
    rest.wait_send()
    send(t == 0, copy(r.embq, r.qrecv, r.s_query.at[0], r.r_query.at[0], dev_y), tail)

    def along(step):
        for s in range(1, line):
            yield line - s, both(z == step, z < line - s), z + 1, 0
        for s in range(line - 1):
            yield s, both(z == line - 1 - step, z > s), z - 1, 1

    def added(refs):
        total = refs[0][...].astype(F32)
        for ref in refs[1:]:
            total = total + ref[...].astype(F32)
        return total

    def line_step(step, parts, sem, slot, nth):
        for k, (dest, cond, nxt, way) in enumerate(along(step)):
            if k % (line - 1) != nth:
                continue
            into = slot(dest + 1 if way == 0 else dest)
            refs = parts(dest)

            def move(into=into, refs=refs, dest=dest, way=way):
                if step:
                    copy(into, into, r.s_query.at[0], sem(1, way, dest), dev_x).wait_recv()
                    refs[0][...] = added(refs + (into,)).astype(BF)
                else:
                    refs[0][...] = added(refs).astype(BF)

            do(cond, move)
            send(cond, copy(refs[0], into, sem(0, way, dest), sem(1, way, dest),
                            dev_z(nxt)), tail)

    def line_end(parts, sem, slot, put):
        for cond, ways in ((z == 0, (1,)), (z == line - 1, (0,)),
                           (both(z > 0, z < line - 1), (0, 1))):
            def finish(ways=ways):
                refs = parts(z)
                for way in ways:
                    into = slot(z + 1 if way == 0 else z)
                    copy(into, into, r.s_query.at[0], sem(1, way, z), dev_x).wait_recv()
                    refs = refs + (into,)
                put[...] = added(refs).astype(BF)

            do(cond, finish)

    gd = r.gd

    def down_grad(s):
        val = jnp.dot(r.hidt[pl.ds(s * stripe, stripe), :], r.dbr[...],
                      preferred_element_type=F32)
        gd[s] = val.astype(BF).reshape(2, shard_ff, D)
        send(None, copy(gd.at[s, 1 - c], r.gd_rc.at[s], r.gd_c.at[0, s],
                        r.gd_c.at[1, s], dev_c), tail)

    def down_parts(dest):
        return gd.at[dest, c], r.gd_rc.at[dest]

    def down_arrive():
        for s in range(line):
            got(None, r.gd_rc.at[s], r.gd_c.at[1, s])

    def down_line(step, nth):
        line_step(step, down_parts, lambda *i: r.gd_z.at[i], lambda k: r.gd_rz.at[k], nth)

    def down_end():
        line_end(down_parts, lambda *i: r.gd_z.at[i], lambda k: r.gd_rz.at[k], r.gd_f)
        send(x != t, copy(r.gd_f, r.gd_rx, r.gd_x.at[0], r.gd_x.at[1], dev_x), tail)

    out_copies = []

    def keep_out(k, src, dst, cond=None):
        what = pltpu.make_async_copy(src, dst, r.fin.at[k])
        do(cond, what.start)
        out_copies.append((cond, what))

    def down_out():
        def total():
            copy(r.gd_rx, r.gd_rx, r.s_query.at[0], r.gd_x.at[1], dev_x).wait_recv()
            r.gd_f[...] = added((r.gd_f, r.gd_rx)).astype(BF)

        do(x == t, total)
        keep_out(0, r.gd_f, r.o_dn, x == t)
        send(x == t, copy(r.gd_f, r.o_dn, r.gd_y.at[0], r.gd_y.at[1], dev_y), tail)

    gg = r.gg
    part_gu = ff // 4

    def gate_grad(k):
        span = pl.ds(k * part_gu, part_gu)
        val = jnp.dot(r.feedt[...], r.dgu[:, span], preferred_element_type=F32)
        gg[:, :, :, :, span] = val.astype(BF).reshape(line, 2, 2, shard, part_gu)
        send(None, copy(gg.at[:, :, 1 - c, :, span], r.gg_rc.at[:, :, :, span],
                        r.gg_c.at[0, k], r.gg_c.at[1, k], dev_c), tail)

    def gate_cross(k):
        span = pl.ds(k * part_gu, part_gu)
        got(None, r.gg_rc.at[:, :, :, span], r.gg_c.at[1, k])
        for s in range(line):
            mine_k = gg.at[s, 1 - x, c, :, span]
            mine_k[...] = added((mine_k, r.gg_rc.at[s, 1 - x, :, span])).astype(BF)
        send(None, copy(gg.at[:, 1 - x, c, :, span], r.gg_rx.at[:, :, span],
                        r.gg_x.at[0, k], r.gg_x.at[1, k], dev_x), tail)

    def gate_parts(k):
        span = pl.ds(k * part_gu, part_gu)
        return lambda dest: (gg.at[dest, x, c, :, span], r.gg_rc.at[dest, x, :, span],
                             r.gg_rx.at[dest, :, span])

    def gate_ready(k):
        span = pl.ds(k * part_gu, part_gu)
        got(None, r.gg_rx.at[:, :, span], r.gg_x.at[1, k])

    def gate_line(k, step, nth):
        span = pl.ds(k * part_gu, part_gu)
        line_step(step, gate_parts(k), lambda a, *i: r.gg_z.at[(a, k) + i],
                  lambda s: r.gg_rz.at[s, :, span], nth)

    def gate_end(k):
        span = pl.ds(k * part_gu, part_gu)
        line_end(gate_parts(k), lambda a, *i: r.gg_z.at[(a, k) + i], lambda s: r.gg_rz.at[s, :, span],
                 r.gg_f.at[:, span])
        keep_out(1 + k, r.gg_f.at[:, span], r.o_gu.at[t, :, span])
        send(None, copy(r.gg_f.at[:, span], r.o_gu.at[t, :, span], r.gg_y.at[0, k],
                        r.gg_y.at[1, k], dev_y), tail)

    ga = wg
    sizes = (3 * LANES, 3 * LANES, 3 * LANES, out_w)
    starts = (0, 3 * LANES, 6 * LANES, third)

    def cols_a(k, h):
        return pl.ds(aligned(h * half_a + starts[k], LANES), sizes[k])

    def store_a(k, h, left, right):
        val = jnp.dot(left[...], right, preferred_element_type=F32)
        ga[:, :, :, :, cols_a(k, h)] = val.astype(BF).reshape(line, 2, 2, shard, sizes[k])
        send(None, copy(ga.at[:, :, 1 - c, :, cols_a(k, h)],
                        r.ga_rc.at[:, :, :, cols_a(k, h)],
                        r.ga_c.at[0, h, k], r.ga_c.at[1, h, k], dev_c), tail)

    def store_qkv(k, h):
        store_a(k, h, r.tokt, dqkv[:, pl.ds(aligned(h * third + starts[k], LANES), sizes[k])])

    def span_a(k):
        return pl.ds(starts[k], sizes[k])

    def tower_a(k):
        gone = cols_a(k, 1 - t)
        got(None, r.ga_rc.at[:, :, :, gone], r.ga_c.at[1, 1 - t, k])
        for s in range(line):
            for xx in range(2):
                ref = ga.at[s, xx, c, :, gone]
                ref[...] = added((ref, r.ga_rc.at[s, xx, :, gone])).astype(BF)
        send(None, copy(ga.at[:, :, c, :, gone], r.ga_rt.at[:, :, :, span_a(k)],
                        r.ga_t.at[0, k], r.ga_t.at[1, k], dev_y), tail)

    def cross_a(k):
        got(None, r.ga_rt.at[:, :, :, span_a(k)], r.ga_t.at[1, k])
        here = cols_a(k, t)
        got(None, r.ga_rc.at[:, :, :, here], r.ga_c.at[1, t, k])
        for s in range(line):
            ref = ga.at[s, 1 - x, c, :, here]
            ref[...] = added((ref, r.ga_rc.at[s, 1 - x, :, here],
                              r.ga_rt.at[s, 1 - x, :, span_a(k)])).astype(BF)
        send(None, copy(ga.at[:, 1 - x, c, :, here], r.ga_rx.at[:, :, span_a(k)],
                        r.ga_x.at[0, k], r.ga_x.at[1, k], dev_x), tail)

    def parts_a(k):
        here = cols_a(k, t)
        return lambda dest: (ga.at[dest, x, c, :, here], r.ga_rc.at[dest, x, :, here],
                             r.ga_rt.at[dest, x, :, span_a(k)],
                             r.ga_rx.at[dest, :, span_a(k)])

    def ready_a(k):
        got(None, r.ga_rx.at[:, :, span_a(k)], r.ga_x.at[1, k])

    def line_a(k, step, nth):
        line_step(step, parts_a(k), lambda a, *i: r.ga_z.at[(a, k) + i],
                  lambda s: r.ga_rz.at[s, :, span_a(k)], nth)

    def end_a(k):
        line_end(parts_a(k), lambda a, *i: r.ga_z.at[(a, k) + i], lambda s: r.ga_rz.at[s, :, span_a(k)],
                 r.ga_f.at[:, span_a(k)])
        keep_out(5 + k, r.ga_f.at[:, span_a(k)], r.o_a.at[:, cols_a(k, t)])
        send(None, copy(r.ga_f.at[:, span_a(k)], r.o_a.at[:, cols_a(k, t)],
                        r.ga_y.at[0, k], r.ga_y.at[1, k], dev_y), tail)

    some = 2 * 4 * shard

    def rows_of_weight(ref, j, lo, n):
        return ref[pl.ds(2 * j, 2), :, :, :, pl.ds(lo, n)].reshape(some, n)

    def feed_part(rows_of, j, store):
        store(j, pl.ds(j * some, some), dot_tt(r.dgu[rows_of, :], rows_of_weight(wg, j, 0, ff)))

    def back_send(j, span, val):
        r.dsend[:, span] = val.astype(BF)
        send(None, copy(r.dsend.at[:, span], r.drecv.at[:, span], r.s_back.at[j], r.r_back.at[j],
                        dev_y), tail)

    def feed_own(j, span, val):
        r.bown[:, span] = val

    def norm_one_back(b, sums):
        part = pl.ds(aligned(b * quarter, quarter), quarter)
        top = r.n1[part, :] + r.bown[part, :] + r.drecv[part, :].astype(F32)
        hat = r.h1[part, :]
        inner = top * r.vec[0:1, :]
        grad = r.rs1[part, :] * (
            inner - jnp.mean(inner, -1, keepdims=True)
            - hat * jnp.mean(inner * hat, -1, keepdims=True))
        r.n1[part, :] = grad
        r.datt[part, :] = grad.astype(BF)
        return (sums[0] + jnp.sum(top * hat, 0, keepdims=True),
                sums[1] + jnp.sum(top, 0, keepdims=True))

    def norm_back():
        for j in range(line // 2):
            got(None, r.drecv.at[:, pl.ds(j * some, some)], r.r_back.at[j])
        gain_one, bias_one = lax.fori_loop(0, blocks, norm_one_back, (zero_row, zero_row))
        r.ln[0] = (r.ln[0] + jnp.where(row8 == 0, gain_one, 0.0)
                   + jnp.where(row8 == 1, bias_one, 0.0))

    ln_peers = [dev_y, dev_c, dev_x]
    for bit in range(line.bit_length() - 1):
        apart = 1 << bit
        ln_peers.append(dev_z(z + apart * (1 - 2 * ((z // apart) % 2))))
    last = len(ln_peers)

    def small_sums(k):
        if k:
            got(None, r.lnr.at[k - 1], r.r_ln.at[k - 1])
            r.ln[k] = r.ln[k - 1] + r.lnr[k - 1]
        if k < last:
            send(None, copy(r.ln.at[k], r.lnr.at[k], r.s_ln.at[k], r.r_ln.at[k],
                            ln_peers[k]), tail)

    def out_grad():
        for h in range(2):
            store_a(3, h, r.mixt, r.datt[:, pl.ds(h * out_w, out_w)])

    def mix_back():
        lax.fori_loop(0, line // 2, mixed_back, 0)

    dqkv = r.dgu.at[pl.ds(0, count), pl.ds(0, 3 * D)]
    dmix = r.dgu.at[pl.ds(count, count), pl.ds(0, D)]

    def mixed_back(j, carry):
        val = sum(dot_tt(r.datt[:, pl.ds(h * out_w, out_w)],
                         rows_of_weight(wa, j, h * half_a + third, out_w)) for h in range(2))
        dmix[:, pl.ds(aligned(j * some, LANES), some)] = val.astype(BF)
        return carry

    def attend_back(p):
        q2, k2, v2 = triple(p)
        o = aligned(p * LANES, LANES)
        dm2 = dmix[:, pl.ds(o, LANES)]
        parts = []
        for h in range(2):
            probs = r.probs[2 * p + h]
            dprobs = dot_tt(only(h, dm2), v2)
            mean = jnp.sum(probs * dprobs, -1, keepdims=True)
            dscores = (probs * (dprobs - mean)).astype(BF)
            parts.append((jnp.dot(dscores, k2, preferred_element_type=F32),
                          dot_t0(dscores, q2), dot_t0(probs.astype(BF), dm2)))
        dq, dk, dv = (jnp.where(first_head, a, b) for a, b in zip(*parts))
        half = p // half_pairs
        o = half * third + (p - half * half_pairs) * LANES
        for k, part in enumerate((turn_back(dq * scale), turn_back(dk), dv)):
            dqkv[:, pl.ds(aligned(o + k * half_d, LANES), LANES)] = part.astype(BF)

    def token_back(j, carry):
        val = sum(dot_tt(dqkv[:, pl.ds(h * third, third)],
                         rows_of_weight(wa, j, h * half_a, third)) for h in range(2))
        span = pl.ds(aligned(j * some, LANES), some)
        r.xh2[:, span] = r.n1[:, span] + val
        return carry

    gate_grad(0)
    feed_part(theirs, 0, back_send)
    down_grad(1)
    down_grad(0)
    gate_cross(0)
    down_grad(3)
    down_grad(2)
    feed_part(theirs, 1, back_send)
    down_arrive()
    down_line(0, 0)
    gate_grad(1)
    down_line(0, 1)
    gate_grad(2)
    feed_part(mine, 0, feed_own)
    gate_cross(1)
    gate_grad(3)
    down_line(0, 2)
    feed_part(mine, 1, feed_own)
    gate_ready(0)
    norm_back()
    settle(pending)
    out_grad()
    gate_cross(3)
    small_sums(0)
    down_line(1, 0)
    mix_back()
    over_pairs(1 - t, attend_back, 0, 1)
    tower_a(3)
    gate_cross(2)
    over_pairs(1 - t, attend_back, 1, 3)
    store_qkv(0, 1 - t)
    over_pairs(t, attend_back, 0, 1)
    store_qkv(1, 1 - t)
    over_pairs(t, attend_back, 1, 2)
    gate_line(0, 0, 0)
    down_line(1, 1)
    tower_a(0)
    gate_line(0, 0, 1)
    down_line(2, 0)
    gate_ready(3)
    tower_a(1)
    over_pairs(t, attend_back, 2, 3)
    cross_a(3)
    store_qkv(2, 1 - t)
    gate_line(3, 0, 0)
    store_qkv(0, t)
    gate_line(0, 0, 2)
    store_qkv(2, t)
    gate_ready(2)
    gate_line(2, 0, 0)
    gate_line(3, 0, 1)
    tower_a(2)
    gate_line(0, 1, 0)
    cross_a(0)
    ready_a(3)
    gate_line(0, 2, 0)
    gate_line(3, 1, 0)
    gate_line(0, 1, 1)
    down_end()
    gate_ready(1)
    gate_line(1, 0, 0)
    gate_line(2, 1, 0)
    store_qkv(1, t)
    line_a(3, 1, 0)
    line_a(3, 0, 0)
    line_a(3, 0, 1)
    lax.fori_loop(0, line // 2, token_back, 0)
    keep_out(9, r.xh2, r.o_tok)
    gate_line(3, 1, 1)
    cross_a(1)
    gate_end(0)
    line_a(3, 2, 0)
    small_sums(1)
    gate_line(2, 2, 0)
    gate_line(2, 0, 1)
    gate_line(1, 0, 1)
    gate_line(1, 1, 0)
    line_a(3, 0, 2)
    gate_line(2, 0, 2)
    ready_a(0)
    down_out()
    gate_line(3, 0, 2)
    gate_line(2, 1, 1)
    line_a(0, 0, 0)
    line_a(3, 1, 1)
    gate_line(1, 1, 1)
    line_a(0, 0, 1)
    gate_line(3, 2, 0)
    cross_a(2)
    gate_end(2)
    ready_a(1)
    small_sums(2)
    line_a(1, 0, 0)
    gate_line(1, 2, 0)
    line_a(1, 0, 2)
    line_a(0, 1, 0)
    line_a(1, 0, 1)
    line_a(1, 1, 0)
    ready_a(2)
    line_a(2, 0, 0)
    end_a(3)
    line_a(1, 1, 1)
    gate_end(3)
    gate_line(1, 0, 2)
    line_a(0, 2, 0)
    line_a(2, 0, 1)
    line_a(2, 1, 0)
    line_a(0, 0, 2)
    line_a(1, 2, 0)
    line_a(0, 1, 1)
    line_a(2, 0, 2)
    gate_end(1)
    small_sums(3)
    line_a(2, 1, 1)
    line_a(2, 2, 0)
    end_a(0)
    end_a(1)
    small_sums(4)
    end_a(2)
    small_sums(5)

    r.o_vec[...] = r.ln[last]
    r.o_loss[...] = r.ln[last][:, 0:LANES] * (1.0 / (groups * QPD))

    r.o_d[...] = r.dbuf[me, :, pl.ds(0, D)]

    def sent(ssem, src, others=False):
        def body(step, carry):
            copy(src, src, ssem.at[(me + step) % groups], r.r_query.at[0], dev_x).wait_send()
            return carry

        lax.fori_loop(1 if others else 0, groups, body, 0)

    @pl.when(t == 0)
    def _():
        r.o_q[...] = r.embq[...]
        sent(r.s_slope, r.csend.at[0])
        sent(r.s_slope_q, r.csend.at[0], True)

    @pl.when(t == 1)
    def _():
        got(None, r.qrecv, r.r_query.at[0])
        r.o_q[...] = r.qrecv[...]
        sent(r.s_doc, r.embd)

    got(x != t, r.o_dn, r.gd_y.at[1])
    for k in range(4):
        got(None, r.o_gu.at[1 - t, :, pl.ds(k * part_gu, part_gu)], r.gg_y.at[1, k])
        got(None, r.o_a.at[:, cols_a(k, 1 - t)], r.ga_y.at[1, k])
    for cond, what in out_copies:
        do(cond, what.wait)
    settle(tail)


def finish(plan, *refs):
    (a_ref, gu_ref, dn_ref, vec_ref, tok_ref, q_ref, d_ref, loss_ref,
     o_loss, o_q, o_d, o_tok, o_qkv, o_out, o_gate, o_up, o_down, *o_vecs) = refs
    third, half_a, half_ff, stripe = 3 * D // 2, plan.half_a, plan.half_ff, plan.stripe
    out_w = half_a - third
    for h in range(2):
        for k in range(3):
            o_qkv[:, pl.ds(k * D + h * (D // 2), D // 2)] = (
                a_ref[:, pl.ds(h * half_a + k * (D // 2), D // 2)].astype(F32))
        o_out[:, h * out_w : (h + 1) * out_w] = (
            a_ref[:, h * half_a + third : (h + 1) * half_a].astype(F32))
        for s in range(plan.line):
            to = pl.ds((2 * s + h) * stripe, stripe)
            per_part, part_ff = plan.line // 2, half_ff // 2
            lo = 2 * (s // per_part) * part_ff + (s % per_part) * stripe
            o_gate[:, to] = gu_ref[h, :, pl.ds(lo, stripe)].astype(F32)
            o_up[:, to] = gu_ref[h, :, pl.ds(lo + part_ff, stripe)].astype(F32)
    o_down[...] = dn_ref[...].astype(F32)
    o_tok[0] = tok_ref[...]
    o_q[...] = q_ref[...]
    o_d[...] = d_ref[...]
    o_loss[...] = loss_ref[4:5, 0:1]
    first = lax.axis_index(DP) * plan.vec
    row = lax.broadcasted_iota(jnp.int32, (D, LANES), 0)
    col = lax.broadcasted_iota(jnp.int32, (D, LANES), 1)
    pick = jnp.where(row == first + col, 1.0, 0.0)
    own = jnp.dot(vec_ref[...], pick, preferred_element_type=F32, precision=exact_product_accuracy)
    for k, out in enumerate(o_vecs):
        out[...] = own[k : k + 1, 0 : plan.vec]


def on_device_kernel(plan, tokens, query_lengths, doc_lengths, positives, w_qkv, w_out, w_gate,
                     w_up, w_down, ln1_gain, first_layernorm_shift, ln2_gain, ln2_bias):
    count, groups, shard, vec = plan.count, plan.groups, plan.shard, plan.vec
    cosines, sines = rotary_constants(count)
    vmem = pl.BlockSpec(memory_space=pltpu.VMEM)
    smem = pl.BlockSpec(memory_space=pltpu.SMEM)
    hbm = pl.BlockSpec(memory_space=pl.ANY)
    shape = jax.ShapeDtypeStruct
    made = pl.pallas_call(
        functools.partial(whole_step, plan),
        out_shape=(
            shape((count, D), F32), shape((shard, plan.width_a), BF), shape((2, shard, plan.ff), BF),
            shape((plan.shard_ff, D), BF), shape((8, D), F32), shape((QPD, D), F32),
            shape((1, D), F32), shape((8, LANES), F32),
        ),
        in_specs=[smem] * 3 + [hbm] * 3 + [vmem] * 4 + [hbm] * 5,
        out_specs=(hbm, hbm, hbm, hbm, vmem, vmem, vmem, vmem),
        scratch_shapes=list(buffers(plan).values()) + list(semaphores(plan).values()),
        compiler_params=pltpu.CompilerParams(
            collective_id=0, has_side_effects=True, vmem_limit_bytes=63 * 1000 * 1000),
        name="whole_step",
    )(query_lengths, doc_lengths, positives, tokens[0], cosines, sines, ln1_gain[None],
      first_layernorm_shift[None], ln2_gain[None], ln2_bias[None],
      w_qkv, w_out, w_gate, w_up, w_down)
    o_tok, o_a, o_gu, o_dn, o_vec, o_q, o_d, o_loss = made
    outs = pl.pallas_call(
        functools.partial(finish, plan),
        out_shape=(
            shape((1, 1), F32), shape((QPD, D), F32), shape((1, D), F32),
            shape((1, count, D), F32), shape((shard, 3 * D), F32), shape((shard, D), F32),
            shape((shard, plan.ff), F32), shape((shard, plan.ff), F32),
            shape((plan.shard_ff, D), F32),
        ) + (shape((1, vec), F32),) * 4,
        in_specs=[vmem] * 8,
        out_specs=[vmem] * 13,
        name="finish",
    )(o_a, o_gu, o_dn, o_vec, o_tok, o_q, o_d, o_loss)
    return (outs[0].reshape(()),) + tuple(outs[1:9]) + tuple(v.reshape(vec) for v in outs[9:])


def fits(plan, towers):
    line = plan.line
    return (towers == 2 and plan.groups % 4 == 0 and line == 4
            and plan.shard % 16 == 0 and plan.shard_ff % 16 == 0 and plan.stripe % LANES == 0
            and plan.count == QPD * QLEN)


def solution(mesh):
    groups = mesh.shape[DP]

    def local_step(*args):
        plan = Plan(groups, args[0].shape[1], args[4].shape[0], args[8].shape[0], args[9].shape[0])
        if fits(plan, mesh.shape[TOWER]):
            return on_device_kernel(plan, *args)
        return on_device(*args)

    return jax.shard_map(
        local_step,
        mesh=mesh,
        in_specs=(
            P(TOWER, DP, None),
            P(DP),
            P(DP),
            P(),
            P(DP, None),
            P(DP, None),
            P(DP, None),
            P(DP, None),
            P(DP, None),
            P(DP),
            P(DP),
            P(DP),
            P(DP),
        ),
        out_specs=(
            P(),
            P(DP, None),
            P(DP, None),
            P(TOWER, DP, None),
            P(DP, None),
            P(DP, None),
            P(DP, None),
            P(DP, None),
            P(DP, None),
            P(DP),
            P(DP),
            P(DP),
            P(DP),
        ),
        check_vma=False,
    )
```

```python
import functools
from types import SimpleNamespace
from typing import Any, NamedTuple

import jax
import jax.numpy as jnp
import numpy as np
from jax import lax
from jax.experimental import pallas as pl
from jax.experimental.pallas import tpu as pltpu
from jax.sharding import PartitionSpec as P

TOWER = "tower"
DP = "dp"
D = 768
HEADS = 12
HEAD = 64
QLEN = 64
QPD = 4


exact_product_accuracy = lax.Precision.HIGHEST
rope_base = 1000.0
contrast_sharpness_factor = 0.02


def product(left, right):
    return jnp.dot(left, right, preferred_element_type=jnp.float32)


def rotary_tables(places):
    freqs = jnp.power(rope_base, -2.0 * jnp.arange(HEAD // 2).astype(jnp.float32) / HEAD)
    angles = places[:, None] * freqs[None, :]
    return (jnp.cos(angles)[:, None, :], jnp.sin(angles)[:, None, :])


def rotate(values, cosines, sines):
    half_dim = values.shape[-1] // 2
    first = values[..., :half_dim]
    second = values[..., half_dim:]
    return jnp.concatenate(
        [first * cosines - second * sines, second * cosines + first * sines], axis=-1
    )


def layer_norm(hidden, gain, offset):
    average = jnp.mean(hidden, -1, keepdims=True)
    centred = hidden - average
    variance = jnp.mean(centred * centred, -1, keepdims=True)
    return centred * lax.rsqrt(variance + 1e-05) * gain + offset


def normalize(pooled):
    return pooled * lax.rsqrt(jnp.sum(pooled * pooled, -1, keepdims=True) + 1e-06)


def layout(tower_id, query_len, doc_len, count):
    places = jnp.arange(count)
    span = jnp.where(tower_id == 0, QLEN, count)
    segment = places // span
    offset_in = places - segment * span
    slots = jnp.arange(QPD)
    seg_limit = jnp.where(tower_id == 0, query_len, doc_len[0] * jnp.ones_like(query_len))
    limit = jnp.sum(jnp.where(segment[:, None] == slots[None, :], seg_limit[None, :], 0), axis=1)
    valid = offset_in < limit
    allowed = (segment[:, None] == segment[None, :]) & valid[None, :]
    member = (segment[None, :] == slots[:, None]) & valid[None, :]
    pool_matrix = jnp.where(member, 1.0 / seg_limit[:, None].astype(jnp.float32), 0.0)
    return (offset_in.astype(jnp.float32), allowed, pool_matrix)


def swish_product(left, right):
    return jax.nn.silu(left) * right


def on_device(
    tokens,
    query_lengths,
    doc_lengths,
    positives,
    w_qkv,
    w_out,
    w_gate,
    w_up,
    w_down,
    ln1_gain,
    first_layernorm_shift,
    ln2_gain,
    ln2_bias,
):
    tower_id = lax.axis_index(TOWER)
    device_id = lax.axis_index(DP)
    groups = lax.axis_size(DP)
    full = (
        lax.all_gather(w_qkv, DP, axis=0, tiled=True),
        lax.all_gather(w_out, DP, axis=0, tiled=True),
        lax.all_gather(w_gate, DP, axis=0, tiled=True),
        lax.all_gather(w_up, DP, axis=0, tiled=True),
        lax.all_gather(w_down, DP, axis=0, tiled=True),
        lax.all_gather(ln1_gain, DP, axis=0, tiled=True),
        lax.all_gather(first_layernorm_shift, DP, axis=0, tiled=True),
        lax.all_gather(ln2_gain, DP, axis=0, tiled=True),
        lax.all_gather(ln2_bias, DP, axis=0, tiled=True),
    )
    qkv_full, out_full, gate_full, up_full, down_full = (
        full[0],
        full[1],
        full[2],
        full[3],
        full[4],
    )
    gain_one = full[5].astype(jnp.float32)
    bias_one = full[6].astype(jnp.float32)
    gain_two = full[7].astype(jnp.float32)
    bias_two = full[8].astype(jnp.float32)
    inputs = tokens[0]
    count = inputs.shape[0]
    places, allowed, pool_matrix = layout(tower_id, query_lengths, doc_lengths, count)
    cosines, sines = rotary_tables(places)
    packed = product(inputs, qkv_full)
    raw_query = packed[:, :D].reshape(count, HEADS, HEAD)
    raw_key = packed[:, D : 2 * D].reshape(count, HEADS, HEAD)

    def rotate_both(first, second):
        return (rotate(first, cosines, sines), rotate(second, cosines, sines))

    rotated, rotary_back = jax.vjp(rotate_both, raw_query, raw_key)
    query_low = rotated[0].astype(jnp.bfloat16)
    key_low = rotated[1].astype(jnp.bfloat16)
    value_low = packed[:, 2 * D :].reshape(count, HEADS, HEAD).astype(jnp.bfloat16)
    scale = HEAD ** (-0.5)

    def masked_scores():
        scores = (
            jnp.einsum("ihd,jhd->hij", query_low, key_low, preferred_element_type=jnp.float32)
            * scale
        )
        return jnp.where(allowed[None], scores, -1e30)

    scores = masked_scores()
    peak = jnp.max(scores, -1, keepdims=True)
    log_total = peak + jnp.log(jnp.sum(jnp.exp(scores - peak), -1, keepdims=True))
    probs_low = jnp.exp(scores - log_total).astype(jnp.bfloat16)
    mixed = jnp.einsum("hij,jhd->ihd", probs_low, value_low, preferred_element_type=jnp.float32)
    mixed_low = mixed.reshape(count, D).astype(jnp.bfloat16)
    attended = product(mixed_low, out_full)
    inputs_wide = inputs.astype(jnp.float32)
    normed_one, norm_one_back = jax.vjp(layer_norm, inputs_wide + attended, gain_one, bias_one)
    feed = normed_one.astype(jnp.bfloat16)
    gate = product(feed, gate_full)
    up_part = product(feed, up_full)
    hidden_wide, swish_back = jax.vjp(swish_product, gate, up_part)
    hidden = hidden_wide.astype(jnp.bfloat16)
    branch = product(hidden, down_full)
    normed_two, norm_two_back = jax.vjp(layer_norm, normed_one + branch, gain_two, bias_two)
    pooled = jnp.dot(pool_matrix, normed_two, precision=exact_product_accuracy)
    embedded, normal_back = jax.vjp(normalize, pooled)
    gathered = lax.all_gather(embedded, (TOWER, DP), axis=0, tiled=True)
    queries_total = groups * QPD
    gathered_query_rows = gathered[:queries_total]
    gathered_document_rows = gathered[queries_total:].reshape(groups, QPD, D)[:, 0]
    pairwise_affinity_matrix = (
        jnp.dot(gathered_query_rows, gathered_document_rows.T, precision=exact_product_accuracy)
        / contrast_sharpness_factor
    )
    peak_logit = jnp.max(pairwise_affinity_matrix, -1, keepdims=True)
    log_partition_norm = peak_logit + jnp.log(
        jnp.sum(jnp.exp(pairwise_affinity_matrix - peak_logit), -1, keepdims=True)
    )
    columns = lax.broadcasted_iota(jnp.int32, pairwise_affinity_matrix.shape, 1)
    matching_labels = columns == positives[:, None]
    picked = jnp.sum(jnp.where(matching_labels, pairwise_affinity_matrix, 0.0), -1, keepdims=True)
    total = jnp.sum(log_partition_norm - picked)
    loss = total / queries_total
    similarity_gradient = (
        jnp.exp(pairwise_affinity_matrix - log_partition_norm) - matching_labels.astype(jnp.float32)
    ) / contrast_sharpness_factor
    own_rows = lax.dynamic_slice_in_dim(similarity_gradient, device_id * QPD, QPD, 0)
    query_side = jnp.dot(own_rows, gathered_document_rows, precision=exact_product_accuracy)
    own_column = lax.dynamic_slice_in_dim(similarity_gradient, device_id, 1, 1)
    doc_side = jnp.dot(own_column.T, gathered_query_rows, precision=exact_product_accuracy)
    doc_side = jnp.concatenate([doc_side, jnp.zeros((QPD - 1, D), jnp.float32)], 0)
    embed_grad = jnp.where(tower_id == 0, query_side, doc_side)
    pooled_grad = normal_back(embed_grad)[0]
    top_grad = jnp.dot(pool_matrix.T, pooled_grad, precision=exact_product_accuracy)
    sum_two, gain_two_grad, bias_two_grad = norm_two_back(top_grad)
    attention_input_cotangent, out_back, gate_back, up_back, down_back = (
        qkv_full,
        out_full,
        gate_full,
        up_full,
        down_full,
    )
    branch_low = sum_two.astype(jnp.bfloat16)
    down_grad = product(hidden.T, branch_low)
    hidden_grad = product(branch_low, down_back.T)
    gate_grad_wide, up_grad_wide = swish_back(hidden_grad)
    gate_low = gate_grad_wide.astype(jnp.bfloat16)
    up_low = up_grad_wide.astype(jnp.bfloat16)
    gate_weight_grad = product(feed.T, gate_low)
    up_weight_grad = product(feed.T, up_low)
    feed_grad = sum_two + product(gate_low, gate_back.T) + product(up_low, up_back.T)
    sum_one, gain_one_grad, bias_one_grad = norm_one_back(feed_grad)
    attend_low = sum_one.astype(jnp.bfloat16)
    out_grad = product(mixed_low.T, attend_low)
    mixed_grad = product(attend_low, out_back.T).astype(jnp.bfloat16).reshape(count, HEADS, HEAD)
    probs_again = jnp.exp(masked_scores() - log_total)
    prob_grad = jnp.einsum(
        "ihd,jhd->hij", mixed_grad, value_low, preferred_element_type=jnp.float32
    )
    score_grad = probs_again * (prob_grad - jnp.sum(probs_again * prob_grad, -1, keepdims=True))
    score_low = score_grad.astype(jnp.bfloat16)
    query_grad = (
        jnp.einsum("hij,jhd->ihd", score_low, key_low, preferred_element_type=jnp.float32) * scale
    )
    key_grad = (
        jnp.einsum("hij,ihd->jhd", score_low, query_low, preferred_element_type=jnp.float32) * scale
    )
    value_grad = jnp.einsum(
        "hij,ihd->jhd",
        probs_again.astype(jnp.bfloat16),
        mixed_grad,
        preferred_element_type=jnp.float32,
    )
    raw_query_grad, raw_key_grad = rotary_back((query_grad, key_grad))
    packed_grad = jnp.concatenate(
        [
            raw_query_grad.reshape(count, D),
            raw_key_grad.reshape(count, D),
            value_grad.reshape(count, D),
        ],
        1,
    ).astype(jnp.bfloat16)
    qkv_grad = product(inputs.T, packed_grad)
    input_grad = sum_one + product(packed_grad, attention_input_cotangent.T)
    gradients = (
        qkv_grad,
        out_grad,
        gate_weight_grad,
        up_weight_grad,
        down_grad,
        gain_one_grad,
        bias_one_grad,
        gain_two_grad,
        bias_two_grad,
    )
    partial_sums = (
        lax.psum_scatter(gradients[0], DP, scatter_dimension=0, tiled=True),
        lax.psum_scatter(gradients[1], DP, scatter_dimension=0, tiled=True),
        lax.psum_scatter(gradients[2], DP, scatter_dimension=0, tiled=True),
        lax.psum_scatter(gradients[3], DP, scatter_dimension=0, tiled=True),
        lax.psum_scatter(gradients[4], DP, scatter_dimension=0, tiled=True),
        lax.psum_scatter(gradients[5], DP, scatter_dimension=0, tiled=True),
        lax.psum_scatter(gradients[6], DP, scatter_dimension=0, tiled=True),
        lax.psum_scatter(gradients[7], DP, scatter_dimension=0, tiled=True),
        lax.psum_scatter(gradients[8], DP, scatter_dimension=0, tiled=True),
    )
    tower_halves = (
        lax.psum_scatter(
            partial_sums[0].astype(jnp.bfloat16), TOWER, scatter_dimension=0, tiled=True
        ).astype(jnp.float32),
        lax.psum_scatter(
            partial_sums[1].astype(jnp.bfloat16), TOWER, scatter_dimension=0, tiled=True
        ).astype(jnp.float32),
        lax.psum_scatter(
            partial_sums[2].astype(jnp.bfloat16), TOWER, scatter_dimension=0, tiled=True
        ).astype(jnp.float32),
        lax.psum_scatter(
            partial_sums[3].astype(jnp.bfloat16), TOWER, scatter_dimension=0, tiled=True
        ).astype(jnp.float32),
        lax.psum_scatter(
            partial_sums[4].astype(jnp.bfloat16), TOWER, scatter_dimension=0, tiled=True
        ).astype(jnp.float32),
        lax.psum_scatter(
            partial_sums[5].astype(jnp.bfloat16), TOWER, scatter_dimension=0, tiled=True
        ).astype(jnp.float32),
        lax.psum_scatter(
            partial_sums[6].astype(jnp.bfloat16), TOWER, scatter_dimension=0, tiled=True
        ).astype(jnp.float32),
        lax.psum_scatter(
            partial_sums[7].astype(jnp.bfloat16), TOWER, scatter_dimension=0, tiled=True
        ).astype(jnp.float32),
        lax.psum_scatter(
            partial_sums[8].astype(jnp.bfloat16), TOWER, scatter_dimension=0, tiled=True
        ).astype(jnp.float32),
    )
    shares = (
        lax.all_gather(tower_halves[0].astype(jnp.bfloat16), TOWER, axis=0, tiled=True).astype(
            jnp.float32
        ),
        lax.all_gather(tower_halves[1].astype(jnp.bfloat16), TOWER, axis=0, tiled=True).astype(
            jnp.float32
        ),
        lax.all_gather(tower_halves[2].astype(jnp.bfloat16), TOWER, axis=0, tiled=True).astype(
            jnp.float32
        ),
        lax.all_gather(tower_halves[3].astype(jnp.bfloat16), TOWER, axis=0, tiled=True).astype(
            jnp.float32
        ),
        lax.all_gather(tower_halves[4].astype(jnp.bfloat16), TOWER, axis=0, tiled=True).astype(
            jnp.float32
        ),
        lax.all_gather(tower_halves[5].astype(jnp.bfloat16), TOWER, axis=0, tiled=True).astype(
            jnp.float32
        ),
        lax.all_gather(tower_halves[6].astype(jnp.bfloat16), TOWER, axis=0, tiled=True).astype(
            jnp.float32
        ),
        lax.all_gather(tower_halves[7].astype(jnp.bfloat16), TOWER, axis=0, tiled=True).astype(
            jnp.float32
        ),
        lax.all_gather(tower_halves[8].astype(jnp.bfloat16), TOWER, axis=0, tiled=True).astype(
            jnp.float32
        ),
    )
    query_rows = lax.dynamic_slice_in_dim(gathered_query_rows, device_id * QPD, QPD, 0)
    doc_row = lax.dynamic_slice_in_dim(gathered_document_rows, device_id, 1, 0)
    return (loss, query_rows, doc_row, input_grad[None]) + tuple(shares)


MESH = pl.DeviceIdType.MESH
BF = jnp.bfloat16
F32 = jnp.float32
LANES = 128


def dot_tt(left, right, precision=None):
    return lax.dot_general(
        left, right, (((1,), (1,)), ((), ())), preferred_element_type=F32, precision=precision
    )


def dot_t0(left, right, precision=None):
    return lax.dot_general(
        left, right, (((0,), (0,)), ((), ())), preferred_element_type=F32, precision=precision
    )


def rotary_constants(count):
    freqs = np.power(
        np.float32(rope_base), (-2.0 * np.arange(HEAD // 2) / HEAD).astype(np.float32)
    ).astype(np.float32)
    angles = (np.arange(count, dtype=np.float32)[:, None] * freqs[None, :]).astype(np.float64)
    cosines, sines = np.cos(angles), np.sin(angles)
    return (
        np.tile(np.concatenate([cosines, cosines], 1), (1, 2)).astype(np.float32),
        np.tile(np.concatenate([-sines, sines], 1), (1, 2)).astype(np.float32),
    )


def aligned(start, unit):
    return start if isinstance(start, int) else pl.multiple_of(start, unit)


def both(first, second):
    return jnp.logical_and(first, second)


def do(condition, action):
    if condition is None:
        action()
    else:
        pl.when(condition)(action)


class Plan:
    def __init__(self, groups, count, shard, shard_ff, vec):
        self.groups = groups
        self.line = groups // 4
        self.count = count
        self.shard = shard
        self.shard_ff = shard_ff
        self.vec = vec
        self.width_a = 4 * D
        self.half_a = 2 * D
        self.ff = shard_ff * groups
        self.half_ff = self.ff // 2
        self.stripe = 2 * shard_ff


def semaphores(plan):
    line, groups = plan.line, plan.groups
    dma = pltpu.SemaphoreType.DMA
    chunks_gu, chunks_a = 4, 4
    return dict(
        loc=dma((40,)),
        ra=dma((groups, 2)),
        sa_z=dma((2, line)),
        sa_x=dma((line, 2)),
        sa_y=dma((line, 2)),
        sa_c=dma((line, 2, 2)),
        rg=dma((groups, 2)),
        sg_z=dma((2, line, 2)),
        sg_x=dma((line, 2)),
        sg_c=dma((line, 2, 2)),
        rd=dma((line, 2, 2)),
        sd_x=dma((2,)),
        sd_z=dma((2, line, 2)),
        sd_c=dma((line, 2)),
        rv=dma((groups,)),
        sv=dma((groups,)),
        turn=pltpu.SemaphoreType.REGULAR,
        s_part=dma((D // (2 * LANES),)),
        r_part=dma((D // (2 * LANES),)),
        s_back=dma((line,)),
        r_back=dma((line,)),
        sx=dma((4,)),
        rx=dma((4,)),
        r_doc=dma((groups,)),
        s_doc=dma((groups,)),
        r_slope=dma((groups,)),
        s_slope=dma((groups,)),
        s_slope_q=dma((groups,)),
        r_query=dma((1,)),
        s_query=dma((1,)),
        s_ln=dma((line.bit_length() + 2,)),
        r_ln=dma((line.bit_length() + 2,)),
        gd_c=dma((2, line)),
        gd_z=dma((2, 2, line)),
        gd_x=dma((2,)),
        gd_y=dma((2,)),
        gg_c=dma((2, chunks_gu)),
        gg_x=dma((2, chunks_gu)),
        gg_z=dma((2, chunks_gu, 2, line)),
        gg_y=dma((2, chunks_gu)),
        ga_c=dma((2, 2, chunks_a)),
        ga_t=dma((2, chunks_a)),
        ga_x=dma((2, chunks_a)),
        ga_z=dma((2, chunks_a, 2, line)),
        ga_y=dma((2, chunks_a)),
        fin=dma((10,)),
    )


def buffers(plan):
    line, count, shard, groups = plan.line, plan.count, plan.shard, plan.groups
    pair = 2 * count
    v = pltpu.VMEM
    return dict(
        wa=v((line, 2, 2, shard, plan.width_a), BF),
        wg=v((line, 2, 2, shard, plan.ff), BF),
        wd=v((line, 2, plan.shard_ff, D), BF),
        tok=v((count, D), BF),
        vt=v((groups, 8, LANES), F32),
        vec=v((8, D), F32),
        cos=v((count, LANES), F32),
        sin=v((count, LANES), F32),
        hide=v((count, count), F32),
        pw=v((count, 1), F32),
        qkv=v((count, 3 * D), BF),
        probs=v((HEADS, count, count), F32),
        mixed=v((count, D), BF),
        mixt=v((D, count), BF),
        tokt=v((D, count), BF),
        h1=v((count, D), F32),
        rs1=v((count, 1), F32),
        n1=v((count, D), F32),
        feed=v((pair, D), BF),
        feedt=v((D, pair), BF),
        gate=v((pair, plan.half_ff), F32),
        up=v((pair, plan.half_ff), F32),
        hidt=v((plan.half_ff, pair), BF),
        dgu=v((pair, plan.ff), BF),
        bown=v((count, D), F32),
        bsend=v((count, D), BF),
        brecv=v((count, D), BF),
        xh2=v((count, D), F32),
        rs2=v((count, 1), F32),
        xh2b=v((count, D), F32),
        rs2b=v((count, 1), F32),
        pwb=v((count, 1), F32),
        brest=v((count, D), BF),
        dpoolb=v((8, D), F32),
        dpoolr=v((8, D), F32),
        dbr=v((pair, D), BF),
        dsend=v((count, D), BF),
        drecv=v((count, D), BF),
        datt=v((count, D), BF),
        pool=v((8, D), F32),
        dpool=v((8, D), F32),
        emb=v((8, D), F32),
        embd=v((1, D + LANES), F32),
        embq=v((QPD, D), F32),
        dbuf=v((groups, 1, D + LANES), F32),
        cbuf=v((groups, 1, D), F32),
        csend=v((groups, 1, D), F32),
        qrecv=v((QPD, D), F32),
        dflat=v((groups, D), F32),
        ln=v((line.bit_length() + 3, 8, D), F32),
        lnr=v((line.bit_length() + 2, 8, D), F32),
        gd=v((line, 2, plan.shard_ff, D), BF),
        gd_rc=v((line, plan.shard_ff, D), BF),
        gd_rz=v((line + 1, plan.shard_ff, D), BF),
        gd_rx=v((plan.shard_ff, D), BF),
        gd_f=v((plan.shard_ff, D), BF),
        gg=v((line, 2, 2, shard, plan.ff), BF),
        gg_rc=v((line, 2, shard, plan.ff), BF),
        gg_rx=v((line, shard, plan.ff), BF),
        gg_rz=v((line + 1, shard, plan.ff), BF),
        gg_f=v((shard, plan.ff), BF),
        ga_rc=v((line, 2, shard, plan.width_a), BF),
        ga_rt=v((line, 2, shard, plan.half_a), BF),
        ga_rx=v((line, shard, plan.half_a), BF),
        ga_rz=v((line + 1, shard, plan.half_a), BF),
        ga_f=v((shard, plan.half_a), BF),
    )


class Operands(NamedTuple):
    qlen: Any
    dlen: Any
    pos: Any
    i_tok: Any
    tcos: Any
    tsin: Any
    g_one: Any
    b_one: Any
    g_two: Any
    b_two: Any
    i_qkv: Any
    i_out: Any
    i_gate: Any
    i_up: Any
    i_down: Any


class Results(NamedTuple):
    o_tok: Any
    o_a: Any
    o_gu: Any
    o_dn: Any
    o_vec: Any
    o_q: Any
    o_d: Any
    o_loss: Any


def whole_step(plan, *refs):
    names = (Operands._fields + Results._fields + tuple(buffers(plan)) + tuple(semaphores(plan)))
    r = SimpleNamespace(**dict(zip(names, refs, strict=True)))
    line, groups, count = plan.line, plan.groups, plan.count
    shard, shard_ff, stripe = plan.shard, plan.shard_ff, plan.stripe
    half_a, half_ff, ff = plan.half_a, plan.half_ff, plan.ff
    quarter = QLEN
    shift = QLEN.bit_length() - 1

    t = lax.axis_index(TOWER)
    me = lax.axis_index(DP)
    z = me // 4
    x = (me // 2) % 2
    c = me % 2

    def at(zz, xx, cc):
        return (zz * 2 + xx) * 2 + cc

    dev_x = {TOWER: t, DP: at(z, 1 - x, c)}
    dev_c = {TOWER: t, DP: at(z, x, 1 - c)}
    dev_y = {TOWER: 1 - t, DP: me}

    def dev_z(zz):
        return {TOWER: t, DP: at(zz, x, c)}

    pending, tail = [], []

    def copy(src, dst, ssem, rsem, dev):
        return pltpu.make_async_remote_copy(
            src_ref=src, dst_ref=dst, send_sem=ssem, recv_sem=rsem,
            device_id=dev, device_id_type=MESH,
        )

    def send(cond, what, keep=pending):
        do(cond, what.start)
        keep.append((cond, what))

    def settle(keep):
        for cond, what in keep:
            do(cond, what.wait_send)
        keep.clear()

    def got(cond, ref, rsem):
        do(cond, copy(ref, ref, r.s_query.at[0], rsem, dev_x).wait_recv)

    wa, wg, wd = r.wa, r.wg, r.wd
    out_w = half_a - 3 * D // 2
    local = []

    def near(src, dst, cond=None):
        what = pltpu.make_async_copy(src, dst, r.loc.at[len(local)])
        do(cond, what.start)
        local.append((cond, what))

    third = 3 * D // 2
    half_d = D // 2
    for h in range(2):
        for k in range(3):
            near(r.i_qkv.at[:, pl.ds(k * D + h * half_d, half_d)],
                 wa.at[z, x, c, :, pl.ds(h * half_a + k * half_d, half_d)])
        near(r.i_out.at[:, pl.ds(h * out_w, out_w)],
             wa.at[z, x, c, :, pl.ds(h * half_a + third, out_w)])
    near(r.i_down, wd.at[z, c], x == t)
    near(r.i_tok, r.tok)
    for s in range(QPD):
        begin = aligned(s * QLEN * t, QLEN)
        near(r.tcos.at[pl.ds(begin, QLEN)], r.cos.at[pl.ds(s * QLEN, QLEN)])
        near(r.tsin.at[pl.ds(begin, QLEN)], r.sin.at[pl.ds(s * QLEN, QLEN)])
    part_ff = half_ff // 2
    per_part = line // 2

    def stripe_at(k, s):
        return (2 * (s // per_part) + k) * part_ff + (s % per_part) * stripe

    for s in range(line):
        for k, ref in enumerate((r.i_gate, r.i_up)):
            near(ref.at[:, pl.ds(aligned((2 * s + t) * stripe, LANES), stripe)],
                 wg.at[z, x, c, :, pl.ds(stripe_at(k, s), stripe)])

    r.vt[me] = jnp.zeros((8, LANES), F32)
    for k, ref in enumerate((r.g_one, r.b_one, r.g_two, r.b_two)):
        r.vt[me, pl.ds(k, 1), pl.ds(0, plan.vec)] = ref[...].astype(F32)

    barrier = pltpu.get_barrier_semaphore()

    def greet(j, carry):
        other = jnp.logical_or(j // groups != t, j % groups != me)

        @pl.when(other)
        def _():
            pl.semaphore_signal(
                barrier, inc=1, device_id={TOWER: j // groups, DP: j % groups},
                device_id_type=MESH,
            )

        return carry

    lax.fori_loop(0, 2 * groups, greet, 0)
    pl.semaphore_wait(barrier, 2 * groups - 1)
    for cond, what in local:
        do(cond, what.wait)

    def piece_a(zz, xx, cc, h):
        return wa.at[zz, xx, cc, :, pl.ds(aligned(h * half_a, LANES), half_a)]

    def send_a(cond, sem, zz, xx, h, dev):
        ref = piece_a(zz, xx, c, h)
        send(cond, copy(ref, ref, sem, r.ra.at[at(zz, xx, c), h], dev))

    def got_a(cond, zz, xx, cc, h):
        got(cond, piece_a(zz, xx, cc, h), r.ra.at[at(zz, xx, cc), h])

    def sides(step):
        return ((z - step, z >= step, z < line - 1, z + 1), (z + step, z < line - step, z > 0, z - 1))

    def a_start():
        for way, (_, _, on, nxt) in enumerate(sides(0)):
            send_a(on, r.sa_z.at[way, z], z, x, t, dev_z(nxt))
        send_a(None, r.sa_x.at[z, t], z, x, t, dev_x)
        send_a(x != t, r.sa_x.at[z, 1 - t], z, x, 1 - t, dev_x)
        send_a(None, r.sa_c.at[z, x, t], z, x, t, dev_c)
        send_a(None, r.sa_c.at[z, x, 1 - t], z, x, 1 - t, dev_c)

    def a_round(step, way):
        zz, there, on, nxt = sides(step)[way]
        got_a(there, zz, x, c, t)
        send_a(both(there, on), r.sa_z.at[way, zz], zz, x, t, dev_z(nxt))
        send_a(there, r.sa_x.at[zz, t], zz, x, t, dev_x)
        send_a(there, r.sa_y.at[zz, x], zz, x, t, dev_y)
        send_a(there, r.sa_c.at[zz, x, t], zz, x, t, dev_c)

    def a_cross(step, way):
        zz, there, _, _ = sides(step)[way]
        got_a(there, zz, 1 - x, c, t)
        send_a(there if step else x == t, r.sa_y.at[zz, 1 - x], zz, 1 - x, t, dev_y)
        send_a(there, r.sa_c.at[zz, 1 - x, t], zz, 1 - x, t, dev_c)

    def a_tower(step, way):
        zz, there, _, _ = sides(step)[way]
        for xx in (x, 1 - x) if step else (1 - x,):
            got_a(there, zz, xx, c, 1 - t)
            send_a(there, r.sa_c.at[zz, xx, 1 - t], zz, xx, 1 - t, dev_c)

    def a_sibling(h):
        for zz in range(line):
            for xx in range(2):
                got_a(None, zz, xx, 1 - c, h)

    def piece_g(zz, xx, cc, h):
        return wg.at[zz, xx, cc, :, pl.ds(h * half_ff, half_ff)]

    def send_g(cond, sem, zz, xx, h, dev):
        ref = piece_g(zz, xx, c, h)
        send(cond, copy(ref, ref, sem, r.rg.at[at(zz, xx, c), h], dev))

    def got_g(cond, zz, xx, cc, h):
        got(cond, piece_g(zz, xx, cc, h), r.rg.at[at(zz, xx, cc), h])

    def g_start(h):
        for way, (_, _, on, nxt) in enumerate(sides(0)):
            send_g(on, r.sg_z.at[way, z, h], z, x, h, dev_z(nxt))

    def g_line(step, way, h):
        zz, there, on, nxt = sides(step)[way]
        got_g(there, zz, x, c, h)
        send_g(both(there, on), r.sg_z.at[way, zz, h], zz, x, h, dev_z(nxt))

    def g_spread(step, way, h):
        zz, there, _, _ = sides(step)[way]
        send_g(there, r.sg_x.at[zz, h], zz, x, h, dev_x)
        send_g(there, r.sg_c.at[zz, x, h], zz, x, h, dev_c)

    def g_cross(step, way, h):
        zz, there, _, _ = sides(step)[way]
        got_g(there, zz, 1 - x, c, h)
        send_g(there, r.sg_c.at[zz, 1 - x, h], zz, 1 - x, h, dev_c)

    def g_sibling(h):
        for zz in range(line):
            for xx in range(2):
                got_g(None, zz, xx, 1 - c, h)

    part_d = (pl.ds(0, 4 * LANES), pl.ds(4 * LANES, D - 4 * LANES))

    def send_d(cond, sem, zz, h, dev):
        ref = wd.at[zz, c, :, part_d[h]]
        send(cond, copy(ref, ref, sem, r.rd.at[zz, c, h], dev))

    def got_d(cond, zz, cc, h):
        got(cond, wd.at[zz, cc, :, part_d[h]], r.rd.at[zz, cc, h])

    def d_cross(h):
        send_d(x == t, r.sd_x.at[h], z, h, dev_x)

    def d_start(h):
        got_d(x != t, z, c, h)
        for way, (_, _, on, nxt) in enumerate(sides(0)):
            send_d(on, r.sd_z.at[way, z, h], z, h, dev_z(nxt))
        send_d(None, r.sd_c.at[z, h], z, h, dev_c)

    def d_round(step, way, ends, h):
        zz, there, on, nxt = sides(step)[way]
        cond = both(there, jnp.logical_not(on) if ends else on)
        got_d(cond, zz, c, h)
        if not ends:
            send_d(cond, r.sd_z.at[way, zz, h], zz, h, dev_z(nxt))
        send_d(cond, r.sd_c.at[zz, h], zz, h, dev_c)

    def d_sibling(h):
        for zz in range(line):
            got_d(None, zz, 1 - c, h)

    def v_send(j, carry):
        @pl.when(j != me)
        def _():
            copy(r.vt.at[me], r.vt.at[me], r.sv.at[j], r.rv.at[me],
                 {TOWER: t, DP: j}).start()

        return carry

    def v_wait(j, carry):
        @pl.when(j != me)
        def _():
            copy(r.vt.at[me], r.vt.at[j], r.sv.at[j], r.rv.at[j],
                 {TOWER: t, DP: j}).wait()

        return carry

    a_start()
    lax.fori_loop(0, groups, v_send, 0)

    tok = r.tok
    rows = lax.broadcasted_iota(jnp.int32, (count, count), 0)
    cols = lax.broadcasted_iota(jnp.int32, (count, count), 1)
    seg = cols >> shift
    limit = jnp.zeros_like(cols)
    for s in range(QPD):
        limit = jnp.where(seg == s, r.qlen[s], limit)
    limit = limit * (1 - t) + r.dlen[0] * t
    place = cols - seg * (quarter * (1 - t))
    apart = ((rows >> shift) - seg) * (1 - t)
    seen = both(apart == 0, place < limit)
    r.hide[...] = jnp.where(seen, 0.0, -1e30)
    for s in range(QPD):
        part = pl.ds(s * quarter, quarter)
        for tower, weights in ((t, r.pw), (1 - t, r.pwb)):
            length = jnp.full((quarter, 1), r.qlen[s] * (1 - tower) + r.dlen[0] * tower, jnp.int32)
            slot = lax.broadcasted_iota(jnp.int32, (quarter, 1), 0) + s * quarter * tower
            weights[part, :] = jnp.where(slot < length, 1.0 / length.astype(F32), 0.0)
    lanes = lax.broadcasted_iota(jnp.int32, (count, LANES), 1)
    first_head = lanes < HEAD
    low_half = (lanes & (HEAD - 1)) < HEAD // 2

    def swap(a):
        return jnp.where(low_half, pltpu.roll(a, LANES - HEAD // 2, 1), pltpu.roll(a, HEAD // 2, 1))

    def turn(a):
        return a * r.cos[...] + swap(a) * r.sin[...]

    def turn_back(a):
        return a * r.cos[...] - swap(a) * r.sin[...]

    def transpose_into(dst, src, width):
        def body(j, carry):
            o = aligned(j * LANES, LANES)
            dst[pl.ds(o, LANES), :] = src[:, pl.ds(o, LANES)].T
            return carry

        lax.fori_loop(0, width // LANES, body, 0)

    def wide(ref, lo, n):
        return ref[:, :, :, :, pl.ds(lo, n)].reshape(groups * shard, n)

    def widen_vec():
        lane = lax.broadcasted_iota(jnp.int32, (8, LANES), 1)
        parts = [jnp.zeros((8, LANES), F32) for _ in range(D // LANES)]
        for j in range(groups):
            block, first = divmod(j * plan.vec, LANES)
            piece = r.vt[j]
            if first:
                piece = pltpu.roll(piece, first, 1)
            parts[block] = parts[block] + jnp.where(lane >= first, piece, 0.0)
            if first + plan.vec > LANES:
                parts[block + 1] = parts[block + 1] + jnp.where(lane < first, piece, 0.0)
        r.vec[...] = jnp.concatenate(parts, axis=1)

    pairs = D // LANES
    half_pairs = pairs // 2

    scale = HEAD ** (-0.5)

    def project(h):
        for k in range(3):
            packed = jnp.dot(tok[...], wide(wa, aligned(h * half_a + k * half_d, LANES), half_d),
                             preferred_element_type=F32)
            for i in range(half_pairs):
                part = packed[:, i * LANES : (i + 1) * LANES]
                if k < 2:
                    part = turn(part)
                if k == 0:
                    part = part * scale
                r.qkv[:, pl.ds(aligned(k * D + h * half_d + i * LANES, LANES), LANES)] = (
                    part.astype(BF))

    def triple(p):
        o = aligned(p * LANES, LANES)
        return tuple(r.qkv[:, pl.ds(k * D + o, LANES)] for k in range(3))

    def only(h, a):
        return jnp.where(first_head if h == 0 else jnp.logical_not(first_head), a, jnp.zeros_like(a))

    def attend(p):
        q2, k2, v2 = triple(p)
        outs = []
        for h in range(2):
            scores = dot_tt(only(h, q2), k2) + r.hide[...]
            grown = jnp.exp(scores - jnp.max(scores, -1, keepdims=True))
            probs = grown * (1.0 / jnp.sum(grown, -1, keepdims=True))
            r.probs[2 * p + h] = probs
            outs.append(jnp.dot(probs.astype(BF), v2, preferred_element_type=F32))
        o = aligned(p * LANES, LANES)
        r.mixed[:, pl.ds(o, LANES)] = jnp.where(first_head, outs[0], outs[1]).astype(BF)

    def over_pairs(h, body, lo=0, hi=half_pairs):
        def step(i, carry):
            body(h * half_pairs + i)
            return carry

        lax.fori_loop(lo, hi, step, 0)

    def vectors():
        lax.fori_loop(0, groups, v_wait, 0)
        widen_vec()

    def out_project():
        for h in range(2):
            part = jnp.dot(r.mixed[...], wide(wa, h * half_a + third, out_w),
                           preferred_element_type=F32)
            r.h1[:, pl.ds(h * out_w, out_w)] = tok[:, pl.ds(h * out_w, out_w)].astype(F32) + part

    def moments(h):
        centred = h - jnp.mean(h, -1, keepdims=True)
        return centred, lax.rsqrt(jnp.mean(centred * centred, -1, keepdims=True) + 1e-05)

    blocks = count // quarter

    def norm_one(b, carry):
        part = pl.ds(aligned(b * quarter, quarter), quarter)
        centred, inverse = moments(r.h1[part, :])
        hat = centred * inverse
        normed = hat * r.vec[0:1, :] + r.vec[1:2, :]
        r.h1[part, :] = hat
        r.rs1[part, :] = inverse
        r.n1[part, :] = normed
        r.feed[pl.ds(aligned(t * count + b * quarter, quarter), quarter), :] = (
            normed.astype(BF))
        return carry

    mine = pl.ds(aligned(t * count, count), count)
    theirs = pl.ds(aligned((1 - t) * count, count), count)

    def swap_rows(k, src, dst):
        send(None, copy(src, dst, r.sx.at[k], r.rx.at[k], dev_y), tail)

    def got_rows(k, ref):
        got(None, ref, r.rx.at[k])

    def norm_rows():
        lax.fori_loop(0, blocks, norm_one, 0)
        swap_rows(0, r.feed.at[mine], r.feed.at[mine])

    step_ff = 2 * LANES

    steps_part = part_ff // step_ff

    def gated(part):
        def body(j, carry):
            o = aligned(part * part_ff + j * step_ff, step_ff)
            w = 2 * part * part_ff + j * step_ff
            gate = jnp.dot(r.feed[...], wide(wg, aligned(w, step_ff), step_ff),
                           preferred_element_type=F32)
            up = jnp.dot(r.feed[...], wide(wg, aligned(w + part_ff, step_ff), step_ff),
                         preferred_element_type=F32)
            r.gate[:, pl.ds(o, step_ff)] = gate
            r.up[:, pl.ds(o, step_ff)] = up
            r.dgu[:, pl.ds(o, step_ff)] = (gate * jax.nn.sigmoid(gate) * up).astype(BF)
            return carry

        lax.fori_loop(0, steps_part, body, 0)

    def down(rows_of, store, which=range(D // (2 * LANES))):
        def body(j):
            o = j * step_ff
            w = wd[:, :, :, pl.ds(o, step_ff)].reshape(half_ff, step_ff)
            store(o, jnp.dot(r.dgu[rows_of, pl.ds(0, half_ff)], w, preferred_element_type=F32))

        for j in which:
            body(j)

    def keep_send(o, val):
        span = pl.ds(o, step_ff)
        r.bsend[:, span] = val.astype(BF)
        send(None, copy(r.bsend.at[:, span], r.brecv.at[:, span], r.s_part.at[o // step_ff],
                        r.r_part.at[o // step_ff], dev_y), tail)

    def keep_own(o, val):
        r.bown[:, pl.ds(o, step_ff)] = val
        r.dsend[:, pl.ds(o, step_ff)] = val.astype(BF)

    rest = copy(r.dsend, r.brest, r.sx.at[1], r.rx.at[1], dev_y)

    def norm_two_partner():
        got_rows(1, r.brest)

        def body(b, carry):
            part = pl.ds(aligned(b * quarter, quarter), quarter)
            feed = r.feed[pl.ds(aligned((1 - t) * count + b * quarter, quarter), quarter), :]
            h = feed.astype(F32) + (r.bsend[part, :].astype(F32) + r.brest[part, :].astype(F32))
            centred, inverse = moments(h)
            r.xh2b[part, :] = centred * inverse
            r.rs2b[part, :] = inverse
            return carry

        lax.fori_loop(0, blocks, body, 0)

    d_cross(1)
    g_start(1)
    a_round(1, 0)
    a_cross(0, 0)
    a_round(1, 1)
    g_spread(0, 0, 0)
    d_cross(0)
    g_start(0)
    a_cross(1, 0)
    a_round(2, 1)
    a_round(2, 0)
    a_round(3, 0)
    g_line(1, 0, 1)
    vectors()
    transpose_into(r.tokt, tok, D)
    g_line(1, 0, 0)
    g_line(1, 1, 1)
    g_line(1, 1, 0)
    a_cross(1, 1)
    a_round(3, 1)
    a_tower(1, 0)
    g_spread(1, 1, 1)
    g_spread(1, 0, 0)
    d_start(1)
    g_line(2, 1, 1)
    d_round(1, 0, False, 1)
    a_tower(0, 0)
    g_spread(0, 0, 1)
    a_cross(2, 0)
    a_cross(2, 1)
    a_cross(3, 0)
    a_tower(1, 1)
    g_line(2, 0, 1)
    g_spread(2, 1, 1)
    g_line(2, 0, 0)
    a_cross(3, 1)
    d_round(1, 1, False, 1)
    d_round(2, 0, False, 1)
    a_sibling(t)
    project(t)
    over_pairs(t, attend, 0, 1)
    g_line(2, 1, 0)
    d_start(0)
    over_pairs(t, attend, 1, 2)
    a_tower(2, 1)
    a_tower(2, 0)
    g_spread(2, 0, 0)
    g_spread(2, 1, 0)
    g_spread(1, 0, 1)
    a_tower(3, 1)
    over_pairs(t, attend, 2, 3)
    g_line(3, 1, 1)
    a_tower(3, 0)
    g_cross(0, 0, 0)
    g_spread(3, 1, 1)
    g_cross(1, 1, 1)
    d_round(1, 1, True, 1)
    a_sibling(1 - t)
    project(1 - t)
    over_pairs(1 - t, attend, 0, 2)
    g_line(3, 0, 1)
    over_pairs(1 - t, attend, 2, 3)
    d_round(1, 1, False, 0)
    g_spread(2, 0, 1)
    out_project()
    g_line(3, 1, 0)
    d_round(2, 1, True, 1)
    g_spread(3, 1, 0)
    norm_rows()
    g_line(3, 0, 0)
    g_spread(3, 0, 1)
    g_cross(2, 1, 1)
    d_round(2, 0, True, 1)
    g_cross(1, 0, 0)
    d_round(1, 0, True, 1)
    d_round(2, 1, False, 1)
    transpose_into(r.mixt, r.mixed, D)
    d_round(1, 0, False, 0)
    g_spread(1, 1, 0)
    d_round(2, 1, False, 0)
    d_round(1, 1, True, 0)
    g_cross(2, 0, 0)
    g_cross(2, 0, 1)
    g_cross(3, 1, 0)
    g_cross(3, 1, 1)
    d_round(2, 0, False, 0)
    g_spread(3, 0, 0)
    g_cross(2, 1, 0)
    g_cross(0, 0, 1)
    d_round(3, 1, True, 1)
    g_cross(3, 0, 1)
    g_cross(1, 0, 1)
    g_sibling(1)
    d_round(3, 0, True, 1)
    d_round(2, 1, True, 0)
    d_round(2, 0, True, 0)
    d_round(1, 0, True, 0)
    g_cross(3, 0, 0)
    g_cross(1, 1, 0)
    got_rows(0, r.feed.at[theirs])
    gated(1)
    g_sibling(0)
    gated(0)
    d_sibling(1)
    down(theirs, keep_send, (2,))
    d_round(3, 1, True, 0)
    d_round(3, 0, True, 0)
    d_sibling(0)
    down(theirs, keep_send, (0, 1))
    down(mine, keep_own)
    transpose_into(r.feedt, r.feed, D)
    transpose_into(r.hidt, r.dgu, half_ff)

    def factors(j, carry):
        span = pl.ds(aligned(j * LANES, LANES), LANES)
        gate, up = r.gate[:, span], r.up[:, span]
        sig = jax.nn.sigmoid(gate)
        r.gate[:, span] = gate * sig
        r.up[:, span] = up * (sig * (1.0 + gate * (1.0 - sig)))
        return carry

    lax.fori_loop(0, half_ff // LANES, factors, 0)
    for j in range(D // step_ff):
        got(None, r.brecv.at[:, pl.ds(j * step_ff, step_ff)], r.r_part.at[j])
        if j == 0:
            do(t == 0, rest.start)

    r.pool[...] = jnp.zeros((8, D), F32)

    def norm_two(b, carry):
        part = pl.ds(aligned(b * quarter, quarter), quarter)
        h = r.n1[part, :] + (r.bown[part, :] + r.brecv[part, :].astype(F32))
        centred, inverse = moments(h)
        hat = centred * inverse
        normed = hat * r.vec[2:3, :] + r.vec[3:4, :]
        r.xh2[part, :] = hat
        r.rs2[part, :] = inverse
        r.pool[pl.ds(b, 1), :] = jnp.sum(normed * r.pw[part, :], 0, keepdims=True)
        return carry

    lax.fori_loop(0, blocks, norm_two, 0)
    row8 = lax.broadcasted_iota(jnp.int32, (8, D), 0)

    @pl.when(t == 1)
    def _():
        all_rows = jnp.sum(r.pool[...], 0, keepdims=True)
        r.pool[...] = jnp.where(row8 == 0, all_rows, 0.0)

    pooled = r.pool[...]
    shrink = lax.rsqrt(jnp.sum(pooled * pooled, -1, keepdims=True) + 1e-06)
    r.emb[...] = pooled * shrink

    best = exact_product_accuracy
    r.dpool[...] = jnp.zeros((8, D), F32)
    r.ln[0] = jnp.zeros((8, D), F32)

    def to_all(tower, src, dst, ssem, rsem, others=False):
        def give(step, carry):
            j = (me + step) % groups
            copy(src(j), dst.at[me], ssem.at[j], rsem.at[me], {TOWER: tower, DP: j}).start()
            return carry

        lax.fori_loop(1 if others else 0, groups, give, 0)

    def from_all(dst, ssem, rsem, others=False):
        def take(step, carry):
            j = (me + step) % groups
            copy(dst.at[j], dst.at[j], ssem.at[j], rsem.at[j], dev_x).wait_recv()
            return carry

        lax.fori_loop(1 if others else 0, groups, take, 0)

    zero_row = jnp.zeros((1, D), F32)

    def norm_two_back(weights, slopes, hats, inverses, tower, own):
        def body(b, sums):
            part = pl.ds(aligned(b * quarter, quarter), quarter)
            top = weights[part, :] * slopes[pl.ds(b, 1), :]
            hat = hats[part, :]
            inner = top * r.vec[2:3, :]
            grad = inverses[part, :] * (
                inner - jnp.mean(inner, -1, keepdims=True)
                - hat * jnp.mean(inner * hat, -1, keepdims=True))
            r.dbr[pl.ds(aligned(tower * count + b * quarter, quarter), quarter), :] = (
                grad.astype(BF))
            if not own:
                return sums
            r.n1[part, :] = grad
            return (sums[0] + jnp.sum(top * hat, 0, keepdims=True),
                    sums[1] + jnp.sum(top, 0, keepdims=True))

        sums = lax.fori_loop(0, blocks, body, (zero_row, zero_row))
        if own:
            r.ln[0] = (r.ln[0] + jnp.where(row8 == 2, sums[0], 0.0)
                       + jnp.where(row8 == 3, sums[1], 0.0))

    def back_own():
        norm_two_back(r.pw, r.dpool, r.xh2, r.rs2, t, True)

    def back_partner():
        norm_two_back(r.pwb, r.dpoolb, r.xh2b, r.rs2b, 1 - t, False)

    def hidden_back(rows_of):
        def body(j, carry):
            o = aligned(j * stripe, LANES)
            w = wd[j].reshape(stripe, D)
            slope = dot_tt(r.dbr[rows_of, :], w)
            w_at = aligned((2 * (j // per_part)) * part_ff + (j % per_part) * stripe, LANES)
            r.dgu[rows_of, pl.ds(w_at, stripe)] = (
                slope * r.up[rows_of, pl.ds(o, stripe)]).astype(BF)
            r.dgu[rows_of, pl.ds(aligned(w_at + part_ff, LANES), stripe)] = (
                slope * r.gate[rows_of, pl.ds(o, stripe)]).astype(BF)
            return carry

        lax.fori_loop(0, line, body, 0)

    def slope_back(slope, emb, scale_of):
        return scale_of * (slope - emb * jnp.sum(slope * emb, -1, keepdims=True))

    def doc_slope():
        total = r.cbuf[0]
        for j in range(1, groups):
            total = total + r.cbuf[j]
        return total

    pool_slope = copy(r.dpool, r.dpoolr, r.sx.at[2], r.rx.at[2], dev_y)
    tail.append((t == 0, pool_slope))

    @pl.when(t == 0)
    def _():
        r.embq[...] = r.emb[0:QPD, :]
        from_all(r.dbuf, r.s_doc, r.r_doc)
        for j in range(groups):
            r.dflat[pl.ds(j, 1), :] = r.dbuf[j, :, pl.ds(0, D)]
        docs, queries = r.dflat[...], r.embq[...]
        logits = dot_tt(queries, docs, best) / contrast_sharpness_factor
        peak = jnp.max(logits, -1, keepdims=True)
        lse = peak + jnp.log(jnp.sum(jnp.exp(logits - peak), -1, keepdims=True))
        col = lax.broadcasted_iota(jnp.int32, (QPD, groups), 1)
        row = lax.broadcasted_iota(jnp.int32, (QPD, groups), 0)
        label = jnp.zeros((QPD, groups), jnp.int32)
        for s in range(QPD):
            label = jnp.where(row == s, r.pos[me * QPD + s], label)
        hot = jnp.where(col == label, 1.0, 0.0)
        slope = (jnp.exp(logits - lse) - hot) / contrast_sharpness_factor
        back = dot_t0(slope, queries, best)
        for j in range(groups):
            r.csend[j] = back[j : j + 1, :]
        to_all(1, lambda j: r.csend.at[j], r.cbuf, r.s_slope, r.r_slope)
        to_all(0, lambda j: r.csend.at[j], r.cbuf, r.s_slope_q, r.r_slope, True)
        r.cbuf[me] = r.csend[me]
        r.dpool[0:QPD, :] = jnp.dot(slope, docs, preferred_element_type=F32, precision=best)
        r.dpool[...] = slope_back(r.dpool[...], r.emb[...], shrink)
        pool_slope.start()
        picked = jnp.sum(jnp.where(hot > 0.5, logits, 0.0), -1, keepdims=True)
        total = jnp.sum(lse - picked, 0, keepdims=True)
        r.ln[0] = jnp.where(row8 == 4, total, 0.0)
        back_own()

    @pl.when(t == 1)
    def _():
        r.embd[:, 0:D] = r.emb[0:1, :]
        r.embd[:, D:] = jnp.broadcast_to(shrink[0:1, :], (1, LANES))
        r.dbuf[me] = r.embd[...]
        to_all(0, lambda j: r.embd, r.dbuf, r.s_doc, r.r_doc)
        pl.semaphore_signal(r.turn, inc=1, device_id=dev_c, device_id_type=MESH)
        pl.semaphore_wait(r.turn, 1)
        rest.start()
        norm_two_partner()
        got_rows(2, r.dpoolr)
        r.dpoolb[...] = r.dpoolr[...]
        back_partner()

    hidden_back(pl.ds(0, count))

    @pl.when(t == 1)
    def _():
        from_all(r.cbuf, r.s_slope, r.r_slope)
        row = slope_back(doc_slope(), r.emb[0:1, :], shrink[0:1, :])
        r.dpool[...] = jnp.broadcast_to(row, (8, D))
        back_own()

    @pl.when(t == 0)
    def _():
        norm_two_partner()
        from_all(r.cbuf, r.s_slope_q, r.r_slope, True)
        doc = r.dbuf[me]
        row = slope_back(doc_slope(), doc[:, 0:D], doc[:, D : D + 1])
        r.dpoolb[...] = jnp.broadcast_to(row, (8, D))
        back_partner()

    hidden_back(pl.ds(count, count))
    rest.wait_send()
    send(t == 0, copy(r.embq, r.qrecv, r.s_query.at[0], r.r_query.at[0], dev_y), tail)

    def along(step):
        for s in range(1, line):
            yield line - s, both(z == step, z < line - s), z + 1, 0
        for s in range(line - 1):
            yield s, both(z == line - 1 - step, z > s), z - 1, 1

    def added(refs):
        total = refs[0][...].astype(F32)
        for ref in refs[1:]:
            total = total + ref[...].astype(F32)
        return total

    def line_step(step, parts, sem, slot, nth):
        for k, (dest, cond, nxt, way) in enumerate(along(step)):
            if k % (line - 1) != nth:
                continue
            into = slot(dest + 1 if way == 0 else dest)
            refs = parts(dest)

            def move(into=into, refs=refs, dest=dest, way=way):
                if step:
                    copy(into, into, r.s_query.at[0], sem(1, way, dest), dev_x).wait_recv()
                    refs[0][...] = added(refs + (into,)).astype(BF)
                else:
                    refs[0][...] = added(refs).astype(BF)

            do(cond, move)
            send(cond, copy(refs[0], into, sem(0, way, dest), sem(1, way, dest),
                            dev_z(nxt)), tail)

    def line_end(parts, sem, slot, put):
        for cond, ways in ((z == 0, (1,)), (z == line - 1, (0,)),
                           (both(z > 0, z < line - 1), (0, 1))):
            def finish(ways=ways):
                refs = parts(z)
                for way in ways:
                    into = slot(z + 1 if way == 0 else z)
                    copy(into, into, r.s_query.at[0], sem(1, way, z), dev_x).wait_recv()
                    refs = refs + (into,)
                put[...] = added(refs).astype(BF)

            do(cond, finish)

    gd = r.gd

    def down_grad(s):
        val = jnp.dot(r.hidt[pl.ds(s * stripe, stripe), :], r.dbr[...],
                      preferred_element_type=F32)
        gd[s] = val.astype(BF).reshape(2, shard_ff, D)
        send(None, copy(gd.at[s, 1 - c], r.gd_rc.at[s], r.gd_c.at[0, s],
                        r.gd_c.at[1, s], dev_c), tail)

    def down_parts(dest):
        return gd.at[dest, c], r.gd_rc.at[dest]

    def down_arrive():
        for s in range(line):
            got(None, r.gd_rc.at[s], r.gd_c.at[1, s])

    def down_line(step, nth):
        line_step(step, down_parts, lambda *i: r.gd_z.at[i], lambda k: r.gd_rz.at[k], nth)

    def down_end():
        line_end(down_parts, lambda *i: r.gd_z.at[i], lambda k: r.gd_rz.at[k], r.gd_f)
        send(x != t, copy(r.gd_f, r.gd_rx, r.gd_x.at[0], r.gd_x.at[1], dev_x), tail)

    out_copies = []

    def keep_out(k, src, dst, cond=None):
        what = pltpu.make_async_copy(src, dst, r.fin.at[k])
        do(cond, what.start)
        out_copies.append((cond, what))

    def down_out():
        def total():
            copy(r.gd_rx, r.gd_rx, r.s_query.at[0], r.gd_x.at[1], dev_x).wait_recv()
            r.gd_f[...] = added((r.gd_f, r.gd_rx)).astype(BF)

        do(x == t, total)
        keep_out(0, r.gd_f, r.o_dn, x == t)
        send(x == t, copy(r.gd_f, r.o_dn, r.gd_y.at[0], r.gd_y.at[1], dev_y), tail)

    gg = r.gg
    part_gu = ff // 4

    def gate_grad(k):
        span = pl.ds(k * part_gu, part_gu)
        val = jnp.dot(r.feedt[...], r.dgu[:, span], preferred_element_type=F32)
        gg[:, :, :, :, span] = val.astype(BF).reshape(line, 2, 2, shard, part_gu)
        send(None, copy(gg.at[:, :, 1 - c, :, span], r.gg_rc.at[:, :, :, span],
                        r.gg_c.at[0, k], r.gg_c.at[1, k], dev_c), tail)

    def gate_cross(k):
        span = pl.ds(k * part_gu, part_gu)
        got(None, r.gg_rc.at[:, :, :, span], r.gg_c.at[1, k])
        for s in range(line):
            mine_k = gg.at[s, 1 - x, c, :, span]
            mine_k[...] = added((mine_k, r.gg_rc.at[s, 1 - x, :, span])).astype(BF)
        send(None, copy(gg.at[:, 1 - x, c, :, span], r.gg_rx.at[:, :, span],
                        r.gg_x.at[0, k], r.gg_x.at[1, k], dev_x), tail)

    def gate_parts(k):
        span = pl.ds(k * part_gu, part_gu)
        return lambda dest: (gg.at[dest, x, c, :, span], r.gg_rc.at[dest, x, :, span],
                             r.gg_rx.at[dest, :, span])

    def gate_ready(k):
        span = pl.ds(k * part_gu, part_gu)
        got(None, r.gg_rx.at[:, :, span], r.gg_x.at[1, k])

    def gate_line(k, step, nth):
        span = pl.ds(k * part_gu, part_gu)
        line_step(step, gate_parts(k), lambda a, *i: r.gg_z.at[(a, k) + i],
                  lambda s: r.gg_rz.at[s, :, span], nth)

    def gate_end(k):
        span = pl.ds(k * part_gu, part_gu)
        line_end(gate_parts(k), lambda a, *i: r.gg_z.at[(a, k) + i], lambda s: r.gg_rz.at[s, :, span],
                 r.gg_f.at[:, span])
        keep_out(1 + k, r.gg_f.at[:, span], r.o_gu.at[t, :, span])
        send(None, copy(r.gg_f.at[:, span], r.o_gu.at[t, :, span], r.gg_y.at[0, k],
                        r.gg_y.at[1, k], dev_y), tail)

    ga = wg
    sizes = (3 * LANES, 3 * LANES, 3 * LANES, out_w)
    starts = (0, 3 * LANES, 6 * LANES, third)

    def cols_a(k, h):
        return pl.ds(aligned(h * half_a + starts[k], LANES), sizes[k])

    def store_a(k, h, left, right):
        val = jnp.dot(left[...], right, preferred_element_type=F32)
        ga[:, :, :, :, cols_a(k, h)] = val.astype(BF).reshape(line, 2, 2, shard, sizes[k])
        send(None, copy(ga.at[:, :, 1 - c, :, cols_a(k, h)],
                        r.ga_rc.at[:, :, :, cols_a(k, h)],
                        r.ga_c.at[0, h, k], r.ga_c.at[1, h, k], dev_c), tail)

    def store_qkv(k, h):
        store_a(k, h, r.tokt, dqkv[:, pl.ds(aligned(h * third + starts[k], LANES), sizes[k])])

    def span_a(k):
        return pl.ds(starts[k], sizes[k])

    def tower_a(k):
        gone = cols_a(k, 1 - t)
        got(None, r.ga_rc.at[:, :, :, gone], r.ga_c.at[1, 1 - t, k])
        for s in range(line):
            for xx in range(2):
                ref = ga.at[s, xx, c, :, gone]
                ref[...] = added((ref, r.ga_rc.at[s, xx, :, gone])).astype(BF)
        send(None, copy(ga.at[:, :, c, :, gone], r.ga_rt.at[:, :, :, span_a(k)],
                        r.ga_t.at[0, k], r.ga_t.at[1, k], dev_y), tail)

    def cross_a(k):
        got(None, r.ga_rt.at[:, :, :, span_a(k)], r.ga_t.at[1, k])
        here = cols_a(k, t)
        got(None, r.ga_rc.at[:, :, :, here], r.ga_c.at[1, t, k])
        for s in range(line):
            ref = ga.at[s, 1 - x, c, :, here]
            ref[...] = added((ref, r.ga_rc.at[s, 1 - x, :, here],
                              r.ga_rt.at[s, 1 - x, :, span_a(k)])).astype(BF)
        send(None, copy(ga.at[:, 1 - x, c, :, here], r.ga_rx.at[:, :, span_a(k)],
                        r.ga_x.at[0, k], r.ga_x.at[1, k], dev_x), tail)

    def parts_a(k):
        here = cols_a(k, t)
        return lambda dest: (ga.at[dest, x, c, :, here], r.ga_rc.at[dest, x, :, here],
                             r.ga_rt.at[dest, x, :, span_a(k)],
                             r.ga_rx.at[dest, :, span_a(k)])

    def ready_a(k):
        got(None, r.ga_rx.at[:, :, span_a(k)], r.ga_x.at[1, k])

    def line_a(k, step, nth):
        line_step(step, parts_a(k), lambda a, *i: r.ga_z.at[(a, k) + i],
                  lambda s: r.ga_rz.at[s, :, span_a(k)], nth)

    def end_a(k):
        line_end(parts_a(k), lambda a, *i: r.ga_z.at[(a, k) + i], lambda s: r.ga_rz.at[s, :, span_a(k)],
                 r.ga_f.at[:, span_a(k)])
        keep_out(5 + k, r.ga_f.at[:, span_a(k)], r.o_a.at[:, cols_a(k, t)])
        send(None, copy(r.ga_f.at[:, span_a(k)], r.o_a.at[:, cols_a(k, t)],
                        r.ga_y.at[0, k], r.ga_y.at[1, k], dev_y), tail)

    some = 2 * 4 * shard

    def rows_of_weight(ref, j, lo, n):
        return ref[pl.ds(2 * j, 2), :, :, :, pl.ds(lo, n)].reshape(some, n)

    def feed_part(rows_of, j, store):
        store(j, pl.ds(j * some, some), dot_tt(r.dgu[rows_of, :], rows_of_weight(wg, j, 0, ff)))

    def back_send(j, span, val):
        r.dsend[:, span] = val.astype(BF)
        send(None, copy(r.dsend.at[:, span], r.drecv.at[:, span], r.s_back.at[j], r.r_back.at[j],
                        dev_y), tail)

    def feed_own(j, span, val):
        r.bown[:, span] = val

    def norm_one_back(b, sums):
        part = pl.ds(aligned(b * quarter, quarter), quarter)
        top = r.n1[part, :] + r.bown[part, :] + r.drecv[part, :].astype(F32)
        hat = r.h1[part, :]
        inner = top * r.vec[0:1, :]
        grad = r.rs1[part, :] * (
            inner - jnp.mean(inner, -1, keepdims=True)
            - hat * jnp.mean(inner * hat, -1, keepdims=True))
        r.n1[part, :] = grad
        r.datt[part, :] = grad.astype(BF)
        return (sums[0] + jnp.sum(top * hat, 0, keepdims=True),
                sums[1] + jnp.sum(top, 0, keepdims=True))

    def norm_back():
        for j in range(line // 2):
            got(None, r.drecv.at[:, pl.ds(j * some, some)], r.r_back.at[j])
        gain_one, bias_one = lax.fori_loop(0, blocks, norm_one_back, (zero_row, zero_row))
        r.ln[0] = (r.ln[0] + jnp.where(row8 == 0, gain_one, 0.0)
                   + jnp.where(row8 == 1, bias_one, 0.0))

    ln_peers = [dev_y, dev_c, dev_x]
    for bit in range(line.bit_length() - 1):
        apart = 1 << bit
        ln_peers.append(dev_z(z + apart * (1 - 2 * ((z // apart) % 2))))
    last = len(ln_peers)

    def small_sums(k):
        if k:
            got(None, r.lnr.at[k - 1], r.r_ln.at[k - 1])
            r.ln[k] = r.ln[k - 1] + r.lnr[k - 1]
        if k < last:
            send(None, copy(r.ln.at[k], r.lnr.at[k], r.s_ln.at[k], r.r_ln.at[k],
                            ln_peers[k]), tail)

    def out_grad():
        for h in range(2):
            store_a(3, h, r.mixt, r.datt[:, pl.ds(h * out_w, out_w)])

    def mix_back():
        lax.fori_loop(0, line // 2, mixed_back, 0)

    dqkv = r.dgu.at[pl.ds(0, count), pl.ds(0, 3 * D)]
    dmix = r.dgu.at[pl.ds(count, count), pl.ds(0, D)]

    def mixed_back(j, carry):
        val = sum(dot_tt(r.datt[:, pl.ds(h * out_w, out_w)],
                         rows_of_weight(wa, j, h * half_a + third, out_w)) for h in range(2))
        dmix[:, pl.ds(aligned(j * some, LANES), some)] = val.astype(BF)
        return carry

    def attend_back(p):
        q2, k2, v2 = triple(p)
        o = aligned(p * LANES, LANES)
        dm2 = dmix[:, pl.ds(o, LANES)]
        parts = []
        for h in range(2):
            probs = r.probs[2 * p + h]
            dprobs = dot_tt(only(h, dm2), v2)
            mean = jnp.sum(probs * dprobs, -1, keepdims=True)
            dscores = (probs * (dprobs - mean)).astype(BF)
            parts.append((jnp.dot(dscores, k2, preferred_element_type=F32),
                          dot_t0(dscores, q2), dot_t0(probs.astype(BF), dm2)))
        dq, dk, dv = (jnp.where(first_head, a, b) for a, b in zip(*parts))
        half = p // half_pairs
        o = half * third + (p - half * half_pairs) * LANES
        for k, part in enumerate((turn_back(dq * scale), turn_back(dk), dv)):
            dqkv[:, pl.ds(aligned(o + k * half_d, LANES), LANES)] = part.astype(BF)

    def token_back(j, carry):
        val = sum(dot_tt(dqkv[:, pl.ds(h * third, third)],
                         rows_of_weight(wa, j, h * half_a, third)) for h in range(2))
        span = pl.ds(aligned(j * some, LANES), some)
        r.xh2[:, span] = r.n1[:, span] + val
        return carry

    gate_grad(0)
    feed_part(theirs, 0, back_send)
    down_grad(1)
    down_grad(0)
    gate_cross(0)
    down_grad(3)
    down_grad(2)
    feed_part(theirs, 1, back_send)
    down_arrive()
    down_line(0, 0)
    gate_grad(1)
    down_line(0, 1)
    gate_grad(2)
    feed_part(mine, 0, feed_own)
    gate_cross(1)
    gate_grad(3)
    down_line(0, 2)
    feed_part(mine, 1, feed_own)
    gate_ready(0)
    norm_back()
    settle(pending)
    out_grad()
    gate_cross(3)
    small_sums(0)
    down_line(1, 0)
    mix_back()
    over_pairs(1 - t, attend_back, 0, 1)
    tower_a(3)
    gate_cross(2)
    over_pairs(1 - t, attend_back, 1, 3)
    store_qkv(0, 1 - t)
    over_pairs(t, attend_back, 0, 1)
    store_qkv(1, 1 - t)
    over_pairs(t, attend_back, 1, 2)
    gate_line(0, 0, 0)
    down_line(1, 1)
    tower_a(0)
    gate_line(0, 0, 1)
    down_line(2, 0)
    gate_ready(3)
    tower_a(1)
    over_pairs(t, attend_back, 2, 3)
    cross_a(3)
    store_qkv(2, 1 - t)
    gate_line(3, 0, 0)
    store_qkv(0, t)
    gate_line(0, 0, 2)
    store_qkv(2, t)
    gate_ready(2)
    gate_line(2, 0, 0)
    gate_line(3, 0, 1)
    tower_a(2)
    gate_line(0, 1, 0)
    cross_a(0)
    ready_a(3)
    gate_line(0, 2, 0)
    gate_line(3, 1, 0)
    gate_line(0, 1, 1)
    down_end()
    gate_ready(1)
    gate_line(1, 0, 0)
    gate_line(2, 1, 0)
    store_qkv(1, t)
    line_a(3, 1, 0)
    line_a(3, 0, 0)
    line_a(3, 0, 1)
    lax.fori_loop(0, line // 2, token_back, 0)
    keep_out(9, r.xh2, r.o_tok)
    gate_line(3, 1, 1)
    cross_a(1)
    gate_end(0)
    line_a(3, 2, 0)
    small_sums(1)
    gate_line(2, 2, 0)
    gate_line(2, 0, 1)
    gate_line(1, 0, 1)
    gate_line(1, 1, 0)
    line_a(3, 0, 2)
    gate_line(2, 0, 2)
    ready_a(0)
    down_out()
    gate_line(3, 0, 2)
    gate_line(2, 1, 1)
    line_a(0, 0, 0)
    line_a(3, 1, 1)
    gate_line(1, 1, 1)
    line_a(0, 0, 1)
    gate_line(3, 2, 0)
    cross_a(2)
    gate_end(2)
    ready_a(1)
    small_sums(2)
    line_a(1, 0, 0)
    gate_line(1, 2, 0)
    line_a(1, 0, 2)
    line_a(0, 1, 0)
    line_a(1, 0, 1)
    line_a(1, 1, 0)
    ready_a(2)
    line_a(2, 0, 0)
    end_a(3)
    line_a(1, 1, 1)
    gate_end(3)
    gate_line(1, 0, 2)
    line_a(0, 2, 0)
    line_a(2, 0, 1)
    line_a(2, 1, 0)
    line_a(0, 0, 2)
    line_a(1, 2, 0)
    line_a(0, 1, 1)
    line_a(2, 0, 2)
    gate_end(1)
    small_sums(3)
    line_a(2, 1, 1)
    line_a(2, 2, 0)
    end_a(0)
    end_a(1)
    small_sums(4)
    end_a(2)
    small_sums(5)

    r.o_vec[...] = r.ln[last]
    r.o_loss[...] = r.ln[last][:, 0:LANES] * (1.0 / (groups * QPD))

    r.o_d[...] = r.dbuf[me, :, pl.ds(0, D)]

    def sent(ssem, src, others=False):
        def body(step, carry):
            copy(src, src, ssem.at[(me + step) % groups], r.r_query.at[0], dev_x).wait_send()
            return carry

        lax.fori_loop(1 if others else 0, groups, body, 0)

    @pl.when(t == 0)
    def _():
        r.o_q[...] = r.embq[...]
        sent(r.s_slope, r.csend.at[0])
        sent(r.s_slope_q, r.csend.at[0], True)

    @pl.when(t == 1)
    def _():
        got(None, r.qrecv, r.r_query.at[0])
        r.o_q[...] = r.qrecv[...]
        sent(r.s_doc, r.embd)

    got(x != t, r.o_dn, r.gd_y.at[1])
    for k in range(4):
        got(None, r.o_gu.at[1 - t, :, pl.ds(k * part_gu, part_gu)], r.gg_y.at[1, k])
        got(None, r.o_a.at[:, cols_a(k, 1 - t)], r.ga_y.at[1, k])
    for cond, what in out_copies:
        do(cond, what.wait)
    settle(tail)


def finish(plan, *refs):
    (a_ref, gu_ref, dn_ref, vec_ref, tok_ref, q_ref, d_ref, loss_ref,
     o_loss, o_q, o_d, o_tok, o_qkv, o_out, o_gate, o_up, o_down, *o_vecs) = refs
    third, half_a, half_ff, stripe = 3 * D // 2, plan.half_a, plan.half_ff, plan.stripe
    out_w = half_a - third
    for h in range(2):
        for k in range(3):
            o_qkv[:, pl.ds(k * D + h * (D // 2), D // 2)] = (
                a_ref[:, pl.ds(h * half_a + k * (D // 2), D // 2)].astype(F32))
        o_out[:, h * out_w : (h + 1) * out_w] = (
            a_ref[:, h * half_a + third : (h + 1) * half_a].astype(F32))
        for s in range(plan.line):
            to = pl.ds((2 * s + h) * stripe, stripe)
            per_part, part_ff = plan.line // 2, half_ff // 2
            lo = 2 * (s // per_part) * part_ff + (s % per_part) * stripe
            o_gate[:, to] = gu_ref[h, :, pl.ds(lo, stripe)].astype(F32)
            o_up[:, to] = gu_ref[h, :, pl.ds(lo + part_ff, stripe)].astype(F32)
    o_down[...] = dn_ref[...].astype(F32)
    o_tok[0] = tok_ref[...]
    o_q[...] = q_ref[...]
    o_d[...] = d_ref[...]
    o_loss[...] = loss_ref[4:5, 0:1]
    first = lax.axis_index(DP) * plan.vec
    row = lax.broadcasted_iota(jnp.int32, (D, LANES), 0)
    col = lax.broadcasted_iota(jnp.int32, (D, LANES), 1)
    pick = jnp.where(row == first + col, 1.0, 0.0)
    own = jnp.dot(vec_ref[...], pick, preferred_element_type=F32, precision=exact_product_accuracy)
    for k, out in enumerate(o_vecs):
        out[...] = own[k : k + 1, 0 : plan.vec]


def on_device_kernel(plan, tokens, query_lengths, doc_lengths, positives, w_qkv, w_out, w_gate,
                     w_up, w_down, ln1_gain, first_layernorm_shift, ln2_gain, ln2_bias):
    count, groups, shard, vec = plan.count, plan.groups, plan.shard, plan.vec
    cosines, sines = rotary_constants(count)
    vmem = pl.BlockSpec(memory_space=pltpu.VMEM)
    smem = pl.BlockSpec(memory_space=pltpu.SMEM)
    hbm = pl.BlockSpec(memory_space=pl.ANY)
    shape = jax.ShapeDtypeStruct
    made = pl.pallas_call(
        functools.partial(whole_step, plan),
        out_shape=(
            shape((count, D), F32), shape((shard, plan.width_a), BF), shape((2, shard, plan.ff), BF),
            shape((plan.shard_ff, D), BF), shape((8, D), F32), shape((QPD, D), F32),
            shape((1, D), F32), shape((8, LANES), F32),
        ),
        in_specs=[smem] * 3 + [hbm] * 3 + [vmem] * 4 + [hbm] * 5,
        out_specs=(hbm, hbm, hbm, hbm, vmem, vmem, vmem, vmem),
        scratch_shapes=list(buffers(plan).values()) + list(semaphores(plan).values()),
        compiler_params=pltpu.CompilerParams(
            collective_id=0, has_side_effects=True, vmem_limit_bytes=63 * 1000 * 1000),
        name="whole_step",
    )(query_lengths, doc_lengths, positives, tokens[0], cosines, sines, ln1_gain[None],
      first_layernorm_shift[None], ln2_gain[None], ln2_bias[None],
      w_qkv, w_out, w_gate, w_up, w_down)
    o_tok, o_a, o_gu, o_dn, o_vec, o_q, o_d, o_loss = made
    outs = pl.pallas_call(
        functools.partial(finish, plan),
        out_shape=(
            shape((1, 1), F32), shape((QPD, D), F32), shape((1, D), F32),
            shape((1, count, D), F32), shape((shard, 3 * D), F32), shape((shard, D), F32),
            shape((shard, plan.ff), F32), shape((shard, plan.ff), F32),
            shape((plan.shard_ff, D), F32),
        ) + (shape((1, vec), F32),) * 4,
        in_specs=[vmem] * 8,
        out_specs=[vmem] * 13,
        name="finish",
    )(o_a, o_gu, o_dn, o_vec, o_tok, o_q, o_d, o_loss)
    return (outs[0].reshape(()),) + tuple(outs[1:9]) + tuple(v.reshape(vec) for v in outs[9:])


def fits(plan, towers):
    line = plan.line
    return (towers == 2 and plan.groups % 4 == 0 and line == 4
            and plan.shard % 16 == 0 and plan.shard_ff % 16 == 0 and plan.stripe % LANES == 0
            and plan.count == QPD * QLEN)


def solution(mesh):
    groups = mesh.shape[DP]

    def local_step(*args):
        plan = Plan(groups, args[0].shape[1], args[4].shape[0], args[8].shape[0], args[9].shape[0])
        if fits(plan, mesh.shape[TOWER]):
            return on_device_kernel(plan, *args)
        return on_device(*args)

    return jax.shard_map(
        local_step,
        mesh=mesh,
        in_specs=(
            P(TOWER, DP, None),
            P(DP),
            P(DP),
            P(),
            P(DP, None),
            P(DP, None),
            P(DP, None),
            P(DP, None),
            P(DP, None),
            P(DP),
            P(DP),
            P(DP),
            P(DP),
        ),
        out_specs=(
            P(),
            P(DP, None),
            P(DP, None),
            P(TOWER, DP, None),
            P(DP, None),
            P(DP, None),
            P(DP, None),
            P(DP, None),
            P(DP, None),
            P(DP),
            P(DP),
            P(DP),
            P(DP),
        ),
        check_vma=False,
    )
```

```python
import functools
from types import SimpleNamespace
from typing import Any, NamedTuple

import jax
import jax.numpy as jnp
import numpy as np
from jax import lax
from jax.experimental import pallas as pl
from jax.experimental.pallas import tpu as pltpu
from jax.sharding import PartitionSpec as P

TOWER = "tower"
DP = "dp"
D = 768
HEADS = 12
HEAD = 64
QLEN = 64
QPD = 4


exact_product_accuracy = lax.Precision.HIGHEST
rope_base = 1000.0
contrast_sharpness_factor = 0.02


def product(left, right):
    return jnp.dot(left, right, preferred_element_type=jnp.float32)


def rotary_tables(places):
    freqs = jnp.power(rope_base, -2.0 * jnp.arange(HEAD // 2).astype(jnp.float32) / HEAD)
    angles = places[:, None] * freqs[None, :]
    return (jnp.cos(angles)[:, None, :], jnp.sin(angles)[:, None, :])


def rotate(values, cosines, sines):
    half_dim = values.shape[-1] // 2
    first = values[..., :half_dim]
    second = values[..., half_dim:]
    return jnp.concatenate(
        [first * cosines - second * sines, second * cosines + first * sines], axis=-1
    )


def layer_norm(hidden, gain, offset):
    average = jnp.mean(hidden, -1, keepdims=True)
    centred = hidden - average
    variance = jnp.mean(centred * centred, -1, keepdims=True)
    return centred * lax.rsqrt(variance + 1e-05) * gain + offset


def normalize(pooled):
    return pooled * lax.rsqrt(jnp.sum(pooled * pooled, -1, keepdims=True) + 1e-06)


def layout(tower_id, query_len, doc_len, count):
    places = jnp.arange(count)
    span = jnp.where(tower_id == 0, QLEN, count)
    segment = places // span
    offset_in = places - segment * span
    slots = jnp.arange(QPD)
    seg_limit = jnp.where(tower_id == 0, query_len, doc_len[0] * jnp.ones_like(query_len))
    limit = jnp.sum(jnp.where(segment[:, None] == slots[None, :], seg_limit[None, :], 0), axis=1)
    valid = offset_in < limit
    allowed = (segment[:, None] == segment[None, :]) & valid[None, :]
    member = (segment[None, :] == slots[:, None]) & valid[None, :]
    pool_matrix = jnp.where(member, 1.0 / seg_limit[:, None].astype(jnp.float32), 0.0)
    return (offset_in.astype(jnp.float32), allowed, pool_matrix)


def swish_product(left, right):
    return jax.nn.silu(left) * right


def on_device(
    tokens,
    query_lengths,
    doc_lengths,
    positives,
    w_qkv,
    w_out,
    w_gate,
    w_up,
    w_down,
    ln1_gain,
    first_layernorm_shift,
    ln2_gain,
    ln2_bias,
):
    tower_id = lax.axis_index(TOWER)
    device_id = lax.axis_index(DP)
    groups = lax.axis_size(DP)
    full = (
        lax.all_gather(w_qkv, DP, axis=0, tiled=True),
        lax.all_gather(w_out, DP, axis=0, tiled=True),
        lax.all_gather(w_gate, DP, axis=0, tiled=True),
        lax.all_gather(w_up, DP, axis=0, tiled=True),
        lax.all_gather(w_down, DP, axis=0, tiled=True),
        lax.all_gather(ln1_gain, DP, axis=0, tiled=True),
        lax.all_gather(first_layernorm_shift, DP, axis=0, tiled=True),
        lax.all_gather(ln2_gain, DP, axis=0, tiled=True),
        lax.all_gather(ln2_bias, DP, axis=0, tiled=True),
    )
    qkv_full, out_full, gate_full, up_full, down_full = (
        full[0],
        full[1],
        full[2],
        full[3],
        full[4],
    )
    gain_one = full[5].astype(jnp.float32)
    bias_one = full[6].astype(jnp.float32)
    gain_two = full[7].astype(jnp.float32)
    bias_two = full[8].astype(jnp.float32)
    inputs = tokens[0]
    count = inputs.shape[0]
    places, allowed, pool_matrix = layout(tower_id, query_lengths, doc_lengths, count)
    cosines, sines = rotary_tables(places)
    packed = product(inputs, qkv_full)
    raw_query = packed[:, :D].reshape(count, HEADS, HEAD)
    raw_key = packed[:, D : 2 * D].reshape(count, HEADS, HEAD)

    def rotate_both(first, second):
        return (rotate(first, cosines, sines), rotate(second, cosines, sines))

    rotated, rotary_back = jax.vjp(rotate_both, raw_query, raw_key)
    query_low = rotated[0].astype(jnp.bfloat16)
    key_low = rotated[1].astype(jnp.bfloat16)
    value_low = packed[:, 2 * D :].reshape(count, HEADS, HEAD).astype(jnp.bfloat16)
    scale = HEAD ** (-0.5)

    def masked_scores():
        scores = (
            jnp.einsum("ihd,jhd->hij", query_low, key_low, preferred_element_type=jnp.float32)
            * scale
        )
        return jnp.where(allowed[None], scores, -1e30)

    scores = masked_scores()
    peak = jnp.max(scores, -1, keepdims=True)
    log_total = peak + jnp.log(jnp.sum(jnp.exp(scores - peak), -1, keepdims=True))
    probs_low = jnp.exp(scores - log_total).astype(jnp.bfloat16)
    mixed = jnp.einsum("hij,jhd->ihd", probs_low, value_low, preferred_element_type=jnp.float32)
    mixed_low = mixed.reshape(count, D).astype(jnp.bfloat16)
    attended = product(mixed_low, out_full)
    inputs_wide = inputs.astype(jnp.float32)
    normed_one, norm_one_back = jax.vjp(layer_norm, inputs_wide + attended, gain_one, bias_one)
    feed = normed_one.astype(jnp.bfloat16)
    gate = product(feed, gate_full)
    up_part = product(feed, up_full)
    hidden_wide, swish_back = jax.vjp(swish_product, gate, up_part)
    hidden = hidden_wide.astype(jnp.bfloat16)
    branch = product(hidden, down_full)
    normed_two, norm_two_back = jax.vjp(layer_norm, normed_one + branch, gain_two, bias_two)
    pooled = jnp.dot(pool_matrix, normed_two, precision=exact_product_accuracy)
    embedded, normal_back = jax.vjp(normalize, pooled)
    gathered = lax.all_gather(embedded, (TOWER, DP), axis=0, tiled=True)
    queries_total = groups * QPD
    gathered_query_rows = gathered[:queries_total]
    gathered_document_rows = gathered[queries_total:].reshape(groups, QPD, D)[:, 0]
    pairwise_affinity_matrix = (
        jnp.dot(gathered_query_rows, gathered_document_rows.T, precision=exact_product_accuracy)
        / contrast_sharpness_factor
    )
    peak_logit = jnp.max(pairwise_affinity_matrix, -1, keepdims=True)
    log_partition_norm = peak_logit + jnp.log(
        jnp.sum(jnp.exp(pairwise_affinity_matrix - peak_logit), -1, keepdims=True)
    )
    columns = lax.broadcasted_iota(jnp.int32, pairwise_affinity_matrix.shape, 1)
    matching_labels = columns == positives[:, None]
    picked = jnp.sum(jnp.where(matching_labels, pairwise_affinity_matrix, 0.0), -1, keepdims=True)
    total = jnp.sum(log_partition_norm - picked)
    loss = total / queries_total
    similarity_gradient = (
        jnp.exp(pairwise_affinity_matrix - log_partition_norm) - matching_labels.astype(jnp.float32)
    ) / contrast_sharpness_factor
    own_rows = lax.dynamic_slice_in_dim(similarity_gradient, device_id * QPD, QPD, 0)
    query_side = jnp.dot(own_rows, gathered_document_rows, precision=exact_product_accuracy)
    own_column = lax.dynamic_slice_in_dim(similarity_gradient, device_id, 1, 1)
    doc_side = jnp.dot(own_column.T, gathered_query_rows, precision=exact_product_accuracy)
    doc_side = jnp.concatenate([doc_side, jnp.zeros((QPD - 1, D), jnp.float32)], 0)
    embed_grad = jnp.where(tower_id == 0, query_side, doc_side)
    pooled_grad = normal_back(embed_grad)[0]
    top_grad = jnp.dot(pool_matrix.T, pooled_grad, precision=exact_product_accuracy)
    sum_two, gain_two_grad, bias_two_grad = norm_two_back(top_grad)
    attention_input_cotangent, out_back, gate_back, up_back, down_back = (
        qkv_full,
        out_full,
        gate_full,
        up_full,
        down_full,
    )
    branch_low = sum_two.astype(jnp.bfloat16)
    down_grad = product(hidden.T, branch_low)
    hidden_grad = product(branch_low, down_back.T)
    gate_grad_wide, up_grad_wide = swish_back(hidden_grad)
    gate_low = gate_grad_wide.astype(jnp.bfloat16)
    up_low = up_grad_wide.astype(jnp.bfloat16)
    gate_weight_grad = product(feed.T, gate_low)
    up_weight_grad = product(feed.T, up_low)
    feed_grad = sum_two + product(gate_low, gate_back.T) + product(up_low, up_back.T)
    sum_one, gain_one_grad, bias_one_grad = norm_one_back(feed_grad)
    attend_low = sum_one.astype(jnp.bfloat16)
    out_grad = product(mixed_low.T, attend_low)
    mixed_grad = product(attend_low, out_back.T).astype(jnp.bfloat16).reshape(count, HEADS, HEAD)
    probs_again = jnp.exp(masked_scores() - log_total)
    prob_grad = jnp.einsum(
        "ihd,jhd->hij", mixed_grad, value_low, preferred_element_type=jnp.float32
    )
    score_grad = probs_again * (prob_grad - jnp.sum(probs_again * prob_grad, -1, keepdims=True))
    score_low = score_grad.astype(jnp.bfloat16)
    query_grad = (
        jnp.einsum("hij,jhd->ihd", score_low, key_low, preferred_element_type=jnp.float32) * scale
    )
    key_grad = (
        jnp.einsum("hij,ihd->jhd", score_low, query_low, preferred_element_type=jnp.float32) * scale
    )
    value_grad = jnp.einsum(
        "hij,ihd->jhd",
        probs_again.astype(jnp.bfloat16),
        mixed_grad,
        preferred_element_type=jnp.float32,
    )
    raw_query_grad, raw_key_grad = rotary_back((query_grad, key_grad))
    packed_grad = jnp.concatenate(
        [
            raw_query_grad.reshape(count, D),
            raw_key_grad.reshape(count, D),
            value_grad.reshape(count, D),
        ],
        1,
    ).astype(jnp.bfloat16)
    qkv_grad = product(inputs.T, packed_grad)
    input_grad = sum_one + product(packed_grad, attention_input_cotangent.T)
    gradients = (
        qkv_grad,
        out_grad,
        gate_weight_grad,
        up_weight_grad,
        down_grad,
        gain_one_grad,
        bias_one_grad,
        gain_two_grad,
        bias_two_grad,
    )
    partial_sums = (
        lax.psum_scatter(gradients[0], DP, scatter_dimension=0, tiled=True),
        lax.psum_scatter(gradients[1], DP, scatter_dimension=0, tiled=True),
        lax.psum_scatter(gradients[2], DP, scatter_dimension=0, tiled=True),
        lax.psum_scatter(gradients[3], DP, scatter_dimension=0, tiled=True),
        lax.psum_scatter(gradients[4], DP, scatter_dimension=0, tiled=True),
        lax.psum_scatter(gradients[5], DP, scatter_dimension=0, tiled=True),
        lax.psum_scatter(gradients[6], DP, scatter_dimension=0, tiled=True),
        lax.psum_scatter(gradients[7], DP, scatter_dimension=0, tiled=True),
        lax.psum_scatter(gradients[8], DP, scatter_dimension=0, tiled=True),
    )
    tower_halves = (
        lax.psum_scatter(
            partial_sums[0].astype(jnp.bfloat16), TOWER, scatter_dimension=0, tiled=True
        ).astype(jnp.float32),
        lax.psum_scatter(
            partial_sums[1].astype(jnp.bfloat16), TOWER, scatter_dimension=0, tiled=True
        ).astype(jnp.float32),
        lax.psum_scatter(
            partial_sums[2].astype(jnp.bfloat16), TOWER, scatter_dimension=0, tiled=True
        ).astype(jnp.float32),
        lax.psum_scatter(
            partial_sums[3].astype(jnp.bfloat16), TOWER, scatter_dimension=0, tiled=True
        ).astype(jnp.float32),
        lax.psum_scatter(
            partial_sums[4].astype(jnp.bfloat16), TOWER, scatter_dimension=0, tiled=True
        ).astype(jnp.float32),
        lax.psum_scatter(
            partial_sums[5].astype(jnp.bfloat16), TOWER, scatter_dimension=0, tiled=True
        ).astype(jnp.float32),
        lax.psum_scatter(
            partial_sums[6].astype(jnp.bfloat16), TOWER, scatter_dimension=0, tiled=True
        ).astype(jnp.float32),
        lax.psum_scatter(
            partial_sums[7].astype(jnp.bfloat16), TOWER, scatter_dimension=0, tiled=True
        ).astype(jnp.float32),
        lax.psum_scatter(
            partial_sums[8].astype(jnp.bfloat16), TOWER, scatter_dimension=0, tiled=True
        ).astype(jnp.float32),
    )
    shares = (
        lax.all_gather(tower_halves[0].astype(jnp.bfloat16), TOWER, axis=0, tiled=True).astype(
            jnp.float32
        ),
        lax.all_gather(tower_halves[1].astype(jnp.bfloat16), TOWER, axis=0, tiled=True).astype(
            jnp.float32
        ),
        lax.all_gather(tower_halves[2].astype(jnp.bfloat16), TOWER, axis=0, tiled=True).astype(
            jnp.float32
        ),
        lax.all_gather(tower_halves[3].astype(jnp.bfloat16), TOWER, axis=0, tiled=True).astype(
            jnp.float32
        ),
        lax.all_gather(tower_halves[4].astype(jnp.bfloat16), TOWER, axis=0, tiled=True).astype(
            jnp.float32
        ),
        lax.all_gather(tower_halves[5].astype(jnp.bfloat16), TOWER, axis=0, tiled=True).astype(
            jnp.float32
        ),
        lax.all_gather(tower_halves[6].astype(jnp.bfloat16), TOWER, axis=0, tiled=True).astype(
            jnp.float32
        ),
        lax.all_gather(tower_halves[7].astype(jnp.bfloat16), TOWER, axis=0, tiled=True).astype(
            jnp.float32
        ),
        lax.all_gather(tower_halves[8].astype(jnp.bfloat16), TOWER, axis=0, tiled=True).astype(
            jnp.float32
        ),
    )
    query_rows = lax.dynamic_slice_in_dim(gathered_query_rows, device_id * QPD, QPD, 0)
    doc_row = lax.dynamic_slice_in_dim(gathered_document_rows, device_id, 1, 0)
    return (loss, query_rows, doc_row, input_grad[None]) + tuple(shares)


MESH = pl.DeviceIdType.MESH
BF = jnp.bfloat16
F32 = jnp.float32
LANES = 128


def dot_tt(left, right, precision=None):
    return lax.dot_general(
        left, right, (((1,), (1,)), ((), ())), preferred_element_type=F32, precision=precision
    )


def dot_t0(left, right, precision=None):
    return lax.dot_general(
        left, right, (((0,), (0,)), ((), ())), preferred_element_type=F32, precision=precision
    )


def rotary_constants(count):
    freqs = np.power(
        np.float32(rope_base), (-2.0 * np.arange(HEAD // 2) / HEAD).astype(np.float32)
    ).astype(np.float32)
    angles = (np.arange(count, dtype=np.float32)[:, None] * freqs[None, :]).astype(np.float64)
    cosines, sines = np.cos(angles), np.sin(angles)
    return (
        np.tile(np.concatenate([cosines, cosines], 1), (1, 2)).astype(np.float32),
        np.tile(np.concatenate([-sines, sines], 1), (1, 2)).astype(np.float32),
    )


def aligned(start, unit):
    return start if isinstance(start, int) else pl.multiple_of(start, unit)


def both(first, second):
    return jnp.logical_and(first, second)


def do(condition, action):
    if condition is None:
        action()
    else:
        pl.when(condition)(action)


class Plan:
    def __init__(self, groups, count, shard, shard_ff, vec):
        self.groups = groups
        self.line = groups // 4
        self.count = count
        self.shard = shard
        self.shard_ff = shard_ff
        self.vec = vec
        self.width_a = 4 * D
        self.half_a = 2 * D
        self.ff = shard_ff * groups
        self.half_ff = self.ff // 2
        self.stripe = 2 * shard_ff


def semaphores(plan):
    line, groups = plan.line, plan.groups
    dma = pltpu.SemaphoreType.DMA
    chunks_gu, chunks_a = 4, 4
    return dict(
        loc=dma((40,)),
        ra=dma((groups, 2)),
        sa_z=dma((2, line)),
        sa_x=dma((line, 2)),
        sa_y=dma((line, 2)),
        sa_c=dma((line, 2, 2)),
        rg=dma((groups, 2)),
        sg_z=dma((2, line, 2)),
        sg_x=dma((line, 2)),
        sg_c=dma((line, 2, 2)),
        rd=dma((line, 2, 2)),
        sd_x=dma((2,)),
        sd_z=dma((2, line, 2)),
        sd_c=dma((line, 2)),
        rv=dma((groups,)),
        sv=dma((groups,)),
        turn=pltpu.SemaphoreType.REGULAR,
        s_part=dma((D // (2 * LANES),)),
        r_part=dma((D // (2 * LANES),)),
        s_back=dma((line,)),
        r_back=dma((line,)),
        sx=dma((4,)),
        rx=dma((4,)),
        r_doc=dma((groups,)),
        s_doc=dma((groups,)),
        r_slope=dma((groups,)),
        s_slope=dma((groups,)),
        s_slope_q=dma((groups,)),
        r_query=dma((1,)),
        s_query=dma((1,)),
        s_ln=dma((line.bit_length() + 2,)),
        r_ln=dma((line.bit_length() + 2,)),
        gd_c=dma((2, line)),
        gd_z=dma((2, 2, line)),
        gd_x=dma((2,)),
        gd_y=dma((2,)),
        gg_c=dma((2, chunks_gu)),
        gg_x=dma((2, chunks_gu)),
        gg_z=dma((2, chunks_gu, 2, line)),
        gg_y=dma((2, chunks_gu)),
        ga_c=dma((2, 2, chunks_a)),
        ga_t=dma((2, chunks_a)),
        ga_x=dma((2, chunks_a)),
        ga_z=dma((2, chunks_a, 2, line)),
        ga_y=dma((2, chunks_a)),
        fin=dma((10,)),
    )


def buffers(plan):
    line, count, shard, groups = plan.line, plan.count, plan.shard, plan.groups
    pair = 2 * count
    v = pltpu.VMEM
    return dict(
        wa=v((line, 2, 2, shard, plan.width_a), BF),
        wg=v((line, 2, 2, shard, plan.ff), BF),
        wd=v((line, 2, plan.shard_ff, D), BF),
        tok=v((count, D), BF),
        vt=v((groups, 8, LANES), F32),
        vec=v((8, D), F32),
        cos=v((count, LANES), F32),
        sin=v((count, LANES), F32),
        hide=v((count, count), F32),
        pw=v((count, 1), F32),
        qkv=v((count, 3 * D), BF),
        probs=v((HEADS, count, count), F32),
        mixed=v((count, D), BF),
        mixt=v((D, count), BF),
        tokt=v((D, count), BF),
        h1=v((count, D), F32),
        rs1=v((count, 1), F32),
        n1=v((count, D), F32),
        feed=v((pair, D), BF),
        feedt=v((D, pair), BF),
        gate=v((pair, plan.half_ff), F32),
        up=v((pair, plan.half_ff), F32),
        hidt=v((plan.half_ff, pair), BF),
        dgu=v((pair, plan.ff), BF),
        bown=v((count, D), F32),
        bsend=v((count, D), BF),
        brecv=v((count, D), BF),
        xh2=v((count, D), F32),
        rs2=v((count, 1), F32),
        xh2b=v((count, D), F32),
        rs2b=v((count, 1), F32),
        pwb=v((count, 1), F32),
        brest=v((count, D), BF),
        dpoolb=v((8, D), F32),
        dpoolr=v((8, D), F32),
        dbr=v((pair, D), BF),
        dsend=v((count, D), BF),
        drecv=v((count, D), BF),
        datt=v((count, D), BF),
        pool=v((8, D), F32),
        dpool=v((8, D), F32),
        emb=v((8, D), F32),
        embd=v((1, D + LANES), F32),
        embq=v((QPD, D), F32),
        dbuf=v((groups, 1, D + LANES), F32),
        cbuf=v((groups, 1, D), F32),
        csend=v((groups, 1, D), F32),
        qrecv=v((QPD, D), F32),
        dflat=v((groups, D), F32),
        ln=v((line.bit_length() + 3, 8, D), F32),
        lnr=v((line.bit_length() + 2, 8, D), F32),
        gd=v((line, 2, plan.shard_ff, D), BF),
        gd_rc=v((line, plan.shard_ff, D), BF),
        gd_rz=v((line + 1, plan.shard_ff, D), BF),
        gd_rx=v((plan.shard_ff, D), BF),
        gd_f=v((plan.shard_ff, D), BF),
        gg=v((line, 2, 2, shard, plan.ff), BF),
        gg_rc=v((line, 2, shard, plan.ff), BF),
        gg_rx=v((line, shard, plan.ff), BF),
        gg_rz=v((line + 1, shard, plan.ff), BF),
        gg_f=v((shard, plan.ff), BF),
        ga_rc=v((line, 2, shard, plan.width_a), BF),
        ga_rt=v((line, 2, shard, plan.half_a), BF),
        ga_rx=v((line, shard, plan.half_a), BF),
        ga_rz=v((line + 1, shard, plan.half_a), BF),
        ga_f=v((shard, plan.half_a), BF),
    )


class Operands(NamedTuple):
    qlen: Any
    dlen: Any
    pos: Any
    i_tok: Any
    tcos: Any
    tsin: Any
    g_one: Any
    b_one: Any
    g_two: Any
    b_two: Any
    i_qkv: Any
    i_out: Any
    i_gate: Any
    i_up: Any
    i_down: Any


class Results(NamedTuple):
    o_tok: Any
    o_a: Any
    o_gu: Any
    o_dn: Any
    o_vec: Any
    o_q: Any
    o_d: Any
    o_loss: Any


def whole_step(plan, *refs):
    names = (Operands._fields + Results._fields + tuple(buffers(plan)) + tuple(semaphores(plan)))
    r = SimpleNamespace(**dict(zip(names, refs, strict=True)))
    line, groups, count = plan.line, plan.groups, plan.count
    shard, shard_ff, stripe = plan.shard, plan.shard_ff, plan.stripe
    half_a, half_ff, ff = plan.half_a, plan.half_ff, plan.ff
    quarter = QLEN
    shift = QLEN.bit_length() - 1

    t = lax.axis_index(TOWER)
    me = lax.axis_index(DP)
    z = me // 4
    x = (me // 2) % 2
    c = me % 2

    def at(zz, xx, cc):
        return (zz * 2 + xx) * 2 + cc

    dev_x = {TOWER: t, DP: at(z, 1 - x, c)}
    dev_c = {TOWER: t, DP: at(z, x, 1 - c)}
    dev_y = {TOWER: 1 - t, DP: me}

    def dev_z(zz):
        return {TOWER: t, DP: at(zz, x, c)}

    pending, tail = [], []

    def copy(src, dst, ssem, rsem, dev):
        return pltpu.make_async_remote_copy(
            src_ref=src, dst_ref=dst, send_sem=ssem, recv_sem=rsem,
            device_id=dev, device_id_type=MESH,
        )

    def send(cond, what, keep=pending):
        do(cond, what.start)
        keep.append((cond, what))

    def settle(keep):
        for cond, what in keep:
            do(cond, what.wait_send)
        keep.clear()

    def got(cond, ref, rsem):
        do(cond, copy(ref, ref, r.s_query.at[0], rsem, dev_x).wait_recv)

    wa, wg, wd = r.wa, r.wg, r.wd
    out_w = half_a - 3 * D // 2
    local = []

    def near(src, dst, cond=None):
        what = pltpu.make_async_copy(src, dst, r.loc.at[len(local)])
        do(cond, what.start)
        local.append((cond, what))

    third = 3 * D // 2
    half_d = D // 2
    for h in range(2):
        for k in range(3):
            near(r.i_qkv.at[:, pl.ds(k * D + h * half_d, half_d)],
                 wa.at[z, x, c, :, pl.ds(h * half_a + k * half_d, half_d)])
        near(r.i_out.at[:, pl.ds(h * out_w, out_w)],
             wa.at[z, x, c, :, pl.ds(h * half_a + third, out_w)])
    near(r.i_down, wd.at[z, c], x == t)
    near(r.i_tok, r.tok)
    for s in range(QPD):
        begin = aligned(s * QLEN * t, QLEN)
        near(r.tcos.at[pl.ds(begin, QLEN)], r.cos.at[pl.ds(s * QLEN, QLEN)])
        near(r.tsin.at[pl.ds(begin, QLEN)], r.sin.at[pl.ds(s * QLEN, QLEN)])
    part_ff = half_ff // 2
    per_part = line // 2

    def stripe_at(k, s):
        return (2 * (s // per_part) + k) * part_ff + (s % per_part) * stripe

    for s in range(line):
        for k, ref in enumerate((r.i_gate, r.i_up)):
            near(ref.at[:, pl.ds(aligned((2 * s + t) * stripe, LANES), stripe)],
                 wg.at[z, x, c, :, pl.ds(stripe_at(k, s), stripe)])

    r.vt[me] = jnp.zeros((8, LANES), F32)
    for k, ref in enumerate((r.g_one, r.b_one, r.g_two, r.b_two)):
        r.vt[me, pl.ds(k, 1), pl.ds(0, plan.vec)] = ref[...].astype(F32)

    barrier = pltpu.get_barrier_semaphore()

    for step in range(1, 2 * groups):
        other = (t * groups + me + step) % (2 * groups)
        pl.semaphore_signal(
            barrier, inc=1, device_id={TOWER: other // groups, DP: other % groups},
            device_id_type=MESH)
    pl.semaphore_wait(barrier, 2 * groups - 1)
    for cond, what in local:
        do(cond, what.wait)

    def piece_a(zz, xx, cc, h):
        return wa.at[zz, xx, cc, :, pl.ds(aligned(h * half_a, LANES), half_a)]

    def send_a(cond, sem, zz, xx, h, dev):
        ref = piece_a(zz, xx, c, h)
        send(cond, copy(ref, ref, sem, r.ra.at[at(zz, xx, c), h], dev))

    def got_a(cond, zz, xx, cc, h):
        got(cond, piece_a(zz, xx, cc, h), r.ra.at[at(zz, xx, cc), h])

    def sides(step):
        return ((z - step, z >= step, z < line - 1, z + 1), (z + step, z < line - step, z > 0, z - 1))

    def a_start():
        for way, (_, _, on, nxt) in enumerate(sides(0)):
            send_a(on, r.sa_z.at[way, z], z, x, t, dev_z(nxt))
        send_a(None, r.sa_x.at[z, t], z, x, t, dev_x)
        send_a(x != t, r.sa_x.at[z, 1 - t], z, x, 1 - t, dev_x)
        send_a(None, r.sa_c.at[z, x, t], z, x, t, dev_c)
        send_a(None, r.sa_c.at[z, x, 1 - t], z, x, 1 - t, dev_c)

    def a_round(step, way):
        zz, there, on, nxt = sides(step)[way]
        got_a(there, zz, x, c, t)
        send_a(both(there, on), r.sa_z.at[way, zz], zz, x, t, dev_z(nxt))
        send_a(there, r.sa_x.at[zz, t], zz, x, t, dev_x)
        send_a(there, r.sa_y.at[zz, x], zz, x, t, dev_y)
        send_a(there, r.sa_c.at[zz, x, t], zz, x, t, dev_c)

    def a_cross(step, way):
        zz, there, _, _ = sides(step)[way]
        got_a(there, zz, 1 - x, c, t)
        send_a(there if step else x == t, r.sa_y.at[zz, 1 - x], zz, 1 - x, t, dev_y)
        send_a(there, r.sa_c.at[zz, 1 - x, t], zz, 1 - x, t, dev_c)

    def a_tower(step, way):
        zz, there, _, _ = sides(step)[way]
        for xx in (x, 1 - x) if step else (1 - x,):
            got_a(there, zz, xx, c, 1 - t)
            send_a(there, r.sa_c.at[zz, xx, 1 - t], zz, xx, 1 - t, dev_c)

    def a_sibling(h):
        for zz in range(line):
            for xx in range(2):
                got_a(None, zz, xx, 1 - c, h)

    def piece_g(zz, xx, cc, h):
        return wg.at[zz, xx, cc, :, pl.ds(h * half_ff, half_ff)]

    def send_g(cond, sem, zz, xx, h, dev):
        ref = piece_g(zz, xx, c, h)
        send(cond, copy(ref, ref, sem, r.rg.at[at(zz, xx, c), h], dev))

    def got_g(cond, zz, xx, cc, h):
        got(cond, piece_g(zz, xx, cc, h), r.rg.at[at(zz, xx, cc), h])

    def g_start(h):
        for way, (_, _, on, nxt) in enumerate(sides(0)):
            send_g(on, r.sg_z.at[way, z, h], z, x, h, dev_z(nxt))

    def g_line(step, way, h):
        zz, there, on, nxt = sides(step)[way]
        got_g(there, zz, x, c, h)
        send_g(both(there, on), r.sg_z.at[way, zz, h], zz, x, h, dev_z(nxt))

    def g_spread(step, way, h):
        zz, there, _, _ = sides(step)[way]
        send_g(there, r.sg_x.at[zz, h], zz, x, h, dev_x)
        send_g(there, r.sg_c.at[zz, x, h], zz, x, h, dev_c)

    def g_cross(step, way, h):
        zz, there, _, _ = sides(step)[way]
        got_g(there, zz, 1 - x, c, h)
        send_g(there, r.sg_c.at[zz, 1 - x, h], zz, 1 - x, h, dev_c)

    def g_sibling(h):
        for zz in range(line):
            for xx in range(2):
                got_g(None, zz, xx, 1 - c, h)

    part_d = (pl.ds(0, 4 * LANES), pl.ds(4 * LANES, D - 4 * LANES))

    def send_d(cond, sem, zz, h, dev):
        ref = wd.at[zz, c, :, part_d[h]]
        send(cond, copy(ref, ref, sem, r.rd.at[zz, c, h], dev))

    def got_d(cond, zz, cc, h):
        got(cond, wd.at[zz, cc, :, part_d[h]], r.rd.at[zz, cc, h])

    def d_cross(h):
        send_d(x == t, r.sd_x.at[h], z, h, dev_x)

    def d_start(h):
        got_d(x != t, z, c, h)
        for way, (_, _, on, nxt) in enumerate(sides(0)):
            send_d(on, r.sd_z.at[way, z, h], z, h, dev_z(nxt))
        send_d(None, r.sd_c.at[z, h], z, h, dev_c)

    def d_round(step, way, ends, h):
        zz, there, on, nxt = sides(step)[way]
        cond = both(there, jnp.logical_not(on) if ends else on)
        got_d(cond, zz, c, h)
        if not ends:
            send_d(cond, r.sd_z.at[way, zz, h], zz, h, dev_z(nxt))
        send_d(cond, r.sd_c.at[zz, h], zz, h, dev_c)

    def d_sibling(h):
        for zz in range(line):
            got_d(None, zz, 1 - c, h)

    def v_send(j, carry):
        @pl.when(j != me)
        def _():
            copy(r.vt.at[me], r.vt.at[me], r.sv.at[j], r.rv.at[me],
                 {TOWER: t, DP: j}).start()

        return carry

    def v_wait(j, carry):
        @pl.when(j != me)
        def _():
            copy(r.vt.at[me], r.vt.at[j], r.sv.at[j], r.rv.at[j],
                 {TOWER: t, DP: j}).wait()

        return carry

    a_start()
    lax.fori_loop(0, groups, v_send, 0)

    tok = r.tok
    rows = lax.broadcasted_iota(jnp.int32, (count, count), 0)
    cols = lax.broadcasted_iota(jnp.int32, (count, count), 1)
    seg = cols >> shift
    limit = jnp.zeros_like(cols)
    for s in range(QPD):
        limit = jnp.where(seg == s, r.qlen[s], limit)
    limit = limit * (1 - t) + r.dlen[0] * t
    place = cols - seg * (quarter * (1 - t))
    apart = ((rows >> shift) - seg) * (1 - t)
    seen = both(apart == 0, place < limit)
    r.hide[...] = jnp.where(seen, 0.0, -1e30)
    for s in range(QPD):
        part = pl.ds(s * quarter, quarter)
        for tower, weights in ((t, r.pw), (1 - t, r.pwb)):
            length = jnp.full((quarter, 1), r.qlen[s] * (1 - tower) + r.dlen[0] * tower, jnp.int32)
            slot = lax.broadcasted_iota(jnp.int32, (quarter, 1), 0) + s * quarter * tower
            weights[part, :] = jnp.where(slot < length, 1.0 / length.astype(F32), 0.0)
    lanes = lax.broadcasted_iota(jnp.int32, (count, LANES), 1)
    first_head = lanes < HEAD
    low_half = (lanes & (HEAD - 1)) < HEAD // 2

    def swap(a):
        return jnp.where(low_half, pltpu.roll(a, LANES - HEAD // 2, 1), pltpu.roll(a, HEAD // 2, 1))

    def turn(a):
        return a * r.cos[...] + swap(a) * r.sin[...]

    def turn_back(a):
        return a * r.cos[...] - swap(a) * r.sin[...]

    def transpose_into(dst, src, width):
        def body(j, carry):
            o = aligned(j * LANES, LANES)
            dst[pl.ds(o, LANES), :] = src[:, pl.ds(o, LANES)].T
            return carry

        lax.fori_loop(0, width // LANES, body, 0)

    def wide(ref, lo, n):
        return ref[:, :, :, :, pl.ds(lo, n)].reshape(groups * shard, n)

    def widen_vec():
        lane = lax.broadcasted_iota(jnp.int32, (8, LANES), 1)
        parts = [jnp.zeros((8, LANES), F32) for _ in range(D // LANES)]
        for j in range(groups):
            block, first = divmod(j * plan.vec, LANES)
            piece = r.vt[j]
            if first:
                piece = pltpu.roll(piece, first, 1)
            parts[block] = parts[block] + jnp.where(lane >= first, piece, 0.0)
            if first + plan.vec > LANES:
                parts[block + 1] = parts[block + 1] + jnp.where(lane < first, piece, 0.0)
        r.vec[...] = jnp.concatenate(parts, axis=1)

    pairs = D // LANES
    half_pairs = pairs // 2

    scale = HEAD ** (-0.5)

    def project(h):
        for k in range(3):
            packed = jnp.dot(tok[...], wide(wa, aligned(h * half_a + k * half_d, LANES), half_d),
                             preferred_element_type=F32)
            for i in range(half_pairs):
                part = packed[:, i * LANES : (i + 1) * LANES]
                if k < 2:
                    part = turn(part)
                if k == 0:
                    part = part * scale
                r.qkv[:, pl.ds(aligned(k * D + h * half_d + i * LANES, LANES), LANES)] = (
                    part.astype(BF))

    def triple(p):
        o = aligned(p * LANES, LANES)
        return tuple(r.qkv[:, pl.ds(k * D + o, LANES)] for k in range(3))

    def only(h, a):
        return jnp.where(first_head if h == 0 else jnp.logical_not(first_head), a, jnp.zeros_like(a))

    def attend(p):
        q2, k2, v2 = triple(p)
        outs = []
        for h in range(2):
            scores = dot_tt(only(h, q2), k2) + r.hide[...]
            grown = jnp.exp(scores - jnp.max(scores, -1, keepdims=True))
            probs = grown * (1.0 / jnp.sum(grown, -1, keepdims=True))
            r.probs[2 * p + h] = probs
            outs.append(jnp.dot(probs.astype(BF), v2, preferred_element_type=F32))
        o = aligned(p * LANES, LANES)
        r.mixed[:, pl.ds(o, LANES)] = jnp.where(first_head, outs[0], outs[1]).astype(BF)

    def over_pairs(h, body, lo=0, hi=half_pairs):
        def step(i, carry):
            body(h * half_pairs + i)
            return carry

        lax.fori_loop(lo, hi, step, 0)

    def vectors():
        lax.fori_loop(0, groups, v_wait, 0)
        widen_vec()

    def out_project():
        for h in range(2):
            part = jnp.dot(r.mixed[...], wide(wa, h * half_a + third, out_w),
                           preferred_element_type=F32)
            r.h1[:, pl.ds(h * out_w, out_w)] = tok[:, pl.ds(h * out_w, out_w)].astype(F32) + part

    def moments(h):
        centred = h - jnp.mean(h, -1, keepdims=True)
        return centred, lax.rsqrt(jnp.mean(centred * centred, -1, keepdims=True) + 1e-05)

    blocks = count // quarter

    def norm_one(b, carry):
        part = pl.ds(aligned(b * quarter, quarter), quarter)
        centred, inverse = moments(r.h1[part, :])
        hat = centred * inverse
        normed = hat * r.vec[0:1, :] + r.vec[1:2, :]
        r.h1[part, :] = hat
        r.rs1[part, :] = inverse
        r.n1[part, :] = normed
        r.feed[pl.ds(aligned(t * count + b * quarter, quarter), quarter), :] = (
            normed.astype(BF))
        return carry

    mine = pl.ds(aligned(t * count, count), count)
    theirs = pl.ds(aligned((1 - t) * count, count), count)

    def swap_rows(k, src, dst):
        send(None, copy(src, dst, r.sx.at[k], r.rx.at[k], dev_y), tail)

    def got_rows(k, ref):
        got(None, ref, r.rx.at[k])

    def norm_rows():
        lax.fori_loop(0, blocks, norm_one, 0)
        swap_rows(0, r.feed.at[mine], r.feed.at[mine])

    step_ff = 2 * LANES

    steps_part = part_ff // step_ff

    def gated(part):
        def body(j, carry):
            o = aligned(part * part_ff + j * step_ff, step_ff)
            w = 2 * part * part_ff + j * step_ff
            gate = jnp.dot(r.feed[...], wide(wg, aligned(w, step_ff), step_ff),
                           preferred_element_type=F32)
            up = jnp.dot(r.feed[...], wide(wg, aligned(w + part_ff, step_ff), step_ff),
                         preferred_element_type=F32)
            r.gate[:, pl.ds(o, step_ff)] = gate
            r.up[:, pl.ds(o, step_ff)] = up
            r.dgu[:, pl.ds(o, step_ff)] = (gate * jax.nn.sigmoid(gate) * up).astype(BF)
            return carry

        lax.fori_loop(0, steps_part, body, 0)

    def down(rows_of, store, which=range(D // (2 * LANES))):
        def body(j):
            o = j * step_ff
            w = wd[:, :, :, pl.ds(o, step_ff)].reshape(half_ff, step_ff)
            store(o, jnp.dot(r.dgu[rows_of, pl.ds(0, half_ff)], w, preferred_element_type=F32))

        for j in which:
            body(j)

    def keep_send(o, val):
        span = pl.ds(o, step_ff)
        r.bsend[:, span] = val.astype(BF)
        send(None, copy(r.bsend.at[:, span], r.brecv.at[:, span], r.s_part.at[o // step_ff],
                        r.r_part.at[o // step_ff], dev_y), tail)

    def keep_own(o, val):
        r.bown[:, pl.ds(o, step_ff)] = val
        r.dsend[:, pl.ds(o, step_ff)] = val.astype(BF)

    rest = copy(r.dsend, r.brest, r.sx.at[1], r.rx.at[1], dev_y)

    def norm_two_partner():
        got_rows(1, r.brest)

        def body(b, carry):
            part = pl.ds(aligned(b * quarter, quarter), quarter)
            feed = r.feed[pl.ds(aligned((1 - t) * count + b * quarter, quarter), quarter), :]
            h = feed.astype(F32) + (r.bsend[part, :].astype(F32) + r.brest[part, :].astype(F32))
            centred, inverse = moments(h)
            r.xh2b[part, :] = centred * inverse
            r.rs2b[part, :] = inverse
            return carry

        lax.fori_loop(0, blocks, body, 0)

    d_cross(1)
    g_start(1)
    a_round(1, 0)
    a_cross(0, 0)
    a_round(1, 1)
    g_spread(0, 0, 0)
    d_cross(0)
    g_start(0)
    a_cross(1, 0)
    a_round(2, 1)
    a_round(2, 0)
    a_round(3, 0)
    g_line(1, 0, 1)
    vectors()
    transpose_into(r.tokt, tok, D)
    g_line(1, 0, 0)
    g_line(1, 1, 1)
    g_line(1, 1, 0)
    a_cross(1, 1)
    a_round(3, 1)
    a_tower(1, 0)
    g_spread(1, 1, 1)
    g_spread(1, 0, 0)
    d_start(1)
    g_line(2, 1, 1)
    d_round(1, 0, False, 1)
    a_tower(0, 0)
    g_spread(0, 0, 1)
    a_cross(2, 0)
    a_cross(2, 1)
    a_cross(3, 0)
    a_tower(1, 1)
    g_line(2, 0, 1)
    g_spread(2, 1, 1)
    g_line(2, 0, 0)
    a_cross(3, 1)
    d_round(1, 1, False, 1)
    d_round(2, 0, False, 1)
    a_sibling(t)
    project(t)
    over_pairs(t, attend, 0, 1)
    g_line(2, 1, 0)
    d_start(0)
    over_pairs(t, attend, 1, 2)
    a_tower(2, 1)
    a_tower(2, 0)
    g_spread(2, 0, 0)
    g_spread(2, 1, 0)
    g_spread(1, 0, 1)
    a_tower(3, 1)
    over_pairs(t, attend, 2, 3)
    g_line(3, 1, 1)
    a_tower(3, 0)
    g_cross(0, 0, 0)
    g_spread(3, 1, 1)
    g_cross(1, 1, 1)
    d_round(1, 1, True, 1)
    a_sibling(1 - t)
    project(1 - t)
    over_pairs(1 - t, attend, 0, 2)
    g_line(3, 0, 1)
    over_pairs(1 - t, attend, 2, 3)
    d_round(1, 1, False, 0)
    g_spread(2, 0, 1)
    out_project()
    g_line(3, 1, 0)
    d_round(2, 1, True, 1)
    g_spread(3, 1, 0)
    norm_rows()
    g_line(3, 0, 0)
    g_spread(3, 0, 1)
    g_cross(2, 1, 1)
    d_round(2, 0, True, 1)
    g_cross(1, 0, 0)
    d_round(1, 0, True, 1)
    d_round(2, 1, False, 1)
    transpose_into(r.mixt, r.mixed, D)
    d_round(1, 0, False, 0)
    g_spread(1, 1, 0)
    d_round(2, 1, False, 0)
    d_round(1, 1, True, 0)
    g_cross(2, 0, 0)
    g_cross(2, 0, 1)
    g_cross(3, 1, 0)
    g_cross(3, 1, 1)
    d_round(2, 0, False, 0)
    g_spread(3, 0, 0)
    g_cross(2, 1, 0)
    g_cross(0, 0, 1)
    d_round(3, 1, True, 1)
    g_cross(3, 0, 1)
    g_cross(1, 0, 1)
    g_sibling(1)
    d_round(3, 0, True, 1)
    d_round(2, 1, True, 0)
    d_round(2, 0, True, 0)
    d_round(1, 0, True, 0)
    g_cross(3, 0, 0)
    g_cross(1, 1, 0)
    got_rows(0, r.feed.at[theirs])
    gated(1)
    g_sibling(0)
    gated(0)
    d_sibling(1)
    down(theirs, keep_send, (2,))
    d_round(3, 1, True, 0)
    d_round(3, 0, True, 0)
    d_sibling(0)
    down(theirs, keep_send, (0, 1))
    down(mine, keep_own)
    transpose_into(r.feedt, r.feed, D)
    transpose_into(r.hidt, r.dgu, half_ff)

    def factors(j, carry):
        span = pl.ds(aligned(j * LANES, LANES), LANES)
        gate, up = r.gate[:, span], r.up[:, span]
        sig = jax.nn.sigmoid(gate)
        r.gate[:, span] = gate * sig
        r.up[:, span] = up * (sig * (1.0 + gate * (1.0 - sig)))
        return carry

    lax.fori_loop(0, half_ff // LANES, factors, 0)
    for j in range(D // step_ff):
        got(None, r.brecv.at[:, pl.ds(j * step_ff, step_ff)], r.r_part.at[j])
        if j == 0:
            do(t == 0, rest.start)

    r.pool[...] = jnp.zeros((8, D), F32)

    def norm_two(b, carry):
        part = pl.ds(aligned(b * quarter, quarter), quarter)
        h = r.n1[part, :] + (r.bown[part, :] + r.brecv[part, :].astype(F32))
        centred, inverse = moments(h)
        hat = centred * inverse
        normed = hat * r.vec[2:3, :] + r.vec[3:4, :]
        r.xh2[part, :] = hat
        r.rs2[part, :] = inverse
        r.pool[pl.ds(b, 1), :] = jnp.sum(normed * r.pw[part, :], 0, keepdims=True)
        return carry

    lax.fori_loop(0, blocks, norm_two, 0)
    row8 = lax.broadcasted_iota(jnp.int32, (8, D), 0)

    @pl.when(t == 1)
    def _():
        all_rows = jnp.sum(r.pool[...], 0, keepdims=True)
        r.pool[...] = jnp.where(row8 == 0, all_rows, 0.0)

    pooled = r.pool[...]
    shrink = lax.rsqrt(jnp.sum(pooled * pooled, -1, keepdims=True) + 1e-06)
    r.emb[...] = pooled * shrink

    best = exact_product_accuracy
    r.dpool[...] = jnp.zeros((8, D), F32)
    r.ln[0] = jnp.zeros((8, D), F32)

    def to_all(tower, src, dst, ssem, rsem, others=False):
        def give(step, carry):
            j = (me + step) % groups
            copy(src(j), dst.at[me], ssem.at[j], rsem.at[me], {TOWER: tower, DP: j}).start()
            return carry

        lax.fori_loop(1 if others else 0, groups, give, 0)

    def from_all(dst, ssem, rsem, others=False):
        def take(step, carry):
            j = (me + step) % groups
            copy(dst.at[j], dst.at[j], ssem.at[j], rsem.at[j], dev_x).wait_recv()
            return carry

        lax.fori_loop(1 if others else 0, groups, take, 0)

    zero_row = jnp.zeros((1, D), F32)

    def norm_two_back(weights, slopes, hats, inverses, tower, own):
        def body(b, sums):
            part = pl.ds(aligned(b * quarter, quarter), quarter)
            top = weights[part, :] * slopes[pl.ds(b, 1), :]
            hat = hats[part, :]
            inner = top * r.vec[2:3, :]
            grad = inverses[part, :] * (
                inner - jnp.mean(inner, -1, keepdims=True)
                - hat * jnp.mean(inner * hat, -1, keepdims=True))
            r.dbr[pl.ds(aligned(tower * count + b * quarter, quarter), quarter), :] = (
                grad.astype(BF))
            if not own:
                return sums
            r.n1[part, :] = grad
            return (sums[0] + jnp.sum(top * hat, 0, keepdims=True),
                    sums[1] + jnp.sum(top, 0, keepdims=True))

        sums = lax.fori_loop(0, blocks, body, (zero_row, zero_row))
        if own:
            r.ln[0] = (r.ln[0] + jnp.where(row8 == 2, sums[0], 0.0)
                       + jnp.where(row8 == 3, sums[1], 0.0))

    def back_own():
        norm_two_back(r.pw, r.dpool, r.xh2, r.rs2, t, True)

    def back_partner():
        norm_two_back(r.pwb, r.dpoolb, r.xh2b, r.rs2b, 1 - t, False)

    def hidden_back(rows_of):
        def body(j, carry):
            o = aligned(j * stripe, LANES)
            w = wd[j].reshape(stripe, D)
            slope = dot_tt(r.dbr[rows_of, :], w)
            w_at = aligned((2 * (j // per_part)) * part_ff + (j % per_part) * stripe, LANES)
            r.dgu[rows_of, pl.ds(w_at, stripe)] = (
                slope * r.up[rows_of, pl.ds(o, stripe)]).astype(BF)
            r.dgu[rows_of, pl.ds(aligned(w_at + part_ff, LANES), stripe)] = (
                slope * r.gate[rows_of, pl.ds(o, stripe)]).astype(BF)
            return carry

        lax.fori_loop(0, line, body, 0)

    def slope_back(slope, emb, scale_of):
        return scale_of * (slope - emb * jnp.sum(slope * emb, -1, keepdims=True))

    def doc_slope():
        total = r.cbuf[0]
        for j in range(1, groups):
            total = total + r.cbuf[j]
        return total

    pool_slope = copy(r.dpool, r.dpoolr, r.sx.at[2], r.rx.at[2], dev_y)
    tail.append((t == 0, pool_slope))

    @pl.when(t == 0)
    def _():
        r.embq[...] = r.emb[0:QPD, :]
        from_all(r.dbuf, r.s_doc, r.r_doc)
        for j in range(groups):
            r.dflat[pl.ds(j, 1), :] = r.dbuf[j, :, pl.ds(0, D)]
        docs, queries = r.dflat[...], r.embq[...]
        logits = dot_tt(queries, docs, best) / contrast_sharpness_factor
        peak = jnp.max(logits, -1, keepdims=True)
        lse = peak + jnp.log(jnp.sum(jnp.exp(logits - peak), -1, keepdims=True))
        col = lax.broadcasted_iota(jnp.int32, (QPD, groups), 1)
        row = lax.broadcasted_iota(jnp.int32, (QPD, groups), 0)
        label = jnp.zeros((QPD, groups), jnp.int32)
        for s in range(QPD):
            label = jnp.where(row == s, r.pos[me * QPD + s], label)
        hot = jnp.where(col == label, 1.0, 0.0)
        slope = (jnp.exp(logits - lse) - hot) / contrast_sharpness_factor
        back = dot_t0(slope, queries, best)
        for j in range(groups):
            r.csend[j] = back[j : j + 1, :]
        to_all(1, lambda j: r.csend.at[j], r.cbuf, r.s_slope, r.r_slope)
        to_all(0, lambda j: r.csend.at[j], r.cbuf, r.s_slope_q, r.r_slope, True)
        r.cbuf[me] = r.csend[me]
        r.dpool[0:QPD, :] = jnp.dot(slope, docs, preferred_element_type=F32, precision=best)
        r.dpool[...] = slope_back(r.dpool[...], r.emb[...], shrink)
        pool_slope.start()
        picked = jnp.sum(jnp.where(hot > 0.5, logits, 0.0), -1, keepdims=True)
        total = jnp.sum(lse - picked, 0, keepdims=True)
        r.ln[0] = jnp.where(row8 == 4, total, 0.0)
        back_own()

    @pl.when(t == 1)
    def _():
        r.embd[:, 0:D] = r.emb[0:1, :]
        r.embd[:, D:] = jnp.broadcast_to(shrink[0:1, :], (1, LANES))
        r.dbuf[me] = r.embd[...]
        to_all(0, lambda j: r.embd, r.dbuf, r.s_doc, r.r_doc)
        pl.semaphore_signal(r.turn, inc=1, device_id=dev_c, device_id_type=MESH)
        pl.semaphore_wait(r.turn, 1)
        rest.start()
        norm_two_partner()
        got_rows(2, r.dpoolr)
        r.dpoolb[...] = r.dpoolr[...]
        back_partner()

    hidden_back(pl.ds(0, count))

    @pl.when(t == 1)
    def _():
        from_all(r.cbuf, r.s_slope, r.r_slope)
        row = slope_back(doc_slope(), r.emb[0:1, :], shrink[0:1, :])
        r.dpool[...] = jnp.broadcast_to(row, (8, D))
        back_own()

    @pl.when(t == 0)
    def _():
        norm_two_partner()
        from_all(r.cbuf, r.s_slope_q, r.r_slope, True)
        doc = r.dbuf[me]
        row = slope_back(doc_slope(), doc[:, 0:D], doc[:, D : D + 1])
        r.dpoolb[...] = jnp.broadcast_to(row, (8, D))
        back_partner()

    hidden_back(pl.ds(count, count))
    rest.wait_send()
    send(t == 0, copy(r.embq, r.qrecv, r.s_query.at[0], r.r_query.at[0], dev_y), tail)

    def along(step):
        for s in range(1, line):
            yield line - s, both(z == step, z < line - s), z + 1, 0
        for s in range(line - 1):
            yield s, both(z == line - 1 - step, z > s), z - 1, 1

    def added(refs):
        total = refs[0][...].astype(F32)
        for ref in refs[1:]:
            total = total + ref[...].astype(F32)
        return total

    def line_step(step, parts, sem, slot, nth):
        for k, (dest, cond, nxt, way) in enumerate(along(step)):
            if k % (line - 1) != nth:
                continue
            into = slot(dest + 1 if way == 0 else dest)
            refs = parts(dest)

            def move(into=into, refs=refs, dest=dest, way=way):
                if step:
                    copy(into, into, r.s_query.at[0], sem(1, way, dest), dev_x).wait_recv()
                    refs[0][...] = added(refs + (into,)).astype(BF)
                else:
                    refs[0][...] = added(refs).astype(BF)

            do(cond, move)
            send(cond, copy(refs[0], into, sem(0, way, dest), sem(1, way, dest),
                            dev_z(nxt)), tail)

    def line_end(parts, sem, slot, put):
        for cond, ways in ((z == 0, (1,)), (z == line - 1, (0,)),
                           (both(z > 0, z < line - 1), (0, 1))):
            def finish(ways=ways):
                refs = parts(z)
                for way in ways:
                    into = slot(z + 1 if way == 0 else z)
                    copy(into, into, r.s_query.at[0], sem(1, way, z), dev_x).wait_recv()
                    refs = refs + (into,)
                put[...] = added(refs).astype(BF)

            do(cond, finish)

    gd = r.gd

    def down_grad(s):
        val = jnp.dot(r.hidt[pl.ds(s * stripe, stripe), :], r.dbr[...],
                      preferred_element_type=F32)
        gd[s] = val.astype(BF).reshape(2, shard_ff, D)
        send(None, copy(gd.at[s, 1 - c], r.gd_rc.at[s], r.gd_c.at[0, s],
                        r.gd_c.at[1, s], dev_c), tail)

    def down_parts(dest):
        return gd.at[dest, c], r.gd_rc.at[dest]

    def down_arrive():
        for s in range(line):
            got(None, r.gd_rc.at[s], r.gd_c.at[1, s])

    def down_line(step, nth):
        line_step(step, down_parts, lambda *i: r.gd_z.at[i], lambda k: r.gd_rz.at[k], nth)

    def down_end():
        line_end(down_parts, lambda *i: r.gd_z.at[i], lambda k: r.gd_rz.at[k], r.gd_f)
        send(x != t, copy(r.gd_f, r.gd_rx, r.gd_x.at[0], r.gd_x.at[1], dev_x), tail)

    out_copies = []

    def keep_out(k, src, dst, cond=None):
        what = pltpu.make_async_copy(src, dst, r.fin.at[k])
        do(cond, what.start)
        out_copies.append((cond, what))

    def down_out():
        def total():
            copy(r.gd_rx, r.gd_rx, r.s_query.at[0], r.gd_x.at[1], dev_x).wait_recv()
            r.gd_f[...] = added((r.gd_f, r.gd_rx)).astype(BF)

        do(x == t, total)
        keep_out(0, r.gd_f, r.o_dn, x == t)
        send(x == t, copy(r.gd_f, r.o_dn, r.gd_y.at[0], r.gd_y.at[1], dev_y), tail)

    gg = r.gg
    part_gu = ff // 4

    def gate_grad(k):
        span = pl.ds(k * part_gu, part_gu)
        val = jnp.dot(r.feedt[...], r.dgu[:, span], preferred_element_type=F32)
        gg[:, :, :, :, span] = val.astype(BF).reshape(line, 2, 2, shard, part_gu)
        send(None, copy(gg.at[:, :, 1 - c, :, span], r.gg_rc.at[:, :, :, span],
                        r.gg_c.at[0, k], r.gg_c.at[1, k], dev_c), tail)

    def gate_cross(k):
        span = pl.ds(k * part_gu, part_gu)
        got(None, r.gg_rc.at[:, :, :, span], r.gg_c.at[1, k])
        for s in range(line):
            mine_k = gg.at[s, 1 - x, c, :, span]
            mine_k[...] = added((mine_k, r.gg_rc.at[s, 1 - x, :, span])).astype(BF)
        send(None, copy(gg.at[:, 1 - x, c, :, span], r.gg_rx.at[:, :, span],
                        r.gg_x.at[0, k], r.gg_x.at[1, k], dev_x), tail)

    def gate_parts(k):
        span = pl.ds(k * part_gu, part_gu)
        return lambda dest: (gg.at[dest, x, c, :, span], r.gg_rc.at[dest, x, :, span],
                             r.gg_rx.at[dest, :, span])

    def gate_ready(k):
        span = pl.ds(k * part_gu, part_gu)
        got(None, r.gg_rx.at[:, :, span], r.gg_x.at[1, k])

    def gate_line(k, step, nth):
        span = pl.ds(k * part_gu, part_gu)
        line_step(step, gate_parts(k), lambda a, *i: r.gg_z.at[(a, k) + i],
                  lambda s: r.gg_rz.at[s, :, span], nth)

    def gate_end(k):
        span = pl.ds(k * part_gu, part_gu)
        line_end(gate_parts(k), lambda a, *i: r.gg_z.at[(a, k) + i], lambda s: r.gg_rz.at[s, :, span],
                 r.gg_f.at[:, span])
        keep_out(1 + k, r.gg_f.at[:, span], r.o_gu.at[t, :, span])
        send(None, copy(r.gg_f.at[:, span], r.o_gu.at[t, :, span], r.gg_y.at[0, k],
                        r.gg_y.at[1, k], dev_y), tail)

    ga = wg
    sizes = (3 * LANES, 3 * LANES, 3 * LANES, out_w)
    starts = (0, 3 * LANES, 6 * LANES, third)

    def cols_a(k, h):
        return pl.ds(aligned(h * half_a + starts[k], LANES), sizes[k])

    def store_a(k, h, left, right):
        val = jnp.dot(left[...], right, preferred_element_type=F32)
        ga[:, :, :, :, cols_a(k, h)] = val.astype(BF).reshape(line, 2, 2, shard, sizes[k])
        send(None, copy(ga.at[:, :, 1 - c, :, cols_a(k, h)],
                        r.ga_rc.at[:, :, :, cols_a(k, h)],
                        r.ga_c.at[0, h, k], r.ga_c.at[1, h, k], dev_c), tail)

    def store_qkv(k, h):
        store_a(k, h, r.tokt, dqkv[:, pl.ds(aligned(h * third + starts[k], LANES), sizes[k])])

    def span_a(k):
        return pl.ds(starts[k], sizes[k])

    def tower_a(k):
        gone = cols_a(k, 1 - t)
        got(None, r.ga_rc.at[:, :, :, gone], r.ga_c.at[1, 1 - t, k])
        for s in range(line):
            for xx in range(2):
                ref = ga.at[s, xx, c, :, gone]
                ref[...] = added((ref, r.ga_rc.at[s, xx, :, gone])).astype(BF)
        send(None, copy(ga.at[:, :, c, :, gone], r.ga_rt.at[:, :, :, span_a(k)],
                        r.ga_t.at[0, k], r.ga_t.at[1, k], dev_y), tail)

    def cross_a(k):
        got(None, r.ga_rt.at[:, :, :, span_a(k)], r.ga_t.at[1, k])
        here = cols_a(k, t)
        got(None, r.ga_rc.at[:, :, :, here], r.ga_c.at[1, t, k])
        for s in range(line):
            ref = ga.at[s, 1 - x, c, :, here]
            ref[...] = added((ref, r.ga_rc.at[s, 1 - x, :, here],
                              r.ga_rt.at[s, 1 - x, :, span_a(k)])).astype(BF)
        send(None, copy(ga.at[:, 1 - x, c, :, here], r.ga_rx.at[:, :, span_a(k)],
                        r.ga_x.at[0, k], r.ga_x.at[1, k], dev_x), tail)

    def parts_a(k):
        here = cols_a(k, t)
        return lambda dest: (ga.at[dest, x, c, :, here], r.ga_rc.at[dest, x, :, here],
                             r.ga_rt.at[dest, x, :, span_a(k)],
                             r.ga_rx.at[dest, :, span_a(k)])

    def ready_a(k):
        got(None, r.ga_rx.at[:, :, span_a(k)], r.ga_x.at[1, k])

    def line_a(k, step, nth):
        line_step(step, parts_a(k), lambda a, *i: r.ga_z.at[(a, k) + i],
                  lambda s: r.ga_rz.at[s, :, span_a(k)], nth)

    def end_a(k):
        line_end(parts_a(k), lambda a, *i: r.ga_z.at[(a, k) + i], lambda s: r.ga_rz.at[s, :, span_a(k)],
                 r.ga_f.at[:, span_a(k)])
        keep_out(5 + k, r.ga_f.at[:, span_a(k)], r.o_a.at[:, cols_a(k, t)])
        send(None, copy(r.ga_f.at[:, span_a(k)], r.o_a.at[:, cols_a(k, t)],
                        r.ga_y.at[0, k], r.ga_y.at[1, k], dev_y), tail)

    some = 2 * 4 * shard

    def rows_of_weight(ref, j, lo, n):
        return ref[pl.ds(2 * j, 2), :, :, :, pl.ds(lo, n)].reshape(some, n)

    def feed_part(rows_of, j, store):
        store(j, pl.ds(j * some, some), dot_tt(r.dgu[rows_of, :], rows_of_weight(wg, j, 0, ff)))

    def back_send(j, span, val):
        r.dsend[:, span] = val.astype(BF)
        send(None, copy(r.dsend.at[:, span], r.drecv.at[:, span], r.s_back.at[j], r.r_back.at[j],
                        dev_y), tail)

    def feed_own(j, span, val):
        r.bown[:, span] = val

    def norm_one_back(b, sums):
        part = pl.ds(aligned(b * quarter, quarter), quarter)
        top = r.n1[part, :] + r.bown[part, :] + r.drecv[part, :].astype(F32)
        hat = r.h1[part, :]
        inner = top * r.vec[0:1, :]
        grad = r.rs1[part, :] * (
            inner - jnp.mean(inner, -1, keepdims=True)
            - hat * jnp.mean(inner * hat, -1, keepdims=True))
        r.n1[part, :] = grad
        r.datt[part, :] = grad.astype(BF)
        return (sums[0] + jnp.sum(top * hat, 0, keepdims=True),
                sums[1] + jnp.sum(top, 0, keepdims=True))

    def norm_back():
        for j in range(line // 2):
            got(None, r.drecv.at[:, pl.ds(j * some, some)], r.r_back.at[j])
        gain_one, bias_one = lax.fori_loop(0, blocks, norm_one_back, (zero_row, zero_row))
        r.ln[0] = (r.ln[0] + jnp.where(row8 == 0, gain_one, 0.0)
                   + jnp.where(row8 == 1, bias_one, 0.0))

    ln_peers = [dev_y, dev_c, dev_x]
    for bit in range(line.bit_length() - 1):
        apart = 1 << bit
        ln_peers.append(dev_z(z + apart * (1 - 2 * ((z // apart) % 2))))
    last = len(ln_peers)

    def small_sums(k):
        if k:
            got(None, r.lnr.at[k - 1], r.r_ln.at[k - 1])
            r.ln[k] = r.ln[k - 1] + r.lnr[k - 1]
        if k < last:
            send(None, copy(r.ln.at[k], r.lnr.at[k], r.s_ln.at[k], r.r_ln.at[k],
                            ln_peers[k]), tail)

    def out_grad():
        for h in range(2):
            store_a(3, h, r.mixt, r.datt[:, pl.ds(h * out_w, out_w)])

    def mix_back():
        lax.fori_loop(0, line // 2, mixed_back, 0)

    dqkv = r.dgu.at[pl.ds(0, count), pl.ds(0, 3 * D)]
    dmix = r.dgu.at[pl.ds(count, count), pl.ds(0, D)]

    def mixed_back(j, carry):
        val = sum(dot_tt(r.datt[:, pl.ds(h * out_w, out_w)],
                         rows_of_weight(wa, j, h * half_a + third, out_w)) for h in range(2))
        dmix[:, pl.ds(aligned(j * some, LANES), some)] = val.astype(BF)
        return carry

    def attend_back(p):
        q2, k2, v2 = triple(p)
        o = aligned(p * LANES, LANES)
        dm2 = dmix[:, pl.ds(o, LANES)]
        parts = []
        for h in range(2):
            probs = r.probs[2 * p + h]
            dprobs = dot_tt(only(h, dm2), v2)
            mean = jnp.sum(probs * dprobs, -1, keepdims=True)
            dscores = (probs * (dprobs - mean)).astype(BF)
            parts.append((jnp.dot(dscores, k2, preferred_element_type=F32),
                          dot_t0(dscores, q2), dot_t0(probs.astype(BF), dm2)))
        dq, dk, dv = (jnp.where(first_head, a, b) for a, b in zip(*parts))
        half = p // half_pairs
        o = half * third + (p - half * half_pairs) * LANES
        for k, part in enumerate((turn_back(dq * scale), turn_back(dk), dv)):
            dqkv[:, pl.ds(aligned(o + k * half_d, LANES), LANES)] = part.astype(BF)

    def token_back(j, carry):
        val = sum(dot_tt(dqkv[:, pl.ds(h * third, third)],
                         rows_of_weight(wa, j, h * half_a, third)) for h in range(2))
        span = pl.ds(aligned(j * some, LANES), some)
        r.xh2[:, span] = r.n1[:, span] + val
        return carry

    gate_grad(0)
    feed_part(theirs, 0, back_send)
    down_grad(1)
    down_grad(0)
    gate_cross(0)
    down_grad(3)
    down_grad(2)
    feed_part(theirs, 1, back_send)
    down_arrive()
    down_line(0, 0)
    gate_grad(1)
    down_line(0, 1)
    gate_grad(2)
    feed_part(mine, 0, feed_own)
    gate_cross(1)
    gate_grad(3)
    down_line(0, 2)
    feed_part(mine, 1, feed_own)
    gate_ready(0)
    norm_back()
    settle(pending)
    out_grad()
    gate_cross(3)
    small_sums(0)
    down_line(1, 0)
    mix_back()
    over_pairs(1 - t, attend_back, 0, 1)
    tower_a(3)
    gate_cross(2)
    over_pairs(1 - t, attend_back, 1, 3)
    store_qkv(0, 1 - t)
    over_pairs(t, attend_back, 0, 1)
    store_qkv(1, 1 - t)
    over_pairs(t, attend_back, 1, 2)
    gate_line(0, 0, 0)
    down_line(1, 1)
    tower_a(0)
    gate_line(0, 0, 1)
    down_line(2, 0)
    gate_ready(3)
    tower_a(1)
    over_pairs(t, attend_back, 2, 3)
    cross_a(3)
    store_qkv(2, 1 - t)
    gate_line(3, 0, 0)
    store_qkv(0, t)
    gate_line(0, 0, 2)
    store_qkv(2, t)
    gate_ready(2)
    gate_line(2, 0, 0)
    gate_line(3, 0, 1)
    tower_a(2)
    gate_line(0, 1, 0)
    cross_a(0)
    ready_a(3)
    gate_line(0, 2, 0)
    gate_line(3, 1, 0)
    gate_line(0, 1, 1)
    down_end()
    gate_ready(1)
    gate_line(1, 0, 0)
    gate_line(2, 1, 0)
    store_qkv(1, t)
    line_a(3, 1, 0)
    line_a(3, 0, 0)
    line_a(3, 0, 1)
    lax.fori_loop(0, line // 2, token_back, 0)
    keep_out(9, r.xh2, r.o_tok)
    gate_line(3, 1, 1)
    cross_a(1)
    gate_end(0)
    line_a(3, 2, 0)
    small_sums(1)
    gate_line(2, 2, 0)
    gate_line(2, 0, 1)
    gate_line(1, 0, 1)
    gate_line(1, 1, 0)
    line_a(3, 0, 2)
    gate_line(2, 0, 2)
    ready_a(0)
    down_out()
    gate_line(3, 0, 2)
    gate_line(2, 1, 1)
    line_a(0, 0, 0)
    line_a(3, 1, 1)
    gate_line(1, 1, 1)
    line_a(0, 0, 1)
    gate_line(3, 2, 0)
    cross_a(2)
    gate_end(2)
    ready_a(1)
    small_sums(2)
    line_a(1, 0, 0)
    gate_line(1, 2, 0)
    line_a(1, 0, 2)
    line_a(0, 1, 0)
    line_a(1, 0, 1)
    line_a(1, 1, 0)
    ready_a(2)
    line_a(2, 0, 0)
    end_a(3)
    line_a(1, 1, 1)
    gate_end(3)
    gate_line(1, 0, 2)
    line_a(0, 2, 0)
    line_a(2, 0, 1)
    line_a(2, 1, 0)
    line_a(0, 0, 2)
    line_a(1, 2, 0)
    line_a(0, 1, 1)
    line_a(2, 0, 2)
    gate_end(1)
    small_sums(3)
    line_a(2, 1, 1)
    line_a(2, 2, 0)
    end_a(0)
    end_a(1)
    small_sums(4)
    end_a(2)
    small_sums(5)

    lane_row = lax.broadcasted_iota(jnp.int32, (D, LANES), 0)
    lane_col = lax.broadcasted_iota(jnp.int32, (D, LANES), 1)
    pick = jnp.where(lane_row == me * plan.vec + lane_col, 1.0, 0.0)
    r.o_vec[...] = jnp.dot(r.ln[last], pick, preferred_element_type=F32, precision=best)
    r.o_loss[...] = r.ln[last][:, 0:LANES] * (1.0 / (groups * QPD))

    r.o_d[...] = r.dbuf[me, :, pl.ds(0, D)]

    def sent(ssem, src, others=False):
        def body(step, carry):
            copy(src, src, ssem.at[(me + step) % groups], r.r_query.at[0], dev_x).wait_send()
            return carry

        lax.fori_loop(1 if others else 0, groups, body, 0)

    @pl.when(t == 0)
    def _():
        r.o_q[...] = r.embq[...]
        sent(r.s_slope, r.csend.at[0])
        sent(r.s_slope_q, r.csend.at[0], True)

    @pl.when(t == 1)
    def _():
        got(None, r.qrecv, r.r_query.at[0])
        r.o_q[...] = r.qrecv[...]
        sent(r.s_doc, r.embd)

    got(x != t, r.o_dn, r.gd_y.at[1])
    for k in range(4):
        got(None, r.o_gu.at[1 - t, :, pl.ds(k * part_gu, part_gu)], r.gg_y.at[1, k])
        got(None, r.o_a.at[:, cols_a(k, 1 - t)], r.ga_y.at[1, k])
    for cond, what in out_copies:
        do(cond, what.wait)
    settle(tail)


def finish(plan, *refs):
    (a_ref, gu_ref, dn_ref, vec_ref, tok_ref, q_ref, d_ref, loss_ref,
     o_loss, o_q, o_d, o_tok, o_qkv, o_out, o_gate, o_up, o_down, *o_vecs) = refs
    third, half_a, half_ff, stripe = 3 * D // 2, plan.half_a, plan.half_ff, plan.stripe
    out_w = half_a - third
    for h in range(2):
        for k in range(3):
            o_qkv[:, pl.ds(k * D + h * (D // 2), D // 2)] = (
                a_ref[:, pl.ds(h * half_a + k * (D // 2), D // 2)].astype(F32))
        o_out[:, h * out_w : (h + 1) * out_w] = (
            a_ref[:, h * half_a + third : (h + 1) * half_a].astype(F32))
        for s in range(plan.line):
            to = pl.ds((2 * s + h) * stripe, stripe)
            per_part, part_ff = plan.line // 2, half_ff // 2
            lo = 2 * (s // per_part) * part_ff + (s % per_part) * stripe
            o_gate[:, to] = gu_ref[h, :, pl.ds(lo, stripe)].astype(F32)
            o_up[:, to] = gu_ref[h, :, pl.ds(lo + part_ff, stripe)].astype(F32)
    o_down[...] = dn_ref[...].astype(F32)
    o_tok[0] = tok_ref[...]
    o_q[...] = q_ref[...]
    o_d[...] = d_ref[...]
    o_loss[...] = loss_ref[4:5, 0:1]
    for k, out in enumerate(o_vecs):
        out[...] = vec_ref[k : k + 1, 0 : plan.vec]


def on_device_kernel(plan, tokens, query_lengths, doc_lengths, positives, w_qkv, w_out, w_gate,
                     w_up, w_down, ln1_gain, first_layernorm_shift, ln2_gain, ln2_bias):
    count, groups, shard, vec = plan.count, plan.groups, plan.shard, plan.vec
    cosines, sines = rotary_constants(count)
    vmem = pl.BlockSpec(memory_space=pltpu.VMEM)
    smem = pl.BlockSpec(memory_space=pltpu.SMEM)
    hbm = pl.BlockSpec(memory_space=pl.ANY)
    shape = jax.ShapeDtypeStruct
    made = pl.pallas_call(
        functools.partial(whole_step, plan),
        out_shape=(
            shape((count, D), F32), shape((shard, plan.width_a), BF), shape((2, shard, plan.ff), BF),
            shape((plan.shard_ff, D), BF), shape((8, LANES), F32), shape((QPD, D), F32),
            shape((1, D), F32), shape((8, LANES), F32),
        ),
        in_specs=[smem] * 3 + [hbm] * 3 + [vmem] * 4 + [hbm] * 5,
        out_specs=(hbm, hbm, hbm, hbm, vmem, vmem, vmem, vmem),
        scratch_shapes=list(buffers(plan).values()) + list(semaphores(plan).values()),
        compiler_params=pltpu.CompilerParams(
            collective_id=0, has_side_effects=True, vmem_limit_bytes=63 * 1000 * 1000),
        name="whole_step",
    )(query_lengths, doc_lengths, positives, tokens[0], cosines, sines, ln1_gain[None],
      first_layernorm_shift[None], ln2_gain[None], ln2_bias[None],
      w_qkv, w_out, w_gate, w_up, w_down)
    o_tok, o_a, o_gu, o_dn, o_vec, o_q, o_d, o_loss = made
    outs = pl.pallas_call(
        functools.partial(finish, plan),
        out_shape=(
            shape((1, 1), F32), shape((QPD, D), F32), shape((1, D), F32),
            shape((1, count, D), F32), shape((shard, 3 * D), F32), shape((shard, D), F32),
            shape((shard, plan.ff), F32), shape((shard, plan.ff), F32),
            shape((plan.shard_ff, D), F32),
        ) + (shape((1, vec), F32),) * 4,
        in_specs=[vmem] * 8,
        out_specs=[vmem] * 13,
        name="finish",
    )(o_a, o_gu, o_dn, o_vec, o_tok, o_q, o_d, o_loss)
    return (outs[0].reshape(()),) + tuple(outs[1:9]) + tuple(v.reshape(vec) for v in outs[9:])


def fits(plan, towers):
    line = plan.line
    return (towers == 2 and plan.groups % 4 == 0 and line == 4
            and plan.shard % 16 == 0 and plan.shard_ff % 16 == 0 and plan.stripe % LANES == 0
            and plan.count == QPD * QLEN)


def solution(mesh):
    groups = mesh.shape[DP]

    def local_step(*args):
        plan = Plan(groups, args[0].shape[1], args[4].shape[0], args[8].shape[0], args[9].shape[0])
        if fits(plan, mesh.shape[TOWER]):
            return on_device_kernel(plan, *args)
        return on_device(*args)

    return jax.shard_map(
        local_step,
        mesh=mesh,
        in_specs=(
            P(TOWER, DP, None),
            P(DP),
            P(DP),
            P(),
            P(DP, None),
            P(DP, None),
            P(DP, None),
            P(DP, None),
            P(DP, None),
            P(DP),
            P(DP),
            P(DP),
            P(DP),
        ),
        out_specs=(
            P(),
            P(DP, None),
            P(DP, None),
            P(TOWER, DP, None),
            P(DP, None),
            P(DP, None),
            P(DP, None),
            P(DP, None),
            P(DP, None),
            P(DP),
            P(DP),
            P(DP),
            P(DP),
        ),
        check_vma=False,
    )
```
